32 devices in a mesh: section: 2 (over core), tensor: 4 (over z), dp: 4 (over y, x).
Axes of the slice: x: 2, y: 2, z: 4, core: 2. Of those that a mesh axis runs over, the one named last changes fastest.
Arguments:
- inputs: bfloat16 [2, 2560, 2048], P(None, 'dp'), may hold values from -6 to 6
- cotangent: bfloat16 [2, 2560, 2048], P(None, 'dp'), may hold values from -6 to 6
- seg_ids: int32 [2, 2560], replicated, may hold values from 0 to 12, as said below
- positions: int32 [2, 2560], replicated, may hold values from 0 to 1343, as said below
- parents: int32 [2, 13], replicated, may hold values from 0 to 12, as said below
- gain_attn: float32 [2, 2048], P('section', 'dp'), may hold values from 0.5 to 1.5
- w_query: float32 [2, 2048, 2048], P('section', 'dp', 'tensor'), may hold values from -0.125 to 0.125
- key_weight: float32 [2, 2048, 256], P('section', 'dp', 'tensor'), may hold values from -0.125 to 0.125
- value_weight: float32 [2, 2048, 256], P('section', 'dp', 'tensor'), may hold values from -0.125 to 0.125
- w_out: float32 [2, 2048, 2048], P('section', 'tensor', 'dp'), may hold values from -1 to 1
- gain_mlp: float32 [2, 2048], P('section', 'dp'), may hold values from 0.5 to 1.5
- w_gate: float32 [2, 2048, 5632], P('section', 'dp', 'tensor'), may hold values from -0.125 to 0.125
- w_up: float32 [2, 2048, 5632], P('section', 'dp', 'tensor'), may hold values from -0.125 to 0.125
- w_down: float32 [2, 5632, 2048], P('section', 'tensor', 'dp'), may hold values from -0.078125 to 0.078125
Outputs:
- layer_output: bfloat16 [2, 2, 2560, 2048], P('section', None, 'dp')
- input_grad: float32 [2, 2, 2560, 2048], P('section', None, 'dp')
- grad_gain_attn: float32 [2, 2048], P('section', 'dp')
- grad_w_query: float32 [2, 2048, 2048], P('section', 'dp', 'tensor')
- grad_w_key: float32 [2, 2048, 256], P('section', 'dp', 'tensor')
- grad_w_value: float32 [2, 2048, 256], P('section', 'dp', 'tensor')
- grad_w_out: float32 [2, 2048, 2048], P('section', 'tensor', 'dp')
- grad_gain_mlp: float32 [2, 2048], P('section', 'dp')
- grad_w_gate: float32 [2, 2048, 5632], P('section', 'dp', 'tensor')
- grad_w_up: float32 [2, 2048, 5632], P('section', 'dp', 'tensor')
- grad_w_down: float32 [2, 5632, 2048], P('section', 'tensor', 'dp')
The draws below stay inside these ranges and needn't reach their ends.
Inputs may be any that keep to these rules, and one draw needn't show every extreme that they name: `seg_ids`: each tree is a trunk of 1024 tokens followed by 4 groups of 384 tokens, each group a branch and then its two leaves with varying lengths; segment numbers label the tree's segments in a drawn order. `positions`: positions count along the trunk from 0 and go on along the branch and then the leaf. `parents`: the trunk's entry is its own number, a branch's is the trunk's, a leaf's is its branch's.
All inputs are finite; a program needn't handle non-finite values.
Results may differ from the reference program's by a relative error of at most 0.03.
Values may be sent and summed in bfloat16 or wider, within the bound.
A program may use at most 512 MiB of HBM per device.

```python
from functools import partial
import jax
import jax.numpy as jnp
from jax import lax

MODEL_DIMENSION = 2048
QUERY_HEAD_COUNT = 32
KEY_VALUE_HEADS = 4
HEAD_DIMENSION = 64
FF = 5632
TRUNK = 1024
BR = 128
LEAF = 128
NB = 4
MB = 2
TREE_TOKENS = 2560
SEGS = 13
N_SECTION = 2


def tree_layout(key):
    micro_keys = jax.random.split(jax.random.fold_in(key, 11), MB)
    group_len = BR + 2 * LEAF

    def one_tree(tree_key):
        perm_key, branch_key, leaf_key = jax.random.split(tree_key, 3)
        middle_labels = 1 + jax.random.permutation(perm_key, SEGS - 2).astype(jnp.int32)
        labels = jnp.concatenate([jnp.full((1,), SEGS - 1, jnp.int32), jnp.zeros((1,), jnp.int32), middle_labels]).astype(jnp.int32)
        branch_len = jax.random.randint(branch_key, (NB,), BR // 2, 3 * BR // 2 + 1, dtype=jnp.int32)
        branch_len = branch_len.at[0].set(BR // 2)
        rest_len = group_len - branch_len
        spread_len = rest_len - 2 * (LEAF // 2) + 1
        leaf_len = LEAF // 2 + jax.random.randint(leaf_key, (NB,), 0, 1 << 20, dtype=jnp.int32) % spread_len
        leaf_len = leaf_len.at[0].set(LEAF // 2)
        token_index = jnp.arange(TREE_TOKENS, dtype=jnp.int32)
        in_trunk = token_index < TRUNK
        offset = jnp.maximum(token_index - TRUNK, 0)
        group_index = jnp.minimum(offset // group_len, NB - 1)
        inside = offset - group_index * group_len
        branch_here = branch_len[group_index]
        leaf_here = leaf_len[group_index]
        in_branch = inside < branch_here
        in_first = inside < branch_here + leaf_here
        node_index = jnp.where(in_trunk, 0, jnp.where(in_branch, 1 + group_index, jnp.where(in_first, 1 + NB + 2 * group_index, 2 + NB + 2 * group_index)))
        depth_pos = jnp.where(in_trunk, token_index, TRUNK + jnp.where(in_branch, inside, branch_here + jnp.where(in_first, inside - branch_here, inside - branch_here - leaf_here)))
        node_ids = jnp.arange(SEGS, dtype=jnp.int32)
        parent_node = jnp.where(node_ids <= NB, 0, 1 + (node_ids - 1 - NB) // 2)
        parent_table = jnp.zeros((SEGS,), jnp.int32).at[labels].set(labels[parent_node])
        return (labels[node_index].astype(jnp.int32), depth_pos.astype(jnp.int32), parent_table)
    return jax.vmap(one_tree)(micro_keys)


def draw_seg_ids(key, part):
    return tree_layout(key)[0]


def draw_positions(key, part):
    return tree_layout(key)[1]


def draw_parents(key, part):
    return tree_layout(key)[2]


def levels(stream_key, dims, shards, low, top_value):
    level = 1.0
    for position, shards_of in shards:
        steps = jax.random.uniform(jax.random.fold_in(jax.random.fold_in(stream_key, 6), position), (shards_of,), jnp.float32, low / len(shards), top_value / len(shards))
        level = level * jnp.repeat(jnp.exp(steps), dims[position] // shards_of).reshape((-1,) + (1,) * (len(dims) - 1 - position))
    return level


def gaussian(key, dims, deviation, limit, shards=(), held_as=jnp.bfloat16):
    drawn = jax.random.normal(key, dims, jnp.float32) * deviation
    if len(shards) > 0:
        drawn = levels(key, dims, shards, -0.22, 0.18) * drawn
    return jnp.clip(drawn, min=-limit, max=limit).astype(held_as)


def setup_inputs(seed: int = 0) -> dict:
    key_list = jax.random.split(jax.random.key(seed), 15)
    return {
        "inputs": gaussian(key_list[0], (MB, TREE_TOKENS, MODEL_DIMENSION), 1.0, 6.0, ((1, 4),)),
        "cotangent": gaussian(key_list[1], (MB, TREE_TOKENS, MODEL_DIMENSION), 1.0, 6.0, ((1, 4),)),
        "seg_ids": draw_seg_ids(jax.random.fold_in(key_list[14], 71), 0),
        "positions": draw_positions(jax.random.fold_in(key_list[14], 71), 0),
        "parents": draw_parents(jax.random.fold_in(key_list[14], 71), 0),
        "gain_attn": jnp.clip(1.0 + 0.1 * jax.random.normal(key_list[5], (N_SECTION, MODEL_DIMENSION), jnp.float32), 0.5, 1.5),
        "w_query": gaussian(key_list[6], (N_SECTION, MODEL_DIMENSION, QUERY_HEAD_COUNT * HEAD_DIMENSION), MODEL_DIMENSION ** -0.5, 0.125, ((0, 2), (1, 4), (2, 4)), jnp.float32),
        "key_weight": gaussian(key_list[7], (N_SECTION, MODEL_DIMENSION, KEY_VALUE_HEADS * HEAD_DIMENSION), MODEL_DIMENSION ** -0.5, 0.125, ((0, 2), (1, 4), (2, 4)), jnp.float32),
        "value_weight": gaussian(key_list[8], (N_SECTION, MODEL_DIMENSION, KEY_VALUE_HEADS * HEAD_DIMENSION), MODEL_DIMENSION ** -0.5, 0.125, ((0, 2), (1, 4), (2, 4)), jnp.float32),
        "w_out": gaussian(key_list[9], (N_SECTION, QUERY_HEAD_COUNT * HEAD_DIMENSION, MODEL_DIMENSION), (QUERY_HEAD_COUNT * HEAD_DIMENSION // 64) ** -0.5, 1.0, ((0, 2), (1, 4), (2, 4)), jnp.float32),
        "gain_mlp": jnp.clip(1.0 + 0.1 * jax.random.normal(key_list[10], (N_SECTION, MODEL_DIMENSION), jnp.float32), 0.5, 1.5),
        "w_gate": gaussian(key_list[11], (N_SECTION, MODEL_DIMENSION, FF), MODEL_DIMENSION ** -0.5, 0.125, ((0, 2), (1, 4), (2, 4)), jnp.float32),
        "w_up": gaussian(key_list[12], (N_SECTION, MODEL_DIMENSION, FF), MODEL_DIMENSION ** -0.5, 0.125, ((0, 2), (1, 4), (2, 4)), jnp.float32),
        "w_down": gaussian(key_list[13], (N_SECTION, FF, MODEL_DIMENSION), FF ** -0.5, 0.078125, ((0, 2), (1, 4), (2, 4)), jnp.float32),
    }


EPSILON = 1e-05
THETA = 10000.0
MASKED = -1e+30

@jax.custom_vjp
def lower_precision(v):
    return lax.optimization_barrier(v.astype(jnp.bfloat16)).astype(jnp.float32)

@jax.custom_vjp
def lower_precision_back(v):
    return v

def low_keep(v):
    return (lower_precision(v), None)

def low_pass(kept, grad):
    return (grad,)

def back_keep(v):
    return (v, None)

def back_low(kept, grad):
    return (lower_precision(grad),)
lower_precision.defvjp(low_keep, low_pass)
lower_precision_back.defvjp(back_keep, back_low)

def matrix_product(left, right):
    return jnp.dot(left, right, precision=lax.Precision.HIGHEST, preferred_element_type=jnp.float32)

def rms_norm(hidden, gain):
    return hidden * lax.rsqrt(lax.optimization_barrier(jnp.mean(hidden * hidden, -1, keepdims=True)) + EPSILON) * gain

def rope_tables(position_row):
    half_dim = HEAD_DIMENSION // 2
    frequency = THETA ** (-(jnp.arange(half_dim, dtype=jnp.float32) * 2.0 / HEAD_DIMENSION))
    angles = position_row.astype(jnp.float32)[:, None] * frequency[None, :]
    return (jnp.cos(angles)[:, None, :], jnp.sin(angles)[:, None, :])

def apply_rotary(rotated_in, cosine_table, sine_values):
    half_dim = rotated_in.shape[-1] // 2
    first_half = rotated_in[..., :half_dim]
    second_half = rotated_in[..., half_dim:]
    return jnp.concatenate([first_half * cosine_table - second_half * sine_values, second_half * cosine_table + first_half * sine_values], -1)

def tree_allowed(segment_row, position_row, parent_row):
    labels = jnp.arange(SEGS, dtype=jnp.int32)
    parent_hot = (parent_row[:, None] == labels[None, :]).astype(jnp.float32)
    ancestry = jnp.eye(SEGS, dtype=jnp.float32) + parent_hot + matrix_product(parent_hot, parent_hot) > 0.5
    reachable = ancestry[segment_row][:, segment_row]
    return reachable & (position_row[None, :] <= position_row[:, None])

def attend_group(members, allowed):
    query_block, key_block, value_block = members
    scores = lower_precision_back(jnp.einsum('gid,jd->gij', query_block, key_block, precision=lax.Precision.HIGHEST) * HEAD_DIMENSION ** (-0.5))
    scores = jnp.where(allowed[None], scores, MASKED)
    row_max = lax.optimization_barrier(jnp.max(scores, -1, keepdims=True))
    exponent = jnp.exp(scores - row_max)
    attn_probs = exponent / lax.optimization_barrier(jnp.sum(exponent, -1, keepdims=True))
    return jnp.einsum('gij,jd->gid', lower_precision(attn_probs), value_block, precision=lax.Precision.HIGHEST)

def one_layer(hidden, layer_weights, position_row, allowed):
    gain_one, w_query, key_weight, value_weight, w_out, gain_two, w_gate, w_up, w_down = layer_weights
    cosine_table, sine_values = rope_tables(position_row)
    first_normed = lower_precision(rms_norm(hidden, gain_one))
    query_rows = lower_precision(apply_rotary(lower_precision_back(matrix_product(first_normed, w_query)).reshape(TREE_TOKENS, QUERY_HEAD_COUNT, HEAD_DIMENSION), cosine_table, sine_values))
    key_matrix = lower_precision(apply_rotary(lower_precision_back(matrix_product(first_normed, key_weight)).reshape(TREE_TOKENS, KEY_VALUE_HEADS, HEAD_DIMENSION), cosine_table, sine_values))
    value_matrix = lower_precision(lower_precision_back(matrix_product(first_normed, value_weight))).reshape(TREE_TOKENS, KEY_VALUE_HEADS, HEAD_DIMENSION)
    grouped_heads = query_rows.reshape(TREE_TOKENS, KEY_VALUE_HEADS, QUERY_HEAD_COUNT // KEY_VALUE_HEADS, HEAD_DIMENSION).transpose(1, 2, 0, 3)
    context = lax.map(jax.checkpoint(partial(attend_group, allowed=allowed)), (grouped_heads, key_matrix.transpose(1, 0, 2), value_matrix.transpose(1, 0, 2)))
    context = lower_precision(lower_precision_back(context.transpose(2, 0, 1, 3).reshape(TREE_TOKENS, QUERY_HEAD_COUNT * HEAD_DIMENSION)))
    middle = hidden + lower_precision_back(matrix_product(context, w_out))
    normed_two = lower_precision(rms_norm(middle, gain_two))
    gate_proj = lower_precision_back(matrix_product(normed_two, w_gate))
    up_proj = lower_precision_back(matrix_product(normed_two, w_up))
    inner_act = lower_precision(gate_proj * jax.nn.sigmoid(gate_proj) * up_proj)
    return middle + lower_precision_back(matrix_product(inner_act, w_down))

def reference(inputs, cotangent, seg_ids, positions, parents, gain_attn, w_query, key_weight, value_weight, w_out, gain_mlp, w_gate, w_up, w_down):
    source_rows = inputs.astype(jnp.float32)
    probe_zero = jnp.zeros_like(source_rows)

    def forward(source_arg, probe_arg, *masters):
        rounded = [lower_precision(member) for member in masters]
        first_weights = [member[0] for member in rounded]
        second_weights = [member[1] for member in rounded]

        def per_tree(members):
            source_row, probe_row, segment_row, position_row, parent_row = members
            allowed = tree_allowed(segment_row, position_row, parent_row)
            first_out = one_layer(source_row, first_weights, position_row, allowed)
            handed = lower_precision(first_out)
            final_out = one_layer(lower_precision_back(handed) + probe_row, second_weights, position_row, allowed)
            return (handed, final_out)
        return lax.map(jax.checkpoint(per_tree), (source_arg, probe_arg, seg_ids, positions, parents))
    (handed, final_out), pullback = jax.vjp(forward, source_rows, probe_zero, gain_attn, w_query, key_weight, value_weight, w_out, gain_mlp, w_gate, w_up, w_down)
    gradients = pullback((jnp.zeros_like(handed), cotangent.astype(jnp.float32)))
    layer_output = jnp.stack([handed, final_out]).astype(jnp.bfloat16)
    input_grad = jnp.stack([gradients[0], gradients[1]])
    return (layer_output, input_grad, gradients[2], gradients[3], gradients[4], gradients[5], gradients[6], gradients[7], gradients[8], gradients[9], gradients[10])
```

```python
import functools

import jax
import jax.numpy as jnp
from jax import lax
from jax.experimental import pallas as pl
from jax.experimental.pallas import tpu as pltpu
from jax.sharding import PartitionSpec as P

HEAD = 64
HALF = HEAD // 2
TRUNK = 1024
GROUP = 384
EPSILON = 1e-05
THETA = 10000.0
MASKED = -1e30
BF = jnp.bfloat16
F32 = jnp.float32
MESH = pl.DeviceIdType.MESH


def dot_f32(a, b, ca, cb):
    return lax.dot_general(a, b, (((ca,), (cb,)), ((), ())), preferred_element_type=F32)


def sum_kernel(pieces, p_ref, o_ref, a_buf, s_buf, b_buf, sa, ra, sb, rb, sc, rc):
    t = lax.axis_index("tensor")
    sec = lax.axis_index("section")
    dat = lax.axis_index("dp")
    inner = (t == 1) | (t == 2)
    pair = (sec, t + 1 - 2 * lax.rem(t, 2), dat)
    mid = (sec, 3 - t, dat)
    rows = p_ref.shape[0] // pieces

    def part(ref, i):
        return ref.at[pl.ds(i * rows, rows)]

    def to_inner(i):
        return pltpu.make_async_remote_copy(
            part(p_ref, i), part(a_buf, i), sa.at[i], ra.at[i], device_id=pair, device_id_type=MESH
        )

    def across(i):
        return pltpu.make_async_remote_copy(
            part(s_buf, i), part(b_buf, i), sb.at[i], rb.at[i], device_id=mid, device_id_type=MESH
        )

    def to_outer(i):
        return pltpu.make_async_remote_copy(
            part(o_ref, i), part(o_ref, i), sc.at[i], rc.at[i], device_id=pair, device_id_type=MESH
        )

    barrier = pltpu.get_barrier_semaphore()
    pl.semaphore_signal(barrier, inc=1, device_id=pair, device_id_type=MESH)

    @pl.when(inner)
    def _():
        pl.semaphore_signal(barrier, inc=1, device_id=mid, device_id_type=MESH)
        pl.semaphore_wait(barrier, 2)

    @pl.when(jnp.logical_not(inner))
    def _():
        pl.semaphore_wait(barrier, 1)
        for i in range(pieces):
            to_inner(i).start()
        for i in range(pieces):
            to_inner(i).wait_send()
        for i in range(pieces):
            to_outer(i).wait_recv()

    @pl.when(inner)
    def _():
        def first(i):
            to_inner(i).wait_recv()
            at = pl.ds(i * rows, rows)
            s_buf[at] = (p_ref[at].astype(F32) + a_buf[at].astype(F32)).astype(BF)
            across(i).start()

        def second(i):
            across(i).wait_recv()
            at = pl.ds(i * rows, rows)
            o_ref[at] = (s_buf[at].astype(F32) + b_buf[at].astype(F32)).astype(BF)
            to_outer(i).start()

        for i in range(pieces):
            first(i)
            if i >= 1:
                second(i - 1)
        second(pieces - 1)
        for i in range(pieces):
            across(i).wait_send()
            to_outer(i).wait_send()


def sum_over_tensor(part):
    if lax.axis_size("tensor") != 4:
        return lax.psum(part, "tensor")
    rows, width = part.shape
    pieces = next(n for n in (10, 5, 4, 2, 1) if rows % (16 * n) == 0)
    buf = pltpu.VMEM((rows, width), BF)
    sem = pltpu.SemaphoreType.DMA((pieces,))
    return pl.pallas_call(
        functools.partial(sum_kernel, pieces),
        out_shape=jax.ShapeDtypeStruct((rows, width), BF),
        in_specs=[pl.BlockSpec(memory_space=pltpu.VMEM)],
        out_specs=pl.BlockSpec(memory_space=pltpu.VMEM),
        scratch_shapes=[buf, buf, buf, sem, sem, sem, sem, sem, sem],
        compiler_params=pltpu.CompilerParams(
            collective_id=1, has_side_effects=True, vmem_limit_bytes=24 << 20
        ),
        name="sum_tensor",
    )(part)


def group_start(first_row):
    past = lax.max(first_row - TRUNK, 0)
    return pl.multiple_of(TRUNK + GROUP * lax.div(past, GROUP), 128)


def windows(tree_len, rows, tile, first_row):
    if tile % 128 == 0 and GROUP % tile == 0 and TRUNK % tile == 0 and rows % tile == 0:
        return (pl.ds(0, TRUNK), pl.ds(group_start(first_row), GROUP))
    return (pl.ds(0, tree_len),)


def beside(ref, head, count):
    parts = [ref[HEAD * (head + k) : HEAD * (head + k + 1), :] for k in range(count)]
    return parts[0] if count == 1 else jnp.concatenate(parts, axis=1)


def row_beside(ref, head, count):
    parts = [ref[head + k : head + k + 1, :] for k in range(count)]
    return parts[0] if count == 1 else jnp.concatenate(parts, axis=1)


def attend_kernel(rows, step, start_ref, q_ref, kv_ref, kvt_ref, bias_ref, o_ref, lse_ref):
    tile = q_ref.shape[1]
    heads = q_ref.shape[0] // HEAD
    first_row = start_ref[0] + pl.program_id(0) * tile
    wins = windows(kv_ref.shape[0], rows, tile, first_row)
    for head in range(0, heads, step):
        q = beside(q_ref, head, step)
        scores = []
        for win in wins:
            bias = bias_ref[win, :].astype(F32)
            bias = bias if step == 1 else jnp.concatenate([bias] * step, axis=1)
            scores.append(dot_f32(kv_ref[win, :HEAD], q, 1, 0) + bias)
        top = functools.reduce(jnp.maximum, [jnp.max(s, 0, keepdims=True) for s in scores])
        expo = [jnp.exp(s - top) for s in scores]
        total = sum(jnp.sum(e, 0, keepdims=True) for e in expo)
        out = sum(dot_f32(kvt_ref[HEAD:, win], e.astype(BF), 1, 0) for win, e in zip(wins, expo))
        out = (out / total).astype(BF)
        lse = top + jnp.log(total)
        for k in range(step):
            o_ref[HEAD * (head + k) : HEAD * (head + k + 1), :] = out[:, k * tile : (k + 1) * tile]
            lse_ref[head + k : head + k + 1, :] = lse[:, k * tile : (k + 1) * tile]


def attend_back_kernel(
    rows, step, start_ref, q_ref, do_ref, o_ref, lse_ref, kv_ref, kvt_ref, bias_ref, cos_ref, sin_ref,
    dq_ref, dkv_ref, dk_acc, dv_acc,
):
    tile = q_ref.shape[1]
    heads = q_ref.shape[0] // HEAD
    first_row = start_ref[0] + pl.program_id(0) * tile
    wins = windows(kv_ref.shape[0], rows, tile, first_row)

    @pl.when(pl.program_id(0) == 0)
    def _():
        dk_acc[...] = jnp.zeros_like(dk_acc)
        dv_acc[...] = jnp.zeros_like(dv_acc)

    for head in range(0, heads, step):
        q = beside(q_ref, head, step)
        do = beside(do_ref, head, step)
        out = beside(o_ref, head, step)
        lse = row_beside(lse_ref, head, step)
        delta = jnp.sum(do.astype(F32) * out.astype(F32), 0, keepdims=True)
        dq = jnp.zeros((HEAD, step * tile), F32)
        for win in wins:
            bias = bias_ref[win, :].astype(F32)
            bias = bias if step == 1 else jnp.concatenate([bias] * step, axis=1)
            p = jnp.exp(dot_f32(kv_ref[win, :HEAD], q, 1, 0) + bias - lse)
            dp = dot_f32(kv_ref[win, HEAD:], do, 1, 0)
            ds = (p * (dp - delta)).astype(BF)
            dk_acc[win, :] += dot_f32(ds, q, 1, 1)
            dv_acc[win, :] += dot_f32(p.astype(BF), do, 1, 1)
            dq = dq + dot_f32(kvt_ref[:HEAD, win], ds, 1, 0)
        dq = dq * HEAD**-0.5
        cos, sin = cos_ref[...], sin_ref[...]
        for k in range(step):
            first = dq[:HALF, k * tile : (k + 1) * tile]
            second = dq[HALF:, k * tile : (k + 1) * tile]
            base = HEAD * (head + k)
            dq_ref[base : base + HALF, :] = (first * cos + second * sin).astype(BF)
            dq_ref[base + HALF : base + HEAD, :] = (second * cos - first * sin).astype(BF)

    @pl.when(pl.program_id(0) == pl.num_programs(0) - 1)
    def _():
        dkv_ref[...] = jnp.concatenate([dk_acc[...], dv_acc[...]], axis=1).astype(BF)


def row_tile(rows):
    return 128 if rows % 128 == 0 else rows


def attend(start, q_t, kv, kv_t, bias_t):
    width, rows = q_t.shape
    heads, tree_len, tile = width // HEAD, kv.shape[0], row_tile(rows)
    step = 2 if tile % 128 == 0 and heads % 2 == 0 else 1
    column = lambda i, s: (0, i)
    whole = lambda i, s: (0, 0)
    return pl.pallas_call(
        functools.partial(attend_kernel, rows, step),
        out_shape=(
            jax.ShapeDtypeStruct((width, rows), BF),
            jax.ShapeDtypeStruct((heads, rows), F32),
        ),
        grid_spec=pltpu.PrefetchScalarGridSpec(
            num_scalar_prefetch=1,
            grid=(rows // tile,),
            in_specs=[
                pl.BlockSpec((width, tile), column),
                pl.BlockSpec((tree_len, 2 * HEAD), whole),
                pl.BlockSpec((2 * HEAD, tree_len), whole),
                pl.BlockSpec((tree_len, tile), column),
            ],
            out_specs=(pl.BlockSpec((width, tile), column), pl.BlockSpec((heads, tile), column)),
        ),
        compiler_params=pltpu.CompilerParams(vmem_limit_bytes=40 << 20),
        cost_estimate=pl.CostEstimate(
            flops=16 * heads * rows * tree_len * HEAD,
            transcendentals=heads * rows * tree_len,
            bytes_accessed=2 * rows * tree_len,
        ),
        name="attend",
    )(start, q_t, kv, kv_t, bias_t)


def attend_back(start, q_t, do_t, o_t, lse, kv, kv_t, bias_t, cos_t, sin_t):
    width, rows = q_t.shape
    heads, tree_len, tile = width // HEAD, kv.shape[0], row_tile(rows)
    step = 2 if tile % 128 == 0 and heads % 2 == 0 else 1
    column = lambda i, s: (0, i)
    whole = lambda i, s: (0, 0)
    return pl.pallas_call(
        functools.partial(attend_back_kernel, rows, step),
        out_shape=(
            jax.ShapeDtypeStruct((width, rows), BF),
            jax.ShapeDtypeStruct((tree_len, 2 * HEAD), BF),
        ),
        grid_spec=pltpu.PrefetchScalarGridSpec(
            num_scalar_prefetch=1,
            grid=(rows // tile,),
            in_specs=[
                pl.BlockSpec((width, tile), column),
                pl.BlockSpec((width, tile), column),
                pl.BlockSpec((width, tile), column),
                pl.BlockSpec((heads, tile), column),
                pl.BlockSpec((tree_len, 2 * HEAD), whole),
                pl.BlockSpec((2 * HEAD, tree_len), whole),
                pl.BlockSpec((tree_len, tile), column),
                pl.BlockSpec((HALF, tile), column),
                pl.BlockSpec((HALF, tile), column),
            ],
            out_specs=(
                pl.BlockSpec((width, tile), column),
                pl.BlockSpec((tree_len, 2 * HEAD), whole),
            ),
            scratch_shapes=[pltpu.VMEM((tree_len, HEAD), F32), pltpu.VMEM((tree_len, HEAD), F32)],
        ),
        compiler_params=pltpu.CompilerParams(vmem_limit_bytes=48 << 20),
        cost_estimate=pl.CostEstimate(
            flops=40 * heads * rows * tree_len * HEAD,
            transcendentals=heads * rows * tree_len,
            bytes_accessed=2 * rows * tree_len,
        ),
        name="attend_back",
    )(start, q_t, do_t, o_t, lse, kv, kv_t, bias_t, cos_t, sin_t)


def inverse_rms(hidden):
    return lax.rsqrt(jnp.mean(hidden * hidden, -1, keepdims=True) + EPSILON)


def norm_back(grad_normed, hidden, scale_rows, gain):
    unit = hidden * scale_rows
    grad_unit = grad_normed * gain
    grad_hidden = scale_rows * (grad_unit - unit * jnp.mean(grad_unit * unit, -1, keepdims=True))
    return grad_hidden, jnp.sum(grad_normed * unit, 0)


def rope_t(x, cos_t, sin_t):
    heads = x.shape[0] // HEAD
    halves = x.reshape(heads, 2, HALF, x.shape[1])
    first, second = halves[:, 0], halves[:, 1]
    turned = jnp.stack(
        [first * cos_t - second * sin_t, second * cos_t + first * sin_t], axis=1
    )
    return turned.reshape(x.shape).astype(BF)


def layer_forward(hidden, weights, tables):
    gain_one, gain_two, w_in, w_out, w_gu, w_down = weights
    start, bias_t, cos_t, sin_t = tables
    width = w_out.shape[0]
    span = (w_in.shape[1] - width) // 2
    scale_one = inverse_rms(hidden)
    normed_one = (hidden * scale_one * gain_one).astype(BF)
    qkv_t = dot_f32(w_in, normed_one, 0, 1)
    q_t = rope_t(qkv_t[:width], cos_t, sin_t) * jnp.asarray(HEAD**-0.5, BF)
    k_t = rope_t(qkv_t[width : width + span], cos_t, sin_t)
    kv_rows = jnp.concatenate([k_t, qkv_t[width + span :].astype(BF)], 0).T
    kv = lax.all_gather(kv_rows, "dp", axis=0, tiled=True)
    kv_t = kv.T
    o_t, lse = attend(start, q_t, kv, kv_t, bias_t)
    attn_part = dot_f32(o_t, w_out, 0, 0).astype(BF)
    middle = hidden + sum_over_tensor(attn_part).astype(F32)
    scale_two = inverse_rms(middle)
    normed_two = (middle * scale_two * gain_two).astype(BF)
    gate_up = jnp.dot(normed_two, w_gu, preferred_element_type=F32)
    units = w_down.shape[0]
    gate, up = gate_up[:, :units], gate_up[:, units:]
    inner = (gate * jax.nn.sigmoid(gate) * up).astype(BF)
    mlp_part = jnp.dot(inner, w_down, preferred_element_type=F32).astype(BF)
    result = (middle + sum_over_tensor(mlp_part).astype(F32)).astype(BF)
    kept = (hidden, scale_one, normed_one, q_t, kv, kv_t, o_t, lse, middle, scale_two, normed_two, gate_up, inner)
    return result, kept


def layer_backward(grad_out, weights, tables, rope_rows, kept):
    gain_one, gain_two, w_in, w_out, w_gu, w_down = weights
    start, bias_t, cos_t, sin_t = tables
    cos_rows, sin_rows = rope_rows
    hidden, scale_one, normed_one, q_t, kv, kv_t, o_t, lse, middle, scale_two, normed_two, gate_up, inner = kept
    units = w_down.shape[0]
    gate, up = gate_up[:, :units], gate_up[:, units:]
    branch = grad_out.astype(BF)
    d_w_down = dot_f32(inner, branch, 0, 0).astype(BF)
    d_inner = dot_f32(branch, w_down, 1, 1)
    sig = jax.nn.sigmoid(gate)
    d_gate = (d_inner * up * sig * (1.0 + gate * (1.0 - sig))).astype(BF)
    d_up = (d_inner * gate * sig).astype(BF)
    d_gu = jnp.concatenate([d_gate, d_up], 1)
    d_w_gu = dot_f32(normed_two, d_gu, 0, 0).astype(BF)
    d_two = sum_over_tensor(dot_f32(d_gu, w_gu, 1, 1).astype(BF)).astype(F32)
    grad_norm, d_gain_two = norm_back(d_two, middle, scale_two, gain_two)
    grad_middle = grad_out + grad_norm
    grad_attn = grad_middle.astype(BF)
    d_w_out = dot_f32(o_t, grad_attn, 1, 0).astype(BF)
    do_t = dot_f32(w_out, grad_attn, 1, 1).astype(BF)
    dq_t, dkv_part = attend_back(start, q_t, do_t, o_t, lse, kv, kv_t, bias_t, cos_t, sin_t)
    dkv = lax.psum_scatter(dkv_part, "dp", scatter_dimension=0, tiled=True).astype(F32)
    first, second = dkv[:, :HALF], dkv[:, HALF:HEAD]
    dkv = jnp.concatenate(
        [first * cos_rows + second * sin_rows, second * cos_rows - first * sin_rows, dkv[:, HEAD:]], 1
    ).astype(BF)
    d_in = jnp.concatenate([dq_t.T, dkv], 1)
    d_w_in = dot_f32(normed_one, d_in, 0, 0).astype(BF)
    d_one = sum_over_tensor(dot_f32(d_in, w_in, 1, 1).astype(BF)).astype(F32)
    grad_norm, d_gain_one = norm_back(d_one, hidden, scale_one, gain_one)
    grad_input = grad_middle + grad_norm
    return grad_input, (d_w_in, d_w_out, d_w_gu, d_w_down), (d_gain_one, d_gain_two)


def shards(
    inputs, cotangent, seg_ids, positions, parents, gain_attn, w_query, key_weight, value_weight,
    w_out, gain_mlp, w_gate, w_up, w_down,
):
    sec = lax.axis_index("section")
    data = lax.axis_index("dp")
    sections = lax.axis_size("section")
    devices = lax.axis_size("dp")
    assert sections == 2 and inputs.shape[0] == 2
    first_core = sec == 0
    rows, model = inputs.shape[1], inputs.shape[2]
    swap = [(0, 1), (1, 0)]
    both = ("dp", "section")

    hidden = lax.dynamic_index_in_dim(inputs, sec, 0, keepdims=False).astype(F32)
    cot = lax.dynamic_index_in_dim(cotangent, sec, 0, keepdims=False).astype(F32)
    segments = lax.dynamic_index_in_dim(seg_ids, sec, 0, keepdims=False)
    places = lax.dynamic_index_in_dim(positions, sec, 0, keepdims=False)
    parent = lax.dynamic_index_in_dim(parents, sec, 0, keepdims=False)

    shard_list = (
        (jnp.concatenate([w_query[0], key_weight[0], value_weight[0]], 1).astype(BF), 0),
        (w_out[0].astype(BF), 1),
        (jnp.concatenate([w_gate[0], w_up[0]], 1).astype(BF), 0),
        (w_down[0].astype(BF), 1),
    )
    gains_all = lax.all_gather(
        jnp.concatenate([gain_attn, gain_mlp], 0).astype(BF), ("section", "dp"), axis=0, tiled=False
    )
    gains_all = gains_all.reshape(sections, devices, 2, -1).astype(F32)
    gain = [[gains_all[l, :, k].reshape(-1) for k in range(2)] for l in range(2)]
    halves = []
    for shard, axis in shard_list:
        half = shard.shape[axis] // 2
        low = lax.slice_in_dim(shard, 0, half, axis=axis)
        high = lax.slice_in_dim(shard, half, 2 * half, axis=axis)
        got = lax.ppermute(jnp.where(first_core, high, low), "section", swap)
        halves.append((jnp.where(first_core, low, got), jnp.where(first_core, got, high), axis))
    weights = []
    for l in range(2):
        whole = [lax.all_gather(h[l], both, axis=h[2], tiled=True) for h in halves]
        weights.append((gain[l][0], gain[l][1], *whole))

    seg_count = parent.shape[0]
    labels = jnp.arange(seg_count, dtype=jnp.int32)
    parent_hot = (parent[:, None] == labels[None, :]).astype(F32)
    ancestry = jnp.eye(seg_count, dtype=F32) + parent_hot + jnp.dot(parent_hot, parent_hot)
    ancestry = (ancestry > 0.5).astype(F32)
    row_start = data * rows
    seg_rows = lax.dynamic_slice_in_dim(segments, row_start, rows, 0)
    pos_rows = lax.dynamic_slice_in_dim(places, row_start, rows, 0)
    key_hot = (segments[:, None] == labels[None, :]).astype(F32)
    query_hot = (labels[:, None] == seg_rows[None, :]).astype(F32)
    reach = jnp.dot(key_hot, jnp.dot(ancestry.T, query_hot))
    allowed = (reach > 0.5) & (places[:, None] <= pos_rows[None, :])
    bias_t = jnp.where(allowed, 0.0, MASKED).astype(BF)
    frequency = THETA ** (-(jnp.arange(HALF, dtype=F32) * 2.0 / HEAD))
    angles = frequency[:, None] * pos_rows.astype(F32)[None, :]
    cos_t, sin_t = jnp.cos(angles), jnp.sin(angles)
    tables = (row_start.astype(jnp.int32).reshape(1), bias_t, cos_t, sin_t)
    rope_rows = (cos_t.T, sin_t.T)

    out_zero, kept_zero = layer_forward(hidden, weights[0], tables)
    out_one, kept_one = layer_forward(out_zero.astype(F32), weights[1], tables)
    grad_one, d_one, d_gain_one = layer_backward(cot, weights[1], tables, rope_rows, kept_one)
    grad_zero, d_zero, d_gain_zero = layer_backward(
        grad_one.astype(BF).astype(F32), weights[0], tables, rope_rows, kept_zero
    )

    out_got = lax.ppermute(jnp.where(first_core, out_one, out_zero), "section", swap)
    layer_output = jnp.stack(
        [jnp.where(first_core, out_zero, out_got), jnp.where(first_core, out_got, out_one)]
    )
    one_got = lax.ppermute(grad_one.astype(BF), "section", [(0, 1)]).astype(F32)
    zero_got = lax.ppermute(grad_zero.astype(BF), "section", [(1, 0)]).astype(F32)
    input_grad = jnp.stack(
        [jnp.where(first_core, grad_zero, one_got), jnp.where(first_core, zero_got, grad_one)]
    )

    def own_shard(zero, one, axis):
        zero = lax.psum_scatter(zero, both, scatter_dimension=axis, tiled=True)
        one = lax.psum_scatter(one, both, scatter_dimension=axis, tiled=True)
        got = lax.ppermute(jnp.where(first_core, one, zero), "section", swap)
        low = jnp.where(first_core, zero, got)
        high = jnp.where(first_core, got, one)
        return jnp.concatenate([low, high], axis).astype(F32)

    g_in, g_out, g_gu, g_down = [
        own_shard(zero, one, axis) for zero, one, axis in zip(d_zero, d_one, (0, 1, 0, 1))
    ]
    g_gain = lax.psum(jnp.stack([*d_gain_zero, *d_gain_one]).reshape(2, 2, model), both)
    g_gain = lax.dynamic_index_in_dim(g_gain, sec, 0, keepdims=False)
    g_gain = lax.dynamic_slice_in_dim(g_gain, data * (model // devices), model // devices, 1)
    width, span = w_query.shape[2], key_weight.shape[2]
    units = w_gate.shape[2]
    return (
        layer_output[None],
        input_grad[None],
        g_gain[0][None],
        g_in[None, :, :width],
        g_in[None, :, width : width + span],
        g_in[None, :, width + span :],
        g_out[None],
        g_gain[1][None],
        g_gu[None, :, :units],
        g_gu[None, :, units:],
        g_down[None],
    )


def solution(mesh):
    in_specs = (
        P(None, "dp", None),
        P(None, "dp", None),
        P(),
        P(),
        P(),
        P("section", "dp"),
        P("section", "dp", "tensor"),
        P("section", "dp", "tensor"),
        P("section", "dp", "tensor"),
        P("section", "tensor", "dp"),
        P("section", "dp"),
        P("section", "dp", "tensor"),
        P("section", "dp", "tensor"),
        P("section", "tensor", "dp"),
    )
    out_specs = (
        P("section", None, "dp", None),
        P("section", None, "dp", None),
        P("section", "dp"),
        P("section", "dp", "tensor"),
        P("section", "dp", "tensor"),
        P("section", "dp", "tensor"),
        P("section", "tensor", "dp"),
        P("section", "dp"),
        P("section", "dp", "tensor"),
        P("section", "dp", "tensor"),
        P("section", "tensor", "dp"),
    )
    return jax.shard_map(shards, mesh=mesh, in_specs=in_specs, out_specs=out_specs, check_vma=False)
```

```python
import functools

import jax
import jax.numpy as jnp
from jax import lax
from jax.experimental import pallas as pl
from jax.experimental.pallas import tpu as pltpu
from jax.sharding import PartitionSpec as P

HEAD = 64
HALF = HEAD // 2
TRUNK = 1024
GROUP = 384
EPSILON = 1e-05
THETA = 10000.0
MASKED = -1e30
BF = jnp.bfloat16
F32 = jnp.float32
MESH = pl.DeviceIdType.MESH
BOTH = ("dp", "section")


def dot_f32(a, b, ca, cb):
    return lax.dot_general(a, b, (((ca,), (cb,)), ((), ())), preferred_element_type=F32)


BLOCK = 256
PIECE = 128
NO_COST = pl.CostEstimate(flops=1, transcendentals=0, bytes_accessed=1)


def product_sum_kernel(cfg, *refs):
    n_arrays, n_x, first_column, sides, stagger = cfg
    refs = list(refs)
    take = lambda n: [refs.pop(0) for _ in range(n)]
    from_hbm = take(n_arrays)
    (w_hbm,) = take(1)
    (o_ref,) = take(1)
    (g_hbm,) = take(1) if sides else (None,)
    arrays = take(n_arrays)
    load_sem, w_buf, p_buf, a_buf, s_buf, b_buf, c_buf, w_sem, sa, ra, sb, rb, sc, rc, so, turn = take(16)
    g_buf, g_sem = take(2) if sides else (None, None)
    pieces = p_buf.shape[0]
    per_block = BLOCK // PIECE
    blocks = pieces // per_block
    depth = w_buf.shape[2]

    t = lax.axis_index("tensor")
    sec = lax.axis_index("section")
    dat = lax.axis_index("dp")
    inner = (t == 1) | (t == 2)
    outer = jnp.logical_not(inner)
    pair = (sec, t + 1 - 2 * lax.rem(t, 2), dat)
    mid = (sec, 3 - t, dat)
    mate = (1 - sec, t, dat)

    def columns(j):
        return pl.ds(pl.multiple_of(j * BLOCK, BLOCK), BLOCK)

    def lanes(i):
        return pl.ds(pl.multiple_of(i * PIECE, PIECE), PIECE)

    def to_inner(i):
        return pltpu.make_async_remote_copy(
            p_buf.at[i], a_buf.at[i], sa.at[i], ra.at[i], device_id=pair, device_id_type=MESH
        )

    def across(i):
        return pltpu.make_async_remote_copy(
            s_buf.at[i], b_buf.at[i], sb.at[i], rb.at[i], device_id=mid, device_id_type=MESH
        )

    def to_outer(i):
        return pltpu.make_async_remote_copy(
            c_buf.at[i], c_buf.at[i], sc.at[i], rc.at[i], device_id=pair, device_id_type=MESH
        )

    def store(i):
        return pltpu.make_async_copy(c_buf.at[i], o_ref.at[:, lanes(i)], so.at[i])

    def load(k):
        return pltpu.make_async_copy(from_hbm[k], arrays[k], load_sem.at[k])

    def fetch(j, slot):
        return pltpu.make_async_copy(
            w_hbm.at[columns(j), pl.ds(first_column, depth)], w_buf.at[slot], w_sem.at[slot]
        )

    def flush(j, slot):
        return pltpu.make_async_copy(g_buf.at[slot], g_hbm.at[columns(j), :], g_sem.at[slot])

    for k in range(n_x):
        load(k).start()
    fetch(0, 0).start()
    for k in range(n_x, n_arrays):
        load(k).start()
    barrier = pltpu.get_barrier_semaphore()
    extra = 1 if stagger else 0
    pl.semaphore_signal(barrier, inc=1, device_id=pair, device_id_type=MESH)
    if stagger:
        pl.semaphore_signal(barrier, inc=1, device_id=mate, device_id_type=MESH)

    @pl.when(inner)
    def _():
        pl.semaphore_signal(barrier, inc=1, device_id=mid, device_id_type=MESH)
        pl.semaphore_wait(barrier, 2 + extra)

    @pl.when(outer)
    def _():
        pl.semaphore_wait(barrier, 1 + extra)

    if stagger:
        @pl.when(sec == 1)
        def _():
            pl.semaphore_wait(turn, 1)

    for k in range(n_x):
        load(k).wait()

    def first(i):
        to_inner(i).wait_recv()
        s_buf[i] = (p_buf[i].astype(F32) + a_buf[i].astype(F32)).astype(BF)
        across(i).start()

    def second(i):
        across(i).wait_recv()
        c_buf[i] = (s_buf[i].astype(F32) + b_buf[i].astype(F32)).astype(BF)
        to_outer(i).start()
        store(i).start()

    def step(j, _):
        slot = lax.rem(j, 2)
        fetch(j, slot).wait()

        @pl.when(j + 1 < blocks)
        def _():
            fetch(j + 1, 1 - slot).start()

        total, start = None, 0
        for x_ref in arrays[:n_x]:
            width = x_ref.shape[1]
            term = dot_f32(x_ref[...], w_buf[slot, :, start : start + width], 1, 1)
            total = term if total is None else total + term
            start += width
        total = total.astype(BF)
        for u in range(per_block):
            p_buf[per_block * j + u] = total[:, u * PIECE : (u + 1) * PIECE]

        @pl.when(outer)
        def _():
            for u in range(per_block):
                to_inner(per_block * j + u).start()

        @pl.when(inner)
        def _():
            for u in range(per_block):
                i = per_block * j + u
                first(i)

                @pl.when(j >= 1)
                def _():
                    second(i - per_block)

        if sides:

            @pl.when(j == 0)
            def _():
                for k in range(n_x, n_arrays):
                    load(k).wait()

            @pl.when(j >= 2)
            def _():
                flush(j - 2, slot).wait()

            start = 0
            for a, bs in sides:
                a_t = arrays[a][:, columns(j)].T
                for b in bs:
                    width = arrays[b].shape[1]
                    g_buf[slot, :, start : start + width] = jnp.dot(
                        a_t, arrays[b][...], preferred_element_type=F32
                    ).astype(BF)
                    start += width
            flush(j, slot).start()
        return 0

    lax.fori_loop(0, blocks, step, 0)

    @pl.when(inner)
    def _():
        for u in range(per_block):
            second(pieces - per_block + u)

        def last(i, _):
            across(i).wait_send()
            to_outer(i).wait_send()
            store(i).wait()
            return 0

        lax.fori_loop(0, pieces, last, 0)

    @pl.when(outer)
    def _():
        def arrive(i, _):
            to_outer(i).wait_recv()
            store(i).start()
            return 0

        def last(i, _):
            to_inner(i).wait_send()
            store(i).wait()
            return 0

        lax.fori_loop(0, pieces, arrive, 0)
        lax.fori_loop(0, pieces, last, 0)

    if sides:
        flush(blocks - 2, (blocks - 2) % 2).wait()
        flush(blocks - 1, (blocks - 1) % 2).wait()

    if stagger:

        @pl.when(sec == 0)
        def _():
            pl.semaphore_signal(turn, inc=1, device_id=mate, device_id_type=MESH)


def product_sum(xs, weights, first_column, others=(), sides=(), stagger=False, key=1):
    assert lax.axis_size("tensor") == 4
    arrays = (*xs, *others)
    rows, model = xs[0].shape[0], weights.shape[0]
    depth = sum(x.shape[1] for x in xs)
    pieces = model // PIECE
    anywhere = pl.BlockSpec(memory_space=pl.ANY)
    buf = pltpu.VMEM((pieces, rows, PIECE), BF)
    sem = pltpu.SemaphoreType.DMA((pieces,))
    two = pltpu.SemaphoreType.DMA((2,))
    out_shape = [jax.ShapeDtypeStruct((rows, model), BF)]
    out_specs = [anywhere]
    scratch = [pltpu.VMEM(x.shape, x.dtype) for x in arrays]
    scratch += [pltpu.SemaphoreType.DMA((len(arrays),)), pltpu.VMEM((2, BLOCK, depth), BF)]
    scratch += [buf, buf, buf, buf, buf, two, *[sem] * 7, pltpu.SemaphoreType.REGULAR]
    side_width = sum(arrays[b].shape[1] for _, bs in sides for b in bs)
    if sides:
        out_shape.append(jax.ShapeDtypeStruct((model, side_width), BF))
        out_specs.append(anywhere)
        scratch += [pltpu.VMEM((2, BLOCK, side_width), BF), two]
    cfg = (len(arrays), len(xs), first_column, tuple(sides), stagger)
    out = pl.pallas_call(
        functools.partial(product_sum_kernel, cfg),
        out_shape=out_shape,
        in_specs=[anywhere] * (len(arrays) + 1),
        out_specs=out_specs,
        scratch_shapes=scratch,
        compiler_params=pltpu.CompilerParams(
            collective_id=key, has_side_effects=True, vmem_limit_bytes=56 << 20
        ),
        cost_estimate=NO_COST,
        name=f"product_sum_{key}",
    )(*arrays, weights)
    return out if sides else out[0]


def dp_peers(count):
    me = lax.axis_index("dp")
    sec, t = lax.axis_index("section"), lax.axis_index("tensor")
    others = [lax.rem(me + k, count) for k in range(1, count)]
    return me, others, [(sec, t, other) for other in others]


def greet(ids):
    barrier = pltpu.get_barrier_semaphore()
    for device in ids:
        pl.semaphore_signal(barrier, inc=1, device_id=device, device_id_type=MESH)
    pl.semaphore_wait(barrier, len(ids))


def turn_rows(x, cos_ref, sin_ref):
    lane = lax.broadcasted_iota(jnp.int32, x.shape, 1)
    width = x.shape[1]
    partner = jnp.where(lane < HALF, pltpu.roll(x, width - HALF, 1), pltpu.roll(x, HALF, 1))
    return x * cos_ref[...] + partner * sin_ref[...]


def gather_kernel(count, raw_ref, cos_ref, sin_ref, o_ref, t_ref, x_ref, send, recv):
    me, _, ids = dp_peers(count)
    x_ref[...] = turn_rows(raw_ref[...], cos_ref, sin_ref).astype(BF)
    greet(ids)
    copies = [
        pltpu.make_async_remote_copy(
            x_ref, o_ref.at[me], send.at[k], recv.at[k], device_id=device, device_id_type=MESH
        )
        for k, device in enumerate(ids)
    ]
    for copy in copies:
        copy.start()
    o_ref[me] = x_ref[...]
    for copy in copies:
        copy.wait()
    t_ref[...] = o_ref[...].reshape(t_ref.shape[1], t_ref.shape[0]).T


def scatter_kernel(count, x_ref, cos_ref, sin_ref, o_ref, buf, send, recv):
    me, others, ids = dp_peers(count)
    greet(ids)
    copies = [
        pltpu.make_async_remote_copy(
            x_ref.at[others[k]], buf.at[k], send.at[k], recv.at[k], device_id=device, device_id_type=MESH
        )
        for k, device in enumerate(ids)
    ]
    for copy in copies:
        copy.start()
    total = x_ref[me].astype(F32)
    for k, copy in enumerate(copies):
        copy.wait()
        total = total + buf[k].astype(F32)
    o_ref[...] = turn_rows(total, cos_ref, sin_ref).astype(BF)


def gather_rows(raw, cos_rows, sin_rows):
    count = lax.axis_size("dp")
    rows, width = raw.shape
    in_vmem = pl.BlockSpec(memory_space=pltpu.VMEM)
    sem = pltpu.SemaphoreType.DMA((count - 1,))
    out, out_t = pl.pallas_call(
        functools.partial(gather_kernel, count),
        out_shape=(
            jax.ShapeDtypeStruct((count, rows, width), BF),
            jax.ShapeDtypeStruct((width, count * rows), BF),
        ),
        in_specs=[in_vmem] * 3,
        out_specs=(in_vmem, in_vmem),
        scratch_shapes=[pltpu.VMEM((rows, width), BF), sem, sem],
        compiler_params=pltpu.CompilerParams(collective_id=3, has_side_effects=True),
        cost_estimate=NO_COST,
        name="gather_rows",
    )(raw, cos_rows, sin_rows)
    return out.reshape(-1, width), out_t


def scatter_rows(x, cos_rows, sin_rows):
    count = lax.axis_size("dp")
    rows, width = x.shape[0] // count, x.shape[1]
    in_vmem = pl.BlockSpec(memory_space=pltpu.VMEM)
    sem = pltpu.SemaphoreType.DMA((count - 1,))
    return pl.pallas_call(
        functools.partial(scatter_kernel, count),
        out_shape=jax.ShapeDtypeStruct((rows, width), BF),
        in_specs=[in_vmem] * 3,
        out_specs=in_vmem,
        scratch_shapes=[pltpu.VMEM((count - 1, rows, width), x.dtype), sem, sem],
        compiler_params=pltpu.CompilerParams(collective_id=4, has_side_effects=True),
        cost_estimate=NO_COST,
        name="scatter_rows",
    )(x.reshape(count, rows, width), cos_rows, sin_rows)


def reduce_kernel(g_hbm, o_ref, mine, away, got, xs, ys, xr, yr, load_sem, send, recv):
    sec, t, dat = lax.axis_index("section"), lax.axis_index("tensor"), lax.axis_index("dp")
    flip_x = dat + 1 - 2 * lax.rem(dat, 2)
    flip_y = lax.rem(dat + 2, 4)
    across = lax.rem(flip_x + 2, 4)
    by_x, by_y, mate = (sec, t, flip_x), (sec, t, flip_y), (1 - sec, t, dat)
    rows = g_hbm.shape[1] // 2
    upper, lower = pl.ds(0, rows), pl.ds(rows, rows)
    order = (across, flip_x, flip_y, dat)
    loads = []
    for k, block in enumerate(order):
        loads.append(pltpu.make_async_copy(g_hbm.at[2 * block + 1 - sec], away.at[k], load_sem.at[k]))
        loads.append(pltpu.make_async_copy(g_hbm.at[2 * block + sec], mine.at[k], load_sem.at[4 + k]))
    for copy in loads:
        copy.start()
    greet([by_x, by_y, mate])

    def remote(src, dst, k, device):
        return pltpu.make_async_remote_copy(
            src, dst, send.at[k], recv.at[k], device_id=device, device_id_type=MESH
        )

    swaps = [remote(away.at[k], got.at[k], k, mate) for k in range(4)]
    for k in range(4):
        loads[2 * k].wait()
        swaps[k].start()
    outs = []
    for k in range(4):
        loads[2 * k + 1].wait()
        swaps[k].wait_recv()
        mine[k] = (mine[k].astype(F32) + got[k].astype(F32)).astype(BF)
        if k == 0:
            outs += [remote(mine.at[0, upper], xs.at[0], 4, by_x), remote(mine.at[0, lower], ys.at[0], 5, by_y)]
        if k == 1:
            outs += [remote(mine.at[1, upper], xs.at[1], 6, by_x)]
        if k == 2:
            outs += [remote(mine.at[2, lower], ys.at[1], 7, by_y)]
        for copy in outs[-(2 if k == 0 else 1) :]:
            if k < 3:
                copy.start()
    outs[0].wait_recv()
    mine[2, upper] = (mine[2, upper].astype(F32) + xs[0].astype(F32)).astype(BF)
    outs.append(remote(mine.at[2, upper], yr, 8, by_y))
    outs[4].start()
    outs[1].wait_recv()
    mine[1, lower] = (mine[1, lower].astype(F32) + ys[0].astype(F32)).astype(BF)
    outs.append(remote(mine.at[1, lower], xr, 9, by_x))
    outs[5].start()
    outs[2].wait_recv()
    outs[3].wait_recv()
    outs[4].wait_recv()
    o_ref[upper] = (mine[3, upper].astype(F32) + xs[1].astype(F32) + yr[...].astype(F32)).astype(BF)
    outs[5].wait_recv()
    o_ref[lower] = (mine[3, lower].astype(F32) + ys[1].astype(F32) + xr[...].astype(F32)).astype(BF)
    for copy in swaps + outs:
        copy.wait_send()


def reduce_now(g):
    if lax.axis_size("dp") != 4:
        return reduce_gradient(g)
    rows, width = g.shape[0] // 8, g.shape[1]
    part = pltpu.VMEM((2, rows // 2, width), BF)
    whole = pltpu.VMEM((4, rows, width), BF)
    end = pltpu.VMEM((rows // 2, width), BF)
    return pl.pallas_call(
        reduce_kernel,
        out_shape=jax.ShapeDtypeStruct((rows, width), BF),
        in_specs=[pl.BlockSpec(memory_space=pl.ANY)],
        out_specs=pl.BlockSpec(memory_space=pltpu.VMEM),
        scratch_shapes=[
            whole, whole, whole, part, part, end, end,
            pltpu.SemaphoreType.DMA((8,)), pltpu.SemaphoreType.DMA((10,)), pltpu.SemaphoreType.DMA((10,)),
        ],
        compiler_params=pltpu.CompilerParams(
            collective_id=12, has_side_effects=True, vmem_limit_bytes=40 << 20
        ),
        cost_estimate=NO_COST,
        name="reduce_now",
    )(g.reshape(8, rows, width))


def share_kernel(count, x_ref, o_ref, buf, send, recv):
    sec, t, dat = lax.axis_index("section"), lax.axis_index("tensor"), lax.axis_index("dp")
    peers = [
        (lax.rem(sec + k // count, 2), t, lax.rem(dat + k % count, count)) for k in range(1, 2 * count)
    ]
    greet(peers)
    copies = [
        pltpu.make_async_remote_copy(
            x_ref.at[peer[0], peer[2]], buf.at[k], send.at[k], recv.at[k], device_id=peer, device_id_type=MESH
        )
        for k, peer in enumerate(peers)
    ]
    for copy in copies:
        copy.start()
    total = x_ref[sec, dat]
    for k, copy in enumerate(copies):
        copy.wait()
        total = total + buf[k]
    o_ref[...] = total


def share_sums(x):
    count = lax.axis_size("dp")
    in_vmem = pl.BlockSpec(memory_space=pltpu.VMEM)
    sem = pltpu.SemaphoreType.DMA((2 * count - 1,))
    return pl.pallas_call(
        functools.partial(share_kernel, count),
        out_shape=jax.ShapeDtypeStruct(x.shape[2:], F32),
        in_specs=[in_vmem],
        out_specs=in_vmem,
        scratch_shapes=[pltpu.VMEM((2 * count - 1, *x.shape[2:]), F32), sem, sem],
        compiler_params=pltpu.CompilerParams(collective_id=8, has_side_effects=True),
        cost_estimate=NO_COST,
        name="share_sums",
    )(x)


def group_start(first_row):
    past = lax.max(first_row - TRUNK, 0)
    return pl.multiple_of(TRUNK + GROUP * lax.div(past, GROUP), 128)


def windows(tree_len, rows, tile, first_row):
    if tile % 128 == 0 and GROUP % tile == 0 and TRUNK % tile == 0 and rows % tile == 0:
        return (pl.ds(0, TRUNK), pl.ds(group_start(first_row), GROUP))
    return (pl.ds(0, tree_len),)


def beside(ref, head, count):
    parts = [ref[HEAD * (head + k) : HEAD * (head + k + 1), :] for k in range(count)]
    return parts[0] if count == 1 else jnp.concatenate(parts, axis=1)


def turned_beside(ref, cos, sin, head, count):
    parts = []
    for k in range(count):
        base = HEAD * (head + k)
        first, second = ref[base : base + HALF, :], ref[base + HALF : base + HEAD, :]
        parts.append(jnp.concatenate([first * cos - second * sin, second * cos + first * sin], axis=0))
    whole = parts[0] if count == 1 else jnp.concatenate(parts, axis=1)
    return (whole.astype(BF).astype(F32) * HEAD**-0.5).astype(BF)


def as_rows(x, tile, count):
    parts = [x[:, k * tile : (k + 1) * tile] for k in range(count)]
    return (parts[0] if count == 1 else jnp.concatenate(parts, axis=0)).T


def row_beside(ref, head, count):
    parts = [ref[head + k : head + k + 1, :] for k in range(count)]
    return parts[0] if count == 1 else jnp.concatenate(parts, axis=1)


def attend_kernel(
    rows, step, start_ref, q_ref, kv_ref, kvt_ref, bias_ref, cos_ref, sin_ref, o_ref, on_ref, lse_ref
):
    tile = q_ref.shape[1]
    heads = q_ref.shape[0] // HEAD
    first_row = start_ref[0] + pl.program_id(0) * tile
    wins = windows(kv_ref.shape[0], rows, tile, first_row)
    for head in range(0, heads, step):
        q = turned_beside(q_ref, cos_ref[...], sin_ref[...], head, step)
        scores = []
        for win in wins:
            bias = bias_ref[win, :].astype(F32)
            bias = bias if step == 1 else jnp.concatenate([bias] * step, axis=1)
            scores.append(dot_f32(kv_ref[win, :HEAD], q, 1, 0) + bias)
        top = functools.reduce(jnp.maximum, [jnp.max(s, 0, keepdims=True) for s in scores])
        expo = [jnp.exp(s - top) for s in scores]
        total = sum(jnp.sum(e, 0, keepdims=True) for e in expo)
        out = sum(dot_f32(kvt_ref[HEAD:, win], e.astype(BF), 1, 0) for win, e in zip(wins, expo))
        out = out / total
        on_ref[:, HEAD * head : HEAD * (head + step)] = as_rows(out, tile, step).astype(BF)
        out = out.astype(BF)
        lse = top + jnp.log(total)
        for k in range(step):
            o_ref[HEAD * (head + k) : HEAD * (head + k + 1), :] = out[:, k * tile : (k + 1) * tile]
            lse_ref[head + k : head + k + 1, :] = lse[:, k * tile : (k + 1) * tile]


def attend_back_kernel(
    rows, step, start_ref, q_ref, do_ref, o_ref, lse_ref, kv_ref, kvt_ref, bias_ref, cos_ref, sin_ref,
    dq_ref, dkv_ref, dk_acc, dv_acc,
):
    tile = q_ref.shape[1]
    heads = q_ref.shape[0] // HEAD
    first_row = start_ref[0] + pl.program_id(0) * tile
    wins = windows(kv_ref.shape[0], rows, tile, first_row)

    @pl.when(pl.program_id(0) == 0)
    def _():
        dk_acc[...] = jnp.zeros_like(dk_acc)
        dv_acc[...] = jnp.zeros_like(dv_acc)

    for head in range(0, heads, step):
        q = turned_beside(q_ref, cos_ref[...], sin_ref[...], head, step)
        do = beside(do_ref, head, step)
        out = beside(o_ref, head, step)
        lse = row_beside(lse_ref, head, step)
        delta = jnp.sum(do.astype(F32) * out.astype(F32), 0, keepdims=True)
        dq = jnp.zeros((HEAD, step * tile), F32)
        for win in wins:
            bias = bias_ref[win, :].astype(F32)
            bias = bias if step == 1 else jnp.concatenate([bias] * step, axis=1)
            p = jnp.exp(dot_f32(kv_ref[win, :HEAD], q, 1, 0) + bias - lse)
            dp = dot_f32(kv_ref[win, HEAD:], do, 1, 0)
            ds = (p * (dp - delta)).astype(BF)
            dk_acc[win, :] += dot_f32(ds, q, 1, 1)
            dv_acc[win, :] += dot_f32(p.astype(BF), do, 1, 1)
            dq = dq + dot_f32(kvt_ref[:HEAD, win], ds, 1, 0)
        dq = dq * HEAD**-0.5
        cos, sin = cos_ref[...], sin_ref[...]
        turned = []
        for k in range(step):
            first = dq[:HALF, k * tile : (k + 1) * tile]
            second = dq[HALF:, k * tile : (k + 1) * tile]
            turned += [first * cos + second * sin, second * cos - first * sin]
        dq_ref[:, HEAD * head : HEAD * (head + step)] = jnp.concatenate(turned, axis=0).T.astype(BF)

    @pl.when(pl.program_id(0) == pl.num_programs(0) - 1)
    def _():
        dkv_ref[...] = jnp.concatenate([dk_acc[...], dv_acc[...]], axis=1).astype(BF)


def row_tile(rows):
    return 128 if rows % 128 == 0 else rows


def attend(start, q_t, kv, kv_t, bias_t, cos_t, sin_t):
    width, rows = q_t.shape
    heads, tree_len, tile = width // HEAD, kv.shape[0], row_tile(rows)
    step = 2 if tile % 128 == 0 and heads % 2 == 0 else 1
    column = lambda i, s: (0, i)
    whole = lambda i, s: (0, 0)
    return pl.pallas_call(
        functools.partial(attend_kernel, rows, step),
        out_shape=(
            jax.ShapeDtypeStruct((width, rows), BF),
            jax.ShapeDtypeStruct((rows, width), BF),
            jax.ShapeDtypeStruct((heads, rows), F32),
        ),
        grid_spec=pltpu.PrefetchScalarGridSpec(
            num_scalar_prefetch=1,
            grid=(rows // tile,),
            in_specs=[
                pl.BlockSpec((width, tile), column),
                pl.BlockSpec((tree_len, 2 * HEAD), whole),
                pl.BlockSpec((2 * HEAD, tree_len), whole),
                pl.BlockSpec((tree_len, tile), column),
                pl.BlockSpec((HALF, tile), column),
                pl.BlockSpec((HALF, tile), column),
            ],
            out_specs=(
                pl.BlockSpec((width, tile), column),
                pl.BlockSpec((tile, width), lambda i, s: (i, 0)),
                pl.BlockSpec((heads, tile), column),
            ),
        ),
        compiler_params=pltpu.CompilerParams(vmem_limit_bytes=40 << 20),
        cost_estimate=NO_COST,
        name="attend",
    )(start, q_t, kv, kv_t, bias_t, cos_t, sin_t)


def attend_back(start, q_t, do_t, o_t, lse, kv, kv_t, bias_t, cos_t, sin_t):
    width, rows = q_t.shape
    heads, tree_len, tile = width // HEAD, kv.shape[0], row_tile(rows)
    step = 2 if tile % 128 == 0 and heads % 2 == 0 else 1
    column = lambda i, s: (0, i)
    whole = lambda i, s: (0, 0)
    return pl.pallas_call(
        functools.partial(attend_back_kernel, rows, step),
        out_shape=(
            jax.ShapeDtypeStruct((rows, width), BF),
            jax.ShapeDtypeStruct((tree_len, 2 * HEAD), BF),
        ),
        grid_spec=pltpu.PrefetchScalarGridSpec(
            num_scalar_prefetch=1,
            grid=(rows // tile,),
            in_specs=[
                pl.BlockSpec((width, tile), column),
                pl.BlockSpec((width, tile), column),
                pl.BlockSpec((width, tile), column),
                pl.BlockSpec((heads, tile), column),
                pl.BlockSpec((tree_len, 2 * HEAD), whole),
                pl.BlockSpec((2 * HEAD, tree_len), whole),
                pl.BlockSpec((tree_len, tile), column),
                pl.BlockSpec((HALF, tile), column),
                pl.BlockSpec((HALF, tile), column),
            ],
            out_specs=(
                pl.BlockSpec((tile, width), lambda i, s: (i, 0)),
                pl.BlockSpec((tree_len, 2 * HEAD), whole),
            ),
            scratch_shapes=[pltpu.VMEM((tree_len, HEAD), F32), pltpu.VMEM((tree_len, HEAD), F32)],
        ),
        compiler_params=pltpu.CompilerParams(vmem_limit_bytes=48 << 20),
        cost_estimate=NO_COST,
        name="attend_back",
    )(start, q_t, do_t, o_t, lse, kv, kv_t, bias_t, cos_t, sin_t)


def inverse_rms(hidden):
    return lax.rsqrt(jnp.mean(hidden * hidden, -1, keepdims=True) + EPSILON)


def norm_back(grad_normed, hidden, scale_rows, gain):
    unit = hidden * scale_rows
    grad_unit = grad_normed * gain
    grad_hidden = scale_rows * (grad_unit - unit * jnp.mean(grad_unit * unit, -1, keepdims=True))
    return grad_hidden, jnp.sum(grad_normed * unit, 0)


def layer_forward(hidden, weights, tables, stagger):
    gain_one, gain_two, w_attn, w_mlp, width, split, units = weights
    start, bias_t, cos_t, sin_t, cos_rows, sin_rows = tables
    scale_one = inverse_rms(hidden)
    normed_one = (hidden * scale_one * gain_one).astype(BF)
    q_t = dot_f32(w_attn[:, :width], normed_one, 0, 1)
    kv, kv_t = gather_rows(
        jnp.dot(normed_one, w_attn[:, width:split], preferred_element_type=F32), cos_rows, -sin_rows
    )
    o_t, o, lse = attend(start, q_t, kv, kv_t, bias_t, cos_t, sin_t)
    attn_sum = product_sum((o,), w_attn, split, stagger=stagger, key=1 if stagger else 2)
    middle = hidden + attn_sum.astype(F32)
    scale_two = inverse_rms(middle)
    normed_two = (middle * scale_two * gain_two).astype(BF)
    gate_up = jnp.dot(normed_two, w_mlp[:, : 2 * units], preferred_element_type=F32)
    gate, up = gate_up[:, :units], gate_up[:, units:]
    inner = (gate * jax.nn.sigmoid(gate) * up).astype(BF)
    return (hidden, scale_one, normed_one, q_t, kv, kv_t, o_t, o, lse, middle, scale_two, normed_two, gate, up, inner)


def units_backward(branch, weights, kept):
    gate, up = kept[12:14]
    units = weights[-1]
    d_inner = dot_f32(branch, weights[3][:, 2 * units :], 1, 0)
    sig = jax.nn.sigmoid(gate)
    d_gate = (d_inner * up * sig * (1.0 + gate * (1.0 - sig))).astype(BF)
    d_up = (d_inner * gate * sig).astype(BF)
    return d_gate, d_up


def middle_backward(grad_out, d_two, weights, tables, kept):
    gain_one, gain_two, w_attn, w_mlp, width, split, units = weights
    start, bias_t, cos_t, sin_t, cos_rows, sin_rows = tables
    hidden, scale_one, normed_one, q_t, kv, kv_t, o_t, o, lse, middle, scale_two = kept[:11]
    grad_norm, d_gain_two = norm_back(d_two.astype(F32), middle, scale_two, gain_two)
    grad_middle = grad_out + grad_norm
    grad_attn = grad_middle.astype(BF)
    do_t = dot_f32(w_attn[:, split : split + width], grad_attn, 0, 1).astype(BF)
    return grad_middle, grad_attn, do_t, d_gain_two


def attention_backward(do_t, tables, kept):
    start, bias_t, cos_t, sin_t, cos_rows, sin_rows = tables
    q_t, kv, kv_t, o_t, o, lse = kept[3:9]
    dq, dkv_part = attend_back(start, q_t, do_t, o_t, lse, kv, kv_t, bias_t, cos_t, sin_t)
    return dq, scatter_rows(dkv_part, cos_rows, sin_rows)


def first_backward(grad_middle, d_one, weights, kept):
    hidden, scale_one = kept[:2]
    grad_norm, d_gain_one = norm_back(d_one.astype(F32), hidden, scale_one, weights[0])
    return grad_middle + grad_norm, d_gain_one


def reduce_gradient(x):
    return lax.psum_scatter(x, BOTH, scatter_dimension=0, tiled=True)


def shards(
    inputs, cotangent, seg_ids, positions, parents, gain_attn, w_query, key_weight, value_weight,
    w_out, gain_mlp, w_gate, w_up, w_down,
):
    sec = lax.axis_index("section")
    data = lax.axis_index("dp")
    sections = lax.axis_size("section")
    devices = lax.axis_size("dp")
    assert sections == 2 and inputs.shape[0] == 2
    first_core = sec == 0
    rows, model = inputs.shape[1], inputs.shape[2]
    swap = [(0, 1), (1, 0)]

    hidden = lax.dynamic_index_in_dim(inputs, sec, 0, keepdims=False).astype(F32)
    cot = lax.dynamic_index_in_dim(cotangent, sec, 0, keepdims=False).astype(F32)
    segments = lax.dynamic_index_in_dim(seg_ids, sec, 0, keepdims=False)
    places = lax.dynamic_index_in_dim(positions, sec, 0, keepdims=False)
    parent = lax.dynamic_index_in_dim(parents, sec, 0, keepdims=False)

    width, span, units = w_query.shape[2], key_weight.shape[2], w_gate.shape[2]
    split = width + 2 * span
    shard_list = (
        jnp.concatenate(
            [w_query[0], key_weight[0], value_weight[0], w_out[0].T, gain_attn.T, gain_mlp.T], 1
        ).astype(BF),
        jnp.concatenate([w_gate[0], w_up[0], w_down[0].T], 1).astype(BF),
    )
    halves = []
    for shard in shard_list:
        half = shard.shape[0] // 2
        low, high = shard[:half], shard[half:]
        got = lax.ppermute(jnp.where(first_core, high, low), "section", swap)
        halves.append((jnp.where(first_core, low, got), jnp.where(first_core, got, high)))
    def gathered(halves):
        return [lax.all_gather(half, BOTH, axis=0, tiled=True) for half in halves]

    def with_gains(w_attn, w_mlp):
        gains = w_attn[:, split + width :].astype(F32).T
        return (gains[0:1], gains[1:2], w_attn, w_mlp, width, split, units)

    (attn_zero, attn_one), (mlp_zero, mlp_one) = halves
    zero = with_gains(*gathered((attn_zero, mlp_zero)))
    attn_one, mlp_one = gathered((attn_one, mlp_one))

    seg_count = parent.shape[0]
    labels = jnp.arange(seg_count, dtype=jnp.int32)
    parent_hot = (parent[:, None] == labels[None, :]).astype(F32)
    ancestry = jnp.eye(seg_count, dtype=F32) + parent_hot + jnp.dot(parent_hot, parent_hot)
    ancestry = (ancestry > 0.5).astype(F32)
    row_start = data * rows
    seg_rows = lax.dynamic_slice_in_dim(segments, row_start, rows, 0)
    pos_rows = lax.dynamic_slice_in_dim(places, row_start, rows, 0)
    key_hot = (segments[:, None] == labels[None, :]).astype(F32)
    query_hot = (labels[:, None] == seg_rows[None, :]).astype(F32)
    reach = jnp.dot(key_hot, jnp.dot(ancestry.T, query_hot))
    allowed = (reach > 0.5) & (places[:, None] <= pos_rows[None, :])
    bias_t = jnp.where(allowed, 0.0, MASKED).astype(BF)
    frequency = THETA ** (-(jnp.arange(HALF, dtype=F32) * 2.0 / HEAD))
    angles = frequency[:, None] * pos_rows.astype(F32)[None, :]
    cos_t, sin_t = jnp.cos(angles), jnp.sin(angles)
    ones = jnp.ones((rows, HEAD), F32)
    cos_rows = jnp.concatenate([cos_t.T, cos_t.T, ones], 1)
    sin_rows = jnp.concatenate([sin_t.T, -sin_t.T, 0 * ones], 1)
    tables = (row_start.astype(jnp.int32).reshape(1), bias_t, cos_t, sin_t, cos_rows, sin_rows)

    kept_zero = layer_forward(hidden, zero, tables, True)
    mlp_sum = product_sum(kept_zero[-1:], zero[3], 2 * units, key=5)
    out_zero = (kept_zero[9] + mlp_sum.astype(F32)).astype(BF)

    out_zero, attn_one = lax.optimization_barrier((out_zero, attn_one))
    one = with_gains(attn_one, mlp_one)
    kept_one = layer_forward(out_zero.astype(F32), one, tables, False)
    branch = cot.astype(BF)
    d_gate, d_up = units_backward(branch, one, kept_one)
    mlp_sum, d_mlp_one = product_sum(
        kept_one[-1:], one[3], 2 * units, (kept_one[11], branch, d_gate, d_up), ((1, (3, 4)), (2, (0,))), key=6
    )
    out_one = (kept_one[9] + mlp_sum.astype(F32)).astype(BF)
    g_mlp_one = reduce_gradient(d_mlp_one)
    d_gate, d_up, mlp_sum = lax.optimization_barrier((d_gate, d_up, mlp_sum))
    d_two = product_sum((d_gate, d_up), one[3], 0, key=7)
    grad_middle, grad_attn, do_t, d_gain_mlp_one = middle_backward(cot, d_two, one, tables, kept_one)
    dq, dkv = attention_backward(do_t, tables, kept_one)
    d_one, d_attn_one = product_sum(
        (dq, dkv), one[2], 0, (kept_one[2], grad_attn, kept_one[7]), ((2, (0, 1)), (3, (4,))), key=9
    )
    g_attn_one = reduce_gradient(d_attn_one)
    grad_one, d_gain_attn_one = first_backward(grad_middle, d_one, one, kept_one)

    branch = grad_one.astype(BF)
    d_gate, d_up = units_backward(branch, zero, kept_zero)
    d_gate, d_up, g_mlp_one = lax.optimization_barrier((d_gate, d_up, g_mlp_one))
    d_two, d_mlp_zero = product_sum(
        (d_gate, d_up), zero[3], 0, (kept_zero[11], branch, kept_zero[14]), ((2, (0, 1)), (3, (4,))), key=10
    )
    g_mlp_zero = reduce_gradient(d_mlp_zero)
    grad_middle, grad_attn, do_t, d_gain_mlp_zero = middle_backward(
        branch.astype(F32), d_two, zero, tables, kept_zero
    )
    do_t, g_attn_one = lax.optimization_barrier((do_t, g_attn_one))
    dq, dkv = attention_backward(do_t, tables, kept_zero)
    d_one, d_attn_zero = product_sum(
        (dq, dkv), zero[2], 0, (kept_zero[2], grad_attn, kept_zero[7]), ((2, (0, 1)), (3, (4,))), key=9
    )
    g_attn_zero = reduce_now(d_attn_zero)
    grad_zero, d_gain_attn_zero = first_backward(grad_middle, d_one, zero, kept_zero)

    grad_zero, grad_one, out_zero, out_one, g_mlp_zero, g_mlp_one, g_attn_one, d_gain_attn_zero = (
        lax.optimization_barrier(
            (grad_zero, grad_one, out_zero, out_one, g_mlp_zero, g_mlp_one, g_attn_one, d_gain_attn_zero)
        )
    )

    out_got = lax.ppermute(jnp.where(first_core, out_one, out_zero), "section", swap)
    layer_output = jnp.stack(
        [jnp.where(first_core, out_zero, out_got), jnp.where(first_core, out_got, out_one)]
    )
    one_got = lax.ppermute(grad_one.astype(BF), "section", [(0, 1)]).astype(F32)
    zero_got = lax.ppermute(grad_zero.astype(BF), "section", [(1, 0)]).astype(F32)
    input_grad = jnp.stack(
        [jnp.where(first_core, grad_zero, one_got), jnp.where(first_core, zero_got, grad_one)]
    )

    def own_shard(zero, one):
        got = lax.ppermute(jnp.where(first_core, one, zero), "section", swap)
        return jnp.where(first_core, zero, got), jnp.where(first_core, got, one)

    def joined(halves, start, stop):
        return jnp.concatenate([h[:, start:stop] for h in halves], 0).astype(F32)

    g_mlp = own_shard(g_mlp_zero, g_mlp_one)
    g_attn = own_shard(g_attn_zero, g_attn_one)
    d_gains = jnp.stack([d_gain_attn_zero, d_gain_mlp_zero, d_gain_attn_one, d_gain_mlp_one])
    d_gains = d_gains.reshape(2, 2, devices, -1).swapaxes(1, 2).reshape(2, devices, -1, 128)
    g_gain = share_sums(d_gains).reshape(2, -1)
    return (
        layer_output[None],
        input_grad[None],
        g_gain[0][None],
        joined(g_attn, 0, width)[None],
        joined(g_attn, width, width + span)[None],
        joined(g_attn, width + span, split)[None],
        joined(g_attn, split, split + width).T[None],
        g_gain[1][None],
        joined(g_mlp, 0, units)[None],
        joined(g_mlp, units, 2 * units)[None],
        joined(g_mlp, 2 * units, 3 * units).T[None],
    )


def solution(mesh):
    in_specs = (
        P(None, "dp", None),
        P(None, "dp", None),
        P(),
        P(),
        P(),
        P("section", "dp"),
        P("section", "dp", "tensor"),
        P("section", "dp", "tensor"),
        P("section", "dp", "tensor"),
        P("section", "tensor", "dp"),
        P("section", "dp"),
        P("section", "dp", "tensor"),
        P("section", "dp", "tensor"),
        P("section", "tensor", "dp"),
    )
    out_specs = (
        P("section", None, "dp", None),
        P("section", None, "dp", None),
        P("section", "dp"),
        P("section", "dp", "tensor"),
        P("section", "dp", "tensor"),
        P("section", "dp", "tensor"),
        P("section", "tensor", "dp"),
        P("section", "dp"),
        P("section", "dp", "tensor"),
        P("section", "dp", "tensor"),
        P("section", "tensor", "dp"),
    )
    return jax.shard_map(shards, mesh=mesh, in_specs=in_specs, out_specs=out_specs, check_vma=False)
```

```python
import functools

import jax
import jax.numpy as jnp
from jax import lax
from jax.experimental import pallas as pl
from jax.experimental.pallas import tpu as pltpu
from jax.sharding import PartitionSpec as P

HEAD = 64
HALF = HEAD // 2
TRUNK = 1024
GROUP = 384
EPSILON = 1e-05
THETA = 10000.0
MASKED = -1e30
BF = jnp.bfloat16
F32 = jnp.float32
MESH = pl.DeviceIdType.MESH
BOTH = ("dp", "section")


def dot_f32(a, b, ca, cb):
    return lax.dot_general(a, b, (((ca,), (cb,)), ((), ())), preferred_element_type=F32)


BLOCK = 256
PIECE = 128
NO_COST = pl.CostEstimate(flops=1, transcendentals=0, bytes_accessed=1)


def columns_of(i):
    return pl.ds(pl.multiple_of(i * PIECE, PIECE), PIECE)


def row_scale(squares, model):
    return lax.rsqrt(jnp.sum(squares, 1, keepdims=True) * (1.0 / model) + EPSILON)


def before_sum(job, arrays, keep):
    kind, places = job[2]
    if kind == "back":
        value = arrays[places[0]]
        model = value.shape[1]
        squares = jnp.zeros(keep.shape, F32)
        for i in range(model // PIECE):
            x = value[:, i * PIECE : (i + 1) * PIECE].astype(F32)
            squares += x * x
        keep[...] = jnp.broadcast_to(row_scale(squares, model), keep.shape)


def with_piece(job, i, total, arrays, outs, keep, sums):
    kind, places = job[2]
    at = columns_of(i)
    if kind == "add":
        y = (arrays[places[0]][:, at].astype(F32) + total).astype(outs[0].dtype)
        outs[0][:, at] = y
        if len(outs) > 1:
            sums[...] += y.astype(F32) * y.astype(F32)
    if kind == "back":
        product = total * arrays[places[0]][:, at].astype(F32) * keep[...]
        sums[...] += product * arrays[places[2]][:, at]
        outs[2][:, at] = jnp.sum(product.reshape(-1, 8, PIECE), 0)


def after_sum(job, rows, total, arrays, outs, keep, sums):
    kind, places = job[2]
    model = arrays[places[0]].shape[1]
    at = lambda i: slice(i * PIECE, (i + 1) * PIECE)
    if kind == "add" and len(outs) > 1:
        scale = row_scale(sums[rows], model)
        for i in range(model // PIECE):
            y = outs[0][rows, at(i)].astype(F32)
            outs[1][rows, at(i)] = (y * scale * arrays[places[1]][:, at(i)]).astype(BF)
    if kind == "back":
        mean = jnp.sum(sums[rows], 1, keepdims=True) * (1.0 / model)
        scale = keep[rows]
        for i in range(model // PIECE):
            unit = arrays[places[0]][rows, at(i)].astype(F32) * scale
            grad = total(i)[rows].astype(F32) * arrays[places[2]][:, at(i)]
            out = arrays[places[1]][rows, at(i)].astype(F32) + scale * (grad - unit * mean)
            outs[0][rows, at(i)] = out
            outs[1][rows, at(i)] = out.astype(BF)


def product_sum_kernel(cfg, *refs):
    n_arrays, job, sides, stagger = cfg
    xs, first_column = job[:2]
    refs = list(refs)
    take = lambda n: [refs.pop(0) for _ in range(n)]
    from_hbm = take(n_arrays)
    (w_hbm,) = take(1)
    outs_hbm = take(len(job[3]))
    (g_hbm,) = take(1) if sides else (None,)
    arrays = take(n_arrays)
    outs = take(len(job[3]))
    load_sem, out_sem, w_buf, p_buf, a_buf, b_buf, w_sem, sa, ra, sb, rb, sc, rc, turn, keep, sums = take(16)
    g_buf, g_sem = take(2) if sides else (None, None)
    per_block = BLOCK // PIECE
    pieces = p_buf.shape[0]
    blocks = pieces // per_block
    n_rows = p_buf.shape[1]
    early = len(xs)

    t = lax.axis_index("tensor")
    sec = lax.axis_index("section")
    dat = lax.axis_index("dp")
    inner = (t == 1) | (t == 2)
    outer = jnp.logical_not(inner)
    pair = (sec, t + 1 - 2 * lax.rem(t, 2), dat)
    mid = (sec, 3 - t, dat)
    mate = (1 - sec, t, dat)

    def columns(j):
        return pl.ds(pl.multiple_of(j * BLOCK, BLOCK), BLOCK)

    def to_inner(i):
        return pltpu.make_async_remote_copy(
            p_buf.at[i], a_buf.at[i], sa.at[i], ra.at[i], device_id=pair, device_id_type=MESH
        )

    def across(i):
        return pltpu.make_async_remote_copy(
            p_buf.at[i], b_buf.at[i], sb.at[i], rb.at[i], device_id=mid, device_id_type=MESH
        )

    def to_outer(i):
        return pltpu.make_async_remote_copy(
            b_buf.at[i], b_buf.at[i], sc.at[i], rc.at[i], device_id=pair, device_id_type=MESH
        )

    def load(k):
        return pltpu.make_async_copy(from_hbm[k], arrays[k], load_sem.at[k])

    def fetch(j, slot):
        return pltpu.make_async_copy(
            w_hbm.at[columns(j), pl.ds(first_column, w_buf.shape[2])], w_buf.at[slot], w_sem.at[slot]
        )

    def flush(j, slot):
        return pltpu.make_async_copy(g_buf.at[slot], g_hbm.at[columns(j), :], g_sem.at[slot])

    def every_piece(body):
        def turn_of(i, _):
            body(i)
            return 0

        lax.fori_loop(0, pieces, turn_of, 0)

    for k in range(early):
        load(k).start()
    fetch(0, 0).start()
    for k in range(early, n_arrays):
        load(k).start()
    barrier = pltpu.get_barrier_semaphore()
    pl.semaphore_signal(barrier, inc=1, device_id=pair, device_id_type=MESH)
    sums[...] = jnp.zeros_like(sums)

    @pl.when(inner)
    def _():
        pl.semaphore_signal(barrier, inc=1, device_id=mid, device_id_type=MESH)
        pl.semaphore_wait(barrier, 2)

    @pl.when(outer)
    def _():
        if stagger:
            pl.semaphore_signal(barrier, inc=1, device_id=mate, device_id_type=MESH)
            pl.semaphore_wait(barrier, 2)

            @pl.when(sec == 1)
            def _():
                pl.semaphore_wait(turn, 1)

        else:
            pl.semaphore_wait(barrier, 1)

    for k in range(early):
        load(k).wait()

    def done(i):
        with_piece(job, i, b_buf[i].astype(F32), arrays, outs, keep, sums)

    def first(i):
        to_inner(i).wait_recv()
        p_buf[i] = (p_buf[i].astype(F32) + a_buf[i].astype(F32)).astype(BF)
        across(i).start()

    def second(i):
        across(i).wait_recv()
        b_buf[i] = (p_buf[i].astype(F32) + b_buf[i].astype(F32)).astype(BF)
        to_outer(i).start()
        done(i)

    def step(j, _):
        slot = lax.rem(j, 2)
        fetch(j, slot).wait()

        @pl.when(j + 1 < blocks)
        def _():
            fetch(j + 1, 1 - slot).start()

        total, start = None, 0
        for x in xs:
            width = arrays[x].shape[1]
            term = dot_f32(arrays[x][...], w_buf[slot, :, start : start + width], 1, 1)
            total = term if total is None else total + term
            start += width
        total = total.astype(BF)
        for u in range(per_block):
            p_buf[per_block * j + u] = total[:, u * PIECE : (u + 1) * PIECE]

        @pl.when(outer)
        def _():
            for u in range(per_block):
                to_inner(per_block * j + u).start()

        @pl.when(j == 0)
        def _():
            for k in range(early, n_arrays):
                load(k).wait()
            before_sum(job, arrays, keep)

        @pl.when(inner)
        def _():
            for u in range(per_block):
                i = per_block * j + u
                first(i)

                @pl.when(j >= 1)
                def _():
                    second(i - per_block)

        if sides:

            @pl.when(j >= 2)
            def _():
                flush(j - 2, slot).wait()

            start = 0
            for a, bs in sides:
                a_t = arrays[a][:, columns(j)].T
                for b in bs:
                    width = arrays[b].shape[1]
                    g_buf[slot, :, start : start + width] = jnp.dot(
                        a_t, arrays[b][...], preferred_element_type=F32
                    ).astype(BF)
                    start += width
            flush(j, slot).start()

        return 0

    lax.fori_loop(0, blocks, step, 0)

    @pl.when(inner)
    def _():
        for u in range(per_block):
            second(pieces - per_block + u)

    @pl.when(outer)
    def _():
        every_piece(lambda i: to_inner(i).wait_send())
        if stagger:

            @pl.when(sec == 0)
            def _():
                pl.semaphore_signal(turn, inc=1, device_id=mate, device_id_type=MESH)

        def arrive(i):
            to_outer(i).wait_recv()
            done(i)

        every_piece(arrive)

    chunks = 5 if n_rows % (5 * 32) == 0 else 1
    chunk = n_rows // chunks
    block = 32 if chunk % 32 == 0 else 16
    height = lambda m: 8 if job[2][0] == "back" and m == 2 else n_rows
    stores = []

    def store(m, rows):
        copy = pltpu.make_async_copy(outs[m].at[rows], outs_hbm[m].at[rows], out_sem.at[len(stores)])
        copy.start()
        stores.append(copy)

    for c in range(chunks):

        def turn_rows(r, _):
            rows = pl.ds(pl.multiple_of(c * chunk + r * block, block), block)
            after_sum(job, rows, lambda i: b_buf.at[i], arrays, outs, keep, sums)
            return 0

        if job[2][0] == "back" or len(outs) > 1:
            lax.fori_loop(0, chunk // block, turn_rows, 0)
        for m in range(len(outs)):
            if height(m) == n_rows:
                store(m, pl.ds(c * chunk, chunk))
    for m in range(len(outs)):
        if height(m) != n_rows:
            store(m, pl.ds(0, height(m)))

    @pl.when(inner)
    def _():
        def sent(i):
            across(i).wait_send()
            to_outer(i).wait_send()

        every_piece(sent)

    if sides:
        flush(blocks - 2, (blocks - 2) % 2).wait()
        flush(blocks - 1, (blocks - 1) % 2).wait()
    for copy in stores:
        copy.wait()


def product_sum(arrays, job, weights, sides=(), stagger=False, key=1):
    assert lax.axis_size("tensor") == 4
    rows, model = arrays[0].shape[0], weights.shape[0]
    pieces = model // PIECE
    depth = sum(arrays[x].shape[1] for x in job[0])
    anywhere = pl.BlockSpec(memory_space=pl.ANY)
    buf = pltpu.VMEM((pieces, rows, PIECE), BF)
    sem = pltpu.SemaphoreType.DMA((pieces,))
    two = pltpu.SemaphoreType.DMA((2,))
    out_shape = []
    for m, dtype in enumerate(job[3]):
        height = 8 if job[2][0] == "back" and m == 2 else rows
        out_shape.append(jax.ShapeDtypeStruct((height, model), dtype))
    scratch = [pltpu.VMEM(x.shape, x.dtype) for x in (*arrays, *out_shape)]
    scratch += [pltpu.SemaphoreType.DMA((len(arrays),)), pltpu.SemaphoreType.DMA((16,))]
    scratch += [pltpu.VMEM((2, BLOCK, depth), BF), buf, buf, buf, two, *[sem] * 6, pltpu.SemaphoreType.REGULAR]
    scratch += [pltpu.VMEM((rows, PIECE), F32)] * 2
    if sides:
        side_width = sum(arrays[b].shape[1] for _, bs in sides for b in bs)
        out_shape.append(jax.ShapeDtypeStruct((model, side_width), BF))
        scratch += [pltpu.VMEM((2, BLOCK, side_width), BF), two]
    out = pl.pallas_call(
        functools.partial(product_sum_kernel, (len(arrays), job, tuple(sides), stagger)),
        out_shape=out_shape,
        in_specs=[anywhere] * (len(arrays) + 1),
        out_specs=[anywhere] * len(out_shape),
        scratch_shapes=scratch,
        compiler_params=pltpu.CompilerParams(
            collective_id=key, has_side_effects=True, vmem_limit_bytes=62 << 20
        ),
        cost_estimate=NO_COST,
        name=f"product_sum_{key}",
    )(*arrays, weights)
    return out if len(out) > 1 else out[0]


def dp_peers(count):
    me = lax.axis_index("dp")
    sec, t = lax.axis_index("section"), lax.axis_index("tensor")
    others = [lax.rem(me + k, count) for k in range(1, count)]
    return me, others, [(sec, t, other) for other in others]


def greet(ids):
    barrier = pltpu.get_barrier_semaphore()
    for device in ids:
        pl.semaphore_signal(barrier, inc=1, device_id=device, device_id_type=MESH)
    pl.semaphore_wait(barrier, len(ids))


def turn_rows(x, cos_ref, sin_ref):
    lane = lax.broadcasted_iota(jnp.int32, x.shape, 1)
    width = x.shape[1]
    partner = jnp.where(lane < HALF, pltpu.roll(x, width - HALF, 1), pltpu.roll(x, HALF, 1))
    return x * cos_ref[...] + partner * sin_ref[...]


def gather_kernel(count, raw_ref, cos_ref, sin_ref, o_ref, t_ref, x_ref, send, recv):
    me, _, ids = dp_peers(count)
    x_ref[...] = turn_rows(raw_ref[...], cos_ref, sin_ref).astype(BF)
    greet(ids)
    copies = [
        pltpu.make_async_remote_copy(
            x_ref, o_ref.at[me], send.at[k], recv.at[k], device_id=device, device_id_type=MESH
        )
        for k, device in enumerate(ids)
    ]
    for copy in copies:
        copy.start()
    o_ref[me] = x_ref[...]
    for copy in copies:
        copy.wait()
    t_ref[...] = o_ref[...].reshape(t_ref.shape[1], t_ref.shape[0]).T


def scatter_kernel(count, x_ref, cos_ref, sin_ref, o_ref, buf, send, recv):
    me, others, ids = dp_peers(count)
    greet(ids)
    copies = [
        pltpu.make_async_remote_copy(
            x_ref.at[others[k]], buf.at[k], send.at[k], recv.at[k], device_id=device, device_id_type=MESH
        )
        for k, device in enumerate(ids)
    ]
    for copy in copies:
        copy.start()
    total = x_ref[me].astype(F32)
    for k, copy in enumerate(copies):
        copy.wait()
        total = total + buf[k].astype(F32)
    o_ref[...] = turn_rows(total, cos_ref, sin_ref).astype(BF)


def gather_rows(raw, cos_rows, sin_rows):
    count = lax.axis_size("dp")
    rows, width = raw.shape
    in_vmem = pl.BlockSpec(memory_space=pltpu.VMEM)
    sem = pltpu.SemaphoreType.DMA((count - 1,))
    out, out_t = pl.pallas_call(
        functools.partial(gather_kernel, count),
        out_shape=(
            jax.ShapeDtypeStruct((count, rows, width), BF),
            jax.ShapeDtypeStruct((width, count * rows), BF),
        ),
        in_specs=[in_vmem] * 3,
        out_specs=(in_vmem, in_vmem),
        scratch_shapes=[pltpu.VMEM((rows, width), BF), sem, sem],
        compiler_params=pltpu.CompilerParams(collective_id=3, has_side_effects=True),
        cost_estimate=NO_COST,
        name="gather_rows",
    )(raw, cos_rows, sin_rows)
    return out.reshape(-1, width), out_t


def scatter_rows(x, cos_rows, sin_rows):
    count = lax.axis_size("dp")
    rows, width = x.shape[0] // count, x.shape[1]
    in_vmem = pl.BlockSpec(memory_space=pltpu.VMEM)
    sem = pltpu.SemaphoreType.DMA((count - 1,))
    return pl.pallas_call(
        functools.partial(scatter_kernel, count),
        out_shape=jax.ShapeDtypeStruct((rows, width), BF),
        in_specs=[in_vmem] * 3,
        out_specs=in_vmem,
        scratch_shapes=[pltpu.VMEM((count - 1, rows, width), x.dtype), sem, sem],
        compiler_params=pltpu.CompilerParams(collective_id=4, has_side_effects=True),
        cost_estimate=NO_COST,
        name="scatter_rows",
    )(x.reshape(count, rows, width), cos_rows, sin_rows)


def finish_kernel(
    g_hbm, gain_ref, out_zero, out_one, in_zero, in_one, mlp_zero, mlp_one, attn_one,
    o_ref, gain_out, got_out, got_in, got_mlp, got_attn,
    mine, away, got, xs, ys, xr, yr, gains, load_sem, send, recv, mate_send, mate_recv, gain_send, gain_recv,
):
    sec, t, dat = lax.axis_index("section"), lax.axis_index("tensor"), lax.axis_index("dp")
    flip_x = dat + 1 - 2 * lax.rem(dat, 2)
    flip_y = lax.rem(dat + 2, 4)
    across = lax.rem(flip_x + 2, 4)
    by_x, by_y, mate = (sec, t, flip_x), (sec, t, flip_y), (1 - sec, t, dat)
    peers = [
        mate, by_x, by_y, (sec, t, across),
        (1 - sec, t, flip_x), (1 - sec, t, flip_y), (1 - sec, t, across),
    ]
    rows = g_hbm.shape[1] // 2
    upper, lower = pl.ds(0, rows), pl.ds(rows, rows)
    order = (across, flip_x, flip_y, dat)
    loads = []
    for k, block in enumerate(order):
        loads.append(pltpu.make_async_copy(g_hbm.at[2 * block + 1 - sec], away.at[k], load_sem.at[k]))
        loads.append(pltpu.make_async_copy(g_hbm.at[2 * block + sec], mine.at[k], load_sem.at[4 + k]))
    for copy in loads:
        copy.start()
    greet(peers)

    def remote(src, dst, k, device):
        return pltpu.make_async_remote_copy(
            src, dst, send.at[k], recv.at[k], device_id=device, device_id_type=MESH
        )

    def to_mate(src, dst, k):
        return pltpu.make_async_remote_copy(
            src, dst, mate_send.at[k], mate_recv.at[k], device_id=mate, device_id_type=MESH
        )

    swaps = [remote(away.at[k], got.at[k], k, mate) for k in range(4)]
    for k in range(4):
        loads[2 * k].wait()
        swaps[k].start()
    gain_copies = [
        pltpu.make_async_remote_copy(
            gain_ref.at[peer[0], peer[2]], gains.at[k], gain_send.at[k], gain_recv.at[k],
            device_id=peer, device_id_type=MESH,
        )
        for k, peer in enumerate(peers)
    ]
    for copy in gain_copies:
        copy.start()
    outs = []
    for k in range(4):
        loads[2 * k + 1].wait()
        swaps[k].wait_recv()
        mine[k] = (mine[k].astype(F32) + got[k].astype(F32)).astype(BF)
        if k == 0:
            outs += [remote(mine.at[0, upper], xs.at[0], 4, by_x), remote(mine.at[0, lower], ys.at[0], 5, by_y)]
        if k == 1:
            outs += [remote(mine.at[1, upper], xs.at[1], 6, by_x)]
        if k == 2:
            outs += [remote(mine.at[2, lower], ys.at[1], 7, by_y)]
        for copy in outs[-(2 if k == 0 else 1) :]:
            if k < 3:
                copy.start()

    @pl.when(sec == 0)
    def _():
        to_mate(in_one, got_in, 0).start()
        to_mate(out_one, got_out, 1).start()
        to_mate(mlp_one, got_mlp, 2).start()
        to_mate(attn_one, got_attn, 3).start()

    @pl.when(sec == 1)
    def _():
        to_mate(in_zero, got_in, 0).start()
        to_mate(out_zero, got_out, 1).start()
        to_mate(mlp_zero, got_mlp, 2).start()

    outs[0].wait_recv()
    mine[2, upper] = (mine[2, upper].astype(F32) + xs[0].astype(F32)).astype(BF)
    outs.append(remote(mine.at[2, upper], yr, 8, by_y))
    outs[4].start()
    outs[1].wait_recv()
    mine[1, lower] = (mine[1, lower].astype(F32) + ys[0].astype(F32)).astype(BF)
    outs.append(remote(mine.at[1, lower], xr, 9, by_x))
    outs[5].start()
    total = gain_ref[sec, dat]
    for k, copy in enumerate(gain_copies):
        copy.wait()
        total = total + gains[k]
    gain_out[...] = total
    outs[2].wait_recv()
    outs[3].wait_recv()
    outs[4].wait_recv()
    o_ref[upper] = (mine[3, upper].astype(F32) + xs[1].astype(F32) + yr[...].astype(F32)).astype(BF)
    outs[5].wait_recv()
    o_ref[lower] = (mine[3, lower].astype(F32) + ys[1].astype(F32) + xr[...].astype(F32)).astype(BF)

    @pl.when(sec == 1)
    def _():
        to_mate(o_ref, got_attn, 3).start()

    for copy in swaps + outs:
        copy.wait_send()
    to_mate(in_one, got_in, 0).wait()
    to_mate(out_one, got_out, 1).wait()
    to_mate(mlp_one, got_mlp, 2).wait()
    to_mate(attn_one, got_attn, 3).wait()


def finish(g, gains, out_zero, out_one, in_zero, in_one, mlp_zero, mlp_one, attn_one):
    rows, width = g.shape[0] // 8, g.shape[1]
    part = pltpu.VMEM((2, rows // 2, width), BF)
    whole = pltpu.VMEM((4, rows, width), BF)
    end = pltpu.VMEM((rows // 2, width), BF)
    in_vmem, anywhere = pl.BlockSpec(memory_space=pltpu.VMEM), pl.BlockSpec(memory_space=pl.ANY)
    like = lambda x: jax.ShapeDtypeStruct(x.shape, x.dtype)
    dma = lambda n: pltpu.SemaphoreType.DMA((n,))
    return pl.pallas_call(
        finish_kernel,
        out_shape=(
            jax.ShapeDtypeStruct((rows, width), BF),
            jax.ShapeDtypeStruct(gains.shape[2:], F32),
            like(out_zero), like(in_zero), like(mlp_zero), like(attn_one),
        ),
        in_specs=[anywhere, in_vmem, *[anywhere] * 7],
        out_specs=(in_vmem, in_vmem, *[anywhere] * 4),
        scratch_shapes=[
            whole, whole, whole, part, part, end, end, pltpu.VMEM((7, *gains.shape[2:]), F32),
            dma(8), dma(10), dma(10), dma(4), dma(4), dma(7), dma(7),
        ],
        compiler_params=pltpu.CompilerParams(
            collective_id=12, has_side_effects=True, vmem_limit_bytes=40 << 20
        ),
        cost_estimate=NO_COST,
        name="finish",
    )(g.reshape(8, rows, width), gains, out_zero, out_one, in_zero, in_one, mlp_zero, mlp_one, attn_one)


def finish_apart(g, gains, out_zero, out_one, in_zero, in_one, mlp_zero, mlp_one, attn_one):
    first_core = lax.axis_index("section") == 0
    half = reduce_gradient(g)
    swap = lambda zero, one: lax.ppermute(jnp.where(first_core, one, zero), "section", [(0, 1), (1, 0)])
    return (
        half, share_sums(gains), swap(out_zero, out_one), swap(in_zero, in_one), swap(mlp_zero, mlp_one),
        swap(half, attn_one),
    )


def write_kernel(
    split, out_zero, out_one, got_out, in_zero, in_one, got_in, mlp_zero, mlp_one, got_mlp, attn_zero, attn_one, got_attn,
    out_hbm, in_hbm, q_hbm, k_hbm, v_hbm, o_hbm, gate_hbm, up_hbm, down_hbm,
    mlp, attn, got_narrow, got_wide, q_buf, k_buf, v_buf, o_buf, gate_buf, up_buf, down_buf, load_sem, store_sem,
):
    sec = lax.axis_index("section")
    half = mlp_zero.shape[0]
    low, high = pl.ds(0, half), pl.ds(half, half)

    def start(own_out, own_in, mlp_low, mlp_high, attn_low, attn_high):
        pltpu.make_async_copy(mlp_low, mlp.at[low], load_sem.at[0]).start()
        pltpu.make_async_copy(mlp_high, mlp.at[high], load_sem.at[1]).start()
        pltpu.make_async_copy(attn_low, attn.at[low], load_sem.at[2]).start()
        pltpu.make_async_copy(attn_high, attn.at[high], load_sem.at[3]).start()
        pltpu.make_async_copy(own_out, out_hbm.at[sec], store_sem.at[0]).start()
        pltpu.make_async_copy(own_in, in_hbm.at[sec], store_sem.at[1]).start()

    load_in = pltpu.make_async_copy(got_in, got_narrow, load_sem.at[4])
    load_in.start()

    @pl.when(sec == 0)
    def _():
        start(out_zero, in_zero, mlp_zero, got_mlp, attn_zero, got_attn)

    @pl.when(sec == 1)
    def _():
        start(out_one, in_one, got_mlp, mlp_one, got_attn, attn_one)

    other = pltpu.make_async_copy(got_out, out_hbm.at[1 - sec], store_sem.at[2])
    other.start()
    stores = [other]

    def store(src, dst, k):
        stores.append(pltpu.make_async_copy(src, dst, store_sem.at[k]))
        stores[-1].start()

    def in_rows(count, block, body):
        def turn(r, _):
            body(pl.ds(pl.multiple_of(r * block, block), block))
            return 0

        lax.fori_loop(0, count // block, turn, 0)

    def widen(rows):
        got_wide[rows] = got_narrow[rows].astype(F32)

    load_in.wait()
    in_rows(got_narrow.shape[0], 32, widen)
    store(got_wide, in_hbm.at[1 - sec], 3)
    units = gate_buf.shape[1]
    width = q_buf.shape[1]
    span = k_buf.shape[1]
    pltpu.make_async_copy(mlp_zero, mlp.at[low], load_sem.at[0]).wait()
    pltpu.make_async_copy(mlp_zero, mlp.at[high], load_sem.at[1]).wait()

    def gates(rows):
        gate_buf[rows] = mlp[rows, :units].astype(F32)
        up_buf[rows] = mlp[rows, units : 2 * units].astype(F32)

    in_rows(2 * half, 32, gates)
    store(gate_buf, gate_hbm, 4)
    store(up_buf, up_hbm, 5)
    for c in range(0, units, 128):
        down_buf[c : c + 128] = mlp[:, 2 * units + c : 2 * units + c + 128].astype(F32).T
    store(down_buf, down_hbm, 6)
    pltpu.make_async_copy(attn_one, attn.at[low], load_sem.at[2]).wait()
    pltpu.make_async_copy(attn_one, attn.at[high], load_sem.at[3]).wait()

    def projections(rows):
        q_buf[rows] = attn[rows, :width].astype(F32)
        k_buf[rows] = attn[rows, width : width + span].astype(F32)
        v_buf[rows] = attn[rows, width + span : split].astype(F32)

    in_rows(2 * half, 32, projections)
    for c in range(0, width, 128):
        o_buf[c : c + 128] = attn[:, split + c : split + c + 128].astype(F32).T
    store(q_buf, q_hbm, 7)
    store(k_buf, k_hbm, 8)
    store(v_buf, v_hbm, 9)
    store(o_buf, o_hbm, 10)
    for copy in stores:
        copy.wait()
    pltpu.make_async_copy(out_zero, out_hbm.at[sec], store_sem.at[0]).wait()
    pltpu.make_async_copy(in_zero, in_hbm.at[sec], store_sem.at[1]).wait()


def write_results(outs, ins, mlps, attns, width, span, units):
    rows, model = outs[0].shape
    shard = 2 * mlps[0].shape[0]
    anywhere = pl.BlockSpec(memory_space=pl.ANY)
    shapes = [
        (shard, width), (shard, span), (shard, span), (width, shard), (shard, units), (shard, units), (units, shard),
    ]
    return pl.pallas_call(
        functools.partial(write_kernel, width + 2 * span),
        out_shape=[
            jax.ShapeDtypeStruct((2, rows, model), BF),
            jax.ShapeDtypeStruct((2, rows, model), F32),
            *[jax.ShapeDtypeStruct(shape, F32) for shape in shapes],
        ],
        in_specs=[anywhere] * 12,
        out_specs=[anywhere] * 9,
        scratch_shapes=[
            pltpu.VMEM((shard, mlps[0].shape[1]), BF),
            pltpu.VMEM((shard, attns[0].shape[1]), BF),
            pltpu.VMEM((rows, model), BF),
            pltpu.VMEM((rows, model), F32),
            *[pltpu.VMEM(shape, F32) for shape in shapes],
            pltpu.SemaphoreType.DMA((5,)),
            pltpu.SemaphoreType.DMA((11,)),
        ],
        compiler_params=pltpu.CompilerParams(vmem_limit_bytes=56 << 20),
        cost_estimate=NO_COST,
        name="write_results",
    )(*outs, *ins, *mlps, *attns)


def share_kernel(count, x_ref, o_ref, buf, send, recv):
    sec, t, dat = lax.axis_index("section"), lax.axis_index("tensor"), lax.axis_index("dp")
    peers = [
        (lax.rem(sec + k // count, 2), t, lax.rem(dat + k % count, count)) for k in range(1, 2 * count)
    ]
    greet(peers)
    copies = [
        pltpu.make_async_remote_copy(
            x_ref.at[peer[0], peer[2]], buf.at[k], send.at[k], recv.at[k], device_id=peer, device_id_type=MESH
        )
        for k, peer in enumerate(peers)
    ]
    for copy in copies:
        copy.start()
    total = x_ref[sec, dat]
    for k, copy in enumerate(copies):
        copy.wait()
        total = total + buf[k]
    o_ref[...] = total


def share_sums(x):
    count = lax.axis_size("dp")
    in_vmem = pl.BlockSpec(memory_space=pltpu.VMEM)
    sem = pltpu.SemaphoreType.DMA((2 * count - 1,))
    return pl.pallas_call(
        functools.partial(share_kernel, count),
        out_shape=jax.ShapeDtypeStruct(x.shape[2:], F32),
        in_specs=[in_vmem],
        out_specs=in_vmem,
        scratch_shapes=[pltpu.VMEM((2 * count - 1, *x.shape[2:]), F32), sem, sem],
        compiler_params=pltpu.CompilerParams(collective_id=13, has_side_effects=True),
        cost_estimate=NO_COST,
        name="share_sums",
    )(x)


def group_start(first_row):
    past = lax.max(first_row - TRUNK, 0)
    return pl.multiple_of(TRUNK + GROUP * lax.div(past, GROUP), 128)


def windows(tree_len, rows, tile, first_row):
    if tile % 128 == 0 and GROUP % tile == 0 and TRUNK % tile == 0 and rows % tile == 0:
        return (pl.ds(0, TRUNK), pl.ds(group_start(first_row), GROUP))
    return (pl.ds(0, tree_len),)


def head_rows(ref, head):
    return ref[head * HEAD : (head + 1) * HEAD, :]


def beside(ref, head, count):
    parts = [head_rows(ref, head + k) for k in range(count)]
    return parts[0] if count == 1 else jnp.concatenate(parts, axis=1)


def turned_beside(ref, cos, sin, head, count):
    parts = []
    for k in range(count):
        rows = head_rows(ref, head + k)
        first, second = rows[:HALF], rows[HALF:]
        parts.append(jnp.concatenate([first * cos - second * sin, second * cos + first * sin], axis=0))
    whole = parts[0] if count == 1 else jnp.concatenate(parts, axis=1)
    return (whole.astype(BF).astype(F32) * HEAD**-0.5).astype(BF)


def as_rows(x, tile, count):
    parts = [x[:, k * tile : (k + 1) * tile] for k in range(count)]
    return (parts[0] if count == 1 else jnp.concatenate(parts, axis=0)).T


def over_groups(groups, step, body):
    for group in range(groups):
        body(group, slice(group * step * HEAD, (group + 1) * step * HEAD))


def attend_kernel(
    rows, step, start_ref, q_ref, kv_ref, kvt_ref, bias_ref, cos_ref, sin_ref, o_ref, on_ref, lse_ref
):
    tile = q_ref.shape[1]
    heads = q_ref.shape[0] // HEAD
    first_row = start_ref[0] + pl.program_id(0) * tile
    wins = windows(kv_ref.shape[0], rows, tile, first_row)

    def body(group, lanes):
        head = group * step
        q = turned_beside(q_ref, cos_ref[...], sin_ref[...], head, step)
        scores = []
        for win in wins:
            bias = bias_ref[win, :].astype(F32)
            bias = bias if step == 1 else jnp.concatenate([bias] * step, axis=1)
            scores.append(dot_f32(kv_ref[win, :HEAD], q, 1, 0) + bias)
        top = functools.reduce(jnp.maximum, [jnp.max(s, 0, keepdims=True) for s in scores])
        expo = [jnp.exp(s - top) for s in scores]
        total = sum(jnp.sum(e, 0, keepdims=True) for e in expo)
        out = sum(dot_f32(kvt_ref[HEAD:, win], e.astype(BF), 1, 0) for win, e in zip(wins, expo))
        out = out / total
        on_ref[:, lanes] = as_rows(out, tile, step).astype(BF)
        lse_ref[group, 0] = top + jnp.log(total)
        out = out.astype(BF)
        for k in range(step):
            o_ref[(head + k) * HEAD : (head + k + 1) * HEAD, :] = out[:, k * tile : (k + 1) * tile]

    over_groups(heads // step, step, body)


def attend_back_kernel(
    rows, step, start_ref, q_ref, do_ref, o_ref, lse_ref, kv_ref, kvt_ref, bias_ref, cos_ref, sin_ref,
    dq_ref, dkv_ref, dk_acc, dv_acc,
):
    tile = q_ref.shape[1]
    heads = q_ref.shape[0] // HEAD
    first_row = start_ref[0] + pl.program_id(0) * tile
    wins = windows(kv_ref.shape[0], rows, tile, first_row)

    @pl.when(pl.program_id(0) == 0)
    def _():
        dk_acc[...] = jnp.zeros_like(dk_acc)
        dv_acc[...] = jnp.zeros_like(dv_acc)

    def body(group, lanes):
        head = group * step
        cos, sin = cos_ref[...], sin_ref[...]
        q = turned_beside(q_ref, cos, sin, head, step)
        do = beside(do_ref, head, step)
        out = beside(o_ref, head, step)
        lse = lse_ref[group, 0]
        delta = jnp.sum(do.astype(F32) * out.astype(F32), 0, keepdims=True)
        dq = jnp.zeros((HEAD, step * tile), F32)
        for win in wins:
            bias = bias_ref[win, :].astype(F32)
            bias = bias if step == 1 else jnp.concatenate([bias] * step, axis=1)
            p = jnp.exp(dot_f32(kv_ref[win, :HEAD], q, 1, 0) + bias - lse)
            dp = dot_f32(kv_ref[win, HEAD:], do, 1, 0)
            ds = (p * (dp - delta)).astype(BF)
            dk_acc[win, :] += dot_f32(ds, q, 1, 1)
            dv_acc[win, :] += dot_f32(p.astype(BF), do, 1, 1)
            dq = dq + dot_f32(kvt_ref[:HEAD, win], ds, 1, 0)
        dq = dq * HEAD**-0.5
        turned = []
        for k in range(step):
            first = dq[:HALF, k * tile : (k + 1) * tile]
            second = dq[HALF:, k * tile : (k + 1) * tile]
            turned += [first * cos + second * sin, second * cos - first * sin]
        dq_ref[:, lanes] = jnp.concatenate(turned, axis=0).T.astype(BF)

    over_groups(heads // step, step, body)

    @pl.when(pl.program_id(0) == pl.num_programs(0) - 1)
    def _():
        dkv_ref[...] = jnp.concatenate([dk_acc[...], dv_acc[...]], axis=1).astype(BF)


def row_tile(rows):
    return 128 if rows % 128 == 0 else rows


def attend(start, q_t, kv, kv_t, bias_t, cos_t, sin_t):
    width, rows = q_t.shape
    heads, tree_len, tile = width // HEAD, kv.shape[0], row_tile(rows)
    step = 2 if tile % 128 == 0 and heads % 2 == 0 else 1
    column = lambda i, s: (0, i)
    whole = lambda i, s: (0, 0)
    return pl.pallas_call(
        functools.partial(attend_kernel, rows, step),
        out_shape=(
            jax.ShapeDtypeStruct((width, rows), BF),
            jax.ShapeDtypeStruct((rows, width), BF),
            jax.ShapeDtypeStruct((heads // step, rows // tile, 1, step * tile), F32),
        ),
        grid_spec=pltpu.PrefetchScalarGridSpec(
            num_scalar_prefetch=1,
            grid=(rows // tile,),
            in_specs=[
                pl.BlockSpec((width, tile), column),
                pl.BlockSpec((tree_len, 2 * HEAD), whole),
                pl.BlockSpec((2 * HEAD, tree_len), whole),
                pl.BlockSpec((tree_len, tile), column),
                pl.BlockSpec((HALF, tile), column),
                pl.BlockSpec((HALF, tile), column),
            ],
            out_specs=(
                pl.BlockSpec((width, tile), column),
                pl.BlockSpec((tile, width), lambda i, s: (i, 0)),
                pl.BlockSpec((heads // step, 1, 1, step * tile), lambda i, s: (0, i, 0, 0)),
            ),
        ),
        compiler_params=pltpu.CompilerParams(vmem_limit_bytes=40 << 20),
        cost_estimate=NO_COST,
        name="attend",
    )(start, q_t, kv, kv_t, bias_t, cos_t, sin_t)


def attend_back(start, q_t, do_t, o_t, lse, kv, kv_t, bias_t, cos_t, sin_t):
    width, rows = q_t.shape
    heads, tree_len, tile = width // HEAD, kv.shape[0], row_tile(rows)
    step = 2 if tile % 128 == 0 and heads % 2 == 0 else 1
    column = lambda i, s: (0, i)
    whole = lambda i, s: (0, 0)
    return pl.pallas_call(
        functools.partial(attend_back_kernel, rows, step),
        out_shape=(
            jax.ShapeDtypeStruct((rows, width), BF),
            jax.ShapeDtypeStruct((tree_len, 2 * HEAD), BF),
        ),
        grid_spec=pltpu.PrefetchScalarGridSpec(
            num_scalar_prefetch=1,
            grid=(rows // tile,),
            in_specs=[
                pl.BlockSpec((width, tile), column),
                pl.BlockSpec((width, tile), column),
                pl.BlockSpec((width, tile), column),
                pl.BlockSpec((heads // step, 1, 1, step * tile), lambda i, s: (0, i, 0, 0)),
                pl.BlockSpec((tree_len, 2 * HEAD), whole),
                pl.BlockSpec((2 * HEAD, tree_len), whole),
                pl.BlockSpec((tree_len, tile), column),
                pl.BlockSpec((HALF, tile), column),
                pl.BlockSpec((HALF, tile), column),
            ],
            out_specs=(
                pl.BlockSpec((tile, width), lambda i, s: (i, 0)),
                pl.BlockSpec((tree_len, 2 * HEAD), whole),
            ),
            scratch_shapes=[pltpu.VMEM((tree_len, HEAD), F32), pltpu.VMEM((tree_len, HEAD), F32)],
        ),
        compiler_params=pltpu.CompilerParams(vmem_limit_bytes=48 << 20),
        cost_estimate=NO_COST,
        name="attend_back",
    )(start, q_t, do_t, o_t, lse, kv, kv_t, bias_t, cos_t, sin_t)


def layer_attention(normed, weights, tables):
    gain_one, gain_two, w_attn, w_mlp, width, split, units = weights
    start, bias_t, cos_t, sin_t, cos_rows, sin_rows = tables
    q_t = dot_f32(w_attn[:, :width], normed, 0, 1)
    kv, kv_t = gather_rows(
        jnp.dot(normed, w_attn[:, width:split], preferred_element_type=F32), cos_rows, -sin_rows
    )
    o_t, o, lse = attend(start, q_t, kv, kv_t, bias_t, cos_t, sin_t)
    return (q_t, kv, kv_t, o_t, lse), o


def attention_backward(grad_attn, weights, tables, kept):
    gain_one, gain_two, w_attn, w_mlp, width, split, units = weights
    start, bias_t, cos_t, sin_t, cos_rows, sin_rows = tables
    q_t, kv, kv_t, o_t, lse = kept
    do_t = dot_f32(w_attn[:, split : split + width], grad_attn, 0, 1).astype(BF)
    dq, dkv_part = attend_back(start, q_t, do_t, o_t, lse, kv, kv_t, bias_t, cos_t, sin_t)
    return dq, scatter_rows(dkv_part, cos_rows, sin_rows)


def layer_units(normed, weights):
    units = weights[-1]
    gate_up = jnp.dot(normed, weights[3][:, : 2 * units], preferred_element_type=F32)
    gate, up = gate_up[:, :units], gate_up[:, units:]
    return gate, up, (gate * jax.nn.sigmoid(gate) * up).astype(BF)


def units_backward(branch, weights, gate, up):
    units = weights[-1]
    d_inner = dot_f32(branch, weights[3][:, 2 * units :], 1, 0)
    sig = jax.nn.sigmoid(gate)
    d_gate = (d_inner * up * sig * (1.0 + gate * (1.0 - sig))).astype(BF)
    d_up = (d_inner * gate * sig).astype(BF)
    return d_gate, d_up


def reduce_gradient(x):
    return lax.psum_scatter(x, BOTH, scatter_dimension=0, tiled=True)


def shards(
    inputs, cotangent, seg_ids, positions, parents, gain_attn, w_query, key_weight, value_weight,
    w_out, gain_mlp, w_gate, w_up, w_down,
):
    sec = lax.axis_index("section")
    data = lax.axis_index("dp")
    sections = lax.axis_size("section")
    devices = lax.axis_size("dp")
    assert sections == 2 and inputs.shape[0] == 2
    first_core = sec == 0
    rows, model = inputs.shape[1], inputs.shape[2]
    swap = [(0, 1), (1, 0)]

    tree = lax.dynamic_index_in_dim(inputs, sec, 0, keepdims=False)
    hidden = tree.astype(F32)
    segments = lax.dynamic_index_in_dim(seg_ids, sec, 0, keepdims=False)
    places = lax.dynamic_index_in_dim(positions, sec, 0, keepdims=False)
    parent = lax.dynamic_index_in_dim(parents, sec, 0, keepdims=False)

    width, span, units = w_query.shape[2], key_weight.shape[2], w_gate.shape[2]
    split = width + 2 * span
    shard_list = (
        jnp.concatenate(
            [w_query[0], key_weight[0], value_weight[0], w_out[0].T, gain_attn.T, gain_mlp.T], 1
        ).astype(BF),
        jnp.concatenate([w_gate[0], w_up[0], w_down[0].T], 1).astype(BF),
    )
    halves = []
    for shard in shard_list:
        half = shard.shape[0] // 2
        low, high = shard[:half], shard[half:]
        got = lax.ppermute(jnp.where(first_core, high, low), "section", swap)
        halves.append((jnp.where(first_core, low, got), jnp.where(first_core, got, high)))
    def gathered(halves):
        return [lax.all_gather(half, BOTH, axis=0, tiled=True) for half in halves]

    def with_gains(w_attn, w_mlp):
        gains = w_attn[:, split + width :].astype(F32).T
        return (gains[0:1], gains[1:2], w_attn, w_mlp, width, split, units)

    (attn_zero, attn_one), (mlp_zero, mlp_one) = halves
    attn_zero = jnp.concatenate([attn_zero, attn_one[:, split + width : split + width + 1]], 1)
    attn_zero, mlp_zero = gathered((attn_zero, mlp_zero))
    zero = with_gains(attn_zero, mlp_zero)
    attn_one, mlp_one = gathered((attn_one, mlp_one))
    one_gain = attn_zero[:, split + width + 2 :].astype(F32).T

    seg_count = parent.shape[0]
    labels = jnp.arange(seg_count, dtype=jnp.int32)
    parent_hot = (parent[:, None] == labels[None, :]).astype(F32)
    ancestry = jnp.eye(seg_count, dtype=F32) + parent_hot + jnp.dot(parent_hot, parent_hot)
    ancestry = (ancestry > 0.5).astype(F32)
    row_start = data * rows
    seg_rows = lax.dynamic_slice_in_dim(segments, row_start, rows, 0)
    pos_rows = lax.dynamic_slice_in_dim(places, row_start, rows, 0)
    key_hot = (segments[:, None] == labels[None, :]).astype(F32)
    query_hot = (labels[:, None] == seg_rows[None, :]).astype(F32)
    reach = jnp.dot(key_hot, jnp.dot(ancestry.T, query_hot))
    allowed = (reach > 0.5) & (places[:, None] <= pos_rows[None, :])
    bias_t = jnp.where(allowed, 0.0, MASKED).astype(BF)
    frequency = THETA ** (-(jnp.arange(HALF, dtype=F32) * 2.0 / HEAD))
    angles = frequency[:, None] * pos_rows.astype(F32)[None, :]
    cos_t, sin_t = jnp.cos(angles), jnp.sin(angles)
    ones = jnp.ones((rows, HEAD), F32)
    cos_rows = jnp.concatenate([cos_t.T, cos_t.T, ones], 1)
    sin_rows = jnp.concatenate([sin_t.T, -sin_t.T, 0 * ones], 1)
    tables = (row_start.astype(jnp.int32).reshape(1), bias_t, cos_t, sin_t, cos_rows, sin_rows)

    split_out, split_down = split, 2 * units
    wide, narrow = (F32, BF), (BF, BF)
    back = (F32, BF, F32)

    normed_zero = (hidden * lax.rsqrt(jnp.mean(hidden * hidden, -1, keepdims=True) + EPSILON) * zero[0]).astype(BF)
    kept_zero, o_zero = layer_attention(normed_zero, zero, tables)
    middle_zero, r_zero = product_sum(
        (o_zero, tree, zero[1]), ((0,), split_out, ("add", (1, 2)), wide), zero[2], stagger=True, key=1
    )
    gate_zero, up_zero, inner_zero = layer_units(r_zero, zero)
    out_zero, normed_one = product_sum(
        (inner_zero, middle_zero, one_gain), ((0,), split_down, ("add", (1, 2)), narrow), zero[3], key=5
    )

    out_zero, normed_one, attn_one = lax.optimization_barrier((out_zero, normed_one, attn_one))
    one = with_gains(attn_one, mlp_one)
    kept_one, o_one = layer_attention(normed_one, one, tables)
    middle_one, r_one = product_sum(
        (o_one, out_zero, one[1]), ((0,), split_out, ("add", (1, 2)), wide), one[2], key=2
    )
    gate_one, up_one, inner_one = layer_units(r_one, one)
    branch = lax.dynamic_index_in_dim(cotangent, sec, 0, keepdims=False)
    d_gate, d_up = units_backward(branch, one, gate_one, up_one)
    out_one, d_mlp_one = product_sum(
        (inner_one, middle_one, r_one, branch, d_gate, d_up), ((0,), split_down, ("add", (1,)), (BF,)),
        one[3], ((2, (4, 5)), (3, (0,))), key=6,
    )
    d_gate, out_one = lax.optimization_barrier((d_gate, out_one))
    grad_middle, grad_attn, d_gain_mlp_one = product_sum(
        (d_gate, d_up, middle_one, branch, one[1]), ((0, 1), 0, ("back", (2, 3, 4)), back), one[3], key=8
    )
    g_mlp_one = reduce_gradient(d_mlp_one)
    dq, dkv = attention_backward(grad_attn, one, tables, kept_one)
    grad_one, branch, d_gain_attn_one, d_attn_one = product_sum(
        (dq, dkv, out_zero, grad_middle, one[0], normed_one, grad_attn, o_one),
        ((0, 1), 0, ("back", (2, 3, 4)), back),
        one[2], ((5, (0, 1)), (6, (7,))), key=7,
    )
    g_attn_one = reduce_gradient(d_attn_one)

    d_gate, d_up = units_backward(branch, zero, gate_zero, up_zero)
    grad_middle, grad_attn, d_gain_mlp_zero, d_mlp_zero = product_sum(
        (d_gate, d_up, inner_zero, middle_zero, branch, r_zero, zero[1]),
        ((0, 1), 0, ("back", (3, 4, 6)), back),
        zero[3], ((5, (0, 1)), (4, (2,))), key=9,
    )
    g_mlp_zero = reduce_gradient(d_mlp_zero)
    grad_attn, g_mlp_one = lax.optimization_barrier((grad_attn, g_mlp_one))
    dq, dkv = attention_backward(grad_attn, zero, tables, kept_zero)
    dq, g_attn_one = lax.optimization_barrier((dq, g_attn_one))
    grad_zero, send_zero, d_gain_attn_zero, d_attn_zero = product_sum(
        (dq, dkv, tree, grad_middle, zero[0], normed_zero, grad_attn, o_zero),
        ((0, 1), 0, ("back", (2, 3, 4)), back),
        zero[2], ((5, (0, 1)), (6, (7,))), key=11,
    )
    d_gain_attn_zero, d_gain_mlp_zero, d_gain_attn_one, d_gain_mlp_one = [
        jnp.sum(x, 0) for x in (d_gain_attn_zero, d_gain_mlp_zero, d_gain_attn_one, d_gain_mlp_one)
    ]
    d_gains = jnp.stack([d_gain_attn_zero, d_gain_mlp_zero, d_gain_attn_one, d_gain_mlp_one])
    d_gains = d_gains.reshape(2, 2, devices, -1).swapaxes(1, 2).reshape(2, devices, -1, 128)

    ending = finish if devices == 4 else finish_apart
    g_attn_zero, g_gain, got_out, got_in, got_mlp, got_attn = ending(
        d_attn_zero, d_gains, out_zero, out_one, send_zero, branch,
        g_mlp_zero, g_mlp_one, g_attn_one,
    )

    layer_output, input_grad, *grads = write_results(
        (out_zero, out_one, got_out), (grad_zero, grad_one, got_in), (g_mlp_zero, g_mlp_one, got_mlp),
        (g_attn_zero, g_attn_one, got_attn), width, span, units,
    )
    g_query, g_key, g_value, g_out, g_gate, g_up, g_down = [grad[None] for grad in grads]
    g_gain = g_gain.reshape(2, 1, -1)
    return (
        layer_output[None], input_grad[None], g_gain[0], g_query, g_key, g_value, g_out, g_gain[1], g_gate, g_up, g_down,
    )


def solution(mesh):
    in_specs = (
        P(None, "dp", None),
        P(None, "dp", None),
        P(),
        P(),
        P(),
        P("section", "dp"),
        P("section", "dp", "tensor"),
        P("section", "dp", "tensor"),
        P("section", "dp", "tensor"),
        P("section", "tensor", "dp"),
        P("section", "dp"),
        P("section", "dp", "tensor"),
        P("section", "dp", "tensor"),
        P("section", "tensor", "dp"),
    )
    out_specs = (
        P("section", None, "dp", None),
        P("section", None, "dp", None),
        P("section", "dp"),
        P("section", "dp", "tensor"),
        P("section", "dp", "tensor"),
        P("section", "dp", "tensor"),
        P("section", "tensor", "dp"),
        P("section", "dp"),
        P("section", "dp", "tensor"),
        P("section", "dp", "tensor"),
        P("section", "tensor", "dp"),
    )
    return jax.shard_map(shards, mesh=mesh, in_specs=in_specs, out_specs=out_specs, check_vma=False)
```

```python
import functools

import jax
import jax.numpy as jnp
from jax import lax
from jax.experimental import pallas as pl
from jax.experimental.pallas import tpu as pltpu
from jax.sharding import PartitionSpec as P

HEAD = 64
HALF = HEAD // 2
TRUNK = 1024
GROUP = 384
EPSILON = 1e-05
THETA = 10000.0
MASKED = -1e30
BF = jnp.bfloat16
F32 = jnp.float32
MESH = pl.DeviceIdType.MESH
BOTH = ("dp", "section")


def dot_f32(a, b, ca, cb):
    return lax.dot_general(a, b, (((ca,), (cb,)), ((), ())), preferred_element_type=F32)


BLOCK = 256
PIECE = 128
NO_COST = pl.CostEstimate(flops=1, transcendentals=0, bytes_accessed=1)


def columns_of(i):
    return pl.ds(pl.multiple_of(i * PIECE, PIECE), PIECE)


def gain_row(arrays, place, at):
    return arrays[place[0]][place[1] : place[1] + 1, at]


def row_scale(squares, model):
    return lax.rsqrt(jnp.sum(squares, 1, keepdims=True) * (1.0 / model) + EPSILON)


def before_sum(job, arrays, keep):
    kind, places = job[2]
    if kind == "back":
        value = arrays[places[0]]
        model = value.shape[1]
        squares = jnp.zeros(keep.shape, F32)
        for i in range(model // PIECE):
            x = value[:, i * PIECE : (i + 1) * PIECE].astype(F32)
            squares += x * x
        keep[...] = jnp.broadcast_to(row_scale(squares, model), keep.shape)


def with_piece(job, i, total, arrays, outs, keep, sums):
    kind, places = job[2]
    at = columns_of(i)
    if kind == "add":
        y = (arrays[places[0]][:, at].astype(F32) + total).astype(outs[0].dtype)
        outs[0][:, at] = y
        if len(outs) > 1:
            sums[...] += y.astype(F32) * y.astype(F32)
    if kind == "back":
        product = total * arrays[places[0]][:, at].astype(F32) * keep[...]
        sums[...] += product * gain_row(arrays, places[2], at)
        outs[2][:, at] = jnp.sum(product.reshape(-1, 8, PIECE), 0)


def after_sum(job, rows, total, arrays, outs, keep, sums):
    kind, places = job[2]
    model = arrays[places[0]].shape[1]
    at = lambda i: slice(i * PIECE, (i + 1) * PIECE)
    if kind == "add" and len(outs) > 1:
        scale = row_scale(sums[rows], model)
        for i in range(model // PIECE):
            y = outs[0][rows, at(i)].astype(F32)
            outs[1][rows, at(i)] = (y * scale * gain_row(arrays, places[1], at(i))).astype(BF)
    if kind == "back":
        mean = jnp.sum(sums[rows], 1, keepdims=True) * (1.0 / model)
        scale = keep[rows]
        for i in range(model // PIECE):
            unit = arrays[places[0]][rows, at(i)].astype(F32) * scale
            grad = total(i)[rows].astype(F32) * gain_row(arrays, places[2], at(i))
            out = arrays[places[1]][rows, at(i)].astype(F32) + scale * (grad - unit * mean)
            outs[0][rows, at(i)] = out
            outs[1][rows, at(i)] = out.astype(BF)


def product_sum_kernel(cfg, *refs):
    n_arrays, job, sides, stagger = cfg
    xs, first_column = job[:2]
    refs = list(refs)
    take = lambda n: [refs.pop(0) for _ in range(n)]
    from_hbm = take(n_arrays)
    (w_hbm,) = take(1)
    outs_hbm = take(len(job[3]))
    (g_hbm,) = take(1) if sides else (None,)
    arrays = take(n_arrays)
    outs = take(len(job[3]))
    load_sem, out_sem, w_buf, p_buf, a_buf, b_buf, w_sem, sa, ra, sb, rb, sc, rc, turn, keep, sums = take(16)
    g_buf, g_sem = take(2) if sides else (None, None)
    per_block = BLOCK // PIECE
    pieces = p_buf.shape[0]
    blocks = pieces // per_block
    n_rows = p_buf.shape[1]
    early = len(xs)

    t = lax.axis_index("tensor")
    sec = lax.axis_index("section")
    dat = lax.axis_index("dp")
    inner = (t == 1) | (t == 2)
    outer = jnp.logical_not(inner)
    pair = (sec, t + 1 - 2 * lax.rem(t, 2), dat)
    mid = (sec, 3 - t, dat)
    mate = (1 - sec, t, dat)

    def columns(j):
        return pl.ds(pl.multiple_of(j * BLOCK, BLOCK), BLOCK)

    def to_inner(i):
        return pltpu.make_async_remote_copy(
            p_buf.at[i], a_buf.at[i], sa.at[i], ra.at[i], device_id=pair, device_id_type=MESH
        )

    def across(i):
        return pltpu.make_async_remote_copy(
            p_buf.at[i], b_buf.at[i], sb.at[i], rb.at[i], device_id=mid, device_id_type=MESH
        )

    def to_outer(i):
        return pltpu.make_async_remote_copy(
            b_buf.at[i], b_buf.at[i], sc.at[i], rc.at[i], device_id=pair, device_id_type=MESH
        )

    def load(k):
        return pltpu.make_async_copy(from_hbm[k], arrays[k], load_sem.at[k])

    def fetch(j, slot):
        return pltpu.make_async_copy(
            w_hbm.at[columns(j), pl.ds(first_column, w_buf.shape[2])], w_buf.at[slot], w_sem.at[slot]
        )

    def flush(j, slot):
        return pltpu.make_async_copy(g_buf.at[slot], g_hbm.at[columns(j), :], g_sem.at[slot])

    def every_piece(body):
        def turn_of(i, _):
            body(i)
            return 0

        lax.fori_loop(0, pieces, turn_of, 0)

    for k in range(early):
        load(k).start()
    fetch(0, 0).start()
    for k in range(early, n_arrays):
        load(k).start()
    barrier = pltpu.get_barrier_semaphore()
    pl.semaphore_signal(barrier, inc=1, device_id=pair, device_id_type=MESH)
    sums[...] = jnp.zeros_like(sums)

    @pl.when(inner)
    def _():
        pl.semaphore_signal(barrier, inc=1, device_id=mid, device_id_type=MESH)
        pl.semaphore_wait(barrier, 2)

    @pl.when(outer)
    def _():
        if stagger:
            pl.semaphore_signal(barrier, inc=1, device_id=mate, device_id_type=MESH)
            pl.semaphore_wait(barrier, 2)

            @pl.when(sec == 1)
            def _():
                pl.semaphore_wait(turn, 1)

        else:
            pl.semaphore_wait(barrier, 1)

    for k in range(early):
        load(k).wait()

    def done(i):
        with_piece(job, i, b_buf[i].astype(F32), arrays, outs, keep, sums)

    def first(i):
        to_inner(i).wait_recv()
        p_buf[i] = p_buf[i] + a_buf[i]
        across(i).start()

    def second(i):
        across(i).wait_recv()
        b_buf[i] = p_buf[i] + b_buf[i]
        to_outer(i).start()
        done(i)

    def step(j, _):
        slot = lax.rem(j, 2)
        fetch(j, slot).wait()

        @pl.when(j + 1 < blocks)
        def _():
            fetch(j + 1, 1 - slot).start()

        total, start = None, 0
        for x in xs:
            width = arrays[x].shape[1]
            term = dot_f32(arrays[x][...], w_buf[slot, :, start : start + width], 1, 1)
            total = term if total is None else total + term
            start += width
        total = total.astype(BF)
        for u in range(per_block):
            p_buf[per_block * j + u] = total[:, u * PIECE : (u + 1) * PIECE]

        @pl.when(outer)
        def _():
            for u in range(per_block):
                to_inner(per_block * j + u).start()

        @pl.when(j == 0)
        def _():
            for k in range(early, n_arrays):
                load(k).wait()
            before_sum(job, arrays, keep)

        @pl.when(inner)
        def _():
            for u in range(per_block):
                i = per_block * j + u
                first(i)

                @pl.when(j >= 1)
                def _():
                    second(i - per_block)

        if sides:

            @pl.when(j >= 2)
            def _():
                flush(j - 2, slot).wait()

            start = 0
            for a, bs in sides:
                a_t = arrays[a][:, columns(j)].T
                for b in bs:
                    width = arrays[b].shape[1]
                    g_buf[slot, :, start : start + width] = jnp.dot(
                        a_t, arrays[b][...], preferred_element_type=F32
                    ).astype(BF)
                    start += width
            flush(j, slot).start()

        return 0

    lax.fori_loop(0, blocks, step, 0)

    @pl.when(inner)
    def _():
        for u in range(per_block):
            second(pieces - per_block + u)

    @pl.when(outer)
    def _():
        every_piece(lambda i: to_inner(i).wait_send())
        if stagger:

            @pl.when(sec == 0)
            def _():
                pl.semaphore_signal(turn, inc=1, device_id=mate, device_id_type=MESH)

        def arrive(i):
            to_outer(i).wait_recv()
            done(i)

        every_piece(arrive)

    chunks = 5 if n_rows % (5 * 32) == 0 else 1
    chunk = n_rows // chunks
    block = 32 if chunk % 32 == 0 else 16
    height = lambda m: 8 if job[2][0] == "back" and m == 2 else n_rows
    stores = []

    def store(m, rows):
        copy = pltpu.make_async_copy(outs[m].at[rows], outs_hbm[m].at[rows], out_sem.at[len(stores)])
        copy.start()
        stores.append(copy)

    for c in range(chunks):

        def turn_rows(r, _):
            rows = pl.ds(pl.multiple_of(c * chunk + r * block, block), block)
            after_sum(job, rows, lambda i: b_buf.at[i], arrays, outs, keep, sums)
            return 0

        if job[2][0] == "back" or len(outs) > 1:
            lax.fori_loop(0, chunk // block, turn_rows, 0)
        for m in range(len(outs)):
            if height(m) == n_rows:
                store(m, pl.ds(c * chunk, chunk))
    for m in range(len(outs)):
        if height(m) != n_rows:
            store(m, pl.ds(0, height(m)))

    @pl.when(inner)
    def _():
        def sent(i):
            across(i).wait_send()
            to_outer(i).wait_send()

        every_piece(sent)

    if sides:
        flush(blocks - 2, (blocks - 2) % 2).wait()
        flush(blocks - 1, (blocks - 1) % 2).wait()
    for copy in stores:
        copy.wait()


def product_sum(arrays, job, weights, sides=(), stagger=False, key=1):
    assert lax.axis_size("tensor") == 4
    rows, model = arrays[0].shape[0], weights.shape[0]
    pieces = model // PIECE
    depth = sum(arrays[x].shape[1] for x in job[0])
    anywhere = pl.BlockSpec(memory_space=pl.ANY)
    buf = pltpu.VMEM((pieces, rows, PIECE), BF)
    sem = pltpu.SemaphoreType.DMA((pieces,))
    two = pltpu.SemaphoreType.DMA((2,))
    out_shape = []
    for m, dtype in enumerate(job[3]):
        height = 8 if job[2][0] == "back" and m == 2 else rows
        out_shape.append(jax.ShapeDtypeStruct((height, model), dtype))
    scratch = [pltpu.VMEM(x.shape, x.dtype) for x in (*arrays, *out_shape)]
    scratch += [pltpu.SemaphoreType.DMA((len(arrays),)), pltpu.SemaphoreType.DMA((16,))]
    scratch += [pltpu.VMEM((2, BLOCK, depth), BF), buf, buf, buf, two, *[sem] * 6, pltpu.SemaphoreType.REGULAR]
    scratch += [pltpu.VMEM((rows, PIECE), F32)] * 2
    if sides:
        side_width = sum(arrays[b].shape[1] for _, bs in sides for b in bs)
        out_shape.append(jax.ShapeDtypeStruct((model, side_width), BF))
        scratch += [pltpu.VMEM((2, BLOCK, side_width), BF), two]
    out = pl.pallas_call(
        functools.partial(product_sum_kernel, (len(arrays), job, tuple(sides), stagger)),
        out_shape=out_shape,
        in_specs=[anywhere] * (len(arrays) + 1),
        out_specs=[anywhere] * len(out_shape),
        scratch_shapes=scratch,
        compiler_params=pltpu.CompilerParams(
            collective_id=key, has_side_effects=True, vmem_limit_bytes=62 << 20
        ),
        cost_estimate=NO_COST,
        name=f"product_sum_{key}",
    )(*arrays, weights)
    return out if len(out) > 1 else out[0]


def dp_peers(count):
    me = lax.axis_index("dp")
    sec, t = lax.axis_index("section"), lax.axis_index("tensor")
    others = [lax.rem(me + k, count) for k in range(1, count)]
    return me, others, [(sec, t, other) for other in others]


def greet(ids):
    barrier = pltpu.get_barrier_semaphore()
    for device in ids:
        pl.semaphore_signal(barrier, inc=1, device_id=device, device_id_type=MESH)
    pl.semaphore_wait(barrier, len(ids))


def turn_rows(x, cos_ref, sin_ref):
    lane = lax.broadcasted_iota(jnp.int32, x.shape, 1)
    width = x.shape[1]
    partner = jnp.where(lane < HALF, pltpu.roll(x, width - HALF, 1), pltpu.roll(x, HALF, 1))
    return x * cos_ref[...] + partner * sin_ref[...]


def gather_kernel(count, raw_ref, cos_ref, sin_ref, o_ref, t_ref, x_ref, send, recv):
    me, _, ids = dp_peers(count)
    x_ref[...] = turn_rows(raw_ref[...], cos_ref, sin_ref).astype(BF)
    greet(ids)
    copies = [
        pltpu.make_async_remote_copy(
            x_ref, o_ref.at[me], send.at[k], recv.at[k], device_id=device, device_id_type=MESH
        )
        for k, device in enumerate(ids)
    ]
    for copy in copies:
        copy.start()
    o_ref[me] = x_ref[...]
    for copy in copies:
        copy.wait()
    t_ref[...] = o_ref[...].reshape(t_ref.shape[1], t_ref.shape[0]).T


def scatter_kernel(count, x_ref, cos_ref, sin_ref, o_ref, buf, send, recv):
    me, others, ids = dp_peers(count)
    greet(ids)
    copies = [
        pltpu.make_async_remote_copy(
            x_ref.at[others[k]], buf.at[k], send.at[k], recv.at[k], device_id=device, device_id_type=MESH
        )
        for k, device in enumerate(ids)
    ]
    for copy in copies:
        copy.start()
    total = x_ref[me].astype(F32)
    for k, copy in enumerate(copies):
        copy.wait()
        total = total + buf[k].astype(F32)
    o_ref[...] = turn_rows(total, cos_ref, sin_ref).astype(BF)


def gather_rows(raw, cos_rows, sin_rows):
    count = lax.axis_size("dp")
    rows, width = raw.shape
    in_vmem = pl.BlockSpec(memory_space=pltpu.VMEM)
    sem = pltpu.SemaphoreType.DMA((count - 1,))
    out, out_t = pl.pallas_call(
        functools.partial(gather_kernel, count),
        out_shape=(
            jax.ShapeDtypeStruct((count, rows, width), BF),
            jax.ShapeDtypeStruct((width, count * rows), BF),
        ),
        in_specs=[in_vmem] * 3,
        out_specs=(in_vmem, in_vmem),
        scratch_shapes=[pltpu.VMEM((rows, width), BF), sem, sem],
        compiler_params=pltpu.CompilerParams(collective_id=3, has_side_effects=True),
        cost_estimate=NO_COST,
        name="gather_rows",
    )(raw, cos_rows, sin_rows)
    return out.reshape(-1, width), out_t


def scatter_rows(x, cos_rows, sin_rows):
    count = lax.axis_size("dp")
    rows, width = x.shape[0] // count, x.shape[1]
    in_vmem = pl.BlockSpec(memory_space=pltpu.VMEM)
    sem = pltpu.SemaphoreType.DMA((count - 1,))
    return pl.pallas_call(
        functools.partial(scatter_kernel, count),
        out_shape=jax.ShapeDtypeStruct((rows, width), BF),
        in_specs=[in_vmem] * 3,
        out_specs=in_vmem,
        scratch_shapes=[pltpu.VMEM((count - 1, rows, width), x.dtype), sem, sem],
        compiler_params=pltpu.CompilerParams(collective_id=4, has_side_effects=True),
        cost_estimate=NO_COST,
        name="scatter_rows",
    )(x.reshape(count, rows, width), cos_rows, sin_rows)


def finish_kernel(
    g_hbm, gain_ref, out_zero, out_one, in_zero, in_one, mlp_one, attn_one,
    o_ref, gain_out, got_out, got_in, got_mlp, got_attn,
    mine, away, got, xs, ys, xr, yr, gains, load_sem, send, recv, mate_send, mate_recv, gain_send, gain_recv,
):
    sec, t, dat = lax.axis_index("section"), lax.axis_index("tensor"), lax.axis_index("dp")
    flip_x = dat + 1 - 2 * lax.rem(dat, 2)
    flip_y = lax.rem(dat + 2, 4)
    across = lax.rem(flip_x + 2, 4)
    by_x, by_y, mate = (sec, t, flip_x), (sec, t, flip_y), (1 - sec, t, dat)
    peers = [
        mate, by_x, by_y, (sec, t, across),
        (1 - sec, t, flip_x), (1 - sec, t, flip_y), (1 - sec, t, across),
    ]
    rows = g_hbm.shape[1] // 2
    upper, lower = pl.ds(0, rows), pl.ds(rows, rows)
    order = (across, flip_x, flip_y, dat)
    loads = []
    for k, block in enumerate(order):
        loads.append(pltpu.make_async_copy(g_hbm.at[2 * block + 1 - sec], away.at[k], load_sem.at[k]))
        loads.append(pltpu.make_async_copy(g_hbm.at[2 * block + sec], mine.at[k], load_sem.at[4 + k]))
    for copy in loads:
        copy.start()
    greet(peers)

    def remote(src, dst, k, device):
        return pltpu.make_async_remote_copy(
            src, dst, send.at[k], recv.at[k], device_id=device, device_id_type=MESH
        )

    def to_mate(src, dst, k):
        return pltpu.make_async_remote_copy(
            src, dst, mate_send.at[k], mate_recv.at[k], device_id=mate, device_id_type=MESH
        )

    swaps = [remote(away.at[k], got.at[k], k, mate) for k in range(4)]
    for k in range(4):
        loads[2 * k].wait()
        swaps[k].start()
    gain_copies = [
        pltpu.make_async_remote_copy(
            gain_ref.at[peer[0], peer[2]], gains.at[k], gain_send.at[k], gain_recv.at[k],
            device_id=peer, device_id_type=MESH,
        )
        for k, peer in enumerate(peers)
    ]
    for copy in gain_copies:
        copy.start()
    outs = []
    for k in range(4):
        loads[2 * k + 1].wait()
        swaps[k].wait_recv()
        mine[k] = (mine[k].astype(F32) + got[k].astype(F32)).astype(BF)
        if k == 0:
            outs += [remote(mine.at[0, upper], xs.at[0], 4, by_x), remote(mine.at[0, lower], ys.at[0], 5, by_y)]
        if k == 1:
            outs += [remote(mine.at[1, upper], xs.at[1], 6, by_x)]
        if k == 2:
            outs += [remote(mine.at[2, lower], ys.at[1], 7, by_y)]
        for copy in outs[-(2 if k == 0 else 1) :]:
            if k < 3:
                copy.start()

    @pl.when(sec == 0)
    def _():
        to_mate(in_one, got_in, 0).start()
        to_mate(out_one, got_out, 1).start()
        to_mate(mlp_one, got_mlp, 2).start()
        to_mate(attn_one, got_attn, 3).start()

    @pl.when(sec == 1)
    def _():
        to_mate(in_zero, got_in, 0).start()
        to_mate(out_zero, got_out, 1).start()

    outs[0].wait_recv()
    mine[2, upper] = (mine[2, upper].astype(F32) + xs[0].astype(F32)).astype(BF)
    outs.append(remote(mine.at[2, upper], yr, 8, by_y))
    outs[4].start()
    outs[1].wait_recv()
    mine[1, lower] = (mine[1, lower].astype(F32) + ys[0].astype(F32)).astype(BF)
    outs.append(remote(mine.at[1, lower], xr, 9, by_x))
    outs[5].start()
    total = gain_ref[sec, dat]
    for k, copy in enumerate(gain_copies):
        copy.wait()
        total = total + gains[k]
    gain_out[...] = total
    outs[2].wait_recv()
    outs[3].wait_recv()
    outs[4].wait_recv()
    o_ref[upper] = (mine[3, upper].astype(F32) + xs[1].astype(F32) + yr[...].astype(F32)).astype(BF)
    outs[5].wait_recv()
    o_ref[lower] = (mine[3, lower].astype(F32) + ys[1].astype(F32) + xr[...].astype(F32)).astype(BF)

    @pl.when(sec == 1)
    def _():
        to_mate(o_ref, got_attn, 3).start()

    for copy in swaps + outs:
        copy.wait_send()
    to_mate(in_one, got_in, 0).wait()
    to_mate(out_one, got_out, 1).wait()
    to_mate(attn_one, got_attn, 3).wait()

    @pl.when(sec == 0)
    def _():
        to_mate(mlp_one, got_mlp, 2).wait_send()

    @pl.when(sec == 1)
    def _():
        to_mate(mlp_one, got_mlp, 2).wait_recv()


def finish(g, gains, out_zero, out_one, in_zero, in_one, mlp_one, attn_one):
    rows, width = g.shape[0] // 8, g.shape[1]
    part = pltpu.VMEM((2, rows // 2, width), BF)
    whole = pltpu.VMEM((4, rows, width), BF)
    end = pltpu.VMEM((rows // 2, width), BF)
    in_vmem, anywhere = pl.BlockSpec(memory_space=pltpu.VMEM), pl.BlockSpec(memory_space=pl.ANY)
    like = lambda x: jax.ShapeDtypeStruct(x.shape, x.dtype)
    dma = lambda n: pltpu.SemaphoreType.DMA((n,))
    return pl.pallas_call(
        finish_kernel,
        out_shape=(
            jax.ShapeDtypeStruct((rows, width), BF),
            jax.ShapeDtypeStruct(gains.shape[2:], F32),
            like(out_zero), like(in_zero), like(mlp_one), like(attn_one),
        ),
        in_specs=[anywhere, in_vmem, *[anywhere] * 6],
        out_specs=(in_vmem, in_vmem, *[anywhere] * 4),
        scratch_shapes=[
            whole, whole, whole, part, part, end, end, pltpu.VMEM((7, *gains.shape[2:]), F32),
            dma(8), dma(10), dma(10), dma(4), dma(4), dma(7), dma(7),
        ],
        compiler_params=pltpu.CompilerParams(
            collective_id=12, has_side_effects=True, vmem_limit_bytes=40 << 20
        ),
        cost_estimate=NO_COST,
        name="finish",
    )(g.reshape(8, rows, width), gains, out_zero, out_one, in_zero, in_one, mlp_one, attn_one)


def finish_apart(g, gains, out_zero, out_one, in_zero, in_one, mlp_one, attn_one):
    first_core = lax.axis_index("section") == 0
    half = reduce_gradient(g)
    swap = lambda zero, one: lax.ppermute(jnp.where(first_core, one, zero), "section", [(0, 1), (1, 0)])
    return (
        half, share_sums(gains), swap(out_zero, out_one), swap(in_zero, in_one),
        lax.ppermute(mlp_one, "section", [(0, 1)]), swap(half, attn_one),
    )


def in_rows(count, block, body):
    def turn(r, _):
        body(pl.ds(pl.multiple_of(r * block, block), block))
        return 0

    lax.fori_loop(0, count // block, turn, 0)


def widen_turned(dst, src, start, width):
    for c in range(0, width, 128):
        dst[c : c + 128] = src[:, start + c : start + c + 128].astype(F32).T


def write_mlp_kernel(
    zero, one, from_one, from_zero, gate_hbm, up_hbm, down_hbm, mlp, gate_buf, up_buf, down_buf, load_sem, store_sem
):
    sec = lax.axis_index("section")
    half, units = zero.shape[0], gate_buf.shape[1]
    low, high = pl.ds(0, half), pl.ds(half, half)
    load = lambda src, at, k: pltpu.make_async_copy(src, mlp.at[at], load_sem.at[k])
    store = lambda src, dst, k: pltpu.make_async_copy(src, dst, store_sem.at[k])

    @pl.when(sec == 0)
    def _():
        load(zero, low, 0).start()
        load(from_one, high, 1).start()

    @pl.when(sec == 1)
    def _():
        load(from_zero, low, 0).start()
        load(one, high, 1).start()

    load(zero, low, 0).wait()
    load(zero, high, 1).wait()

    def gates(rows):
        gate_buf[rows] = mlp[rows, :units].astype(F32)
        up_buf[rows] = mlp[rows, units : 2 * units].astype(F32)

    in_rows(2 * half, 32, gates)
    stores = [store(gate_buf, gate_hbm, 0), store(up_buf, up_hbm, 1), store(down_buf, down_hbm, 2)]
    stores[0].start()
    stores[1].start()
    widen_turned(down_buf, mlp, 2 * units, units)
    stores[2].start()
    for copy in stores:
        copy.wait()


def write_mlp(zero, one, from_one, from_zero, units):
    shard = 2 * zero.shape[0]
    anywhere = pl.BlockSpec(memory_space=pl.ANY)
    shapes = [(shard, units), (shard, units), (units, shard)]
    return pl.pallas_call(
        write_mlp_kernel,
        out_shape=[jax.ShapeDtypeStruct(shape, F32) for shape in shapes],
        in_specs=[anywhere] * 4,
        out_specs=[anywhere] * 3,
        scratch_shapes=[
            pltpu.VMEM((shard, zero.shape[1]), BF),
            *[pltpu.VMEM(shape, F32) for shape in shapes],
            pltpu.SemaphoreType.DMA((2,)),
            pltpu.SemaphoreType.DMA((3,)),
        ],
        compiler_params=pltpu.CompilerParams(vmem_limit_bytes=40 << 20),
        cost_estimate=NO_COST,
        name="write_mlp",
    )(zero, one, from_one, from_zero)


def write_kernel(
    split, out_zero, out_one, got_out, in_zero, in_one, got_in, attn_zero, attn_one, got_attn,
    out_hbm, in_hbm, q_hbm, k_hbm, v_hbm, o_hbm,
    outs, wides, attn, narrow, q_buf, k_buf, v_buf, o_buf, load_sem, store_sem,
):
    sec = lax.axis_index("section")
    half = attn_zero.shape[0]
    low, high = pl.ds(0, half), pl.ds(half, half)
    load = lambda src, dst, k: pltpu.make_async_copy(src, dst, load_sem.at[k])
    store = lambda src, dst, k: pltpu.make_async_copy(src, dst, store_sem.at[k])

    def start(own_out, own_in, attn_low, attn_high):
        load(own_out, outs.at[0], 0).start()
        load(own_in, wides.at[0], 1).start()
        load(attn_low, attn.at[low], 2).start()
        load(attn_high, attn.at[high], 3).start()

    @pl.when(sec == 0)
    def _():
        start(out_zero, in_zero, attn_zero, got_attn)

    @pl.when(sec == 1)
    def _():
        start(out_one, in_one, got_attn, attn_one)

    load(got_in, narrow, 4).start()
    load(got_out, outs.at[1], 5).start()
    stores = [
        store(outs.at[0], out_hbm.at[sec], 0),
        store(wides.at[0], in_hbm.at[sec], 1),
        store(outs.at[1], out_hbm.at[1 - sec], 2),
        store(wides.at[1], in_hbm.at[1 - sec], 3),
        store(q_buf, q_hbm, 4),
        store(k_buf, k_hbm, 5),
        store(v_buf, v_hbm, 6),
        store(o_buf, o_hbm, 7),
    ]
    load(out_zero, outs.at[0], 0).wait()
    stores[0].start()
    load(in_zero, wides.at[0], 1).wait()
    stores[1].start()
    width, span = q_buf.shape[1], k_buf.shape[1]
    load(attn_one, attn.at[low], 2).wait()
    load(attn_one, attn.at[high], 3).wait()

    def projections(rows):
        q_buf[rows] = attn[rows, :width].astype(F32)
        k_buf[rows] = attn[rows, width : width + span].astype(F32)
        v_buf[rows] = attn[rows, width + span : split].astype(F32)

    in_rows(2 * half, 32, projections)
    for k in (4, 5, 6):
        stores[k].start()
    widen_turned(o_buf, attn, split, width)
    stores[7].start()
    load(got_in, narrow, 4).wait()

    def widen(rows):
        wides[1, rows] = narrow[rows].astype(F32)

    in_rows(narrow.shape[0], 32, widen)
    stores[3].start()
    load(got_out, outs.at[1], 5).wait()
    stores[2].start()
    for copy in stores:
        copy.wait()


def write_results(results, ins, attns, width, span):
    rows, model = results[0].shape
    shard = 2 * attns[0].shape[0]
    anywhere = pl.BlockSpec(memory_space=pl.ANY)
    shapes = [(shard, width), (shard, span), (shard, span), (width, shard)]
    return pl.pallas_call(
        functools.partial(write_kernel, width + 2 * span),
        out_shape=[
            jax.ShapeDtypeStruct((2, rows, model), BF),
            jax.ShapeDtypeStruct((2, rows, model), F32),
            *[jax.ShapeDtypeStruct(shape, F32) for shape in shapes],
        ],
        in_specs=[anywhere] * 9,
        out_specs=[anywhere] * 6,
        scratch_shapes=[
            pltpu.VMEM((2, rows, model), BF),
            pltpu.VMEM((2, rows, model), F32),
            pltpu.VMEM((shard, attns[0].shape[1]), BF),
            pltpu.VMEM((rows, model), BF),
            *[pltpu.VMEM(shape, F32) for shape in shapes],
            pltpu.SemaphoreType.DMA((6,)),
            pltpu.SemaphoreType.DMA((8,)),
        ],
        compiler_params=pltpu.CompilerParams(vmem_limit_bytes=40 << 20),
        cost_estimate=NO_COST,
        name="write_results",
    )(*results, *ins, *attns)


def share_kernel(count, x_ref, o_ref, buf, send, recv):
    sec, t, dat = lax.axis_index("section"), lax.axis_index("tensor"), lax.axis_index("dp")
    peers = [
        (lax.rem(sec + k // count, 2), t, lax.rem(dat + k % count, count)) for k in range(1, 2 * count)
    ]
    greet(peers)
    copies = [
        pltpu.make_async_remote_copy(
            x_ref.at[peer[0], peer[2]], buf.at[k], send.at[k], recv.at[k], device_id=peer, device_id_type=MESH
        )
        for k, peer in enumerate(peers)
    ]
    for copy in copies:
        copy.start()
    total = x_ref[sec, dat]
    for k, copy in enumerate(copies):
        copy.wait()
        total = total + buf[k]
    o_ref[...] = total


def share_sums(x):
    count = lax.axis_size("dp")
    in_vmem = pl.BlockSpec(memory_space=pltpu.VMEM)
    sem = pltpu.SemaphoreType.DMA((2 * count - 1,))
    return pl.pallas_call(
        functools.partial(share_kernel, count),
        out_shape=jax.ShapeDtypeStruct(x.shape[2:], F32),
        in_specs=[in_vmem],
        out_specs=in_vmem,
        scratch_shapes=[pltpu.VMEM((2 * count - 1, *x.shape[2:]), F32), sem, sem],
        compiler_params=pltpu.CompilerParams(collective_id=13, has_side_effects=True),
        cost_estimate=NO_COST,
        name="share_sums",
    )(x)


def group_start(first_row):
    past = lax.max(first_row - TRUNK, 0)
    return pl.multiple_of(TRUNK + GROUP * lax.div(past, GROUP), 128)


def windows(tree_len, rows, tile, first_row):
    if tile % 128 == 0 and GROUP % tile == 0 and TRUNK % tile == 0 and rows % tile == 0:
        return (pl.ds(0, TRUNK), pl.ds(group_start(first_row), GROUP))
    return (pl.ds(0, tree_len),)


def head_rows(ref, head):
    return ref[head * HEAD : (head + 1) * HEAD, :]


def beside(ref, head, count):
    parts = [head_rows(ref, head + k) for k in range(count)]
    return parts[0] if count == 1 else jnp.concatenate(parts, axis=1)


def turned_beside(ref, cos, sin, head, count):
    parts = []
    for k in range(count):
        rows = head_rows(ref, head + k)
        first, second = rows[:HALF], rows[HALF:]
        parts.append(jnp.concatenate([first * cos - second * sin, second * cos + first * sin], axis=0))
    whole = parts[0] if count == 1 else jnp.concatenate(parts, axis=1)
    return (whole.astype(BF).astype(F32) * HEAD**-0.5).astype(BF)


def as_rows(x, tile, count):
    parts = [x[:, k * tile : (k + 1) * tile] for k in range(count)]
    return (parts[0] if count == 1 else jnp.concatenate(parts, axis=0)).T


def over_groups(groups, step, body):
    for group in range(groups):
        body(group, slice(group * step * HEAD, (group + 1) * step * HEAD))


def attend_kernel(
    rows, step, start_ref, q_ref, kv_ref, kvt_ref, bias_ref, cos_ref, sin_ref, o_ref, on_ref, lse_ref
):
    tile = q_ref.shape[1]
    heads = q_ref.shape[0] // HEAD
    first_row = start_ref[0] + pl.program_id(0) * tile
    wins = windows(kv_ref.shape[0], rows, tile, first_row)

    def body(group, lanes):
        head = group * step
        q = turned_beside(q_ref, cos_ref[...], sin_ref[...], head, step)
        scores = []
        for win in wins:
            bias = bias_ref[win, :].astype(F32)
            bias = bias if step == 1 else jnp.concatenate([bias] * step, axis=1)
            scores.append(dot_f32(kv_ref[win, :HEAD], q, 1, 0) + bias)
        top = functools.reduce(jnp.maximum, [jnp.max(s, 0, keepdims=True) for s in scores])
        expo = [jnp.exp(s - top) for s in scores]
        total = sum(jnp.sum(e, 0, keepdims=True) for e in expo)
        out = sum(dot_f32(kvt_ref[HEAD:, win], e.astype(BF), 1, 0) for win, e in zip(wins, expo))
        out = out / total
        on_ref[:, lanes] = as_rows(out, tile, step).astype(BF)
        lse_ref[group, 0] = top + jnp.log(total)
        out = out.astype(BF)
        for k in range(step):
            o_ref[(head + k) * HEAD : (head + k + 1) * HEAD, :] = out[:, k * tile : (k + 1) * tile]

    over_groups(heads // step, step, body)


def attend_back_kernel(
    rows, step, start_ref, q_ref, do_ref, o_ref, lse_ref, kv_ref, kvt_ref, bias_ref, cos_ref, sin_ref,
    dq_ref, dkv_ref, dk_acc, dv_acc,
):
    tile = q_ref.shape[1]
    heads = q_ref.shape[0] // HEAD
    first_row = start_ref[0] + pl.program_id(0) * tile
    wins = windows(kv_ref.shape[0], rows, tile, first_row)

    @pl.when(pl.program_id(0) == 0)
    def _():
        dk_acc[...] = jnp.zeros_like(dk_acc)
        dv_acc[...] = jnp.zeros_like(dv_acc)

    def body(group, lanes):
        head = group * step
        cos, sin = cos_ref[...], sin_ref[...]
        q = turned_beside(q_ref, cos, sin, head, step)
        do = beside(do_ref, head, step)
        out = beside(o_ref, head, step)
        lse = lse_ref[group, 0]
        delta = jnp.sum(do.astype(F32) * out.astype(F32), 0, keepdims=True)
        dq = jnp.zeros((HEAD, step * tile), F32)
        for win in wins:
            bias = bias_ref[win, :].astype(F32)
            bias = bias if step == 1 else jnp.concatenate([bias] * step, axis=1)
            p = jnp.exp(dot_f32(kv_ref[win, :HEAD], q, 1, 0) + bias - lse)
            dp = dot_f32(kv_ref[win, HEAD:], do, 1, 0)
            ds = (p * (dp - delta)).astype(BF)
            dk_acc[win, :] += dot_f32(ds, q, 1, 1)
            dv_acc[win, :] += dot_f32(p.astype(BF), do, 1, 1)
            dq = dq + dot_f32(kvt_ref[:HEAD, win], ds, 1, 0)
        dq = dq * HEAD**-0.5
        turned = []
        for k in range(step):
            first = dq[:HALF, k * tile : (k + 1) * tile]
            second = dq[HALF:, k * tile : (k + 1) * tile]
            turned += [first * cos + second * sin, second * cos - first * sin]
        dq_ref[:, lanes] = jnp.concatenate(turned, axis=0).T.astype(BF)

    over_groups(heads // step, step, body)

    @pl.when(pl.program_id(0) == pl.num_programs(0) - 1)
    def _():
        dkv_ref[...] = jnp.concatenate([dk_acc[...], dv_acc[...]], axis=1).astype(BF)


def row_tile(rows):
    return 128 if rows % 128 == 0 else rows


def attend(start, q_t, kv, kv_t, bias_t, cos_t, sin_t):
    width, rows = q_t.shape
    heads, tree_len, tile = width // HEAD, kv.shape[0], row_tile(rows)
    step = 2 if tile % 128 == 0 and heads % 2 == 0 else 1
    column = lambda i, s: (0, i)
    whole = lambda i, s: (0, 0)
    return pl.pallas_call(
        functools.partial(attend_kernel, rows, step),
        out_shape=(
            jax.ShapeDtypeStruct((width, rows), BF),
            jax.ShapeDtypeStruct((rows, width), BF),
            jax.ShapeDtypeStruct((heads // step, rows // tile, 1, step * tile), F32),
        ),
        grid_spec=pltpu.PrefetchScalarGridSpec(
            num_scalar_prefetch=1,
            grid=(rows // tile,),
            in_specs=[
                pl.BlockSpec((width, tile), column),
                pl.BlockSpec((tree_len, 2 * HEAD), whole),
                pl.BlockSpec((2 * HEAD, tree_len), whole),
                pl.BlockSpec((tree_len, tile), column),
                pl.BlockSpec((HALF, tile), column),
                pl.BlockSpec((HALF, tile), column),
            ],
            out_specs=(
                pl.BlockSpec((width, tile), column),
                pl.BlockSpec((tile, width), lambda i, s: (i, 0)),
                pl.BlockSpec((heads // step, 1, 1, step * tile), lambda i, s: (0, i, 0, 0)),
            ),
        ),
        compiler_params=pltpu.CompilerParams(vmem_limit_bytes=40 << 20),
        cost_estimate=NO_COST,
        name="attend",
    )(start, q_t, kv, kv_t, bias_t, cos_t, sin_t)


def attend_back(start, q_t, do_t, o_t, lse, kv, kv_t, bias_t, cos_t, sin_t):
    width, rows = q_t.shape
    heads, tree_len, tile = width // HEAD, kv.shape[0], row_tile(rows)
    step = 2 if tile % 128 == 0 and heads % 2 == 0 else 1
    column = lambda i, s: (0, i)
    whole = lambda i, s: (0, 0)
    return pl.pallas_call(
        functools.partial(attend_back_kernel, rows, step),
        out_shape=(
            jax.ShapeDtypeStruct((rows, width), BF),
            jax.ShapeDtypeStruct((tree_len, 2 * HEAD), BF),
        ),
        grid_spec=pltpu.PrefetchScalarGridSpec(
            num_scalar_prefetch=1,
            grid=(rows // tile,),
            in_specs=[
                pl.BlockSpec((width, tile), column),
                pl.BlockSpec((width, tile), column),
                pl.BlockSpec((width, tile), column),
                pl.BlockSpec((heads // step, 1, 1, step * tile), lambda i, s: (0, i, 0, 0)),
                pl.BlockSpec((tree_len, 2 * HEAD), whole),
                pl.BlockSpec((2 * HEAD, tree_len), whole),
                pl.BlockSpec((tree_len, tile), column),
                pl.BlockSpec((HALF, tile), column),
                pl.BlockSpec((HALF, tile), column),
            ],
            out_specs=(
                pl.BlockSpec((tile, width), lambda i, s: (i, 0)),
                pl.BlockSpec((tree_len, 2 * HEAD), whole),
            ),
            scratch_shapes=[pltpu.VMEM((tree_len, HEAD), F32), pltpu.VMEM((tree_len, HEAD), F32)],
        ),
        compiler_params=pltpu.CompilerParams(vmem_limit_bytes=48 << 20),
        cost_estimate=NO_COST,
        name="attend_back",
    )(start, q_t, do_t, o_t, lse, kv, kv_t, bias_t, cos_t, sin_t)


def layer_attention(normed, weights, tables):
    gains, w_attn, w_mlp, width, split, units = weights
    start, bias_t, cos_t, sin_t, cos_rows, sin_rows = tables
    q_t = dot_f32(w_attn[:, :width], normed, 0, 1)
    kv, kv_t = gather_rows(
        jnp.dot(normed, w_attn[:, width:split], preferred_element_type=F32), cos_rows, -sin_rows
    )
    o_t, o, lse = attend(start, q_t, kv, kv_t, bias_t, cos_t, sin_t)
    return (q_t, kv, kv_t, o_t, lse), o


def attention_backward(grad_attn, weights, tables, kept):
    gains, w_attn, w_mlp, width, split, units = weights
    start, bias_t, cos_t, sin_t, cos_rows, sin_rows = tables
    q_t, kv, kv_t, o_t, lse = kept
    do_t = dot_f32(w_attn[:, split : split + width], grad_attn, 0, 1).astype(BF)
    dq, dkv_part = attend_back(start, q_t, do_t, o_t, lse, kv, kv_t, bias_t, cos_t, sin_t)
    return dq, scatter_rows(dkv_part, cos_rows, sin_rows)


def layer_units(normed, weights):
    units = weights[-1]
    gate_up = jnp.dot(normed, weights[2][:, : 2 * units], preferred_element_type=F32)
    gate, up = gate_up[:, :units], gate_up[:, units:]
    return gate, up, (gate * jax.nn.sigmoid(gate) * up).astype(BF)


def units_backward(branch, weights, gate, up):
    units = weights[-1]
    d_inner = dot_f32(branch, weights[2][:, 2 * units :], 1, 0)
    sig = jax.nn.sigmoid(gate)
    d_gate = (d_inner * up * sig * (1.0 + gate * (1.0 - sig))).astype(BF)
    d_up = (d_inner * gate * sig).astype(BF)
    return d_gate, d_up


def reduce_gradient(x):
    return lax.psum_scatter(x, BOTH, scatter_dimension=0, tiled=True)


def shards(
    inputs, cotangent, seg_ids, positions, parents, gain_attn, w_query, key_weight, value_weight,
    w_out, gain_mlp, w_gate, w_up, w_down,
):
    sec = lax.axis_index("section")
    data = lax.axis_index("dp")
    sections = lax.axis_size("section")
    devices = lax.axis_size("dp")
    assert sections == 2 and inputs.shape[0] == 2
    first_core = sec == 0
    rows, model = inputs.shape[1], inputs.shape[2]
    swap = [(0, 1), (1, 0)]

    tree = lax.dynamic_index_in_dim(inputs, sec, 0, keepdims=False)
    hidden = tree.astype(F32)
    segments = lax.dynamic_index_in_dim(seg_ids, sec, 0, keepdims=False)
    places = lax.dynamic_index_in_dim(positions, sec, 0, keepdims=False)
    parent = lax.dynamic_index_in_dim(parents, sec, 0, keepdims=False)

    width, span, units = w_query.shape[2], key_weight.shape[2], w_gate.shape[2]
    split = width + 2 * span
    shard_list = (
        jnp.concatenate(
            [w_query[0], key_weight[0], value_weight[0], w_out[0].T, gain_attn.T, gain_mlp.T], 1
        ).astype(BF),
        jnp.concatenate([w_gate[0], w_up[0], w_down[0].T], 1).astype(BF),
    )
    halves = []
    for shard in shard_list:
        half = shard.shape[0] // 2
        low, high = shard[:half], shard[half:]
        got = lax.ppermute(jnp.where(first_core, high, low), "section", swap)
        halves.append((jnp.where(first_core, low, got), jnp.where(first_core, got, high)))
    def gathered(halves):
        return [lax.all_gather(half, BOTH, axis=0, tiled=True) for half in halves]

    def with_gains(w_attn, w_mlp):
        return (w_attn[:, split + width :].astype(F32).T, w_attn, w_mlp, width, split, units)

    (attn_zero, attn_one), (mlp_zero, mlp_one) = halves
    attn_zero = jnp.concatenate([attn_zero, attn_one[:, split + width : split + width + 1]], 1)
    attn_zero, mlp_zero = gathered((attn_zero, mlp_zero))
    cot = lax.dynamic_index_in_dim(cotangent, sec, 0, keepdims=False)
    attn_zero, cot = lax.optimization_barrier((attn_zero, cot))
    zero = with_gains(attn_zero, mlp_zero)
    attn_one, mlp_one = gathered((attn_one, mlp_one))

    seg_count = parent.shape[0]
    labels = jnp.arange(seg_count, dtype=jnp.int32)
    parent_hot = (parent[:, None] == labels[None, :]).astype(F32)
    ancestry = jnp.eye(seg_count, dtype=F32) + parent_hot + jnp.dot(parent_hot, parent_hot)
    ancestry = (ancestry > 0.5).astype(F32)
    row_start = data * rows
    seg_rows = lax.dynamic_slice_in_dim(segments, row_start, rows, 0)
    pos_rows = lax.dynamic_slice_in_dim(places, row_start, rows, 0)
    key_hot = (segments[:, None] == labels[None, :]).astype(F32)
    query_hot = (labels[:, None] == seg_rows[None, :]).astype(F32)
    reach = jnp.dot(key_hot, jnp.dot(ancestry.T, query_hot))
    allowed = (reach > 0.5) & (places[:, None] <= pos_rows[None, :])
    bias_t = jnp.where(allowed, 0.0, MASKED).astype(BF)
    frequency = THETA ** (-(jnp.arange(HALF, dtype=F32) * 2.0 / HEAD))
    angles = frequency[:, None] * pos_rows.astype(F32)[None, :]
    cos_t, sin_t = jnp.cos(angles), jnp.sin(angles)
    ones = jnp.ones((rows, HEAD), F32)
    cos_rows = jnp.concatenate([cos_t.T, cos_t.T, ones], 1)
    sin_rows = jnp.concatenate([sin_t.T, -sin_t.T, 0 * ones], 1)
    tables = (row_start.astype(jnp.int32).reshape(1), bias_t, cos_t, sin_t, cos_rows, sin_rows)

    split_out, split_down = split, 2 * units
    wide, narrow = (F32, BF), (BF, BF)
    back = (F32, BF, F32)

    normed_zero = (hidden * lax.rsqrt(jnp.mean(hidden * hidden, -1, keepdims=True) + EPSILON) * zero[0][:1]).astype(BF)
    kept_zero, o_zero = layer_attention(normed_zero, zero, tables)
    middle_zero, r_zero = product_sum(
        (o_zero, tree, zero[0]), ((0,), split_out, ("add", (1, (2, 1))), wide), zero[1], stagger=True, key=1
    )
    gate_zero, up_zero, inner_zero = layer_units(r_zero, zero)
    out_zero, normed_one = product_sum(
        (inner_zero, middle_zero, zero[0]), ((0,), split_down, ("add", (1, (2, 2))), narrow), zero[2], key=5
    )

    out_zero, normed_one, attn_one = lax.optimization_barrier((out_zero, normed_one, attn_one))
    one = with_gains(attn_one, mlp_one)
    kept_one, o_one = layer_attention(normed_one, one, tables)
    middle_one, r_one = product_sum(
        (o_one, out_zero, one[0]), ((0,), split_out, ("add", (1, (2, 1))), wide), one[1], key=2
    )
    gate_one, up_one, inner_one = layer_units(r_one, one)
    branch = cot
    d_gate, d_up = units_backward(branch, one, gate_one, up_one)
    out_one, d_mlp_one = product_sum(
        (inner_one, middle_one, r_one, branch, d_gate, d_up), ((0,), split_down, ("add", (1,)), (BF,)),
        one[2], ((2, (4, 5)), (3, (0,))), key=6,
    )
    d_gate, out_one = lax.optimization_barrier((d_gate, out_one))
    grad_middle, grad_attn, d_gain_mlp_one = product_sum(
        (d_gate, d_up, middle_one, branch, one[0]), ((0, 1), 0, ("back", (2, 3, (4, 1))), back), one[2], key=8
    )
    g_mlp_one = reduce_gradient(d_mlp_one)
    dq, dkv = attention_backward(grad_attn, one, tables, kept_one)
    grad_one, branch, d_gain_attn_one, d_attn_one = product_sum(
        (dq, dkv, out_zero, grad_middle, one[0], normed_one, grad_attn, o_one),
        ((0, 1), 0, ("back", (2, 3, (4, 0))), back),
        one[1], ((5, (0, 1)), (6, (7,))), stagger=True, key=7,
    )
    g_attn_one = reduce_gradient(d_attn_one)

    d_gate, d_up = units_backward(branch, zero, gate_zero, up_zero)
    grad_middle, grad_attn, d_gain_mlp_zero, d_mlp_zero = product_sum(
        (d_gate, d_up, inner_zero, middle_zero, branch, r_zero, zero[0]),
        ((0, 1), 0, ("back", (3, 4, (6, 1))), back),
        zero[2], ((5, (0, 1)), (4, (2,))), key=9,
    )
    g_mlp_zero = reduce_gradient(d_mlp_zero)
    grad_attn, g_mlp_one = lax.optimization_barrier((grad_attn, g_mlp_one))
    dq, dkv = attention_backward(grad_attn, zero, tables, kept_zero)
    dq, g_attn_one = lax.optimization_barrier((dq, g_attn_one))
    grad_zero, send_zero, d_gain_attn_zero, d_attn_zero = product_sum(
        (dq, dkv, tree, grad_middle, zero[0], normed_zero, grad_attn, o_zero),
        ((0, 1), 0, ("back", (2, 3, (4, 0))), back),
        zero[1], ((5, (0, 1)), (6, (7,))), key=11,
    )
    d_gain_attn_zero, d_gain_mlp_zero, d_gain_attn_one, d_gain_mlp_one = [
        jnp.sum(x, 0) for x in (d_gain_attn_zero, d_gain_mlp_zero, d_gain_attn_one, d_gain_mlp_one)
    ]
    d_gains = jnp.stack([d_gain_attn_zero, d_gain_mlp_zero, d_gain_attn_one, d_gain_mlp_one])
    d_gains = d_gains.reshape(2, 2, devices, -1).swapaxes(1, 2).reshape(2, devices, -1, 128)

    ending = finish if devices == 4 else finish_apart
    g_attn_zero, g_gain, got_out, got_in, got_mlp, got_attn = ending(
        d_attn_zero, d_gains, out_zero, out_one, send_zero, branch,
        g_mlp_one, g_attn_one,
    )

    layer_output, input_grad, *grads = write_results(
        (out_zero, out_one, got_out), (grad_zero, grad_one, got_in), (g_attn_zero, g_attn_one, got_attn), width, span
    )
    input_grad, g_mlp_zero = lax.optimization_barrier((input_grad, g_mlp_zero))
    grads += write_mlp(
        g_mlp_zero, g_mlp_one, lax.ppermute(g_mlp_zero, "section", [(1, 0)]), got_mlp, units
    )
    g_query, g_key, g_value, g_out, g_gate, g_up, g_down = [grad[None] for grad in grads]
    g_gain = g_gain.reshape(2, 1, -1)
    return (
        layer_output[None], input_grad[None], g_gain[0], g_query, g_key, g_value, g_out, g_gain[1], g_gate, g_up, g_down,
    )


def solution(mesh):
    in_specs = (
        P(None, "dp", None),
        P(None, "dp", None),
        P(),
        P(),
        P(),
        P("section", "dp"),
        P("section", "dp", "tensor"),
        P("section", "dp", "tensor"),
        P("section", "dp", "tensor"),
        P("section", "tensor", "dp"),
        P("section", "dp"),
        P("section", "dp", "tensor"),
        P("section", "dp", "tensor"),
        P("section", "tensor", "dp"),
    )
    out_specs = (
        P("section", None, "dp", None),
        P("section", None, "dp", None),
        P("section", "dp"),
        P("section", "dp", "tensor"),
        P("section", "dp", "tensor"),
        P("section", "dp", "tensor"),
        P("section", "tensor", "dp"),
        P("section", "dp"),
        P("section", "dp", "tensor"),
        P("section", "dp", "tensor"),
        P("section", "tensor", "dp"),
    )
    return jax.shard_map(shards, mesh=mesh, in_specs=in_specs, out_specs=out_specs, check_vma=False)
```

```python
import functools

import jax
import jax.numpy as jnp
from jax import lax
from jax.experimental import pallas as pl
from jax.experimental.pallas import tpu as pltpu
from jax.sharding import PartitionSpec as P

HEAD = 64
HALF = HEAD // 2
TRUNK = 1024
GROUP = 384
EPSILON = 1e-05
THETA = 10000.0
MASKED = -1e30
BF = jnp.bfloat16
F32 = jnp.float32
MESH = pl.DeviceIdType.MESH
BOTH = ("dp", "section")


def dot_f32(a, b, ca, cb):
    return lax.dot_general(a, b, (((ca,), (cb,)), ((), ())), preferred_element_type=F32)


BLOCK = 256
PIECE = 128
NO_COST = pl.CostEstimate(flops=1, transcendentals=0, bytes_accessed=1)


def columns_of(i):
    return pl.ds(pl.multiple_of(i * PIECE, PIECE), PIECE)


def gain_row(arrays, place, at):
    return arrays[place[0]][place[1] : place[1] + 1, at]


def row_scale(squares, model):
    return lax.rsqrt(jnp.sum(squares, 1, keepdims=True) * (1.0 / model) + EPSILON)


def before_sum(job, arrays, keep):
    kind, places = job[2]
    if kind == "back":
        value = arrays[places[0]]
        model = value.shape[1]
        squares = jnp.zeros(keep.shape, F32)
        for i in range(model // PIECE):
            x = value[:, i * PIECE : (i + 1) * PIECE].astype(F32)
            squares += x * x
        keep[...] = jnp.broadcast_to(row_scale(squares, model), keep.shape)


def with_piece(job, i, total, arrays, outs, keep, sums):
    kind, places = job[2]
    at = columns_of(i)
    if kind == "add":
        y = (arrays[places[0]][:, at].astype(F32) + total).astype(outs[0].dtype)
        outs[0][:, at] = y
        if len(outs) > 1:
            sums[...] += y.astype(F32) * y.astype(F32)
    if kind == "back":
        product = total * arrays[places[0]][:, at].astype(F32) * keep[...]
        sums[...] += product * gain_row(arrays, places[2], at)
        outs[2][:, at] = jnp.sum(product.reshape(-1, 8, PIECE), 0)


def after_sum(job, rows, total, arrays, outs, keep, sums):
    kind, places = job[2]
    model = arrays[places[0]].shape[1]
    at = lambda i: slice(i * PIECE, (i + 1) * PIECE)
    if kind == "add" and len(outs) > 1:
        scale = row_scale(sums[rows], model)
        for i in range(model // PIECE):
            y = outs[0][rows, at(i)].astype(F32)
            outs[1][rows, at(i)] = (y * scale * gain_row(arrays, places[1], at(i))).astype(BF)
    if kind == "back":
        mean = jnp.sum(sums[rows], 1, keepdims=True) * (1.0 / model)
        scale = keep[rows]
        for i in range(model // PIECE):
            unit = arrays[places[0]][rows, at(i)].astype(F32) * scale
            grad = total(i)[rows].astype(F32) * gain_row(arrays, places[2], at(i))
            out = arrays[places[1]][rows, at(i)].astype(F32) + scale * (grad - unit * mean)
            outs[0][rows, at(i)] = out
            outs[1][rows, at(i)] = out.astype(BF)


def product_sum_kernel(cfg, *refs):
    n_join, n_arrays, job, sides, stagger = cfg
    xs, first_column = job[:2]
    refs = list(refs)
    take = lambda n: [refs.pop(0) for _ in range(n)]
    joined = take(n_join)
    from_hbm = [None, *take(n_arrays - 1)]
    (w_hbm,) = take(1)
    outs_hbm = take(len(job[3]))
    (g_hbm,) = take(1) if sides else (None,)
    arrays = take(n_arrays)
    outs = take(len(job[3]))
    load_sem, out_sem, w_buf, p_buf, a_buf, b_buf, w_sem, sa, ra, sb, rb, sc, rc, turn, keep, sums = take(16)
    g_buf, g_sem = take(2) if sides else (None, None)
    per_block = BLOCK // PIECE
    pieces = p_buf.shape[0]
    blocks = pieces // per_block
    n_rows = p_buf.shape[1]
    early = len(xs)
    lag = 2
    assert xs[0] == 0

    t = lax.axis_index("tensor")
    sec = lax.axis_index("section")
    dat = lax.axis_index("dp")
    inner = (t == 1) | (t == 2)
    outer = jnp.logical_not(inner)
    pair = (sec, t + 1 - 2 * lax.rem(t, 2), dat)
    mid = (sec, 3 - t, dat)
    mate = (1 - sec, t, dat)

    def columns(j):
        return pl.ds(pl.multiple_of(j * BLOCK, BLOCK), BLOCK)

    def to_inner(i):
        return pltpu.make_async_remote_copy(
            p_buf.at[i], a_buf.at[i], sa.at[i], ra.at[i], device_id=pair, device_id_type=MESH
        )

    def across(i):
        return pltpu.make_async_remote_copy(
            p_buf.at[i], b_buf.at[i], sb.at[i], rb.at[i], device_id=mid, device_id_type=MESH
        )

    def to_outer(i):
        return pltpu.make_async_remote_copy(
            b_buf.at[i], b_buf.at[i], sc.at[i], rc.at[i], device_id=pair, device_id_type=MESH
        )

    def load(k):
        return pltpu.make_async_copy(from_hbm[k], arrays[k], load_sem.at[k])

    def join():
        copies, start = [], 0
        for m, src in enumerate(joined):
            at = pl.ds(start, src.shape[1])
            copies.append(pltpu.make_async_copy(src, arrays[0].at[:, at], load_sem.at[n_arrays + m]))
            start += src.shape[1]
        return copies

    def fetch(j, slot):
        return pltpu.make_async_copy(
            w_hbm.at[columns(j), pl.ds(first_column, w_buf.shape[2])], w_buf.at[slot], w_sem.at[slot]
        )

    def flush(j, slot):
        return pltpu.make_async_copy(g_buf.at[slot], g_hbm.at[columns(j), :], g_sem.at[slot])

    def every_piece(body):
        def turn_of(i, _):
            body(i)
            return 0

        lax.fori_loop(0, pieces, turn_of, 0)

    for copy in join():
        copy.start()
    for k in range(1, early):
        load(k).start()
    fetch(0, 0).start()
    for k in range(early, n_arrays):
        load(k).start()
    barrier = pltpu.get_barrier_semaphore()
    pl.semaphore_signal(barrier, inc=1, device_id=pair, device_id_type=MESH)
    sums[...] = jnp.zeros_like(sums)

    @pl.when(inner)
    def _():
        pl.semaphore_signal(barrier, inc=1, device_id=mid, device_id_type=MESH)
        pl.semaphore_wait(barrier, 2)

    @pl.when(outer)
    def _():
        if stagger:
            pl.semaphore_signal(barrier, inc=1, device_id=mate, device_id_type=MESH)
            pl.semaphore_wait(barrier, 2)

            @pl.when(sec == 1)
            def _():
                pl.semaphore_wait(turn, 1)

        else:
            pl.semaphore_wait(barrier, 1)

    for copy in join():
        copy.wait()
    for k in range(1, early):
        load(k).wait()

    def done(i):
        with_piece(job, i, b_buf[i].astype(F32), arrays, outs, keep, sums)

    def first(i):
        to_inner(i).wait_recv()
        p_buf[i] = p_buf[i] + a_buf[i]
        across(i).start()

    def second(i):
        across(i).wait_recv()
        b_buf[i] = p_buf[i] + b_buf[i]
        to_outer(i).start()
        done(i)

    def side(j):
        slot = lax.rem(j, 2)

        @pl.when(j >= 2)
        def _():
            flush(j - 2, slot).wait()

        start = 0
        for a, bs in sides:
            a_t = arrays[a][:, columns(j)].T
            for b in bs:
                width = arrays[b].shape[1]
                g_buf[slot, :, start : start + width] = jnp.dot(
                    a_t, arrays[b][...], preferred_element_type=F32
                ).astype(BF)
                start += width
        flush(j, slot).start()
        return 0

    def step(j, _):
        slot = lax.rem(j, 2)
        fetch(j, slot).wait()

        @pl.when(j + 1 < blocks)
        def _():
            fetch(j + 1, 1 - slot).start()

        total, start = None, 0
        for x in xs:
            width = arrays[x].shape[1]
            term = dot_f32(arrays[x][...], w_buf[slot, :, start : start + width], 1, 1)
            total = term if total is None else total + term
            start += width
        total = total.astype(BF)
        for u in range(per_block):
            p_buf[per_block * j + u] = total[:, u * PIECE : (u + 1) * PIECE]

        @pl.when(outer)
        def _():
            for u in range(per_block):
                to_inner(per_block * j + u).start()

        @pl.when(j == 1)
        def _():
            for k in range(early, n_arrays):
                load(k).wait()
            before_sum(job, arrays, keep)

        if sides:

            @pl.when(j >= lag)
            def _():
                side(j - lag)

        @pl.when(inner)
        def _():
            for u in range(per_block):
                i = per_block * j + u
                first(i)

                @pl.when(j >= 1)
                def _():
                    second(i - per_block)

        return 0

    lax.fori_loop(0, blocks, step, 0)

    @pl.when(inner)
    def _():
        for u in range(per_block):
            second(pieces - per_block + u)

    if stagger:

        @pl.when(outer)
        def _():
            every_piece(lambda i: to_inner(i).wait_send())

            @pl.when(sec == 0)
            def _():
                pl.semaphore_signal(turn, inc=1, device_id=mate, device_id_type=MESH)

    if sides:
        lax.fori_loop(blocks - lag, blocks, lambda j, _: side(j), 0)

    @pl.when(outer)
    def _():
        if not stagger:
            every_piece(lambda i: to_inner(i).wait_send())

        def arrive(i):
            to_outer(i).wait_recv()
            done(i)

        every_piece(arrive)

    chunks = 5 if n_rows % (5 * 32) == 0 else 1
    chunk = n_rows // chunks
    block = 32 if chunk % 32 == 0 else 16
    height = lambda m: 8 if job[2][0] == "back" and m == 2 else n_rows
    stores = []

    def store(m, rows):
        copy = pltpu.make_async_copy(outs[m].at[rows], outs_hbm[m].at[rows], out_sem.at[len(stores)])
        copy.start()
        stores.append(copy)

    for c in range(chunks):

        def turn_rows(r, _):
            rows = pl.ds(pl.multiple_of(c * chunk + r * block, block), block)
            after_sum(job, rows, lambda i: b_buf.at[i], arrays, outs, keep, sums)
            return 0

        if job[2][0] == "back" or len(outs) > 1:
            lax.fori_loop(0, chunk // block, turn_rows, 0)
        for m in range(len(outs)):
            if height(m) == n_rows:
                store(m, pl.ds(c * chunk, chunk))
    for m in range(len(outs)):
        if height(m) != n_rows:
            store(m, pl.ds(0, height(m)))

    @pl.when(inner)
    def _():
        def sent(i):
            across(i).wait_send()
            to_outer(i).wait_send()

        every_piece(sent)

    if sides:
        flush(blocks - 2, (blocks - 2) % 2).wait()
        flush(blocks - 1, (blocks - 1) % 2).wait()
    for copy in stores:
        copy.wait()


def product_sum(arrays, job, weights, sides=(), stagger=False, key=1):
    assert lax.axis_size("tensor") == 4
    first = arrays[0] if isinstance(arrays[0], tuple) else (arrays[0],)
    given = (*first, *arrays[1:])
    rows, model = first[0].shape[0], weights.shape[0]
    arrays = (jax.ShapeDtypeStruct((rows, sum(x.shape[1] for x in first)), BF), *arrays[1:])
    pieces = model // PIECE
    depth = sum(arrays[x].shape[1] for x in job[0])
    anywhere = pl.BlockSpec(memory_space=pl.ANY)
    buf = pltpu.VMEM((pieces, rows, PIECE), BF)
    sem = pltpu.SemaphoreType.DMA((pieces,))
    two = pltpu.SemaphoreType.DMA((2,))
    out_shape = []
    for m, dtype in enumerate(job[3]):
        height = 8 if job[2][0] == "back" and m == 2 else rows
        out_shape.append(jax.ShapeDtypeStruct((height, model), dtype))
    scratch = [pltpu.VMEM(x.shape, x.dtype) for x in (*arrays, *out_shape)]
    scratch += [pltpu.SemaphoreType.DMA((len(arrays) + len(first),)), pltpu.SemaphoreType.DMA((16,))]
    scratch += [pltpu.VMEM((2, BLOCK, depth), BF), buf, buf, buf, two, *[sem] * 6, pltpu.SemaphoreType.REGULAR]
    scratch += [pltpu.VMEM((rows, PIECE), F32)] * 2
    if sides:
        side_width = sum(arrays[b].shape[1] for _, bs in sides for b in bs)
        out_shape.append(jax.ShapeDtypeStruct((model, side_width), BF))
        scratch += [pltpu.VMEM((2, BLOCK, side_width), BF), two]
    out = pl.pallas_call(
        functools.partial(product_sum_kernel, (len(first), len(arrays), job, tuple(sides), stagger)),
        out_shape=out_shape,
        in_specs=[anywhere] * (len(given) + 1),
        out_specs=[anywhere] * len(out_shape),
        scratch_shapes=scratch,
        compiler_params=pltpu.CompilerParams(
            collective_id=key, has_side_effects=True, vmem_limit_bytes=62 << 20
        ),
        cost_estimate=NO_COST,
        name=f"product_sum_{key}",
    )(*given, weights)
    return out if len(out) > 1 else out[0]


def dp_peers(count):
    me = lax.axis_index("dp")
    sec, t = lax.axis_index("section"), lax.axis_index("tensor")
    others = [lax.rem(me + k, count) for k in range(1, count)]
    return me, others, [(sec, t, other) for other in others]


def greet(ids):
    barrier = pltpu.get_barrier_semaphore()
    for device in ids:
        pl.semaphore_signal(barrier, inc=1, device_id=device, device_id_type=MESH)
    pl.semaphore_wait(barrier, len(ids))


def turn_rows(x, cos_ref, sin_ref):
    lane = lax.broadcasted_iota(jnp.int32, x.shape, 1)
    width = x.shape[1]
    partner = jnp.where(lane < HALF, pltpu.roll(x, width - HALF, 1), pltpu.roll(x, HALF, 1))
    return x * cos_ref[...] + partner * sin_ref[...]


def gather_kernel(count, raw_ref, cos_ref, sin_ref, o_ref, t_ref, x_ref, send, recv):
    me, _, ids = dp_peers(count)
    x_ref[...] = turn_rows(raw_ref[...], cos_ref, sin_ref).astype(BF)
    greet(ids)
    copies = [
        pltpu.make_async_remote_copy(
            x_ref, o_ref.at[me], send.at[k], recv.at[k], device_id=device, device_id_type=MESH
        )
        for k, device in enumerate(ids)
    ]
    for copy in copies:
        copy.start()
    o_ref[me] = x_ref[...]
    for copy in copies:
        copy.wait()
    t_ref[...] = o_ref[...].reshape(t_ref.shape[1], t_ref.shape[0]).T


def scatter_kernel(count, x_ref, cos_ref, sin_ref, o_ref, buf, send, recv):
    me, others, ids = dp_peers(count)
    greet(ids)
    copies = [
        pltpu.make_async_remote_copy(
            x_ref.at[others[k]], buf.at[k], send.at[k], recv.at[k], device_id=device, device_id_type=MESH
        )
        for k, device in enumerate(ids)
    ]
    for copy in copies:
        copy.start()
    total = x_ref[me].astype(F32)
    for k, copy in enumerate(copies):
        copy.wait()
        total = total + buf[k].astype(F32)
    o_ref[...] = turn_rows(total, cos_ref, sin_ref).astype(BF)


def gather_rows(raw, cos_rows, sin_rows):
    count = lax.axis_size("dp")
    rows, width = raw.shape
    in_vmem = pl.BlockSpec(memory_space=pltpu.VMEM)
    sem = pltpu.SemaphoreType.DMA((count - 1,))
    out, out_t = pl.pallas_call(
        functools.partial(gather_kernel, count),
        out_shape=(
            jax.ShapeDtypeStruct((count, rows, width), BF),
            jax.ShapeDtypeStruct((width, count * rows), BF),
        ),
        in_specs=[in_vmem] * 3,
        out_specs=(in_vmem, in_vmem),
        scratch_shapes=[pltpu.VMEM((rows, width), BF), sem, sem],
        compiler_params=pltpu.CompilerParams(collective_id=3, has_side_effects=True),
        cost_estimate=NO_COST,
        name="gather_rows",
    )(raw, cos_rows, sin_rows)
    return out.reshape(-1, width), out_t


def scatter_rows(x, cos_rows, sin_rows):
    count = lax.axis_size("dp")
    rows, width = x.shape[0] // count, x.shape[1]
    in_vmem = pl.BlockSpec(memory_space=pltpu.VMEM)
    sem = pltpu.SemaphoreType.DMA((count - 1,))
    return pl.pallas_call(
        functools.partial(scatter_kernel, count),
        out_shape=jax.ShapeDtypeStruct((rows, width), BF),
        in_specs=[in_vmem] * 3,
        out_specs=in_vmem,
        scratch_shapes=[pltpu.VMEM((count - 1, rows, width), x.dtype), sem, sem],
        compiler_params=pltpu.CompilerParams(collective_id=4, has_side_effects=True),
        cost_estimate=NO_COST,
        name="scatter_rows",
    )(x.reshape(count, rows, width), cos_rows, sin_rows)


def finish_kernel(
    g_hbm, gain_ref, out_zero, out_one, in_zero, in_one, mlp_one, attn_one,
    o_ref, gain_out, got_out, got_in, got_mlp, got_attn,
    mine, away, got, xs, ys, xr, yr, gains, load_sem, send, recv, mate_send, mate_recv, gain_send, gain_recv,
):
    sec, t, dat = lax.axis_index("section"), lax.axis_index("tensor"), lax.axis_index("dp")
    flip_x = dat + 1 - 2 * lax.rem(dat, 2)
    flip_y = lax.rem(dat + 2, 4)
    across = lax.rem(flip_x + 2, 4)
    by_x, by_y, mate = (sec, t, flip_x), (sec, t, flip_y), (1 - sec, t, dat)
    peers = [
        mate, by_x, by_y, (sec, t, across),
        (1 - sec, t, flip_x), (1 - sec, t, flip_y), (1 - sec, t, across),
    ]
    rows = g_hbm.shape[1] // 2
    upper, lower = pl.ds(0, rows), pl.ds(rows, rows)
    order = (across, flip_x, flip_y, dat)
    loads = []
    for k, block in enumerate(order):
        loads.append(pltpu.make_async_copy(g_hbm.at[2 * block + 1 - sec], away.at[k], load_sem.at[k]))
        loads.append(pltpu.make_async_copy(g_hbm.at[2 * block + sec], mine.at[k], load_sem.at[4 + k]))
    for copy in loads:
        copy.start()
    greet(peers)

    def remote(src, dst, k, device):
        return pltpu.make_async_remote_copy(
            src, dst, send.at[k], recv.at[k], device_id=device, device_id_type=MESH
        )

    def to_mate(src, dst, k):
        return pltpu.make_async_remote_copy(
            src, dst, mate_send.at[k], mate_recv.at[k], device_id=mate, device_id_type=MESH
        )

    swaps = [remote(away.at[k], got.at[k], k, mate) for k in range(4)]
    for k in range(4):
        loads[2 * k].wait()
        swaps[k].start()
    gain_copies = [
        pltpu.make_async_remote_copy(
            gain_ref.at[peer[0], peer[2]], gains.at[k], gain_send.at[k], gain_recv.at[k],
            device_id=peer, device_id_type=MESH,
        )
        for k, peer in enumerate(peers)
    ]
    for copy in gain_copies:
        copy.start()
    outs = []
    for k in range(4):
        loads[2 * k + 1].wait()
        swaps[k].wait_recv()
        mine[k] = (mine[k].astype(F32) + got[k].astype(F32)).astype(BF)
        if k == 0:
            outs += [remote(mine.at[0, upper], xs.at[0], 4, by_x), remote(mine.at[0, lower], ys.at[0], 5, by_y)]
        if k == 1:
            outs += [remote(mine.at[1, upper], xs.at[1], 6, by_x)]
        if k == 2:
            outs += [remote(mine.at[2, lower], ys.at[1], 7, by_y)]
        for copy in outs[-(2 if k == 0 else 1) :]:
            if k < 3:
                copy.start()

    @pl.when(sec == 0)
    def _():
        to_mate(in_one, got_in, 0).start()
        to_mate(out_one, got_out, 1).start()
        to_mate(mlp_one, got_mlp, 2).start()
        to_mate(attn_one, got_attn, 3).start()

    @pl.when(sec == 1)
    def _():
        to_mate(in_zero, got_in, 0).start()
        to_mate(out_zero, got_out, 1).start()

    outs[0].wait_recv()
    mine[2, upper] = (mine[2, upper].astype(F32) + xs[0].astype(F32)).astype(BF)
    outs.append(remote(mine.at[2, upper], yr, 8, by_y))
    outs[4].start()
    outs[1].wait_recv()
    mine[1, lower] = (mine[1, lower].astype(F32) + ys[0].astype(F32)).astype(BF)
    outs.append(remote(mine.at[1, lower], xr, 9, by_x))
    outs[5].start()
    total = gain_ref[sec, dat]
    for k, copy in enumerate(gain_copies):
        copy.wait()
        total = total + gains[k]
    gain_out[...] = total
    outs[2].wait_recv()
    outs[3].wait_recv()
    outs[4].wait_recv()
    o_ref[upper] = (mine[3, upper].astype(F32) + xs[1].astype(F32) + yr[...].astype(F32)).astype(BF)
    outs[5].wait_recv()
    o_ref[lower] = (mine[3, lower].astype(F32) + ys[1].astype(F32) + xr[...].astype(F32)).astype(BF)

    @pl.when(sec == 1)
    def _():
        to_mate(o_ref, got_attn, 3).start()

    for copy in swaps + outs:
        copy.wait_send()
    to_mate(in_one, got_in, 0).wait()
    to_mate(out_one, got_out, 1).wait()
    to_mate(attn_one, got_attn, 3).wait()

    @pl.when(sec == 0)
    def _():
        to_mate(mlp_one, got_mlp, 2).wait_send()

    @pl.when(sec == 1)
    def _():
        to_mate(mlp_one, got_mlp, 2).wait_recv()


def finish(g, gains, out_zero, out_one, in_zero, in_one, mlp_one, attn_one):
    rows, width = g.shape[0] // 8, g.shape[1]
    part = pltpu.VMEM((2, rows // 2, width), BF)
    whole = pltpu.VMEM((4, rows, width), BF)
    end = pltpu.VMEM((rows // 2, width), BF)
    in_vmem, anywhere = pl.BlockSpec(memory_space=pltpu.VMEM), pl.BlockSpec(memory_space=pl.ANY)
    like = lambda x: jax.ShapeDtypeStruct(x.shape, x.dtype)
    dma = lambda n: pltpu.SemaphoreType.DMA((n,))
    return pl.pallas_call(
        finish_kernel,
        out_shape=(
            jax.ShapeDtypeStruct((rows, width), BF),
            jax.ShapeDtypeStruct(gains.shape[2:], F32),
            like(out_zero), like(in_zero), like(mlp_one), like(attn_one),
        ),
        in_specs=[anywhere, in_vmem, *[anywhere] * 6],
        out_specs=(in_vmem, in_vmem, *[anywhere] * 4),
        scratch_shapes=[
            whole, whole, whole, part, part, end, end, pltpu.VMEM((7, *gains.shape[2:]), F32),
            dma(8), dma(10), dma(10), dma(4), dma(4), dma(7), dma(7),
        ],
        compiler_params=pltpu.CompilerParams(
            collective_id=12, has_side_effects=True, vmem_limit_bytes=62 << 20
        ),
        cost_estimate=NO_COST,
        name="finish",
    )(g.reshape(8, rows, width), gains, out_zero, out_one, in_zero, in_one, mlp_one, attn_one)


def finish_apart(g, gains, out_zero, out_one, in_zero, in_one, mlp_one, attn_one):
    first_core = lax.axis_index("section") == 0
    half = reduce_gradient(g)
    swap = lambda zero, one: lax.ppermute(jnp.where(first_core, one, zero), "section", [(0, 1), (1, 0)])
    return (
        half, share_sums(gains), swap(out_zero, out_one), swap(in_zero, in_one),
        lax.ppermute(mlp_one, "section", [(0, 1)]), swap(half, attn_one),
    )


def in_rows(count, block, body):
    def turn(r, _):
        body(pl.ds(pl.multiple_of(r * block, block), block))
        return 0

    lax.fori_loop(0, count // block, turn, 0)


def widen_turned(dst, src, start, width):
    for c in range(0, width, 128):
        dst[c : c + 128] = src[:, start + c : start + c + 128].astype(F32).T


def write_mlp_kernel(
    zero, one, from_one, from_zero, gate_hbm, up_hbm, down_hbm, mlp, gate_buf, up_buf, down_buf, load_sem, store_sem
):
    sec = lax.axis_index("section")
    half, units = zero.shape[0], gate_buf.shape[1]
    low, high = pl.ds(0, half), pl.ds(half, half)
    load = lambda src, at, k: pltpu.make_async_copy(src, mlp.at[at], load_sem.at[k])
    store = lambda src, dst, k: pltpu.make_async_copy(src, dst, store_sem.at[k])

    @pl.when(sec == 0)
    def _():
        load(zero, low, 0).start()
        load(from_one, high, 1).start()

    @pl.when(sec == 1)
    def _():
        load(from_zero, low, 0).start()
        load(one, high, 1).start()

    load(zero, low, 0).wait()
    load(zero, high, 1).wait()

    def gates(rows):
        gate_buf[rows] = mlp[rows, :units].astype(F32)
        up_buf[rows] = mlp[rows, units : 2 * units].astype(F32)

    in_rows(2 * half, 32, gates)
    stores = [store(gate_buf, gate_hbm, 0), store(up_buf, up_hbm, 1), store(down_buf, down_hbm, 2)]
    stores[0].start()
    stores[1].start()
    widen_turned(down_buf, mlp, 2 * units, units)
    stores[2].start()
    for copy in stores:
        copy.wait()


def write_mlp(zero, one, from_one, from_zero, units):
    shard = 2 * zero.shape[0]
    anywhere = pl.BlockSpec(memory_space=pl.ANY)
    shapes = [(shard, units), (shard, units), (units, shard)]
    return pl.pallas_call(
        write_mlp_kernel,
        out_shape=[jax.ShapeDtypeStruct(shape, F32) for shape in shapes],
        in_specs=[anywhere] * 4,
        out_specs=[anywhere] * 3,
        scratch_shapes=[
            pltpu.VMEM((shard, zero.shape[1]), BF),
            *[pltpu.VMEM(shape, F32) for shape in shapes],
            pltpu.SemaphoreType.DMA((2,)),
            pltpu.SemaphoreType.DMA((3,)),
        ],
        compiler_params=pltpu.CompilerParams(vmem_limit_bytes=62 << 20),
        cost_estimate=NO_COST,
        name="write_mlp",
    )(zero, one, from_one, from_zero)


def write_kernel(
    split, out_zero, out_one, got_out, in_zero, in_one, got_in, attn_zero, attn_one, got_attn,
    out_hbm, in_hbm, q_hbm, k_hbm, v_hbm, o_hbm,
    outs, wides, attn, narrow, q_buf, k_buf, v_buf, o_buf, load_sem, store_sem,
):
    sec = lax.axis_index("section")
    half = attn_zero.shape[0]
    low, high = pl.ds(0, half), pl.ds(half, half)
    load = lambda src, dst, k: pltpu.make_async_copy(src, dst, load_sem.at[k])
    store = lambda src, dst, k: pltpu.make_async_copy(src, dst, store_sem.at[k])

    def start(own_out, own_in, attn_low, attn_high):
        load(own_out, outs.at[0], 0).start()
        load(own_in, wides.at[0], 1).start()
        load(attn_low, attn.at[low], 2).start()
        load(attn_high, attn.at[high], 3).start()

    @pl.when(sec == 0)
    def _():
        start(out_zero, in_zero, attn_zero, got_attn)

    @pl.when(sec == 1)
    def _():
        start(out_one, in_one, got_attn, attn_one)

    load(got_in, narrow, 4).start()
    load(got_out, outs.at[1], 5).start()
    stores = [
        store(outs.at[0], out_hbm.at[sec], 0),
        store(wides.at[0], in_hbm.at[sec], 1),
        store(outs.at[1], out_hbm.at[1 - sec], 2),
        store(wides.at[1], in_hbm.at[1 - sec], 3),
        store(q_buf, q_hbm, 4),
        store(k_buf, k_hbm, 5),
        store(v_buf, v_hbm, 6),
        store(o_buf, o_hbm, 7),
    ]
    load(out_zero, outs.at[0], 0).wait()
    stores[0].start()
    load(in_zero, wides.at[0], 1).wait()
    stores[1].start()
    width, span = q_buf.shape[1], k_buf.shape[1]
    load(attn_one, attn.at[low], 2).wait()
    load(attn_one, attn.at[high], 3).wait()

    def projections(rows):
        q_buf[rows] = attn[rows, :width].astype(F32)
        k_buf[rows] = attn[rows, width : width + span].astype(F32)
        v_buf[rows] = attn[rows, width + span : split].astype(F32)

    in_rows(2 * half, 32, projections)
    for k in (4, 5, 6):
        stores[k].start()
    widen_turned(o_buf, attn, split, width)
    stores[7].start()
    load(got_in, narrow, 4).wait()

    def widen(rows):
        wides[1, rows] = narrow[rows].astype(F32)

    in_rows(narrow.shape[0], 32, widen)
    stores[3].start()
    load(got_out, outs.at[1], 5).wait()
    stores[2].start()
    for copy in stores:
        copy.wait()


def write_results(results, ins, attns, width, span):
    rows, model = results[0].shape
    shard = 2 * attns[0].shape[0]
    anywhere = pl.BlockSpec(memory_space=pl.ANY)
    shapes = [(shard, width), (shard, span), (shard, span), (width, shard)]
    return pl.pallas_call(
        functools.partial(write_kernel, width + 2 * span),
        out_shape=[
            jax.ShapeDtypeStruct((2, rows, model), BF),
            jax.ShapeDtypeStruct((2, rows, model), F32),
            *[jax.ShapeDtypeStruct(shape, F32) for shape in shapes],
        ],
        in_specs=[anywhere] * 9,
        out_specs=[anywhere] * 6,
        scratch_shapes=[
            pltpu.VMEM((2, rows, model), BF),
            pltpu.VMEM((2, rows, model), F32),
            pltpu.VMEM((shard, attns[0].shape[1]), BF),
            pltpu.VMEM((rows, model), BF),
            *[pltpu.VMEM(shape, F32) for shape in shapes],
            pltpu.SemaphoreType.DMA((6,)),
            pltpu.SemaphoreType.DMA((8,)),
        ],
        compiler_params=pltpu.CompilerParams(vmem_limit_bytes=62 << 20),
        cost_estimate=NO_COST,
        name="write_results",
    )(*results, *ins, *attns)


def share_kernel(count, x_ref, o_ref, buf, send, recv):
    sec, t, dat = lax.axis_index("section"), lax.axis_index("tensor"), lax.axis_index("dp")
    peers = [
        (lax.rem(sec + k // count, 2), t, lax.rem(dat + k % count, count)) for k in range(1, 2 * count)
    ]
    greet(peers)
    copies = [
        pltpu.make_async_remote_copy(
            x_ref.at[peer[0], peer[2]], buf.at[k], send.at[k], recv.at[k], device_id=peer, device_id_type=MESH
        )
        for k, peer in enumerate(peers)
    ]
    for copy in copies:
        copy.start()
    total = x_ref[sec, dat]
    for k, copy in enumerate(copies):
        copy.wait()
        total = total + buf[k]
    o_ref[...] = total


def share_sums(x):
    count = lax.axis_size("dp")
    in_vmem = pl.BlockSpec(memory_space=pltpu.VMEM)
    sem = pltpu.SemaphoreType.DMA((2 * count - 1,))
    return pl.pallas_call(
        functools.partial(share_kernel, count),
        out_shape=jax.ShapeDtypeStruct(x.shape[2:], F32),
        in_specs=[in_vmem],
        out_specs=in_vmem,
        scratch_shapes=[pltpu.VMEM((2 * count - 1, *x.shape[2:]), F32), sem, sem],
        compiler_params=pltpu.CompilerParams(collective_id=13, has_side_effects=True),
        cost_estimate=NO_COST,
        name="share_sums",
    )(x)


def group_start(first_row):
    past = lax.max(first_row - TRUNK, 0)
    return pl.multiple_of(TRUNK + GROUP * lax.div(past, GROUP), 128)


def over_windows(tree_len, rows, tile, first_row, run):
    if tile % 128 == 0 and GROUP % tile == 0 and TRUNK % tile == 0 and rows % tile == 0:

        @pl.when(first_row < TRUNK)
        def _():
            run(((pl.ds(0, TRUNK), True),))

        @pl.when(first_row >= TRUNK)
        def _():
            run(((pl.ds(0, TRUNK), False), (pl.ds(group_start(first_row), GROUP), True)))

    else:
        run(((pl.ds(0, tree_len), True),))


def masked(scores, bias_ref, win, step):
    bias = bias_ref[win, :].astype(F32)
    return scores + (bias if step == 1 else jnp.concatenate([bias] * step, axis=1))


def head_rows(ref, head):
    return ref[head * HEAD : (head + 1) * HEAD, :]


def beside(ref, head, count):
    parts = [head_rows(ref, head + k) for k in range(count)]
    return parts[0] if count == 1 else jnp.concatenate(parts, axis=1)


def turned_beside(ref, cos, sin, head, count):
    parts = []
    for k in range(count):
        rows = head_rows(ref, head + k)
        first, second = rows[:HALF], rows[HALF:]
        parts.append(jnp.concatenate([first * cos - second * sin, second * cos + first * sin], axis=0))
    whole = parts[0] if count == 1 else jnp.concatenate(parts, axis=1)
    return (whole.astype(BF).astype(F32) * HEAD**-0.5).astype(BF)


def as_rows(x, tile, count):
    parts = [x[:, k * tile : (k + 1) * tile] for k in range(count)]
    return (parts[0] if count == 1 else jnp.concatenate(parts, axis=0)).T


def over_groups(groups, step, body):
    for group in range(groups):
        body(group, slice(group * step * HEAD, (group + 1) * step * HEAD))


def attend_kernel(
    rows, step, start_ref, q_ref, kv_ref, kvt_ref, bias_ref, cos_ref, sin_ref, o_ref, on_ref, lse_ref
):
    tile = q_ref.shape[1]
    heads = q_ref.shape[0] // HEAD
    first_row = start_ref[0] + pl.program_id(0) * tile

    def body(wins, group, lanes):
        head = group * step
        q = turned_beside(q_ref, cos_ref[...], sin_ref[...], head, step)
        scores = []
        for win, mask in wins:
            score = dot_f32(kv_ref[win, :HEAD], q, 1, 0)
            scores.append(masked(score, bias_ref, win, step) if mask else score)
        top = functools.reduce(jnp.maximum, [jnp.max(s, 0, keepdims=True) for s in scores])
        expo = [jnp.exp(s - top) for s in scores]
        total = sum(jnp.sum(e, 0, keepdims=True) for e in expo)
        out = sum(dot_f32(kvt_ref[HEAD:, win], e.astype(BF), 1, 0) for (win, _), e in zip(wins, expo))
        out = out / total
        on_ref[:, lanes] = as_rows(out, tile, step).astype(BF)
        lse_ref[group, 0] = top + jnp.log(total)
        out = out.astype(BF)
        for k in range(step):
            o_ref[(head + k) * HEAD : (head + k + 1) * HEAD, :] = out[:, k * tile : (k + 1) * tile]

    over_windows(
        kv_ref.shape[0], rows, tile, first_row,
        lambda wins: over_groups(heads // step, step, functools.partial(body, wins)),
    )


def attend_back_kernel(
    rows, step, start_ref, q_ref, do_ref, o_ref, lse_ref, kv_ref, kvt_ref, bias_ref, cos_ref, sin_ref,
    dq_ref, dkv_ref, dk_acc, dv_acc,
):
    tile = q_ref.shape[1]
    heads = q_ref.shape[0] // HEAD
    first_row = start_ref[0] + pl.program_id(0) * tile

    @pl.when(pl.program_id(0) == 0)
    def _():
        dk_acc[...] = jnp.zeros_like(dk_acc)
        dv_acc[...] = jnp.zeros_like(dv_acc)

    def body(wins, group, lanes):
        head = group * step
        cos, sin = cos_ref[...], sin_ref[...]
        q = turned_beside(q_ref, cos, sin, head, step)
        do = beside(do_ref, head, step)
        out = beside(o_ref, head, step)
        lse = lse_ref[group, 0]
        delta = jnp.sum(do.astype(F32) * out.astype(F32), 0, keepdims=True)
        dq = jnp.zeros((HEAD, step * tile), F32)
        for win, mask in wins:
            score = dot_f32(kv_ref[win, :HEAD], q, 1, 0)
            p = jnp.exp((masked(score, bias_ref, win, step) if mask else score) - lse)
            dp = dot_f32(kv_ref[win, HEAD:], do, 1, 0)
            ds = (p * (dp - delta)).astype(BF)
            dk_acc[win, :] += dot_f32(ds, q, 1, 1)
            dv_acc[win, :] += dot_f32(p.astype(BF), do, 1, 1)
            dq = dq + dot_f32(kvt_ref[:HEAD, win], ds, 1, 0)
        dq = dq * HEAD**-0.5
        turned = []
        for k in range(step):
            first = dq[:HALF, k * tile : (k + 1) * tile]
            second = dq[HALF:, k * tile : (k + 1) * tile]
            turned += [first * cos + second * sin, second * cos - first * sin]
        dq_ref[:, lanes] = jnp.concatenate(turned, axis=0).T.astype(BF)

    over_windows(
        kv_ref.shape[0], rows, tile, first_row,
        lambda wins: over_groups(heads // step, step, functools.partial(body, wins)),
    )

    @pl.when(pl.program_id(0) == pl.num_programs(0) - 1)
    def _():
        dkv_ref[...] = jnp.concatenate([dk_acc[...], dv_acc[...]], axis=1).astype(BF)


def row_tile(rows):
    return 128 if rows % 128 == 0 else rows


def attend(start, q_t, kv, kv_t, bias_t, cos_t, sin_t):
    width, rows = q_t.shape
    heads, tree_len, tile = width // HEAD, kv.shape[0], row_tile(rows)
    step = 2 if tile % 128 == 0 and heads % 2 == 0 else 1
    column = lambda i, s: (0, i)
    whole = lambda i, s: (0, 0)
    return pl.pallas_call(
        functools.partial(attend_kernel, rows, step),
        out_shape=(
            jax.ShapeDtypeStruct((width, rows), BF),
            jax.ShapeDtypeStruct((rows, width), BF),
            jax.ShapeDtypeStruct((heads // step, rows // tile, 1, step * tile), F32),
        ),
        grid_spec=pltpu.PrefetchScalarGridSpec(
            num_scalar_prefetch=1,
            grid=(rows // tile,),
            in_specs=[
                pl.BlockSpec((width, tile), column),
                pl.BlockSpec((tree_len, 2 * HEAD), whole),
                pl.BlockSpec((2 * HEAD, tree_len), whole),
                pl.BlockSpec((tree_len, tile), column),
                pl.BlockSpec((HALF, tile), column),
                pl.BlockSpec((HALF, tile), column),
            ],
            out_specs=(
                pl.BlockSpec((width, tile), column),
                pl.BlockSpec((tile, width), lambda i, s: (i, 0)),
                pl.BlockSpec((heads // step, 1, 1, step * tile), lambda i, s: (0, i, 0, 0)),
            ),
        ),
        compiler_params=pltpu.CompilerParams(vmem_limit_bytes=62 << 20),
        cost_estimate=NO_COST,
        name="attend",
    )(start, q_t, kv, kv_t, bias_t, cos_t, sin_t)


def attend_back(start, q_t, do_t, o_t, lse, kv, kv_t, bias_t, cos_t, sin_t):
    width, rows = q_t.shape
    heads, tree_len, tile = width // HEAD, kv.shape[0], row_tile(rows)
    step = 2 if tile % 128 == 0 and heads % 2 == 0 else 1
    column = lambda i, s: (0, i)
    whole = lambda i, s: (0, 0)
    return pl.pallas_call(
        functools.partial(attend_back_kernel, rows, step),
        out_shape=(
            jax.ShapeDtypeStruct((rows, width), BF),
            jax.ShapeDtypeStruct((tree_len, 2 * HEAD), BF),
        ),
        grid_spec=pltpu.PrefetchScalarGridSpec(
            num_scalar_prefetch=1,
            grid=(rows // tile,),
            in_specs=[
                pl.BlockSpec((width, tile), column),
                pl.BlockSpec((width, tile), column),
                pl.BlockSpec((width, tile), column),
                pl.BlockSpec((heads // step, 1, 1, step * tile), lambda i, s: (0, i, 0, 0)),
                pl.BlockSpec((tree_len, 2 * HEAD), whole),
                pl.BlockSpec((2 * HEAD, tree_len), whole),
                pl.BlockSpec((tree_len, tile), column),
                pl.BlockSpec((HALF, tile), column),
                pl.BlockSpec((HALF, tile), column),
            ],
            out_specs=(
                pl.BlockSpec((tile, width), lambda i, s: (i, 0)),
                pl.BlockSpec((tree_len, 2 * HEAD), whole),
            ),
            scratch_shapes=[pltpu.VMEM((tree_len, HEAD), F32), pltpu.VMEM((tree_len, HEAD), F32)],
        ),
        compiler_params=pltpu.CompilerParams(vmem_limit_bytes=62 << 20),
        cost_estimate=NO_COST,
        name="attend_back",
    )(start, q_t, do_t, o_t, lse, kv, kv_t, bias_t, cos_t, sin_t)


def layer_attention(normed, weights, tables):
    gains, w_attn, w_mlp, width, split, units = weights
    start, bias_t, cos_t, sin_t, cos_rows, sin_rows = tables
    q_t = dot_f32(w_attn[:, :width], normed, 0, 1)
    kv, kv_t = gather_rows(
        jnp.dot(normed, w_attn[:, width:split], preferred_element_type=F32), cos_rows, -sin_rows
    )
    o_t, o, lse = attend(start, q_t, kv, kv_t, bias_t, cos_t, sin_t)
    return (q_t, kv, kv_t, o_t, lse), o


def attention_backward(grad_attn, weights, tables, kept):
    gains, w_attn, w_mlp, width, split, units = weights
    start, bias_t, cos_t, sin_t, cos_rows, sin_rows = tables
    q_t, kv, kv_t, o_t, lse = kept
    do_t = dot_f32(w_attn[:, split : split + width], grad_attn, 0, 1).astype(BF)
    dq, dkv_part = attend_back(start, q_t, do_t, o_t, lse, kv, kv_t, bias_t, cos_t, sin_t)
    return dq, scatter_rows(dkv_part, cos_rows, sin_rows)


def layer_units(normed, weights):
    units = weights[-1]
    gate_up = jnp.dot(normed, weights[2][:, : 2 * units], preferred_element_type=F32)
    gate, up = gate_up[:, :units], gate_up[:, units:]
    return gate, up, (gate * jax.nn.sigmoid(gate) * up).astype(BF)


def units_backward(branch, weights, gate, up):
    units = weights[-1]
    d_inner = dot_f32(branch, weights[2][:, 2 * units :], 1, 0)
    sig = jax.nn.sigmoid(gate)
    d_gate = (d_inner * up * sig * (1.0 + gate * (1.0 - sig))).astype(BF)
    d_up = (d_inner * gate * sig).astype(BF)
    return d_gate, d_up


def reduce_gradient(x):
    return lax.psum_scatter(x, BOTH, scatter_dimension=0, tiled=True)


def shards(
    inputs, cotangent, seg_ids, positions, parents, gain_attn, w_query, key_weight, value_weight,
    w_out, gain_mlp, w_gate, w_up, w_down,
):
    sec = lax.axis_index("section")
    data = lax.axis_index("dp")
    sections = lax.axis_size("section")
    devices = lax.axis_size("dp")
    assert sections == 2 and inputs.shape[0] == 2
    first_core = sec == 0
    rows, model = inputs.shape[1], inputs.shape[2]
    swap = [(0, 1), (1, 0)]

    tree = lax.dynamic_index_in_dim(inputs, sec, 0, keepdims=False)
    hidden = tree.astype(F32)
    segments = lax.dynamic_index_in_dim(seg_ids, sec, 0, keepdims=False)
    places = lax.dynamic_index_in_dim(positions, sec, 0, keepdims=False)
    parent = lax.dynamic_index_in_dim(parents, sec, 0, keepdims=False)

    width, span, units = w_query.shape[2], key_weight.shape[2], w_gate.shape[2]
    split = width + 2 * span
    shard_list = (
        jnp.concatenate(
            [w_query[0], key_weight[0], value_weight[0], w_out[0].T, gain_attn.T, gain_mlp.T], 1
        ).astype(BF),
        jnp.concatenate([w_gate[0], w_up[0], w_down[0].T], 1).astype(BF),
    )
    halves = []
    for shard in shard_list:
        half = shard.shape[0] // 2
        low, high = shard[:half], shard[half:]
        got = lax.ppermute(jnp.where(first_core, high, low), "section", swap)
        halves.append((jnp.where(first_core, low, got), jnp.where(first_core, got, high)))
    def gathered(halves):
        return [lax.all_gather(half, BOTH, axis=0, tiled=True) for half in halves]

    def with_gains(w_attn, w_mlp):
        return (w_attn[:, split + width :].astype(F32).T, w_attn, w_mlp, width, split, units)

    (attn_zero, attn_one), (mlp_zero, mlp_one) = halves
    attn_zero = jnp.concatenate([attn_zero, attn_one[:, split + width : split + width + 1]], 1)
    attn_zero, mlp_zero = gathered((attn_zero, mlp_zero))
    cot = lax.dynamic_index_in_dim(cotangent, sec, 0, keepdims=False)
    attn_zero, cot = lax.optimization_barrier((attn_zero, cot))
    zero = with_gains(attn_zero, mlp_zero)
    attn_one, mlp_one = gathered((attn_one, mlp_one))

    seg_count = parent.shape[0]
    labels = jnp.arange(seg_count, dtype=jnp.int32)
    parent_hot = (parent[:, None] == labels[None, :]).astype(F32)
    ancestry = jnp.eye(seg_count, dtype=F32) + parent_hot + jnp.dot(parent_hot, parent_hot)
    ancestry = (ancestry > 0.5).astype(F32)
    row_start = data * rows
    seg_rows = lax.dynamic_slice_in_dim(segments, row_start, rows, 0)
    pos_rows = lax.dynamic_slice_in_dim(places, row_start, rows, 0)
    key_hot = (segments[:, None] == labels[None, :]).astype(F32)
    query_hot = (labels[:, None] == seg_rows[None, :]).astype(F32)
    reach = jnp.dot(key_hot, jnp.dot(ancestry.T, query_hot))
    allowed = (reach > 0.5) & (places[:, None] <= pos_rows[None, :])
    bias_t = jnp.where(allowed, 0.0, MASKED).astype(BF)
    frequency = THETA ** (-(jnp.arange(HALF, dtype=F32) * 2.0 / HEAD))
    angles = frequency[:, None] * pos_rows.astype(F32)[None, :]
    cos_t, sin_t = jnp.cos(angles), jnp.sin(angles)
    ones = jnp.ones((rows, HEAD), F32)
    cos_rows = jnp.concatenate([cos_t.T, cos_t.T, ones], 1)
    sin_rows = jnp.concatenate([sin_t.T, -sin_t.T, 0 * ones], 1)
    tables = (row_start.astype(jnp.int32).reshape(1), bias_t, cos_t, sin_t, cos_rows, sin_rows)

    split_out, split_down = split, 2 * units
    wide, narrow = (F32, BF), (BF, BF)
    back = (F32, BF, F32)

    normed_zero = (hidden * lax.rsqrt(jnp.mean(hidden * hidden, -1, keepdims=True) + EPSILON) * zero[0][:1]).astype(BF)
    kept_zero, o_zero = layer_attention(normed_zero, zero, tables)
    middle_zero, r_zero = product_sum(
        (o_zero, tree, zero[0]), ((0,), split_out, ("add", (1, (2, 1))), wide), zero[1], stagger=True, key=1
    )
    gate_zero, up_zero, inner_zero = layer_units(r_zero, zero)
    out_zero, normed_one = product_sum(
        (inner_zero, middle_zero, zero[0]), ((0,), split_down, ("add", (1, (2, 2))), narrow), zero[2], key=5
    )

    out_zero, normed_one, attn_one = lax.optimization_barrier((out_zero, normed_one, attn_one))
    one = with_gains(attn_one, mlp_one)
    kept_one, o_one = layer_attention(normed_one, one, tables)
    middle_one, r_one = product_sum(
        (o_one, out_zero, one[0]), ((0,), split_out, ("add", (1, (2, 1))), wide), one[1], key=2
    )
    gate_one, up_one, inner_one = layer_units(r_one, one)
    branch = cot
    d_gate, d_up = units_backward(branch, one, gate_one, up_one)
    out_one, d_mlp_one = product_sum(
        (inner_one, middle_one, r_one, branch, d_gate, d_up), ((0,), split_down, ("add", (1,)), (BF,)),
        one[2], ((2, (4, 5)), (3, (0,))), key=6,
    )
    d_gate, out_one = lax.optimization_barrier((d_gate, out_one))
    grad_middle, grad_attn, d_gain_mlp_one = product_sum(
        ((d_gate, d_up), middle_one, branch, one[0]), ((0,), 0, ("back", (1, 2, (3, 1))), back), one[2], key=8
    )
    g_mlp_one = reduce_gradient(d_mlp_one)
    dq, dkv = attention_backward(grad_attn, one, tables, kept_one)
    grad_one, branch, d_gain_attn_one, d_attn_one = product_sum(
        ((dq, dkv), out_zero, grad_middle, one[0], normed_one, grad_attn, o_one),
        ((0,), 0, ("back", (1, 2, (3, 0))), back),
        one[1], ((4, (0,)), (5, (6,))), stagger=True, key=7,
    )
    g_attn_one = reduce_gradient(d_attn_one)

    d_gate, d_up = units_backward(branch, zero, gate_zero, up_zero)
    grad_middle, grad_attn, d_gain_mlp_zero, d_mlp_zero = product_sum(
        ((d_gate, d_up), inner_zero, middle_zero, branch, r_zero, zero[0]),
        ((0,), 0, ("back", (2, 3, (5, 1))), back),
        zero[2], ((4, (0,)), (3, (1,))), key=9,
    )
    g_mlp_zero = reduce_gradient(d_mlp_zero)
    grad_attn, g_mlp_one = lax.optimization_barrier((grad_attn, g_mlp_one))
    dq, dkv = attention_backward(grad_attn, zero, tables, kept_zero)
    dq, g_attn_one = lax.optimization_barrier((dq, g_attn_one))
    grad_zero, send_zero, d_gain_attn_zero, d_attn_zero = product_sum(
        ((dq, dkv), tree, grad_middle, zero[0], normed_zero, grad_attn, o_zero),
        ((0,), 0, ("back", (1, 2, (3, 0))), back),
        zero[1], ((4, (0,)), (5, (6,))), key=11,
    )
    d_gain_attn_zero, d_gain_mlp_zero, d_gain_attn_one, d_gain_mlp_one = [
        jnp.sum(x, 0) for x in (d_gain_attn_zero, d_gain_mlp_zero, d_gain_attn_one, d_gain_mlp_one)
    ]
    d_gains = jnp.stack([d_gain_attn_zero, d_gain_mlp_zero, d_gain_attn_one, d_gain_mlp_one])
    d_gains = d_gains.reshape(2, 2, devices, -1).swapaxes(1, 2).reshape(2, devices, -1, 128)

    ending = finish if devices == 4 else finish_apart
    g_attn_zero, g_gain, got_out, got_in, got_mlp, got_attn = ending(
        d_attn_zero, d_gains, out_zero, out_one, send_zero, branch,
        g_mlp_one, g_attn_one,
    )

    layer_output, input_grad, *grads = write_results(
        (out_zero, out_one, got_out), (grad_zero, grad_one, got_in), (g_attn_zero, g_attn_one, got_attn), width, span
    )
    input_grad, g_mlp_zero = lax.optimization_barrier((input_grad, g_mlp_zero))
    grads += write_mlp(
        g_mlp_zero, g_mlp_one, lax.ppermute(g_mlp_zero, "section", [(1, 0)]), got_mlp, units
    )
    g_query, g_key, g_value, g_out, g_gate, g_up, g_down = [grad[None] for grad in grads]
    g_gain = g_gain.reshape(2, 1, -1)
    return (
        layer_output[None], input_grad[None], g_gain[0], g_query, g_key, g_value, g_out, g_gain[1], g_gate, g_up, g_down,
    )


def solution(mesh):
    in_specs = (
        P(None, "dp", None),
        P(None, "dp", None),
        P(),
        P(),
        P(),
        P("section", "dp"),
        P("section", "dp", "tensor"),
        P("section", "dp", "tensor"),
        P("section", "dp", "tensor"),
        P("section", "tensor", "dp"),
        P("section", "dp"),
        P("section", "dp", "tensor"),
        P("section", "dp", "tensor"),
        P("section", "tensor", "dp"),
    )
    out_specs = (
        P("section", None, "dp", None),
        P("section", None, "dp", None),
        P("section", "dp"),
        P("section", "dp", "tensor"),
        P("section", "dp", "tensor"),
        P("section", "dp", "tensor"),
        P("section", "tensor", "dp"),
        P("section", "dp"),
        P("section", "dp", "tensor"),
        P("section", "dp", "tensor"),
        P("section", "tensor", "dp"),
    )
    return jax.shard_map(shards, mesh=mesh, in_specs=in_specs, out_specs=out_specs, check_vma=False)
```

```python
import functools

import jax
import jax.numpy as jnp
from jax import lax
from jax.experimental import pallas as pl
from jax.experimental.pallas import tpu as pltpu
from jax.sharding import PartitionSpec as P

HEAD = 64
HALF = HEAD // 2
TRUNK = 1024
GROUP = 384
EPSILON = 1e-05
THETA = 10000.0
MASKED = -1e30
BF = jnp.bfloat16
F32 = jnp.float32
MESH = pl.DeviceIdType.MESH
BOTH = ("dp", "section")


def dot_f32(a, b, ca, cb):
    return lax.dot_general(a, b, (((ca,), (cb,)), ((), ())), preferred_element_type=F32)


BLOCK = 256
PIECE = 128
NO_COST = pl.CostEstimate(flops=1, transcendentals=0, bytes_accessed=1)


def columns_of(i):
    return pl.ds(pl.multiple_of(i * PIECE, PIECE), PIECE)


def gain_row(arrays, place, at):
    return arrays[place[0]][place[1] : place[1] + 1, at]


def row_scale(squares, model):
    return lax.rsqrt(jnp.sum(squares, 1, keepdims=True) * (1.0 / model) + EPSILON)


def before_sum(job, arrays, keep):
    kind, places = job[2]
    if kind == "back":
        value = arrays[places[0]]
        model = value.shape[1]
        squares = jnp.zeros(keep.shape, F32)
        for i in range(model // PIECE):
            x = value[:, i * PIECE : (i + 1) * PIECE].astype(F32)
            squares += x * x
        keep[...] = jnp.broadcast_to(row_scale(squares, model), keep.shape)


def with_piece(job, i, total, arrays, outs, keep, sums):
    kind, places = job[2]
    at = columns_of(i)
    if kind == "add":
        y = (arrays[places[0]][:, at].astype(F32) + total).astype(outs[0].dtype)
        outs[0][:, at] = y
        if len(outs) > 1:
            sums[...] += y.astype(F32) * y.astype(F32)
    if kind == "back":
        product = total * arrays[places[0]][:, at].astype(F32) * keep[...]
        sums[...] += product * gain_row(arrays, places[2], at)
        outs[2][:, at] = jnp.sum(product.reshape(-1, 8, PIECE), 0)


def after_sum(job, rows, total, arrays, outs, keep, sums):
    kind, places = job[2]
    model = arrays[places[0]].shape[1]
    at = lambda i: slice(i * PIECE, (i + 1) * PIECE)
    if kind == "add" and len(outs) > 1:
        scale = row_scale(sums[rows], model)
        for i in range(model // PIECE):
            y = outs[0][rows, at(i)].astype(F32)
            outs[1][rows, at(i)] = (y * scale * gain_row(arrays, places[1], at(i))).astype(BF)
    if kind == "back":
        mean = jnp.sum(sums[rows], 1, keepdims=True) * (1.0 / model)
        scale = keep[rows]
        for i in range(model // PIECE):
            unit = arrays[places[0]][rows, at(i)].astype(F32) * scale
            grad = total(i)[rows].astype(F32) * gain_row(arrays, places[2], at(i))
            out = arrays[places[1]][rows, at(i)].astype(F32) + scale * (grad - unit * mean)
            outs[0][rows, at(i)] = out
            outs[1][rows, at(i)] = out.astype(BF)


def product_sum_kernel(cfg, *refs):
    n_join, n_arrays, job, sides, stagger, extra = cfg
    xs, first_column = job[:2]
    refs = list(refs)
    take = lambda n: [refs.pop(0) for _ in range(n)]
    joined = take(n_join)
    from_hbm = [None, *take(n_arrays - 1)]
    (w_hbm,) = take(1)
    extra_in = take(extra[0]) if extra else []
    outs_hbm = take(len(job[3]))
    (g_hbm,) = take(1) if sides else (None,)
    extra_out = take(extra[1]) if extra else []
    arrays = take(n_arrays)
    outs = take(len(job[3]))
    load_sem, out_sem, w_buf, p_buf, a_buf, b_buf, w_sem, sa, ra, sb, rb, sc, rc, turn, keep, sums = take(16)
    g_buf, g_sem = take(2) if sides else (None, None)
    begin, peers, steps, end = extra[2](extra_in, extra_out, refs) if extra else (None, [], [], None)
    per_block = BLOCK // PIECE
    pieces = p_buf.shape[0]
    blocks = pieces // per_block
    n_rows = p_buf.shape[1]
    early = len(xs)
    lag = 2
    assert xs[0] == 0

    t = lax.axis_index("tensor")
    sec = lax.axis_index("section")
    dat = lax.axis_index("dp")
    inner = (t == 1) | (t == 2)
    outer = jnp.logical_not(inner)
    pair = (sec, t + 1 - 2 * lax.rem(t, 2), dat)
    mid = (sec, 3 - t, dat)
    mate = (1 - sec, t, dat)

    def columns(j):
        return pl.ds(pl.multiple_of(j * BLOCK, BLOCK), BLOCK)

    def to_inner(i):
        return pltpu.make_async_remote_copy(
            p_buf.at[i], a_buf.at[i], sa.at[i], ra.at[i], device_id=pair, device_id_type=MESH
        )

    def across(i):
        return pltpu.make_async_remote_copy(
            p_buf.at[i], b_buf.at[i], sb.at[i], rb.at[i], device_id=mid, device_id_type=MESH
        )

    def to_outer(i):
        return pltpu.make_async_remote_copy(
            b_buf.at[i], b_buf.at[i], sc.at[i], rc.at[i], device_id=pair, device_id_type=MESH
        )

    def load(k):
        return pltpu.make_async_copy(from_hbm[k], arrays[k], load_sem.at[k])

    def join():
        copies, start = [], 0
        for m, src in enumerate(joined):
            at = pl.ds(start, src.shape[1])
            copies.append(pltpu.make_async_copy(src, arrays[0].at[:, at], load_sem.at[n_arrays + m]))
            start += src.shape[1]
        return copies

    def fetch(j, slot):
        return pltpu.make_async_copy(
            w_hbm.at[columns(j), pl.ds(first_column, w_buf.shape[2])], w_buf.at[slot], w_sem.at[slot]
        )

    def flush(j, slot):
        return pltpu.make_async_copy(g_buf.at[slot], g_hbm.at[columns(j), :], g_sem.at[slot])

    def every_piece(body):
        def turn_of(i, _):
            body(i)
            return 0

        lax.fori_loop(0, pieces, turn_of, 0)

    for copy in join():
        copy.start()
    for k in range(1, early):
        load(k).start()
    fetch(0, 0).start()
    for k in range(early, n_arrays):
        load(k).start()
    if extra:
        begin()
    barrier = pltpu.get_barrier_semaphore()
    for device in [pair, *peers]:
        pl.semaphore_signal(barrier, inc=1, device_id=device, device_id_type=MESH)
    sums[...] = jnp.zeros_like(sums)

    @pl.when(inner)
    def _():
        pl.semaphore_signal(barrier, inc=1, device_id=mid, device_id_type=MESH)
        pl.semaphore_wait(barrier, 2 + len(peers))

    @pl.when(outer)
    def _():
        if stagger:
            pl.semaphore_signal(barrier, inc=1, device_id=mate, device_id_type=MESH)
            pl.semaphore_wait(barrier, 2)

            @pl.when(sec == 1)
            def _():
                pl.semaphore_wait(turn, 1)

        else:
            pl.semaphore_wait(barrier, 1 + len(peers))

    for copy in join():
        copy.wait()
    for k in range(1, early):
        load(k).wait()

    def done(i):
        with_piece(job, i, b_buf[i].astype(F32), arrays, outs, keep, sums)

    def first(i):
        to_inner(i).wait_recv()
        p_buf[i] = p_buf[i] + a_buf[i]
        across(i).start()

    def second(i):
        across(i).wait_recv()
        b_buf[i] = p_buf[i] + b_buf[i]
        to_outer(i).start()
        done(i)

    def side(j):
        slot = lax.rem(j, 2)

        @pl.when(j >= 2)
        def _():
            flush(j - 2, slot).wait()

        start = 0
        for a, bs in sides:
            a_t = arrays[a][:, columns(j)].T
            for b in bs:
                width = arrays[b].shape[1]
                g_buf[slot, :, start : start + width] = jnp.dot(
                    a_t, arrays[b][...], preferred_element_type=F32
                ).astype(BF)
                start += width
        flush(j, slot).start()
        return 0

    def step(j, _):
        slot = lax.rem(j, 2)
        fetch(j, slot).wait()

        @pl.when(j + 1 < blocks)
        def _():
            fetch(j + 1, 1 - slot).start()

        total, start = None, 0
        for x in xs:
            width = arrays[x].shape[1]
            term = dot_f32(arrays[x][...], w_buf[slot, :, start : start + width], 1, 1)
            total = term if total is None else total + term
            start += width
        total = total.astype(BF)
        for u in range(per_block):
            p_buf[per_block * j + u] = total[:, u * PIECE : (u + 1) * PIECE]

        @pl.when(outer)
        def _():
            for u in range(per_block):
                to_inner(per_block * j + u).start()

        @pl.when(j == 1)
        def _():
            for k in range(early, n_arrays):
                load(k).wait()
            before_sum(job, arrays, keep)

        if sides:

            @pl.when(j >= lag)
            def _():
                side(j - lag)

        @pl.when(inner)
        def _():
            for u in range(per_block):
                i = per_block * j + u
                first(i)

                @pl.when(j >= 1)
                def _():
                    second(i - per_block)

        for at, body in steps:
            pl.when(j == at)(body)

        return 0

    lax.fori_loop(0, blocks, step, 0)

    @pl.when(inner)
    def _():
        for u in range(per_block):
            second(pieces - per_block + u)

    if stagger:

        @pl.when(outer)
        def _():
            every_piece(lambda i: to_inner(i).wait_send())

            @pl.when(sec == 0)
            def _():
                pl.semaphore_signal(turn, inc=1, device_id=mate, device_id_type=MESH)

    if sides:
        lax.fori_loop(blocks - lag, blocks, lambda j, _: side(j), 0)

    @pl.when(outer)
    def _():
        if not stagger:
            every_piece(lambda i: to_inner(i).wait_send())

        def arrive(i):
            to_outer(i).wait_recv()
            done(i)

        every_piece(arrive)

    if extra:
        end(outs[0])
    chunks = 5 if n_rows % (5 * 32) == 0 else 1
    chunk = n_rows // chunks
    block = 32 if chunk % 32 == 0 else 16
    height = lambda m: 8 if job[2][0] == "back" and m == 2 else n_rows
    stores = []

    def store(m, rows):
        copy = pltpu.make_async_copy(outs[m].at[rows], outs_hbm[m].at[rows], out_sem.at[len(stores)])
        copy.start()
        stores.append(copy)

    for c in range(chunks):

        def turn_rows(r, _):
            rows = pl.ds(pl.multiple_of(c * chunk + r * block, block), block)
            after_sum(job, rows, lambda i: b_buf.at[i], arrays, outs, keep, sums)
            return 0

        if job[2][0] == "back" or len(outs) > 1:
            lax.fori_loop(0, chunk // block, turn_rows, 0)
        for m in range(len(outs)):
            if height(m) == n_rows:
                store(m, pl.ds(c * chunk, chunk))
    for m in range(len(outs)):
        if height(m) != n_rows:
            store(m, pl.ds(0, height(m)))

    @pl.when(inner)
    def _():
        def sent(i):
            across(i).wait_send()
            to_outer(i).wait_send()

        every_piece(sent)

    if sides:
        flush(blocks - 2, (blocks - 2) % 2).wait()
        flush(blocks - 1, (blocks - 1) % 2).wait()
    for copy in stores:
        copy.wait()


def product_sum(arrays, job, weights, sides=(), stagger=False, key=1, extra=None):
    assert lax.axis_size("tensor") == 4
    first = arrays[0] if isinstance(arrays[0], tuple) else (arrays[0],)
    given = (*first, *arrays[1:])
    rows, model = first[0].shape[0], weights.shape[0]
    arrays = (jax.ShapeDtypeStruct((rows, sum(x.shape[1] for x in first)), BF), *arrays[1:])
    pieces = model // PIECE
    depth = sum(arrays[x].shape[1] for x in job[0])
    anywhere = pl.BlockSpec(memory_space=pl.ANY)
    buf = pltpu.VMEM((pieces, rows, PIECE), BF)
    sem = pltpu.SemaphoreType.DMA((pieces,))
    two = pltpu.SemaphoreType.DMA((2,))
    out_shape = []
    for m, dtype in enumerate(job[3]):
        height = 8 if job[2][0] == "back" and m == 2 else rows
        out_shape.append(jax.ShapeDtypeStruct((height, model), dtype))
    scratch = [pltpu.VMEM(x.shape, x.dtype) for x in (*arrays, *out_shape)]
    scratch += [pltpu.SemaphoreType.DMA((len(arrays) + len(first),)), pltpu.SemaphoreType.DMA((16,))]
    scratch += [pltpu.VMEM((2, BLOCK, depth), BF), buf, buf, buf, two, *[sem] * 6, pltpu.SemaphoreType.REGULAR]
    scratch += [pltpu.VMEM((rows, PIECE), F32)] * 2
    if sides:
        side_width = sum(arrays[b].shape[1] for _, bs in sides for b in bs)
        out_shape.append(jax.ShapeDtypeStruct((model, side_width), BF))
        scratch += [pltpu.VMEM((2, BLOCK, side_width), BF), two]
    more, plan = (), None
    if extra:
        more, shapes, buffers, steps = extra
        out_shape += shapes
        scratch += buffers
        plan = (len(more), len(shapes), steps)
    out = pl.pallas_call(
        functools.partial(product_sum_kernel, (len(first), len(arrays), job, tuple(sides), stagger, plan)),
        out_shape=out_shape,
        in_specs=[anywhere] * (len(given) + 1 + len(more)),
        out_specs=[anywhere] * len(out_shape),
        scratch_shapes=scratch,
        compiler_params=pltpu.CompilerParams(
            collective_id=key, has_side_effects=True, vmem_limit_bytes=62 << 20
        ),
        cost_estimate=NO_COST,
        name=f"product_sum_{key}",
    )(*given, weights, *more)
    return out if len(out) > 1 else out[0]


def dp_peers(count):
    me = lax.axis_index("dp")
    sec, t = lax.axis_index("section"), lax.axis_index("tensor")
    others = [lax.rem(me + k, count) for k in range(1, count)]
    return me, others, [(sec, t, other) for other in others]


def greet(ids):
    barrier = pltpu.get_barrier_semaphore()
    for device in ids:
        pl.semaphore_signal(barrier, inc=1, device_id=device, device_id_type=MESH)
    pl.semaphore_wait(barrier, len(ids))


def turn_rows(x, cos_ref, sin_ref):
    lane = lax.broadcasted_iota(jnp.int32, x.shape, 1)
    width = x.shape[1]
    partner = jnp.where(lane < HALF, pltpu.roll(x, width - HALF, 1), pltpu.roll(x, HALF, 1))
    return x * cos_ref[...] + partner * sin_ref[...]


def gather_kernel(count, raw_ref, cos_ref, sin_ref, o_ref, t_ref, x_ref, send, recv):
    me, _, ids = dp_peers(count)
    x_ref[...] = turn_rows(raw_ref[...], cos_ref, sin_ref).astype(BF)
    greet(ids)
    copies = [
        pltpu.make_async_remote_copy(
            x_ref, o_ref.at[me], send.at[k], recv.at[k], device_id=device, device_id_type=MESH
        )
        for k, device in enumerate(ids)
    ]
    for copy in copies:
        copy.start()
    o_ref[me] = x_ref[...]
    for copy in copies:
        copy.wait()
    t_ref[...] = o_ref[...].reshape(t_ref.shape[1], t_ref.shape[0]).T


def scatter_kernel(count, x_ref, cos_ref, sin_ref, o_ref, buf, send, recv):
    me, others, ids = dp_peers(count)
    greet(ids)
    copies = [
        pltpu.make_async_remote_copy(
            x_ref.at[others[k]], buf.at[k], send.at[k], recv.at[k], device_id=device, device_id_type=MESH
        )
        for k, device in enumerate(ids)
    ]
    for copy in copies:
        copy.start()
    total = x_ref[me].astype(F32)
    for k, copy in enumerate(copies):
        copy.wait()
        total = total + buf[k].astype(F32)
    o_ref[...] = turn_rows(total, cos_ref, sin_ref).astype(BF)


def gather_rows(raw, cos_rows, sin_rows):
    count = lax.axis_size("dp")
    rows, width = raw.shape
    in_vmem = pl.BlockSpec(memory_space=pltpu.VMEM)
    sem = pltpu.SemaphoreType.DMA((count - 1,))
    out, out_t = pl.pallas_call(
        functools.partial(gather_kernel, count),
        out_shape=(
            jax.ShapeDtypeStruct((count, rows, width), BF),
            jax.ShapeDtypeStruct((width, count * rows), BF),
        ),
        in_specs=[in_vmem] * 3,
        out_specs=(in_vmem, in_vmem),
        scratch_shapes=[pltpu.VMEM((rows, width), BF), sem, sem],
        compiler_params=pltpu.CompilerParams(collective_id=3, has_side_effects=True),
        cost_estimate=NO_COST,
        name="gather_rows",
    )(raw, cos_rows, sin_rows)
    return out.reshape(-1, width), out_t


def scatter_rows(x, cos_rows, sin_rows):
    count = lax.axis_size("dp")
    rows, width = x.shape[0] // count, x.shape[1]
    in_vmem = pl.BlockSpec(memory_space=pltpu.VMEM)
    sem = pltpu.SemaphoreType.DMA((count - 1,))
    return pl.pallas_call(
        functools.partial(scatter_kernel, count),
        out_shape=jax.ShapeDtypeStruct((rows, width), BF),
        in_specs=[in_vmem] * 3,
        out_specs=in_vmem,
        scratch_shapes=[pltpu.VMEM((count - 1, rows, width), x.dtype), sem, sem],
        compiler_params=pltpu.CompilerParams(collective_id=4, has_side_effects=True),
        cost_estimate=NO_COST,
        name="scatter_rows",
    )(x.reshape(count, rows, width), cos_rows, sin_rows)


def finish_steps(ins, outs, scratch):
    g_hbm, gain_hbm, out_zero, in_zero, in_one, mlp_one, attn_one = ins
    o_hbm, gain_out, got_out, got_in, got_mlp, got_attn = outs
    (
        mine, away, got, xs, ys, xr, yr, o_buf, gain, gains, gain_sum,
        load_sem, store_sem, send, recv, mate_send, mate_recv, gain_send, gain_recv,
    ) = scratch
    sec, t, dat = lax.axis_index("section"), lax.axis_index("tensor"), lax.axis_index("dp")
    flip_x = dat + 1 - 2 * lax.rem(dat, 2)
    flip_y = lax.rem(dat + 2, 4)
    across = lax.rem(flip_x + 2, 4)
    by_x, by_y, mate = (sec, t, flip_x), (sec, t, flip_y), (1 - sec, t, dat)
    peers = [
        mate, by_x, by_y, (sec, t, across),
        (1 - sec, t, flip_x), (1 - sec, t, flip_y), (1 - sec, t, across),
    ]
    rows = g_hbm.shape[1] // 2
    upper, lower = pl.ds(0, rows), pl.ds(rows, rows)
    order = (across, flip_x, flip_y, dat)
    load_away = lambda k: pltpu.make_async_copy(g_hbm.at[2 * order[k] + 1 - sec], away.at[k], load_sem.at[k])
    load_mine = lambda k: pltpu.make_async_copy(g_hbm.at[2 * order[k] + sec], mine.at[k], load_sem.at[4 + k])
    load_gain = lambda: pltpu.make_async_copy(gain_hbm, gain, load_sem.at[8])
    store_o = lambda: pltpu.make_async_copy(o_buf, o_hbm, store_sem.at[0])
    store_gain = lambda: pltpu.make_async_copy(gain_sum, gain_out, store_sem.at[1])

    def remote(src, dst, k, device):
        return pltpu.make_async_remote_copy(
            src, dst, send.at[k], recv.at[k], device_id=device, device_id_type=MESH
        )

    def to_mate(src, dst, k):
        return pltpu.make_async_remote_copy(
            src, dst, mate_send.at[k], mate_recv.at[k], device_id=mate, device_id_type=MESH
        )

    def share(k):
        return pltpu.make_async_remote_copy(
            gain.at[peers[k][0], peers[k][2]], gains.at[k], gain_send.at[k], gain_recv.at[k],
            device_id=peers[k], device_id_type=MESH,
        )

    swap = lambda k: remote(away.at[k], got.at[k], k, mate)
    hops = (
        lambda: remote(mine.at[0, upper], xs.at[0], 4, by_x),
        lambda: remote(mine.at[0, lower], ys.at[0], 5, by_y),
        lambda: remote(mine.at[1, upper], xs.at[1], 6, by_x),
        lambda: remote(mine.at[2, lower], ys.at[1], 7, by_y),
        lambda: remote(mine.at[2, upper], yr, 8, by_y),
        lambda: remote(mine.at[1, lower], xr, 9, by_x),
    )

    def begin():
        for k in range(4):
            load_away(k).start()
        for k in range(4):
            load_mine(k).start()
        load_gain().start()

    def exchange():
        for k in range(4):
            load_away(k).wait()
            swap(k).start()
        load_gain().wait()
        for k in range(7):
            share(k).start()

    def add(k):
        load_mine(k).wait()
        swap(k).wait_recv()
        mine[k] = mine[k] + got[k]

    def first_hops():
        add(0)
        hops[0]().start()
        hops[1]().start()
        add(1)
        hops[2]().start()

    def more_hops():
        add(2)
        hops[3]().start()
        add(3)

    def swap_results():
        @pl.when(sec == 0)
        def _():
            to_mate(in_one, got_in, 0).start()
            to_mate(mlp_one, got_mlp, 2).start()
            to_mate(attn_one, got_attn, 3).start()

        @pl.when(sec == 1)
        def _():
            to_mate(in_zero, got_in, 0).start()
            to_mate(out_zero, got_out, 1).start()

    def second_hops():
        hops[0]().wait_recv()
        mine[2, upper] = mine[2, upper] + xs[0]
        hops[4]().start()
        hops[1]().wait_recv()
        mine[1, lower] = mine[1, lower] + ys[0]
        hops[5]().start()

    def gain_sums():
        total = gain[sec, dat]
        for k in range(7):
            share(k).wait()
            total = total + gains[k]
        gain_sum[...] = total
        store_gain().start()

    def last_adds():
        for k in (2, 3, 4, 5):
            hops[k]().wait_recv()
        o_buf[upper] = (mine[3, upper].astype(F32) + xs[1].astype(F32) + yr[...].astype(F32)).astype(BF)
        o_buf[lower] = (mine[3, lower].astype(F32) + ys[1].astype(F32) + xr[...].astype(F32)).astype(BF)
        store_o().start()

        @pl.when(sec == 1)
        def _():
            to_mate(o_buf, got_attn, 3).start()

    def end(out_one):
        @pl.when(sec == 0)
        def _():
            to_mate(out_one, got_out, 1).start()

        for k in range(4):
            swap(k).wait_send()
        for hop in hops:
            hop().wait_send()
        store_o().wait()
        store_gain().wait()
        to_mate(in_one, got_in, 0).wait()
        to_mate(out_one, got_out, 1).wait()
        to_mate(attn_one, got_attn, 3).wait()

        @pl.when(sec == 0)
        def _():
            to_mate(mlp_one, got_mlp, 2).wait_send()

        @pl.when(sec == 1)
        def _():
            to_mate(mlp_one, got_mlp, 2).wait_recv()

    steps = [
        (0, exchange), (1, first_hops), (2, more_hops), (3, swap_results), (4, second_hops), (5, gain_sums),
        (6, last_adds),
    ]
    return begin, peers, steps, end


def finishing(g, gains, out_zero, in_zero, in_one, mlp_one, attn_one):
    rows, width = g.shape[0] // 8, g.shape[1]
    part = pltpu.VMEM((2, rows // 2, width), BF)
    whole = pltpu.VMEM((4, rows, width), BF)
    end = pltpu.VMEM((rows // 2, width), BF)
    like = lambda x: jax.ShapeDtypeStruct(x.shape, x.dtype)
    dma = lambda n: pltpu.SemaphoreType.DMA((n,))
    shape = gains.shape[2:]
    return (
        (g.reshape(8, rows, width), gains, out_zero, in_zero, in_one, mlp_one, attn_one),
        [
            jax.ShapeDtypeStruct((rows, width), BF), jax.ShapeDtypeStruct(shape, F32),
            like(out_zero), like(in_zero), like(mlp_one), like(attn_one),
        ],
        [
            whole, whole, whole, part, part, end, end, pltpu.VMEM((rows, width), BF),
            pltpu.VMEM(gains.shape, F32), pltpu.VMEM((7, *shape), F32), pltpu.VMEM(shape, F32),
            dma(9), dma(2), dma(10), dma(10), dma(4), dma(4), dma(7), dma(7),
        ],
        finish_steps,
    )


def finish_apart(g, gains, out_zero, out_one, in_zero, in_one, mlp_one, attn_one):
    first_core = lax.axis_index("section") == 0
    half = reduce_gradient(g)
    swap = lambda zero, one: lax.ppermute(jnp.where(first_core, one, zero), "section", [(0, 1), (1, 0)])
    return (
        half, share_sums(gains), swap(out_zero, out_one), swap(in_zero, in_one),
        lax.ppermute(mlp_one, "section", [(0, 1)]), swap(half, attn_one),
    )


def in_rows(count, block, body):
    def turn(r, _):
        body(pl.ds(pl.multiple_of(r * block, block), block))
        return 0

    lax.fori_loop(0, count // block, turn, 0)


def widen_turned(dst, src, start, width):
    for c in range(0, width, 128):
        dst[c : c + 128] = src[:, start + c : start + c + 128].astype(F32).T


def write_mlp_kernel(
    zero, one, from_one, from_zero, gate_hbm, up_hbm, down_hbm, mlp, gate_buf, up_buf, down_buf, load_sem, store_sem
):
    sec = lax.axis_index("section")
    half, units = zero.shape[0], gate_buf.shape[1]
    low, high = pl.ds(0, half), pl.ds(half, half)
    load = lambda src, at, k: pltpu.make_async_copy(src, mlp.at[at], load_sem.at[k])
    store = lambda src, dst, k: pltpu.make_async_copy(src, dst, store_sem.at[k])

    @pl.when(sec == 0)
    def _():
        load(zero, low, 0).start()
        load(from_one, high, 1).start()

    @pl.when(sec == 1)
    def _():
        load(from_zero, low, 0).start()
        load(one, high, 1).start()

    load(zero, low, 0).wait()
    load(zero, high, 1).wait()

    def gates(rows):
        gate_buf[rows] = mlp[rows, :units].astype(F32)
        up_buf[rows] = mlp[rows, units : 2 * units].astype(F32)

    in_rows(2 * half, 32, gates)
    stores = [store(gate_buf, gate_hbm, 0), store(up_buf, up_hbm, 1), store(down_buf, down_hbm, 2)]
    stores[0].start()
    stores[1].start()
    widen_turned(down_buf, mlp, 2 * units, units)
    stores[2].start()
    for copy in stores:
        copy.wait()


def write_mlp(zero, one, from_one, from_zero, units):
    shard = 2 * zero.shape[0]
    anywhere = pl.BlockSpec(memory_space=pl.ANY)
    shapes = [(shard, units), (shard, units), (units, shard)]
    return pl.pallas_call(
        write_mlp_kernel,
        out_shape=[jax.ShapeDtypeStruct(shape, F32) for shape in shapes],
        in_specs=[anywhere] * 4,
        out_specs=[anywhere] * 3,
        scratch_shapes=[
            pltpu.VMEM((shard, zero.shape[1]), BF),
            *[pltpu.VMEM(shape, F32) for shape in shapes],
            pltpu.SemaphoreType.DMA((2,)),
            pltpu.SemaphoreType.DMA((3,)),
        ],
        compiler_params=pltpu.CompilerParams(vmem_limit_bytes=62 << 20),
        cost_estimate=NO_COST,
        name="write_mlp",
    )(zero, one, from_one, from_zero)


def write_kernel(
    split, out_zero, out_one, got_out, in_zero, in_one, got_in, attn_zero, attn_one, got_attn,
    out_hbm, in_hbm, q_hbm, k_hbm, v_hbm, o_hbm,
    outs, wides, attn, narrow, q_buf, k_buf, v_buf, o_buf, load_sem, store_sem,
):
    sec = lax.axis_index("section")
    half = attn_zero.shape[0]
    low, high = pl.ds(0, half), pl.ds(half, half)
    load = lambda src, dst, k: pltpu.make_async_copy(src, dst, load_sem.at[k])
    store = lambda src, dst, k: pltpu.make_async_copy(src, dst, store_sem.at[k])

    def start(own_out, own_in, attn_low, attn_high):
        load(own_out, outs.at[0], 0).start()
        load(own_in, wides.at[0], 1).start()
        load(attn_low, attn.at[low], 2).start()
        load(attn_high, attn.at[high], 3).start()

    @pl.when(sec == 0)
    def _():
        start(out_zero, in_zero, attn_zero, got_attn)

    @pl.when(sec == 1)
    def _():
        start(out_one, in_one, got_attn, attn_one)

    load(got_in, narrow, 4).start()
    load(got_out, outs.at[1], 5).start()
    stores = [
        store(outs.at[0], out_hbm.at[sec], 0),
        store(wides.at[0], in_hbm.at[sec], 1),
        store(outs.at[1], out_hbm.at[1 - sec], 2),
        store(wides.at[1], in_hbm.at[1 - sec], 3),
        store(q_buf, q_hbm, 4),
        store(k_buf, k_hbm, 5),
        store(v_buf, v_hbm, 6),
        store(o_buf, o_hbm, 7),
    ]
    load(out_zero, outs.at[0], 0).wait()
    stores[0].start()
    load(in_zero, wides.at[0], 1).wait()
    stores[1].start()
    width, span = q_buf.shape[1], k_buf.shape[1]
    load(attn_one, attn.at[low], 2).wait()
    load(attn_one, attn.at[high], 3).wait()

    def projections(rows):
        q_buf[rows] = attn[rows, :width].astype(F32)
        k_buf[rows] = attn[rows, width : width + span].astype(F32)
        v_buf[rows] = attn[rows, width + span : split].astype(F32)

    in_rows(2 * half, 32, projections)
    for k in (4, 5, 6):
        stores[k].start()
    widen_turned(o_buf, attn, split, width)
    stores[7].start()
    load(got_in, narrow, 4).wait()

    def widen(rows):
        wides[1, rows] = narrow[rows].astype(F32)

    in_rows(narrow.shape[0], 32, widen)
    stores[3].start()
    load(got_out, outs.at[1], 5).wait()
    stores[2].start()
    for copy in stores:
        copy.wait()


def write_results(results, ins, attns, width, span):
    rows, model = results[0].shape
    shard = 2 * attns[0].shape[0]
    anywhere = pl.BlockSpec(memory_space=pl.ANY)
    shapes = [(shard, width), (shard, span), (shard, span), (width, shard)]
    return pl.pallas_call(
        functools.partial(write_kernel, width + 2 * span),
        out_shape=[
            jax.ShapeDtypeStruct((2, rows, model), BF),
            jax.ShapeDtypeStruct((2, rows, model), F32),
            *[jax.ShapeDtypeStruct(shape, F32) for shape in shapes],
        ],
        in_specs=[anywhere] * 9,
        out_specs=[anywhere] * 6,
        scratch_shapes=[
            pltpu.VMEM((2, rows, model), BF),
            pltpu.VMEM((2, rows, model), F32),
            pltpu.VMEM((shard, attns[0].shape[1]), BF),
            pltpu.VMEM((rows, model), BF),
            *[pltpu.VMEM(shape, F32) for shape in shapes],
            pltpu.SemaphoreType.DMA((6,)),
            pltpu.SemaphoreType.DMA((8,)),
        ],
        compiler_params=pltpu.CompilerParams(vmem_limit_bytes=62 << 20),
        cost_estimate=NO_COST,
        name="write_results",
    )(*results, *ins, *attns)


def share_kernel(count, x_ref, o_ref, buf, send, recv):
    sec, t, dat = lax.axis_index("section"), lax.axis_index("tensor"), lax.axis_index("dp")
    peers = [
        (lax.rem(sec + k // count, 2), t, lax.rem(dat + k % count, count)) for k in range(1, 2 * count)
    ]
    greet(peers)
    copies = [
        pltpu.make_async_remote_copy(
            x_ref.at[peer[0], peer[2]], buf.at[k], send.at[k], recv.at[k], device_id=peer, device_id_type=MESH
        )
        for k, peer in enumerate(peers)
    ]
    for copy in copies:
        copy.start()
    total = x_ref[sec, dat]
    for k, copy in enumerate(copies):
        copy.wait()
        total = total + buf[k]
    o_ref[...] = total


def share_sums(x):
    count = lax.axis_size("dp")
    in_vmem = pl.BlockSpec(memory_space=pltpu.VMEM)
    sem = pltpu.SemaphoreType.DMA((2 * count - 1,))
    return pl.pallas_call(
        functools.partial(share_kernel, count),
        out_shape=jax.ShapeDtypeStruct(x.shape[2:], F32),
        in_specs=[in_vmem],
        out_specs=in_vmem,
        scratch_shapes=[pltpu.VMEM((2 * count - 1, *x.shape[2:]), F32), sem, sem],
        compiler_params=pltpu.CompilerParams(collective_id=13, has_side_effects=True),
        cost_estimate=NO_COST,
        name="share_sums",
    )(x)


def group_start(first_row):
    past = lax.max(first_row - TRUNK, 0)
    return pl.multiple_of(TRUNK + GROUP * lax.div(past, GROUP), 128)


def over_windows(tree_len, rows, tile, first_row, run):
    if tile % 128 == 0 and GROUP % tile == 0 and TRUNK % tile == 0 and rows % tile == 0:

        @pl.when(first_row < TRUNK)
        def _():
            run(((pl.ds(0, TRUNK), True),))

        @pl.when(first_row >= TRUNK)
        def _():
            run(((pl.ds(0, TRUNK), False), (pl.ds(group_start(first_row), GROUP), True)))

    else:
        run(((pl.ds(0, tree_len), True),))


def masked(scores, bias_ref, win, step):
    bias = bias_ref[win, :].astype(F32)
    return scores + (bias if step == 1 else jnp.concatenate([bias] * step, axis=1))


def head_rows(ref, head):
    return ref[head * HEAD : (head + 1) * HEAD, :]


def beside(ref, head, count):
    parts = [head_rows(ref, head + k) for k in range(count)]
    return parts[0] if count == 1 else jnp.concatenate(parts, axis=1)


def turned_beside(ref, cos, sin, head, count):
    parts = []
    for k in range(count):
        rows = head_rows(ref, head + k)
        first, second = rows[:HALF], rows[HALF:]
        parts.append(jnp.concatenate([first * cos - second * sin, second * cos + first * sin], axis=0))
    whole = parts[0] if count == 1 else jnp.concatenate(parts, axis=1)
    return (whole.astype(BF).astype(F32) * HEAD**-0.5).astype(BF)


def as_rows(x, tile, count):
    parts = [x[:, k * tile : (k + 1) * tile] for k in range(count)]
    return (parts[0] if count == 1 else jnp.concatenate(parts, axis=0)).T


def over_groups(groups, step, body):
    for group in range(groups):
        body(group, slice(group * step * HEAD, (group + 1) * step * HEAD))


def attend_kernel(
    rows, step, start_ref, q_ref, kv_ref, kvt_ref, bias_ref, cos_ref, sin_ref, o_ref, on_ref, lse_ref
):
    tile = q_ref.shape[1]
    heads = q_ref.shape[0] // HEAD
    first_row = start_ref[0] + pl.program_id(0) * tile

    def body(wins, group, lanes):
        head = group * step
        q = turned_beside(q_ref, cos_ref[...], sin_ref[...], head, step)
        scores = []
        for win, mask in wins:
            score = dot_f32(kv_ref[win, :HEAD], q, 1, 0)
            scores.append(masked(score, bias_ref, win, step) if mask else score)
        top = functools.reduce(jnp.maximum, [jnp.max(s, 0, keepdims=True) for s in scores])
        expo = [jnp.exp(s - top) for s in scores]
        total = sum(jnp.sum(e, 0, keepdims=True) for e in expo)
        out = sum(dot_f32(kvt_ref[HEAD:, win], e.astype(BF), 1, 0) for (win, _), e in zip(wins, expo))
        out = out / total
        on_ref[:, lanes] = as_rows(out, tile, step).astype(BF)
        lse_ref[group, 0] = top + jnp.log(total)
        out = out.astype(BF)
        for k in range(step):
            o_ref[(head + k) * HEAD : (head + k + 1) * HEAD, :] = out[:, k * tile : (k + 1) * tile]

    over_windows(
        kv_ref.shape[0], rows, tile, first_row,
        lambda wins: over_groups(heads // step, step, functools.partial(body, wins)),
    )


def attend_back_kernel(
    rows, step, start_ref, q_ref, do_ref, o_ref, lse_ref, kv_ref, kvt_ref, bias_ref, cos_ref, sin_ref,
    dq_ref, dkv_ref, dk_acc, dv_acc,
):
    tile = q_ref.shape[1]
    heads = q_ref.shape[0] // HEAD
    first_row = start_ref[0] + pl.program_id(0) * tile

    @pl.when(pl.program_id(0) == 0)
    def _():
        dk_acc[...] = jnp.zeros_like(dk_acc)
        dv_acc[...] = jnp.zeros_like(dv_acc)

    def body(wins, group, lanes):
        head = group * step
        cos, sin = cos_ref[...], sin_ref[...]
        q = turned_beside(q_ref, cos, sin, head, step)
        do = beside(do_ref, head, step)
        out = beside(o_ref, head, step)
        lse = lse_ref[group, 0]
        delta = jnp.sum(do.astype(F32) * out.astype(F32), 0, keepdims=True)
        dq = jnp.zeros((HEAD, step * tile), F32)
        for win, mask in wins:
            score = dot_f32(kv_ref[win, :HEAD], q, 1, 0)
            p = jnp.exp((masked(score, bias_ref, win, step) if mask else score) - lse)
            dp = dot_f32(kv_ref[win, HEAD:], do, 1, 0)
            ds = (p * (dp - delta)).astype(BF)
            dk_acc[win, :] += dot_f32(ds, q, 1, 1)
            dv_acc[win, :] += dot_f32(p.astype(BF), do, 1, 1)
            dq = dq + dot_f32(kvt_ref[:HEAD, win], ds, 1, 0)
        dq = dq * HEAD**-0.5
        turned = []
        for k in range(step):
            first = dq[:HALF, k * tile : (k + 1) * tile]
            second = dq[HALF:, k * tile : (k + 1) * tile]
            turned += [first * cos + second * sin, second * cos - first * sin]
        dq_ref[:, lanes] = jnp.concatenate(turned, axis=0).T.astype(BF)

    over_windows(
        kv_ref.shape[0], rows, tile, first_row,
        lambda wins: over_groups(heads // step, step, functools.partial(body, wins)),
    )

    @pl.when(pl.program_id(0) == pl.num_programs(0) - 1)
    def _():
        dkv_ref[...] = jnp.concatenate([dk_acc[...], dv_acc[...]], axis=1).astype(BF)


def row_tile(rows):
    return 128 if rows % 128 == 0 else rows


def attend(start, q_t, kv, kv_t, bias_t, cos_t, sin_t):
    width, rows = q_t.shape
    heads, tree_len, tile = width // HEAD, kv.shape[0], row_tile(rows)
    step = 2 if tile % 128 == 0 and heads % 2 == 0 else 1
    column = lambda i, s: (0, i)
    whole = lambda i, s: (0, 0)
    return pl.pallas_call(
        functools.partial(attend_kernel, rows, step),
        out_shape=(
            jax.ShapeDtypeStruct((width, rows), BF),
            jax.ShapeDtypeStruct((rows, width), BF),
            jax.ShapeDtypeStruct((heads // step, rows // tile, 1, step * tile), F32),
        ),
        grid_spec=pltpu.PrefetchScalarGridSpec(
            num_scalar_prefetch=1,
            grid=(rows // tile,),
            in_specs=[
                pl.BlockSpec((width, tile), column),
                pl.BlockSpec((tree_len, 2 * HEAD), whole),
                pl.BlockSpec((2 * HEAD, tree_len), whole),
                pl.BlockSpec((tree_len, tile), column),
                pl.BlockSpec((HALF, tile), column),
                pl.BlockSpec((HALF, tile), column),
            ],
            out_specs=(
                pl.BlockSpec((width, tile), column),
                pl.BlockSpec((tile, width), lambda i, s: (i, 0)),
                pl.BlockSpec((heads // step, 1, 1, step * tile), lambda i, s: (0, i, 0, 0)),
            ),
        ),
        compiler_params=pltpu.CompilerParams(vmem_limit_bytes=62 << 20),
        cost_estimate=NO_COST,
        name="attend",
    )(start, q_t, kv, kv_t, bias_t, cos_t, sin_t)


def attend_back(start, q_t, do_t, o_t, lse, kv, kv_t, bias_t, cos_t, sin_t):
    width, rows = q_t.shape
    heads, tree_len, tile = width // HEAD, kv.shape[0], row_tile(rows)
    step = 2 if tile % 128 == 0 and heads % 2 == 0 else 1
    column = lambda i, s: (0, i)
    whole = lambda i, s: (0, 0)
    return pl.pallas_call(
        functools.partial(attend_back_kernel, rows, step),
        out_shape=(
            jax.ShapeDtypeStruct((rows, width), BF),
            jax.ShapeDtypeStruct((tree_len, 2 * HEAD), BF),
        ),
        grid_spec=pltpu.PrefetchScalarGridSpec(
            num_scalar_prefetch=1,
            grid=(rows // tile,),
            in_specs=[
                pl.BlockSpec((width, tile), column),
                pl.BlockSpec((width, tile), column),
                pl.BlockSpec((width, tile), column),
                pl.BlockSpec((heads // step, 1, 1, step * tile), lambda i, s: (0, i, 0, 0)),
                pl.BlockSpec((tree_len, 2 * HEAD), whole),
                pl.BlockSpec((2 * HEAD, tree_len), whole),
                pl.BlockSpec((tree_len, tile), column),
                pl.BlockSpec((HALF, tile), column),
                pl.BlockSpec((HALF, tile), column),
            ],
            out_specs=(
                pl.BlockSpec((tile, width), lambda i, s: (i, 0)),
                pl.BlockSpec((tree_len, 2 * HEAD), whole),
            ),
            scratch_shapes=[pltpu.VMEM((tree_len, HEAD), F32), pltpu.VMEM((tree_len, HEAD), F32)],
        ),
        compiler_params=pltpu.CompilerParams(vmem_limit_bytes=62 << 20),
        cost_estimate=NO_COST,
        name="attend_back",
    )(start, q_t, do_t, o_t, lse, kv, kv_t, bias_t, cos_t, sin_t)


def layer_attention(normed, weights, tables):
    gains, w_attn, w_mlp, width, split, units = weights
    start, bias_t, cos_t, sin_t, cos_rows, sin_rows = tables
    q_t = dot_f32(w_attn[:, :width], normed, 0, 1)
    kv, kv_t = gather_rows(
        jnp.dot(normed, w_attn[:, width:split], preferred_element_type=F32), cos_rows, -sin_rows
    )
    o_t, o, lse = attend(start, q_t, kv, kv_t, bias_t, cos_t, sin_t)
    return (q_t, kv, kv_t, o_t, lse), o


def attention_backward(grad_attn, weights, tables, kept):
    gains, w_attn, w_mlp, width, split, units = weights
    start, bias_t, cos_t, sin_t, cos_rows, sin_rows = tables
    q_t, kv, kv_t, o_t, lse = kept
    do_t = dot_f32(w_attn[:, split : split + width], grad_attn, 0, 1).astype(BF)
    dq, dkv_part = attend_back(start, q_t, do_t, o_t, lse, kv, kv_t, bias_t, cos_t, sin_t)
    return dq, scatter_rows(dkv_part, cos_rows, sin_rows)


def layer_units(normed, weights):
    units = weights[-1]
    gate_up = jnp.dot(normed, weights[2][:, : 2 * units], preferred_element_type=F32)
    gate, up = gate_up[:, :units], gate_up[:, units:]
    return gate, up, (gate * jax.nn.sigmoid(gate) * up).astype(BF)


def units_backward(branch, weights, gate, up):
    units = weights[-1]
    d_inner = dot_f32(branch, weights[2][:, 2 * units :], 1, 0)
    sig = jax.nn.sigmoid(gate)
    d_gate = (d_inner * up * sig * (1.0 + gate * (1.0 - sig))).astype(BF)
    d_up = (d_inner * gate * sig).astype(BF)
    return d_gate, d_up


def reduce_gradient(x):
    return lax.psum_scatter(x, BOTH, scatter_dimension=0, tiled=True)


def shards(
    inputs, cotangent, seg_ids, positions, parents, gain_attn, w_query, key_weight, value_weight,
    w_out, gain_mlp, w_gate, w_up, w_down,
):
    sec = lax.axis_index("section")
    data = lax.axis_index("dp")
    sections = lax.axis_size("section")
    devices = lax.axis_size("dp")
    assert sections == 2 and inputs.shape[0] == 2
    first_core = sec == 0
    rows, model = inputs.shape[1], inputs.shape[2]
    swap = [(0, 1), (1, 0)]

    tree = lax.dynamic_index_in_dim(inputs, sec, 0, keepdims=False)
    hidden = tree.astype(F32)
    segments = lax.dynamic_index_in_dim(seg_ids, sec, 0, keepdims=False)
    places = lax.dynamic_index_in_dim(positions, sec, 0, keepdims=False)
    parent = lax.dynamic_index_in_dim(parents, sec, 0, keepdims=False)

    width, span, units = w_query.shape[2], key_weight.shape[2], w_gate.shape[2]
    split = width + 2 * span
    shard_list = (
        jnp.concatenate(
            [w_query[0], key_weight[0], value_weight[0], w_out[0].T, gain_attn.T, gain_mlp.T], 1
        ).astype(BF),
        jnp.concatenate([w_gate[0], w_up[0], w_down[0].T], 1).astype(BF),
    )
    halves = []
    for shard in shard_list:
        half = shard.shape[0] // 2
        low, high = shard[:half], shard[half:]
        got = lax.ppermute(jnp.where(first_core, high, low), "section", swap)
        halves.append((jnp.where(first_core, low, got), jnp.where(first_core, got, high)))
    def gathered(halves):
        return [lax.all_gather(half, BOTH, axis=0, tiled=True) for half in halves]

    def with_gains(w_attn, w_mlp):
        return (w_attn[:, split + width :].astype(F32).T, w_attn, w_mlp, width, split, units)

    (attn_zero, attn_one), (mlp_zero, mlp_one) = halves
    attn_zero = jnp.concatenate([attn_zero, attn_one[:, split + width : split + width + 1]], 1)
    attn_zero, mlp_zero = gathered((attn_zero, mlp_zero))
    cot = lax.dynamic_index_in_dim(cotangent, sec, 0, keepdims=False)
    attn_zero, cot = lax.optimization_barrier((attn_zero, cot))
    zero = with_gains(attn_zero, mlp_zero)
    attn_one, mlp_one = gathered((attn_one, mlp_one))

    seg_count = parent.shape[0]
    labels = jnp.arange(seg_count, dtype=jnp.int32)
    parent_hot = (parent[:, None] == labels[None, :]).astype(F32)
    ancestry = jnp.eye(seg_count, dtype=F32) + parent_hot + jnp.dot(parent_hot, parent_hot)
    ancestry = (ancestry > 0.5).astype(F32)
    row_start = data * rows
    seg_rows = lax.dynamic_slice_in_dim(segments, row_start, rows, 0)
    pos_rows = lax.dynamic_slice_in_dim(places, row_start, rows, 0)
    key_hot = (segments[:, None] == labels[None, :]).astype(F32)
    query_hot = (labels[:, None] == seg_rows[None, :]).astype(F32)
    reach = jnp.dot(key_hot, jnp.dot(ancestry.T, query_hot))
    allowed = (reach > 0.5) & (places[:, None] <= pos_rows[None, :])
    bias_t = jnp.where(allowed, 0.0, MASKED).astype(BF)
    frequency = THETA ** (-(jnp.arange(HALF, dtype=F32) * 2.0 / HEAD))
    angles = frequency[:, None] * pos_rows.astype(F32)[None, :]
    cos_t, sin_t = jnp.cos(angles), jnp.sin(angles)
    ones = jnp.ones((rows, HEAD), F32)
    cos_rows = jnp.concatenate([cos_t.T, cos_t.T, ones], 1)
    sin_rows = jnp.concatenate([sin_t.T, -sin_t.T, 0 * ones], 1)
    tables = (row_start.astype(jnp.int32).reshape(1), bias_t, cos_t, sin_t, cos_rows, sin_rows)

    split_out, split_down = split, 2 * units
    wide, narrow = (F32, BF), (BF, BF)
    back = (F32, BF, F32)

    normed_zero = (hidden * lax.rsqrt(jnp.mean(hidden * hidden, -1, keepdims=True) + EPSILON) * zero[0][:1]).astype(BF)
    kept_zero, o_zero = layer_attention(normed_zero, zero, tables)
    middle_zero, r_zero = product_sum(
        (o_zero, tree, zero[0]), ((0,), split_out, ("add", (1, (2, 1))), wide), zero[1], stagger=True, key=1
    )
    gate_zero, up_zero, inner_zero = layer_units(r_zero, zero)
    out_zero, normed_one = product_sum(
        (inner_zero, middle_zero, zero[0]), ((0,), split_down, ("add", (1, (2, 2))), narrow), zero[2], key=5
    )

    out_zero, normed_one, attn_one = lax.optimization_barrier((out_zero, normed_one, attn_one))
    one = with_gains(attn_one, mlp_one)
    kept_one, o_one = layer_attention(normed_one, one, tables)
    middle_one, r_one = product_sum(
        (o_one, out_zero, one[0]), ((0,), split_out, ("add", (1, (2, 1))), wide), one[1], key=2
    )
    gate_one, up_one, inner_one = layer_units(r_one, one)
    branch = cot
    d_gate, d_up = units_backward(branch, one, gate_one, up_one)
    grad_middle, grad_attn, d_gain_mlp_one, d_mlp_one = product_sum(
        ((d_gate, d_up), inner_one, middle_one, branch, r_one, one[0]), ((0,), 0, ("back", (2, 3, (5, 1))), back),
        one[2], ((4, (0,)), (3, (1,))), key=8,
    )
    g_mlp_one = reduce_gradient(d_mlp_one)
    dq, dkv = attention_backward(grad_attn, one, tables, kept_one)
    grad_one, branch, d_gain_attn_one, d_attn_one = product_sum(
        ((dq, dkv), out_zero, grad_middle, one[0], normed_one, grad_attn, o_one),
        ((0,), 0, ("back", (1, 2, (3, 0))), back),
        one[1], ((4, (0,)), (5, (6,))), stagger=True, key=7,
    )
    g_attn_one = reduce_gradient(d_attn_one)

    d_gate, d_up = units_backward(branch, zero, gate_zero, up_zero)
    grad_middle, grad_attn, d_gain_mlp_zero, d_mlp_zero = product_sum(
        ((d_gate, d_up), inner_zero, middle_zero, branch, r_zero, zero[0]),
        ((0,), 0, ("back", (2, 3, (5, 1))), back),
        zero[2], ((4, (0,)), (3, (1,))), key=9,
    )
    g_mlp_zero = reduce_gradient(d_mlp_zero)
    grad_attn, g_mlp_one = lax.optimization_barrier((grad_attn, g_mlp_one))
    dq, dkv = attention_backward(grad_attn, zero, tables, kept_zero)
    dq, g_attn_one = lax.optimization_barrier((dq, g_attn_one))
    grad_zero, send_zero, d_gain_attn_zero, d_attn_zero = product_sum(
        ((dq, dkv), tree, grad_middle, zero[0], normed_zero, grad_attn, o_zero),
        ((0,), 0, ("back", (1, 2, (3, 0))), back),
        zero[1], ((4, (0,)), (5, (6,))), key=11,
    )
    d_gain_attn_zero, d_gain_mlp_zero, d_gain_attn_one, d_gain_mlp_one = [
        jnp.sum(x, 0) for x in (d_gain_attn_zero, d_gain_mlp_zero, d_gain_attn_one, d_gain_mlp_one)
    ]
    d_gains = jnp.stack([d_gain_attn_zero, d_gain_mlp_zero, d_gain_attn_one, d_gain_mlp_one])
    d_gains = d_gains.reshape(2, 2, devices, -1).swapaxes(1, 2).reshape(2, devices, -1, 128)

    inner_one, send_zero = lax.optimization_barrier((inner_one, send_zero))
    last_sum = functools.partial(
        product_sum, (inner_one, middle_one), ((0,), split_down, ("add", (1,)), (BF,)), one[2], key=6
    )
    if devices == 4:
        out_one, g_attn_zero, g_gain, got_out, got_in, got_mlp, got_attn = last_sum(
            extra=finishing(d_attn_zero, d_gains, out_zero, send_zero, branch, g_mlp_one, g_attn_one)
        )
    else:
        out_one = last_sum()
        g_attn_zero, g_gain, got_out, got_in, got_mlp, got_attn = finish_apart(
            d_attn_zero, d_gains, out_zero, out_one, send_zero, branch, g_mlp_one, g_attn_one
        )

    layer_output, input_grad, *grads = write_results(
        (out_zero, out_one, got_out), (grad_zero, grad_one, got_in), (g_attn_zero, g_attn_one, got_attn), width, span
    )
    input_grad, g_mlp_zero = lax.optimization_barrier((input_grad, g_mlp_zero))
    grads += write_mlp(
        g_mlp_zero, g_mlp_one, lax.ppermute(g_mlp_zero, "section", [(1, 0)]), got_mlp, units
    )
    g_query, g_key, g_value, g_out, g_gate, g_up, g_down = [grad[None] for grad in grads]
    g_gain = g_gain.reshape(2, 1, -1)
    return (
        layer_output[None], input_grad[None], g_gain[0], g_query, g_key, g_value, g_out, g_gain[1], g_gate, g_up, g_down,
    )


def solution(mesh):
    in_specs = (
        P(None, "dp", None),
        P(None, "dp", None),
        P(),
        P(),
        P(),
        P("section", "dp"),
        P("section", "dp", "tensor"),
        P("section", "dp", "tensor"),
        P("section", "dp", "tensor"),
        P("section", "tensor", "dp"),
        P("section", "dp"),
        P("section", "dp", "tensor"),
        P("section", "dp", "tensor"),
        P("section", "tensor", "dp"),
    )
    out_specs = (
        P("section", None, "dp", None),
        P("section", None, "dp", None),
        P("section", "dp"),
        P("section", "dp", "tensor"),
        P("section", "dp", "tensor"),
        P("section", "dp", "tensor"),
        P("section", "tensor", "dp"),
        P("section", "dp"),
        P("section", "dp", "tensor"),
        P("section", "dp", "tensor"),
        P("section", "tensor", "dp"),
    )
    return jax.shard_map(shards, mesh=mesh, in_specs=in_specs, out_specs=out_specs, check_vma=False)
```

```python
import functools

import jax
import jax.numpy as jnp
from jax import lax
from jax.experimental import pallas as pl
from jax.experimental.pallas import tpu as pltpu
from jax.sharding import PartitionSpec as P

HEAD = 64
HALF = HEAD // 2
TRUNK = 1024
GROUP = 384
EPSILON = 1e-05
THETA = 10000.0
MASKED = -1e30
BF = jnp.bfloat16
F32 = jnp.float32
MESH = pl.DeviceIdType.MESH
BOTH = ("dp", "section")


def dot_f32(a, b, ca, cb):
    return lax.dot_general(a, b, (((ca,), (cb,)), ((), ())), preferred_element_type=F32)


BLOCK = 256
PIECE = 128
NO_COST = pl.CostEstimate(flops=1, transcendentals=0, bytes_accessed=1)


def columns_of(i):
    return pl.ds(pl.multiple_of(i * PIECE, PIECE), PIECE)


def gain_row(arrays, place, at):
    return arrays[place[0]][place[1] : place[1] + 1, at]


def row_scale(squares, model):
    return lax.rsqrt(jnp.sum(squares, 1, keepdims=True) * (1.0 / model) + EPSILON)


def before_sum(job, arrays, keep):
    kind, places = job[2]
    if kind == "back":
        value = arrays[places[0]]
        model = value.shape[1]
        squares = jnp.zeros(keep.shape, F32)
        for i in range(model // PIECE):
            x = value[:, i * PIECE : (i + 1) * PIECE].astype(F32)
            squares += x * x
        keep[...] = jnp.broadcast_to(row_scale(squares, model), keep.shape)


def with_piece(job, i, total, arrays, outs, keep, sums):
    kind, places = job[2]
    at = columns_of(i)
    if kind == "add":
        y = (arrays[places[0]][:, at].astype(F32) + total).astype(outs[0].dtype)
        outs[0][:, at] = y
        if len(outs) > 1:
            sums[...] += y.astype(F32) * y.astype(F32)
    if kind == "back":
        product = total * arrays[places[0]][:, at].astype(F32) * keep[...]
        sums[...] += product * gain_row(arrays, places[2], at)
        outs[2][:, at] = jnp.sum(product.reshape(-1, 8, PIECE), 0)


def after_sum(job, rows, total, arrays, outs, keep, sums):
    kind, places = job[2]
    model = arrays[places[0]].shape[1]
    at = lambda i: slice(i * PIECE, (i + 1) * PIECE)
    if kind == "add" and len(outs) > 1:
        scale = row_scale(sums[rows], model)
        for i in range(model // PIECE):
            y = outs[0][rows, at(i)].astype(F32)
            outs[1][rows, at(i)] = (y * scale * gain_row(arrays, places[1], at(i))).astype(BF)
    if kind == "back":
        mean = jnp.sum(sums[rows], 1, keepdims=True) * (1.0 / model)
        scale = keep[rows]
        for i in range(model // PIECE):
            unit = arrays[places[0]][rows, at(i)].astype(F32) * scale
            grad = total(i)[rows].astype(F32) * gain_row(arrays, places[2], at(i))
            out = arrays[places[1]][rows, at(i)].astype(F32) + scale * (grad - unit * mean)
            outs[0][rows, at(i)] = out
            outs[1][rows, at(i)] = out.astype(BF)


def product_sum_kernel(cfg, *refs):
    n_join, n_arrays, job, sides, stagger = cfg
    xs, first_column = job[:2]
    refs = list(refs)
    take = lambda n: [refs.pop(0) for _ in range(n)]
    joined = take(n_join)
    from_hbm = [None, *take(n_arrays - 1)]
    (w_hbm,) = take(1)
    outs_hbm = take(len(job[3]))
    (g_hbm,) = take(1) if sides else (None,)
    arrays = take(n_arrays)
    outs = take(len(job[3]))
    load_sem, out_sem, w_buf, p_buf, a_buf, b_buf, w_sem, sa, ra, sb, rb, sc, rc, turn, keep, sums = take(16)
    g_buf, g_sem = take(2) if sides else (None, None)
    per_block = BLOCK // PIECE
    pieces = p_buf.shape[0]
    blocks = pieces // per_block
    n_rows = p_buf.shape[1]
    early = len(xs)
    lag = 2
    assert xs[0] == 0

    t = lax.axis_index("tensor")
    sec = lax.axis_index("section")
    dat = lax.axis_index("dp")
    inner = (t == 1) | (t == 2)
    outer = jnp.logical_not(inner)
    pair = (sec, t + 1 - 2 * lax.rem(t, 2), dat)
    mid = (sec, 3 - t, dat)
    mate = (1 - sec, t, dat)

    def columns(j):
        return pl.ds(pl.multiple_of(j * BLOCK, BLOCK), BLOCK)

    def to_inner(i):
        return pltpu.make_async_remote_copy(
            p_buf.at[i], a_buf.at[i], sa.at[i], ra.at[i], device_id=pair, device_id_type=MESH
        )

    def across(i):
        return pltpu.make_async_remote_copy(
            p_buf.at[i], b_buf.at[i], sb.at[i], rb.at[i], device_id=mid, device_id_type=MESH
        )

    def to_outer(i):
        return pltpu.make_async_remote_copy(
            b_buf.at[i], b_buf.at[i], sc.at[i], rc.at[i], device_id=pair, device_id_type=MESH
        )

    def load(k):
        return pltpu.make_async_copy(from_hbm[k], arrays[k], load_sem.at[k])

    def join():
        copies, start = [], 0
        for m, src in enumerate(joined):
            at = pl.ds(start, src.shape[1])
            copies.append(pltpu.make_async_copy(src, arrays[0].at[:, at], load_sem.at[n_arrays + m]))
            start += src.shape[1]
        return copies

    def fetch(j, slot):
        return pltpu.make_async_copy(
            w_hbm.at[columns(j), pl.ds(first_column, w_buf.shape[2])], w_buf.at[slot], w_sem.at[slot]
        )

    def flush(j, slot):
        return pltpu.make_async_copy(g_buf.at[slot], g_hbm.at[columns(j), :], g_sem.at[slot])

    def every_piece(body):
        def turn_of(i, _):
            body(i)
            return 0

        lax.fori_loop(0, pieces, turn_of, 0)

    for copy in join():
        copy.start()
    for k in range(1, early):
        load(k).start()
    fetch(0, 0).start()
    for k in range(early, n_arrays):
        load(k).start()
    barrier = pltpu.get_barrier_semaphore()
    pl.semaphore_signal(barrier, inc=1, device_id=pair, device_id_type=MESH)
    sums[...] = jnp.zeros_like(sums)

    @pl.when(inner)
    def _():
        pl.semaphore_signal(barrier, inc=1, device_id=mid, device_id_type=MESH)
        pl.semaphore_wait(barrier, 2)

    @pl.when(outer)
    def _():
        if stagger:
            pl.semaphore_signal(barrier, inc=1, device_id=mate, device_id_type=MESH)
            pl.semaphore_wait(barrier, 2)

            @pl.when(sec == 1)
            def _():
                pl.semaphore_wait(turn, 1)

        else:
            pl.semaphore_wait(barrier, 1)

    for copy in join():
        copy.wait()
    for k in range(1, early):
        load(k).wait()

    def done(i):
        with_piece(job, i, b_buf[i].astype(F32), arrays, outs, keep, sums)

    def first(i):
        to_inner(i).wait_recv()
        p_buf[i] = p_buf[i] + a_buf[i]
        across(i).start()

    def second(i):
        across(i).wait_recv()
        b_buf[i] = p_buf[i] + b_buf[i]
        to_outer(i).start()
        done(i)

    def side(j):
        slot = lax.rem(j, 2)

        @pl.when(j >= 2)
        def _():
            flush(j - 2, slot).wait()

        start = 0
        for a, bs in sides:
            a_t = arrays[a][:, columns(j)].T
            for b in bs:
                width = arrays[b].shape[1]
                g_buf[slot, :, start : start + width] = jnp.dot(
                    a_t, arrays[b][...], preferred_element_type=F32
                ).astype(BF)
                start += width
        flush(j, slot).start()
        return 0

    def step(j, _):
        slot = lax.rem(j, 2)
        fetch(j, slot).wait()

        @pl.when(j + 1 < blocks)
        def _():
            fetch(j + 1, 1 - slot).start()

        total, start = None, 0
        for x in xs:
            width = arrays[x].shape[1]
            term = dot_f32(arrays[x][...], w_buf[slot, :, start : start + width], 1, 1)
            total = term if total is None else total + term
            start += width
        total = total.astype(BF)
        for u in range(per_block):
            p_buf[per_block * j + u] = total[:, u * PIECE : (u + 1) * PIECE]

        @pl.when(outer)
        def _():
            for u in range(per_block):
                to_inner(per_block * j + u).start()

        @pl.when(j == 1)
        def _():
            for k in range(early, n_arrays):
                load(k).wait()
            before_sum(job, arrays, keep)

        if sides:

            @pl.when(j >= lag)
            def _():
                side(j - lag)

        @pl.when(inner)
        def _():
            for u in range(per_block):
                i = per_block * j + u
                first(i)

                @pl.when(j >= 1)
                def _():
                    second(i - per_block)

        return 0

    lax.fori_loop(0, blocks, step, 0)

    @pl.when(inner)
    def _():
        for u in range(per_block):
            second(pieces - per_block + u)

    if stagger:

        @pl.when(outer)
        def _():
            every_piece(lambda i: to_inner(i).wait_send())

            @pl.when(sec == 0)
            def _():
                pl.semaphore_signal(turn, inc=1, device_id=mate, device_id_type=MESH)

    if sides:
        lax.fori_loop(blocks - lag, blocks, lambda j, _: side(j), 0)

    @pl.when(outer)
    def _():
        if not stagger:
            every_piece(lambda i: to_inner(i).wait_send())

        def arrive(i):
            to_outer(i).wait_recv()
            done(i)

        every_piece(arrive)

    chunks = 5 if n_rows % (5 * 32) == 0 else 1
    chunk = n_rows // chunks
    block = 32 if chunk % 32 == 0 else 16
    height = lambda m: 8 if job[2][0] == "back" and m == 2 else n_rows
    stores = []

    def store(m, rows):
        copy = pltpu.make_async_copy(outs[m].at[rows], outs_hbm[m].at[rows], out_sem.at[len(stores)])
        copy.start()
        stores.append(copy)

    for c in range(chunks):

        def turn_rows(r, _):
            rows = pl.ds(pl.multiple_of(c * chunk + r * block, block), block)
            after_sum(job, rows, lambda i: b_buf.at[i], arrays, outs, keep, sums)
            return 0

        if job[2][0] == "back" or len(outs) > 1:
            lax.fori_loop(0, chunk // block, turn_rows, 0)
        for m in range(len(outs)):
            if height(m) == n_rows:
                store(m, pl.ds(c * chunk, chunk))
    for m in range(len(outs)):
        if height(m) != n_rows:
            store(m, pl.ds(0, height(m)))

    @pl.when(inner)
    def _():
        def sent(i):
            across(i).wait_send()
            to_outer(i).wait_send()

        every_piece(sent)

    if sides:
        flush(blocks - 2, (blocks - 2) % 2).wait()
        flush(blocks - 1, (blocks - 1) % 2).wait()
    for copy in stores:
        copy.wait()


def product_sum(arrays, job, weights, sides=(), stagger=False, key=1):
    assert lax.axis_size("tensor") == 4
    first = arrays[0] if isinstance(arrays[0], tuple) else (arrays[0],)
    given = (*first, *arrays[1:])
    rows, model = first[0].shape[0], weights.shape[0]
    arrays = (jax.ShapeDtypeStruct((rows, sum(x.shape[1] for x in first)), BF), *arrays[1:])
    pieces = model // PIECE
    depth = sum(arrays[x].shape[1] for x in job[0])
    anywhere = pl.BlockSpec(memory_space=pl.ANY)
    buf = pltpu.VMEM((pieces, rows, PIECE), BF)
    sem = pltpu.SemaphoreType.DMA((pieces,))
    two = pltpu.SemaphoreType.DMA((2,))
    out_shape = []
    for m, dtype in enumerate(job[3]):
        height = 8 if job[2][0] == "back" and m == 2 else rows
        out_shape.append(jax.ShapeDtypeStruct((height, model), dtype))
    scratch = [pltpu.VMEM(x.shape, x.dtype) for x in (*arrays, *out_shape)]
    scratch += [pltpu.SemaphoreType.DMA((len(arrays) + len(first),)), pltpu.SemaphoreType.DMA((16,))]
    scratch += [pltpu.VMEM((2, BLOCK, depth), BF), buf, buf, buf, two, *[sem] * 6, pltpu.SemaphoreType.REGULAR]
    scratch += [pltpu.VMEM((rows, PIECE), F32)] * 2
    if sides:
        side_width = sum(arrays[b].shape[1] for _, bs in sides for b in bs)
        out_shape.append(jax.ShapeDtypeStruct((model, side_width), BF))
        scratch += [pltpu.VMEM((2, BLOCK, side_width), BF), two]
    out = pl.pallas_call(
        functools.partial(product_sum_kernel, (len(first), len(arrays), job, tuple(sides), stagger)),
        out_shape=out_shape,
        in_specs=[anywhere] * (len(given) + 1),
        out_specs=[anywhere] * len(out_shape),
        scratch_shapes=scratch,
        compiler_params=pltpu.CompilerParams(
            collective_id=key, has_side_effects=True, vmem_limit_bytes=62 << 20
        ),
        cost_estimate=NO_COST,
        name=f"product_sum_{key}",
    )(*given, weights)
    return out if len(out) > 1 else out[0]


def dp_peers(count):
    me = lax.axis_index("dp")
    sec, t = lax.axis_index("section"), lax.axis_index("tensor")
    others = [lax.rem(me + k, count) for k in range(1, count)]
    return me, others, [(sec, t, other) for other in others]


def greet(ids):
    barrier = pltpu.get_barrier_semaphore()
    for device in ids:
        pl.semaphore_signal(barrier, inc=1, device_id=device, device_id_type=MESH)
    pl.semaphore_wait(barrier, len(ids))


def turn_rows(x, cos_ref, sin_ref):
    lane = lax.broadcasted_iota(jnp.int32, x.shape, 1)
    width = x.shape[1]
    partner = jnp.where(lane < HALF, pltpu.roll(x, width - HALF, 1), pltpu.roll(x, HALF, 1))
    return x * cos_ref[...] + partner * sin_ref[...]


def gather_kernel(count, raw_ref, cos_ref, sin_ref, o_ref, t_ref, x_ref, send, recv):
    me, _, ids = dp_peers(count)
    x_ref[...] = turn_rows(raw_ref[...], cos_ref, sin_ref).astype(BF)
    greet(ids)
    copies = [
        pltpu.make_async_remote_copy(
            x_ref, o_ref.at[me], send.at[k], recv.at[k], device_id=device, device_id_type=MESH
        )
        for k, device in enumerate(ids)
    ]
    for copy in copies:
        copy.start()
    o_ref[me] = x_ref[...]
    for copy in copies:
        copy.wait()
    t_ref[...] = o_ref[...].reshape(t_ref.shape[1], t_ref.shape[0]).T


def scatter_kernel(count, x_ref, cos_ref, sin_ref, o_ref, buf, send, recv):
    me, others, ids = dp_peers(count)
    greet(ids)
    copies = [
        pltpu.make_async_remote_copy(
            x_ref.at[others[k]], buf.at[k], send.at[k], recv.at[k], device_id=device, device_id_type=MESH
        )
        for k, device in enumerate(ids)
    ]
    for copy in copies:
        copy.start()
    total = x_ref[me].astype(F32)
    for k, copy in enumerate(copies):
        copy.wait()
        total = total + buf[k].astype(F32)
    o_ref[...] = turn_rows(total, cos_ref, sin_ref).astype(BF)


def gather_rows(raw, cos_rows, sin_rows):
    count = lax.axis_size("dp")
    rows, width = raw.shape
    in_vmem = pl.BlockSpec(memory_space=pltpu.VMEM)
    sem = pltpu.SemaphoreType.DMA((count - 1,))
    out, out_t = pl.pallas_call(
        functools.partial(gather_kernel, count),
        out_shape=(
            jax.ShapeDtypeStruct((count, rows, width), BF),
            jax.ShapeDtypeStruct((width, count * rows), BF),
        ),
        in_specs=[in_vmem] * 3,
        out_specs=(in_vmem, in_vmem),
        scratch_shapes=[pltpu.VMEM((rows, width), BF), sem, sem],
        compiler_params=pltpu.CompilerParams(collective_id=3, has_side_effects=True),
        cost_estimate=NO_COST,
        name="gather_rows",
    )(raw, cos_rows, sin_rows)
    return out.reshape(-1, width), out_t


def scatter_rows(x, cos_rows, sin_rows):
    count = lax.axis_size("dp")
    rows, width = x.shape[0] // count, x.shape[1]
    in_vmem = pl.BlockSpec(memory_space=pltpu.VMEM)
    sem = pltpu.SemaphoreType.DMA((count - 1,))
    return pl.pallas_call(
        functools.partial(scatter_kernel, count),
        out_shape=jax.ShapeDtypeStruct((rows, width), BF),
        in_specs=[in_vmem] * 3,
        out_specs=in_vmem,
        scratch_shapes=[pltpu.VMEM((count - 1, rows, width), x.dtype), sem, sem],
        compiler_params=pltpu.CompilerParams(collective_id=4, has_side_effects=True),
        cost_estimate=NO_COST,
        name="scatter_rows",
    )(x.reshape(count, rows, width), cos_rows, sin_rows)


def finish_kernel(
    g_hbm, gain_ref, out_zero, out_one, in_zero, in_one, mlp_one, attn_one,
    o_ref, gain_out, got_out, got_in, got_mlp, got_attn,
    mine, away, got, xs, ys, xr, yr, gains, load_sem, send, recv, mate_send, mate_recv, gain_send, gain_recv,
):
    sec, t, dat = lax.axis_index("section"), lax.axis_index("tensor"), lax.axis_index("dp")
    flip_x = dat + 1 - 2 * lax.rem(dat, 2)
    flip_y = lax.rem(dat + 2, 4)
    across = lax.rem(flip_x + 2, 4)
    by_x, by_y, mate = (sec, t, flip_x), (sec, t, flip_y), (1 - sec, t, dat)
    peers = [
        mate, by_x, by_y, (sec, t, across),
        (1 - sec, t, flip_x), (1 - sec, t, flip_y), (1 - sec, t, across),
    ]
    rows = g_hbm.shape[1] // 2
    upper, lower = pl.ds(0, rows), pl.ds(rows, rows)
    order = (across, flip_x, flip_y, dat)
    loads = []
    for k, block in enumerate(order):
        loads.append(pltpu.make_async_copy(g_hbm.at[2 * block + 1 - sec], away.at[k], load_sem.at[k]))
        loads.append(pltpu.make_async_copy(g_hbm.at[2 * block + sec], mine.at[k], load_sem.at[4 + k]))
    for copy in loads:
        copy.start()
    greet(peers)

    def remote(src, dst, k, device):
        return pltpu.make_async_remote_copy(
            src, dst, send.at[k], recv.at[k], device_id=device, device_id_type=MESH
        )

    def to_mate(src, dst, k):
        return pltpu.make_async_remote_copy(
            src, dst, mate_send.at[k], mate_recv.at[k], device_id=mate, device_id_type=MESH
        )

    swaps = [remote(away.at[k], got.at[k], k, mate) for k in range(4)]
    for k in range(4):
        loads[2 * k].wait()
        swaps[k].start()
    gain_copies = [
        pltpu.make_async_remote_copy(
            gain_ref.at[peer[0], peer[2]], gains.at[k], gain_send.at[k], gain_recv.at[k],
            device_id=peer, device_id_type=MESH,
        )
        for k, peer in enumerate(peers)
    ]
    for copy in gain_copies:
        copy.start()
    outs = []
    for k in range(4):
        loads[2 * k + 1].wait()
        swaps[k].wait_recv()
        mine[k] = (mine[k].astype(F32) + got[k].astype(F32)).astype(BF)
        if k == 0:
            outs += [remote(mine.at[0, upper], xs.at[0], 4, by_x), remote(mine.at[0, lower], ys.at[0], 5, by_y)]
        if k == 1:
            outs += [remote(mine.at[1, upper], xs.at[1], 6, by_x)]
        if k == 2:
            outs += [remote(mine.at[2, lower], ys.at[1], 7, by_y)]
        for copy in outs[-(2 if k == 0 else 1) :]:
            if k < 3:
                copy.start()

    @pl.when(sec == 0)
    def _():
        to_mate(in_one, got_in, 0).start()
        to_mate(out_one, got_out, 1).start()
        to_mate(mlp_one, got_mlp, 2).start()
        to_mate(attn_one, got_attn, 3).start()

    @pl.when(sec == 1)
    def _():
        to_mate(in_zero, got_in, 0).start()
        to_mate(out_zero, got_out, 1).start()

    outs[0].wait_recv()
    mine[2, upper] = (mine[2, upper].astype(F32) + xs[0].astype(F32)).astype(BF)
    outs.append(remote(mine.at[2, upper], yr, 8, by_y))
    outs[4].start()
    outs[1].wait_recv()
    mine[1, lower] = (mine[1, lower].astype(F32) + ys[0].astype(F32)).astype(BF)
    outs.append(remote(mine.at[1, lower], xr, 9, by_x))
    outs[5].start()
    total = gain_ref[sec, dat]
    for k, copy in enumerate(gain_copies):
        copy.wait()
        total = total + gains[k]
    gain_out[...] = total
    outs[2].wait_recv()
    outs[3].wait_recv()
    outs[4].wait_recv()
    o_ref[upper] = (mine[3, upper].astype(F32) + xs[1].astype(F32) + yr[...].astype(F32)).astype(BF)
    outs[5].wait_recv()
    o_ref[lower] = (mine[3, lower].astype(F32) + ys[1].astype(F32) + xr[...].astype(F32)).astype(BF)

    @pl.when(sec == 1)
    def _():
        to_mate(o_ref, got_attn, 3).start()

    for copy in swaps + outs:
        copy.wait_send()
    to_mate(in_one, got_in, 0).wait()
    to_mate(out_one, got_out, 1).wait()
    to_mate(attn_one, got_attn, 3).wait()

    @pl.when(sec == 0)
    def _():
        to_mate(mlp_one, got_mlp, 2).wait_send()

    @pl.when(sec == 1)
    def _():
        to_mate(mlp_one, got_mlp, 2).wait_recv()


def finish(g, gains, out_zero, out_one, in_zero, in_one, mlp_one, attn_one):
    rows, width = g.shape[0] // 8, g.shape[1]
    part = pltpu.VMEM((2, rows // 2, width), BF)
    whole = pltpu.VMEM((4, rows, width), BF)
    end = pltpu.VMEM((rows // 2, width), BF)
    in_vmem, anywhere = pl.BlockSpec(memory_space=pltpu.VMEM), pl.BlockSpec(memory_space=pl.ANY)
    like = lambda x: jax.ShapeDtypeStruct(x.shape, x.dtype)
    dma = lambda n: pltpu.SemaphoreType.DMA((n,))
    return pl.pallas_call(
        finish_kernel,
        out_shape=(
            jax.ShapeDtypeStruct((rows, width), BF),
            jax.ShapeDtypeStruct(gains.shape[2:], F32),
            like(out_zero), like(in_zero), like(mlp_one), like(attn_one),
        ),
        in_specs=[anywhere, in_vmem, *[anywhere] * 6],
        out_specs=(in_vmem, in_vmem, *[anywhere] * 4),
        scratch_shapes=[
            whole, whole, whole, part, part, end, end, pltpu.VMEM((7, *gains.shape[2:]), F32),
            dma(8), dma(10), dma(10), dma(4), dma(4), dma(7), dma(7),
        ],
        compiler_params=pltpu.CompilerParams(
            collective_id=12, has_side_effects=True, vmem_limit_bytes=62 << 20
        ),
        cost_estimate=NO_COST,
        name="finish",
    )(g.reshape(8, rows, width), gains, out_zero, out_one, in_zero, in_one, mlp_one, attn_one)


def finish_apart(g, gains, out_zero, out_one, in_zero, in_one, mlp_one, attn_one):
    first_core = lax.axis_index("section") == 0
    half = reduce_gradient(g)
    swap = lambda zero, one: lax.ppermute(jnp.where(first_core, one, zero), "section", [(0, 1), (1, 0)])
    return (
        half, share_sums(gains), swap(out_zero, out_one), swap(in_zero, in_one),
        lax.ppermute(mlp_one, "section", [(0, 1)]), swap(half, attn_one),
    )


def in_rows(count, block, body):
    def turn(r, _):
        body(pl.ds(pl.multiple_of(r * block, block), block))
        return 0

    lax.fori_loop(0, count // block, turn, 0)


def widen_turned(dst, src, start, width):
    for c in range(0, width, 128):
        dst[c : c + 128] = src[:, start + c : start + c + 128].astype(F32).T


def write_mlp_kernel(
    zero, one, from_one, from_zero, gate_hbm, up_hbm, down_hbm, mlp, gate_buf, up_buf, down_buf, load_sem, store_sem
):
    sec = lax.axis_index("section")
    half, units = zero.shape[0], gate_buf.shape[1]
    low, high = pl.ds(0, half), pl.ds(half, half)
    load = lambda src, at, k: pltpu.make_async_copy(src, mlp.at[at], load_sem.at[k])
    store = lambda src, dst, k: pltpu.make_async_copy(src, dst, store_sem.at[k])

    @pl.when(sec == 0)
    def _():
        load(zero, low, 0).start()
        load(from_one, high, 1).start()

    @pl.when(sec == 1)
    def _():
        load(from_zero, low, 0).start()
        load(one, high, 1).start()

    load(zero, low, 0).wait()
    load(zero, high, 1).wait()

    def gates(rows):
        gate_buf[rows] = mlp[rows, :units].astype(F32)
        up_buf[rows] = mlp[rows, units : 2 * units].astype(F32)

    in_rows(2 * half, 32, gates)
    stores = [store(gate_buf, gate_hbm, 0), store(up_buf, up_hbm, 1), store(down_buf, down_hbm, 2)]
    stores[0].start()
    stores[1].start()
    widen_turned(down_buf, mlp, 2 * units, units)
    stores[2].start()
    for copy in stores:
        copy.wait()


def write_mlp(zero, one, from_one, from_zero, units):
    shard = 2 * zero.shape[0]
    anywhere = pl.BlockSpec(memory_space=pl.ANY)
    shapes = [(shard, units), (shard, units), (units, shard)]
    return pl.pallas_call(
        write_mlp_kernel,
        out_shape=[jax.ShapeDtypeStruct(shape, F32) for shape in shapes],
        in_specs=[anywhere] * 4,
        out_specs=[anywhere] * 3,
        scratch_shapes=[
            pltpu.VMEM((shard, zero.shape[1]), BF),
            *[pltpu.VMEM(shape, F32) for shape in shapes],
            pltpu.SemaphoreType.DMA((2,)),
            pltpu.SemaphoreType.DMA((3,)),
        ],
        compiler_params=pltpu.CompilerParams(vmem_limit_bytes=62 << 20),
        cost_estimate=NO_COST,
        name="write_mlp",
    )(zero, one, from_one, from_zero)


def write_kernel(
    split, out_zero, out_one, got_out, in_zero, in_one, got_in, attn_zero, attn_one, got_attn,
    out_hbm, in_hbm, q_hbm, k_hbm, v_hbm, o_hbm,
    outs, wides, attn, narrow, q_buf, k_buf, v_buf, o_buf, load_sem, store_sem,
):
    sec = lax.axis_index("section")
    half = attn_zero.shape[0]
    low, high = pl.ds(0, half), pl.ds(half, half)
    load = lambda src, dst, k: pltpu.make_async_copy(src, dst, load_sem.at[k])
    store = lambda src, dst, k: pltpu.make_async_copy(src, dst, store_sem.at[k])

    def start(own_out, own_in, attn_low, attn_high):
        load(own_out, outs.at[0], 0).start()
        load(own_in, wides.at[0], 1).start()
        load(attn_low, attn.at[low], 2).start()
        load(attn_high, attn.at[high], 3).start()

    @pl.when(sec == 0)
    def _():
        start(out_zero, in_zero, attn_zero, got_attn)

    @pl.when(sec == 1)
    def _():
        start(out_one, in_one, got_attn, attn_one)

    load(got_in, narrow, 4).start()
    load(got_out, outs.at[1], 5).start()
    stores = [
        store(outs.at[0], out_hbm.at[sec], 0),
        store(wides.at[0], in_hbm.at[sec], 1),
        store(outs.at[1], out_hbm.at[1 - sec], 2),
        store(wides.at[1], in_hbm.at[1 - sec], 3),
        store(q_buf, q_hbm, 4),
        store(k_buf, k_hbm, 5),
        store(v_buf, v_hbm, 6),
        store(o_buf, o_hbm, 7),
    ]
    load(out_zero, outs.at[0], 0).wait()
    stores[0].start()
    load(in_zero, wides.at[0], 1).wait()
    stores[1].start()
    width, span = q_buf.shape[1], k_buf.shape[1]
    load(attn_one, attn.at[low], 2).wait()
    load(attn_one, attn.at[high], 3).wait()

    def projections(rows):
        q_buf[rows] = attn[rows, :width].astype(F32)
        k_buf[rows] = attn[rows, width : width + span].astype(F32)
        v_buf[rows] = attn[rows, width + span : split].astype(F32)

    in_rows(2 * half, 32, projections)
    for k in (4, 5, 6):
        stores[k].start()
    widen_turned(o_buf, attn, split, width)
    stores[7].start()
    load(got_in, narrow, 4).wait()

    def widen(rows):
        wides[1, rows] = narrow[rows].astype(F32)

    in_rows(narrow.shape[0], 32, widen)
    stores[3].start()
    load(got_out, outs.at[1], 5).wait()
    stores[2].start()
    for copy in stores:
        copy.wait()


def write_results(results, ins, attns, width, span):
    rows, model = results[0].shape
    shard = 2 * attns[0].shape[0]
    anywhere = pl.BlockSpec(memory_space=pl.ANY)
    shapes = [(shard, width), (shard, span), (shard, span), (width, shard)]
    return pl.pallas_call(
        functools.partial(write_kernel, width + 2 * span),
        out_shape=[
            jax.ShapeDtypeStruct((2, rows, model), BF),
            jax.ShapeDtypeStruct((2, rows, model), F32),
            *[jax.ShapeDtypeStruct(shape, F32) for shape in shapes],
        ],
        in_specs=[anywhere] * 9,
        out_specs=[anywhere] * 6,
        scratch_shapes=[
            pltpu.VMEM((2, rows, model), BF),
            pltpu.VMEM((2, rows, model), F32),
            pltpu.VMEM((shard, attns[0].shape[1]), BF),
            pltpu.VMEM((rows, model), BF),
            *[pltpu.VMEM(shape, F32) for shape in shapes],
            pltpu.SemaphoreType.DMA((6,)),
            pltpu.SemaphoreType.DMA((8,)),
        ],
        compiler_params=pltpu.CompilerParams(vmem_limit_bytes=62 << 20),
        cost_estimate=NO_COST,
        name="write_results",
    )(*results, *ins, *attns)


def share_kernel(count, x_ref, o_ref, buf, send, recv):
    sec, t, dat = lax.axis_index("section"), lax.axis_index("tensor"), lax.axis_index("dp")
    peers = [
        (lax.rem(sec + k // count, 2), t, lax.rem(dat + k % count, count)) for k in range(1, 2 * count)
    ]
    greet(peers)
    copies = [
        pltpu.make_async_remote_copy(
            x_ref.at[peer[0], peer[2]], buf.at[k], send.at[k], recv.at[k], device_id=peer, device_id_type=MESH
        )
        for k, peer in enumerate(peers)
    ]
    for copy in copies:
        copy.start()
    total = x_ref[sec, dat]
    for k, copy in enumerate(copies):
        copy.wait()
        total = total + buf[k]
    o_ref[...] = total


def share_sums(x):
    count = lax.axis_size("dp")
    in_vmem = pl.BlockSpec(memory_space=pltpu.VMEM)
    sem = pltpu.SemaphoreType.DMA((2 * count - 1,))
    return pl.pallas_call(
        functools.partial(share_kernel, count),
        out_shape=jax.ShapeDtypeStruct(x.shape[2:], F32),
        in_specs=[in_vmem],
        out_specs=in_vmem,
        scratch_shapes=[pltpu.VMEM((2 * count - 1, *x.shape[2:]), F32), sem, sem],
        compiler_params=pltpu.CompilerParams(collective_id=13, has_side_effects=True),
        cost_estimate=NO_COST,
        name="share_sums",
    )(x)


def group_start(first_row):
    past = lax.max(first_row - TRUNK, 0)
    return pl.multiple_of(TRUNK + GROUP * lax.div(past, GROUP), 128)


def over_windows(tree_len, rows, tile, first_row, run):
    if tile % 128 == 0 and GROUP % tile == 0 and TRUNK % tile == 0 and rows % tile == 0:

        @pl.when(first_row < TRUNK)
        def _():
            run(((pl.ds(0, TRUNK), True),))

        @pl.when(first_row >= TRUNK)
        def _():
            run(((pl.ds(0, TRUNK), False), (pl.ds(group_start(first_row), GROUP), True)))

    else:
        run(((pl.ds(0, tree_len), True),))


def masked(scores, bias_ref, win, step):
    bias = bias_ref[win, :].astype(F32)
    return scores + (bias if step == 1 else jnp.concatenate([bias] * step, axis=1))


def head_rows(ref, head):
    return ref[head * HEAD : (head + 1) * HEAD, :]


def beside(ref, head, count):
    parts = [head_rows(ref, head + k) for k in range(count)]
    return parts[0] if count == 1 else jnp.concatenate(parts, axis=1)


def turned_beside(ref, cos, sin, head, count):
    parts = []
    for k in range(count):
        rows = head_rows(ref, head + k)
        first, second = rows[:HALF], rows[HALF:]
        parts.append(jnp.concatenate([first * cos - second * sin, second * cos + first * sin], axis=0))
    whole = parts[0] if count == 1 else jnp.concatenate(parts, axis=1)
    return (whole.astype(BF).astype(F32) * HEAD**-0.5).astype(BF)


def as_rows(x, tile, count):
    parts = [x[:, k * tile : (k + 1) * tile] for k in range(count)]
    return (parts[0] if count == 1 else jnp.concatenate(parts, axis=0)).T


def over_groups(groups, step, body):
    for group in range(groups):
        body(group, slice(group * step * HEAD, (group + 1) * step * HEAD))


def attend_kernel(
    rows, step, start_ref, q_ref, kv_ref, kvt_ref, bias_ref, cos_ref, sin_ref, o_ref, on_ref, lse_ref
):
    tile = q_ref.shape[1]
    heads = q_ref.shape[0] // HEAD
    first_row = start_ref[0] + pl.program_id(0) * tile

    def body(wins, group, lanes):
        head = group * step
        q = turned_beside(q_ref, cos_ref[...], sin_ref[...], head, step)
        scores = []
        for win, mask in wins:
            score = dot_f32(kv_ref[win, :HEAD], q, 1, 0)
            scores.append(masked(score, bias_ref, win, step) if mask else score)
        top = functools.reduce(jnp.maximum, [jnp.max(s, 0, keepdims=True) for s in scores])
        expo = [jnp.exp(s - top) for s in scores]
        total = sum(jnp.sum(e, 0, keepdims=True) for e in expo)
        out = sum(dot_f32(kvt_ref[HEAD:, win], e.astype(BF), 1, 0) for (win, _), e in zip(wins, expo))
        out = out / total
        on_ref[:, lanes] = as_rows(out, tile, step).astype(BF)
        lse_ref[group, 0] = top + jnp.log(total)
        out = out.astype(BF)
        for k in range(step):
            o_ref[(head + k) * HEAD : (head + k + 1) * HEAD, :] = out[:, k * tile : (k + 1) * tile]

    over_windows(
        kv_ref.shape[0], rows, tile, first_row,
        lambda wins: over_groups(heads // step, step, functools.partial(body, wins)),
    )


def attend_back_kernel(
    rows, step, start_ref, q_ref, do_ref, o_ref, lse_ref, kv_ref, kvt_ref, bias_ref, cos_ref, sin_ref,
    dq_ref, dkv_ref, dk_acc, dv_acc,
):
    tile = q_ref.shape[1]
    heads = q_ref.shape[0] // HEAD
    first_row = start_ref[0] + pl.program_id(0) * tile

    @pl.when(pl.program_id(0) == 0)
    def _():
        dk_acc[...] = jnp.zeros_like(dk_acc)
        dv_acc[...] = jnp.zeros_like(dv_acc)

    def body(wins, group, lanes):
        head = group * step
        cos, sin = cos_ref[...], sin_ref[...]
        q = turned_beside(q_ref, cos, sin, head, step)
        do = beside(do_ref, head, step)
        out = beside(o_ref, head, step)
        lse = lse_ref[group, 0]
        delta = jnp.sum(do.astype(F32) * out.astype(F32), 0, keepdims=True)
        dq = jnp.zeros((HEAD, step * tile), F32)
        for win, mask in wins:
            score = dot_f32(kv_ref[win, :HEAD], q, 1, 0)
            p = jnp.exp((masked(score, bias_ref, win, step) if mask else score) - lse)
            dp = dot_f32(kv_ref[win, HEAD:], do, 1, 0)
            ds = (p * (dp - delta)).astype(BF)
            dk_acc[win, :] += dot_f32(ds, q, 1, 1)
            dv_acc[win, :] += dot_f32(p.astype(BF), do, 1, 1)
            dq = dq + dot_f32(kvt_ref[:HEAD, win], ds, 1, 0)
        dq = dq * HEAD**-0.5
        turned = []
        for k in range(step):
            first = dq[:HALF, k * tile : (k + 1) * tile]
            second = dq[HALF:, k * tile : (k + 1) * tile]
            turned += [first * cos + second * sin, second * cos - first * sin]
        dq_ref[:, lanes] = jnp.concatenate(turned, axis=0).T.astype(BF)

    over_windows(
        kv_ref.shape[0], rows, tile, first_row,
        lambda wins: over_groups(heads // step, step, functools.partial(body, wins)),
    )

    @pl.when(pl.program_id(0) == pl.num_programs(0) - 1)
    def _():
        dkv_ref[...] = jnp.concatenate([dk_acc[...], dv_acc[...]], axis=1).astype(BF)


def row_tile(rows):
    return 128 if rows % 128 == 0 else rows


def attend(start, q_t, kv, kv_t, bias_t, cos_t, sin_t):
    width, rows = q_t.shape
    heads, tree_len, tile = width // HEAD, kv.shape[0], row_tile(rows)
    step = 2 if tile % 128 == 0 and heads % 2 == 0 else 1
    column = lambda i, s: (0, i)
    whole = lambda i, s: (0, 0)
    return pl.pallas_call(
        functools.partial(attend_kernel, rows, step),
        out_shape=(
            jax.ShapeDtypeStruct((width, rows), BF),
            jax.ShapeDtypeStruct((rows, width), BF),
            jax.ShapeDtypeStruct((heads // step, rows // tile, 1, step * tile), F32),
        ),
        grid_spec=pltpu.PrefetchScalarGridSpec(
            num_scalar_prefetch=1,
            grid=(rows // tile,),
            in_specs=[
                pl.BlockSpec((width, tile), column),
                pl.BlockSpec((tree_len, 2 * HEAD), whole),
                pl.BlockSpec((2 * HEAD, tree_len), whole),
                pl.BlockSpec((tree_len, tile), column),
                pl.BlockSpec((HALF, tile), column),
                pl.BlockSpec((HALF, tile), column),
            ],
            out_specs=(
                pl.BlockSpec((width, tile), column),
                pl.BlockSpec((tile, width), lambda i, s: (i, 0)),
                pl.BlockSpec((heads // step, 1, 1, step * tile), lambda i, s: (0, i, 0, 0)),
            ),
        ),
        compiler_params=pltpu.CompilerParams(vmem_limit_bytes=62 << 20),
        cost_estimate=NO_COST,
        name="attend",
    )(start, q_t, kv, kv_t, bias_t, cos_t, sin_t)


def attend_back(start, q_t, do_t, o_t, lse, kv, kv_t, bias_t, cos_t, sin_t):
    width, rows = q_t.shape
    heads, tree_len, tile = width // HEAD, kv.shape[0], row_tile(rows)
    step = 2 if tile % 128 == 0 and heads % 2 == 0 else 1
    column = lambda i, s: (0, i)
    whole = lambda i, s: (0, 0)
    return pl.pallas_call(
        functools.partial(attend_back_kernel, rows, step),
        out_shape=(
            jax.ShapeDtypeStruct((rows, width), BF),
            jax.ShapeDtypeStruct((tree_len, 2 * HEAD), BF),
        ),
        grid_spec=pltpu.PrefetchScalarGridSpec(
            num_scalar_prefetch=1,
            grid=(rows // tile,),
            in_specs=[
                pl.BlockSpec((width, tile), column),
                pl.BlockSpec((width, tile), column),
                pl.BlockSpec((width, tile), column),
                pl.BlockSpec((heads // step, 1, 1, step * tile), lambda i, s: (0, i, 0, 0)),
                pl.BlockSpec((tree_len, 2 * HEAD), whole),
                pl.BlockSpec((2 * HEAD, tree_len), whole),
                pl.BlockSpec((tree_len, tile), column),
                pl.BlockSpec((HALF, tile), column),
                pl.BlockSpec((HALF, tile), column),
            ],
            out_specs=(
                pl.BlockSpec((tile, width), lambda i, s: (i, 0)),
                pl.BlockSpec((tree_len, 2 * HEAD), whole),
            ),
            scratch_shapes=[pltpu.VMEM((tree_len, HEAD), F32), pltpu.VMEM((tree_len, HEAD), F32)],
        ),
        compiler_params=pltpu.CompilerParams(vmem_limit_bytes=62 << 20),
        cost_estimate=NO_COST,
        name="attend_back",
    )(start, q_t, do_t, o_t, lse, kv, kv_t, bias_t, cos_t, sin_t)


def layer_attention(normed, weights, tables):
    gains, w_attn, w_mlp, width, split, units = weights
    start, bias_t, cos_t, sin_t, cos_rows, sin_rows = tables
    q_t = dot_f32(w_attn[:, :width], normed, 0, 1)
    kv, kv_t = gather_rows(
        jnp.dot(normed, w_attn[:, width:split], preferred_element_type=F32), cos_rows, -sin_rows
    )
    o_t, o, lse = attend(start, q_t, kv, kv_t, bias_t, cos_t, sin_t)
    return (q_t, kv, kv_t, o_t, lse), o


def attention_backward(grad_attn, weights, tables, kept):
    gains, w_attn, w_mlp, width, split, units = weights
    start, bias_t, cos_t, sin_t, cos_rows, sin_rows = tables
    q_t, kv, kv_t, o_t, lse = kept
    do_t = dot_f32(w_attn[:, split : split + width], grad_attn, 0, 1).astype(BF)
    dq, dkv_part = attend_back(start, q_t, do_t, o_t, lse, kv, kv_t, bias_t, cos_t, sin_t)
    return dq, scatter_rows(dkv_part, cos_rows, sin_rows)


def layer_units(normed, weights):
    units = weights[-1]
    gate_up = jnp.dot(normed, weights[2][:, : 2 * units], preferred_element_type=F32)
    gate, up = gate_up[:, :units], gate_up[:, units:]
    return gate, up, (gate * jax.nn.sigmoid(gate) * up).astype(BF)


def units_backward(branch, weights, gate, up):
    units = weights[-1]
    d_inner = dot_f32(branch, weights[2][:, 2 * units :], 1, 0)
    sig = jax.nn.sigmoid(gate)
    d_gate = (d_inner * up * sig * (1.0 + gate * (1.0 - sig))).astype(BF)
    d_up = (d_inner * gate * sig).astype(BF)
    return d_gate, d_up


def reduce_gradient(x):
    return lax.psum_scatter(x, BOTH, scatter_dimension=0, tiled=True)


def shards(
    inputs, cotangent, seg_ids, positions, parents, gain_attn, w_query, key_weight, value_weight,
    w_out, gain_mlp, w_gate, w_up, w_down,
):
    sec = lax.axis_index("section")
    data = lax.axis_index("dp")
    sections = lax.axis_size("section")
    devices = lax.axis_size("dp")
    assert sections == 2 and inputs.shape[0] == 2
    first_core = sec == 0
    rows, model = inputs.shape[1], inputs.shape[2]
    swap = [(0, 1), (1, 0)]

    tree = lax.dynamic_index_in_dim(inputs, sec, 0, keepdims=False)
    hidden = tree.astype(F32)
    segments = lax.dynamic_index_in_dim(seg_ids, sec, 0, keepdims=False)
    places = lax.dynamic_index_in_dim(positions, sec, 0, keepdims=False)
    parent = lax.dynamic_index_in_dim(parents, sec, 0, keepdims=False)

    width, span, units = w_query.shape[2], key_weight.shape[2], w_gate.shape[2]
    split = width + 2 * span
    shard_list = (
        jnp.concatenate(
            [w_query[0], key_weight[0], value_weight[0], w_out[0].T, gain_attn.T, gain_mlp.T], 1
        ).astype(BF),
        jnp.concatenate([w_gate[0], w_up[0], w_down[0].T], 1).astype(BF),
    )
    halves = []
    for shard in shard_list:
        half = shard.shape[0] // 2
        low, high = shard[:half], shard[half:]
        got = lax.ppermute(jnp.where(first_core, high, low), "section", swap)
        halves.append((jnp.where(first_core, low, got), jnp.where(first_core, got, high)))
    def gathered(halves):
        return [lax.all_gather(half, BOTH, axis=0, tiled=True) for half in halves]

    def with_gains(w_attn, w_mlp):
        return (w_attn[:, split + width :].astype(F32).T, w_attn, w_mlp, width, split, units)

    (attn_zero, attn_one), (mlp_zero, mlp_one) = halves
    attn_zero = jnp.concatenate([attn_zero, attn_one[:, split + width : split + width + 1]], 1)
    attn_zero, mlp_zero = gathered((attn_zero, mlp_zero))
    cot = lax.dynamic_index_in_dim(cotangent, sec, 0, keepdims=False)
    attn_zero, cot = lax.optimization_barrier((attn_zero, cot))
    zero = with_gains(attn_zero, mlp_zero)
    attn_one, mlp_one = gathered((attn_one, mlp_one))

    seg_count = parent.shape[0]
    labels = jnp.arange(seg_count, dtype=jnp.int32)
    parent_hot = (parent[:, None] == labels[None, :]).astype(F32)
    ancestry = jnp.eye(seg_count, dtype=F32) + parent_hot + jnp.dot(parent_hot, parent_hot)
    ancestry = (ancestry > 0.5).astype(F32)
    row_start = data * rows
    seg_rows = lax.dynamic_slice_in_dim(segments, row_start, rows, 0)
    pos_rows = lax.dynamic_slice_in_dim(places, row_start, rows, 0)
    key_hot = (segments[:, None] == labels[None, :]).astype(F32)
    query_hot = (labels[:, None] == seg_rows[None, :]).astype(F32)
    reach = jnp.dot(key_hot, jnp.dot(ancestry.T, query_hot))
    allowed = (reach > 0.5) & (places[:, None] <= pos_rows[None, :])
    bias_t = jnp.where(allowed, 0.0, MASKED).astype(BF)
    frequency = THETA ** (-(jnp.arange(HALF, dtype=F32) * 2.0 / HEAD))
    angles = frequency[:, None] * pos_rows.astype(F32)[None, :]
    cos_t, sin_t = jnp.cos(angles), jnp.sin(angles)
    ones = jnp.ones((rows, HEAD), F32)
    cos_rows = jnp.concatenate([cos_t.T, cos_t.T, ones], 1)
    sin_rows = jnp.concatenate([sin_t.T, -sin_t.T, 0 * ones], 1)
    tables = (row_start.astype(jnp.int32).reshape(1), bias_t, cos_t, sin_t, cos_rows, sin_rows)

    split_out, split_down = split, 2 * units
    wide, narrow = (F32, BF), (BF, BF)
    back = (F32, BF, F32)

    normed_zero = (hidden * lax.rsqrt(jnp.mean(hidden * hidden, -1, keepdims=True) + EPSILON) * zero[0][:1]).astype(BF)
    kept_zero, o_zero = layer_attention(normed_zero, zero, tables)
    middle_zero, r_zero = product_sum(
        (o_zero, tree, zero[0]), ((0,), split_out, ("add", (1, (2, 1))), wide), zero[1], stagger=True, key=1
    )
    gate_zero, up_zero, inner_zero = layer_units(r_zero, zero)
    out_zero, normed_one = product_sum(
        (inner_zero, middle_zero, zero[0]), ((0,), split_down, ("add", (1, (2, 2))), narrow), zero[2], key=5
    )

    out_zero, normed_one, attn_one = lax.optimization_barrier((out_zero, normed_one, attn_one))
    one = with_gains(attn_one, mlp_one)
    kept_one, o_one = layer_attention(normed_one, one, tables)
    middle_one, r_one = product_sum(
        (o_one, out_zero, one[0]), ((0,), split_out, ("add", (1, (2, 1))), wide), one[1], key=2
    )
    gate_one, up_one, inner_one = layer_units(r_one, one)
    branch = cot
    d_gate, d_up = units_backward(branch, one, gate_one, up_one)
    grad_middle, grad_attn, d_gain_mlp_one, d_mlp_one = product_sum(
        ((d_gate, d_up), inner_one, middle_one, branch, r_one, one[0]), ((0,), 0, ("back", (2, 3, (5, 1))), back),
        one[2], ((4, (0,)), (3, (1,))), key=8,
    )
    g_mlp_one = reduce_gradient(d_mlp_one)
    dq, dkv = attention_backward(grad_attn, one, tables, kept_one)
    grad_one, branch, d_gain_attn_one, d_attn_one = product_sum(
        ((dq, dkv), out_zero, grad_middle, one[0], normed_one, grad_attn, o_one),
        ((0,), 0, ("back", (1, 2, (3, 0))), back),
        one[1], ((4, (0,)), (5, (6,))), key=7,
    )
    g_attn_one = reduce_gradient(d_attn_one)

    d_gate, d_up = units_backward(branch, zero, gate_zero, up_zero)
    grad_middle, grad_attn, d_gain_mlp_zero, d_mlp_zero = product_sum(
        ((d_gate, d_up), inner_zero, middle_zero, branch, r_zero, zero[0]),
        ((0,), 0, ("back", (2, 3, (5, 1))), back),
        zero[2], ((4, (0,)), (3, (1,))), key=9,
    )
    g_mlp_zero = reduce_gradient(d_mlp_zero)
    grad_attn, g_mlp_one = lax.optimization_barrier((grad_attn, g_mlp_one))
    dq, dkv = attention_backward(grad_attn, zero, tables, kept_zero)
    dq, g_attn_one = lax.optimization_barrier((dq, g_attn_one))
    grad_zero, send_zero, d_gain_attn_zero, d_attn_zero = product_sum(
        ((dq, dkv), tree, grad_middle, zero[0], normed_zero, grad_attn, o_zero),
        ((0,), 0, ("back", (1, 2, (3, 0))), back),
        zero[1], ((4, (0,)), (5, (6,))), key=11,
    )
    d_gain_attn_zero, d_gain_mlp_zero, d_gain_attn_one, d_gain_mlp_one = [
        jnp.sum(x, 0) for x in (d_gain_attn_zero, d_gain_mlp_zero, d_gain_attn_one, d_gain_mlp_one)
    ]
    d_gains = jnp.stack([d_gain_attn_zero, d_gain_mlp_zero, d_gain_attn_one, d_gain_mlp_one])
    d_gains = d_gains.reshape(2, 2, devices, -1).swapaxes(1, 2).reshape(2, devices, -1, 128)

    inner_one, send_zero = lax.optimization_barrier((inner_one, send_zero))
    out_one = product_sum(
        (inner_one, middle_one), ((0,), split_down, ("add", (1,)), (BF,)), one[2], key=6
    )
    ending = finish if devices == 4 else finish_apart
    g_attn_zero, g_gain, got_out, got_in, got_mlp, got_attn = ending(
        d_attn_zero, d_gains, out_zero, out_one, send_zero, branch,
        g_mlp_one, g_attn_one,
    )

    layer_output, input_grad, *grads = write_results(
        (out_zero, out_one, got_out), (grad_zero, grad_one, got_in), (g_attn_zero, g_attn_one, got_attn), width, span
    )
    input_grad, g_mlp_zero = lax.optimization_barrier((input_grad, g_mlp_zero))
    grads += write_mlp(
        g_mlp_zero, g_mlp_one, lax.ppermute(g_mlp_zero, "section", [(1, 0)]), got_mlp, units
    )
    g_query, g_key, g_value, g_out, g_gate, g_up, g_down = [grad[None] for grad in grads]
    g_gain = g_gain.reshape(2, 1, -1)
    return (
        layer_output[None], input_grad[None], g_gain[0], g_query, g_key, g_value, g_out, g_gain[1], g_gate, g_up, g_down,
    )


def solution(mesh):
    in_specs = (
        P(None, "dp", None),
        P(None, "dp", None),
        P(),
        P(),
        P(),
        P("section", "dp"),
        P("section", "dp", "tensor"),
        P("section", "dp", "tensor"),
        P("section", "dp", "tensor"),
        P("section", "tensor", "dp"),
        P("section", "dp"),
        P("section", "dp", "tensor"),
        P("section", "dp", "tensor"),
        P("section", "tensor", "dp"),
    )
    out_specs = (
        P("section", None, "dp", None),
        P("section", None, "dp", None),
        P("section", "dp"),
        P("section", "dp", "tensor"),
        P("section", "dp", "tensor"),
        P("section", "dp", "tensor"),
        P("section", "tensor", "dp"),
        P("section", "dp"),
        P("section", "dp", "tensor"),
        P("section", "dp", "tensor"),
        P("section", "tensor", "dp"),
    )
    return jax.shard_map(shards, mesh=mesh, in_specs=in_specs, out_specs=out_specs, check_vma=False)
```

```python
import functools

import jax
import jax.numpy as jnp
from jax import lax
from jax.experimental import pallas as pl
from jax.experimental.pallas import tpu as pltpu
from jax.sharding import PartitionSpec as P

HEAD = 64
HALF = HEAD // 2
TRUNK = 1024
GROUP = 384
EPSILON = 1e-05
THETA = 10000.0
MASKED = -1e30
BF = jnp.bfloat16
F32 = jnp.float32
MESH = pl.DeviceIdType.MESH
BOTH = ("dp", "section")


def dot_f32(a, b, ca, cb):
    return lax.dot_general(a, b, (((ca,), (cb,)), ((), ())), preferred_element_type=F32)


BLOCK = 256
PIECE = 128
NO_COST = pl.CostEstimate(flops=1, transcendentals=0, bytes_accessed=1)


def columns_of(i):
    return pl.ds(pl.multiple_of(i * PIECE, PIECE), PIECE)


def gain_row(arrays, place, at):
    return arrays[place[0]][place[1] : place[1] + 1, at]


def row_scale(squares, model):
    return lax.rsqrt(jnp.sum(squares, 1, keepdims=True) * (1.0 / model) + EPSILON)


def before_sum(job, arrays, keep):
    kind, places = job[2]
    if kind == "back":
        value = arrays[places[0]]
        model = value.shape[1]
        squares = jnp.zeros(keep.shape, F32)
        for i in range(model // PIECE):
            x = value[:, i * PIECE : (i + 1) * PIECE].astype(F32)
            squares += x * x
        keep[...] = jnp.broadcast_to(row_scale(squares, model), keep.shape)


def with_piece(job, i, total, arrays, outs, keep, sums):
    kind, places = job[2]
    at = columns_of(i)
    if kind == "add":
        y = (arrays[places[0]][:, at].astype(F32) + total).astype(outs[0].dtype)
        outs[0][:, at] = y
        if len(outs) > 1:
            sums[...] += y.astype(F32) * y.astype(F32)
    if kind == "back":
        product = total * arrays[places[0]][:, at].astype(F32) * keep[...]
        sums[...] += product * gain_row(arrays, places[2], at)
        outs[2][:, at] = jnp.sum(product.reshape(-1, 8, PIECE), 0)


def after_sum(job, rows, total, arrays, outs, keep, sums):
    kind, places = job[2]
    model = arrays[places[0]].shape[1]
    at = lambda i: slice(i * PIECE, (i + 1) * PIECE)
    if kind == "add" and len(outs) > 1:
        scale = row_scale(sums[rows], model)
        for i in range(model // PIECE):
            y = outs[0][rows, at(i)].astype(F32)
            outs[1][rows, at(i)] = (y * scale * gain_row(arrays, places[1], at(i))).astype(BF)
    if kind == "back":
        mean = jnp.sum(sums[rows], 1, keepdims=True) * (1.0 / model)
        scale = keep[rows]
        for i in range(model // PIECE):
            unit = arrays[places[0]][rows, at(i)].astype(F32) * scale
            grad = total(i)[rows].astype(F32) * gain_row(arrays, places[2], at(i))
            out = arrays[places[1]][rows, at(i)].astype(F32) + scale * (grad - unit * mean)
            outs[0][rows, at(i)] = out
            outs[1][rows, at(i)] = out.astype(BF)


def product_sum_kernel(cfg, *refs):
    n_join, n_arrays, job, sides, stagger = cfg
    xs, first_column = job[:2]
    refs = list(refs)
    take = lambda n: [refs.pop(0) for _ in range(n)]
    joined = take(n_join)
    from_hbm = [None, *take(n_arrays - 1)]
    (w_hbm,) = take(1)
    outs_hbm = take(len(job[3]))
    (g_hbm,) = take(1) if sides else (None,)
    arrays = take(n_arrays)
    outs = take(len(job[3]))
    load_sem, out_sem, w_buf, p_buf, a_buf, b_buf, w_sem, sa, ra, sb, rb, sc, rc, turn, keep, sums = take(16)
    g_buf, g_sem = take(2) if sides else (None, None)
    per_block = BLOCK // PIECE
    pieces = p_buf.shape[0]
    blocks = pieces // per_block
    n_rows = p_buf.shape[1]
    early = len(xs)
    lag = 2
    assert xs[0] == 0

    t = lax.axis_index("tensor")
    sec = lax.axis_index("section")
    dat = lax.axis_index("dp")
    inner = (t == 1) | (t == 2)
    outer = jnp.logical_not(inner)
    pair = (sec, t + 1 - 2 * lax.rem(t, 2), dat)
    mid = (sec, 3 - t, dat)
    mate = (1 - sec, t, dat)

    def columns(j):
        return pl.ds(pl.multiple_of(j * BLOCK, BLOCK), BLOCK)

    def to_inner(i):
        return pltpu.make_async_remote_copy(
            p_buf.at[i], a_buf.at[i], sa.at[i], ra.at[i], device_id=pair, device_id_type=MESH
        )

    def across(i):
        return pltpu.make_async_remote_copy(
            p_buf.at[i], b_buf.at[i], sb.at[i], rb.at[i], device_id=mid, device_id_type=MESH
        )

    def to_outer(i):
        return pltpu.make_async_remote_copy(
            b_buf.at[i], b_buf.at[i], sc.at[i], rc.at[i], device_id=pair, device_id_type=MESH
        )

    def load(k):
        return pltpu.make_async_copy(from_hbm[k], arrays[k], load_sem.at[k])

    def join():
        copies, start = [], 0
        for m, src in enumerate(joined):
            at = pl.ds(start, src.shape[1])
            copies.append(pltpu.make_async_copy(src, arrays[0].at[:, at], load_sem.at[n_arrays + m]))
            start += src.shape[1]
        return copies

    def fetch(j, slot):
        return pltpu.make_async_copy(
            w_hbm.at[columns(j), pl.ds(first_column, w_buf.shape[2])], w_buf.at[slot], w_sem.at[slot]
        )

    def flush(j, slot):
        return pltpu.make_async_copy(g_buf.at[slot], g_hbm.at[columns(j), :], g_sem.at[slot])

    def every_piece(body):
        def turn_of(i, _):
            body(i)
            return 0

        lax.fori_loop(0, pieces, turn_of, 0)

    for copy in join():
        copy.start()
    for k in range(1, early):
        load(k).start()
    fetch(0, 0).start()
    for k in range(early, n_arrays):
        load(k).start()
    barrier = pltpu.get_barrier_semaphore()
    pl.semaphore_signal(barrier, inc=1, device_id=pair, device_id_type=MESH)
    sums[...] = jnp.zeros_like(sums)

    @pl.when(inner)
    def _():
        pl.semaphore_signal(barrier, inc=1, device_id=mid, device_id_type=MESH)
        pl.semaphore_wait(barrier, 2)

    @pl.when(outer)
    def _():
        if stagger:
            pl.semaphore_signal(barrier, inc=1, device_id=mate, device_id_type=MESH)
            pl.semaphore_wait(barrier, 2)

            @pl.when(sec == 1)
            def _():
                pl.semaphore_wait(turn, 1)

        else:
            pl.semaphore_wait(barrier, 1)

    for copy in join():
        copy.wait()
    for k in range(1, early):
        load(k).wait()

    def done(i):
        with_piece(job, i, b_buf[i].astype(F32), arrays, outs, keep, sums)

    def first(i):
        to_inner(i).wait_recv()
        p_buf[i] = p_buf[i] + a_buf[i]
        across(i).start()

    def second(i):
        across(i).wait_recv()
        b_buf[i] = p_buf[i] + b_buf[i]
        to_outer(i).start()
        done(i)

    def side(j):
        slot = lax.rem(j, 2)

        @pl.when(j >= 2)
        def _():
            flush(j - 2, slot).wait()

        start = 0
        for a, bs in sides:
            a_t = arrays[a][:, columns(j)].T
            for b in bs:
                width = arrays[b].shape[1]
                g_buf[slot, :, start : start + width] = jnp.dot(
                    a_t, arrays[b][...], preferred_element_type=F32
                ).astype(BF)
                start += width
        flush(j, slot).start()
        return 0

    def step(j, _):
        slot = lax.rem(j, 2)
        fetch(j, slot).wait()

        @pl.when(j + 1 < blocks)
        def _():
            fetch(j + 1, 1 - slot).start()

        total, start = None, 0
        for x in xs:
            width = arrays[x].shape[1]
            term = dot_f32(arrays[x][...], w_buf[slot, :, start : start + width], 1, 1)
            total = term if total is None else total + term
            start += width
        total = total.astype(BF)
        for u in range(per_block):
            p_buf[per_block * j + u] = total[:, u * PIECE : (u + 1) * PIECE]

        @pl.when(outer)
        def _():
            for u in range(per_block):
                to_inner(per_block * j + u).start()

        @pl.when(j == 1)
        def _():
            for k in range(early, n_arrays):
                load(k).wait()
            before_sum(job, arrays, keep)

        if sides:

            @pl.when(j >= lag)
            def _():
                side(j - lag)

        @pl.when(inner)
        def _():
            for u in range(per_block):
                i = per_block * j + u
                first(i)

                @pl.when(j >= 1)
                def _():
                    second(i - per_block)

        return 0

    lax.fori_loop(0, blocks, step, 0)

    @pl.when(inner)
    def _():
        for u in range(per_block):
            second(pieces - per_block + u)

    if stagger:

        @pl.when(outer)
        def _():
            every_piece(lambda i: to_inner(i).wait_send())

            @pl.when(sec == 0)
            def _():
                pl.semaphore_signal(turn, inc=1, device_id=mate, device_id_type=MESH)

    if sides:
        lax.fori_loop(blocks - lag, blocks, lambda j, _: side(j), 0)

    @pl.when(outer)
    def _():
        if not stagger:
            every_piece(lambda i: to_inner(i).wait_send())

        def arrive(i):
            to_outer(i).wait_recv()
            done(i)

        every_piece(arrive)

    chunks = 5 if n_rows % (5 * 32) == 0 else 1
    chunk = n_rows // chunks
    block = 32 if chunk % 32 == 0 else 16
    height = lambda m: 8 if job[2][0] == "back" and m == 2 else n_rows
    stores = []

    def store(m, rows):
        copy = pltpu.make_async_copy(outs[m].at[rows], outs_hbm[m].at[rows], out_sem.at[len(stores)])
        copy.start()
        stores.append(copy)

    for c in range(chunks):

        def turn_rows(r, _):
            rows = pl.ds(pl.multiple_of(c * chunk + r * block, block), block)
            after_sum(job, rows, lambda i: b_buf.at[i], arrays, outs, keep, sums)
            return 0

        if job[2][0] == "back" or len(outs) > 1:
            lax.fori_loop(0, chunk // block, turn_rows, 0)
        for m in range(len(outs)):
            if height(m) == n_rows:
                store(m, pl.ds(c * chunk, chunk))
    for m in range(len(outs)):
        if height(m) != n_rows:
            store(m, pl.ds(0, height(m)))

    @pl.when(inner)
    def _():
        def sent(i):
            across(i).wait_send()
            to_outer(i).wait_send()

        every_piece(sent)

    if sides:
        flush(blocks - 2, (blocks - 2) % 2).wait()
        flush(blocks - 1, (blocks - 1) % 2).wait()
    for copy in stores:
        copy.wait()


def product_sum(arrays, job, weights, sides=(), stagger=False, key=1):
    assert lax.axis_size("tensor") == 4
    first = arrays[0] if isinstance(arrays[0], tuple) else (arrays[0],)
    given = (*first, *arrays[1:])
    rows, model = first[0].shape[0], weights.shape[0]
    arrays = (jax.ShapeDtypeStruct((rows, sum(x.shape[1] for x in first)), BF), *arrays[1:])
    pieces = model // PIECE
    depth = sum(arrays[x].shape[1] for x in job[0])
    anywhere = pl.BlockSpec(memory_space=pl.ANY)
    buf = pltpu.VMEM((pieces, rows, PIECE), BF)
    sem = pltpu.SemaphoreType.DMA((pieces,))
    two = pltpu.SemaphoreType.DMA((2,))
    out_shape = []
    for m, dtype in enumerate(job[3]):
        height = 8 if job[2][0] == "back" and m == 2 else rows
        out_shape.append(jax.ShapeDtypeStruct((height, model), dtype))
    scratch = [pltpu.VMEM(x.shape, x.dtype) for x in (*arrays, *out_shape)]
    scratch += [pltpu.SemaphoreType.DMA((len(arrays) + len(first),)), pltpu.SemaphoreType.DMA((16,))]
    scratch += [pltpu.VMEM((2, BLOCK, depth), BF), buf, buf, buf, two, *[sem] * 6, pltpu.SemaphoreType.REGULAR]
    scratch += [pltpu.VMEM((rows, PIECE), F32)] * 2
    if sides:
        side_width = sum(arrays[b].shape[1] for _, bs in sides for b in bs)
        out_shape.append(jax.ShapeDtypeStruct((model, side_width), BF))
        scratch += [pltpu.VMEM((2, BLOCK, side_width), BF), two]
    out = pl.pallas_call(
        functools.partial(product_sum_kernel, (len(first), len(arrays), job, tuple(sides), stagger)),
        out_shape=out_shape,
        in_specs=[anywhere] * (len(given) + 1),
        out_specs=[anywhere] * len(out_shape),
        scratch_shapes=scratch,
        compiler_params=pltpu.CompilerParams(
            collective_id=key, has_side_effects=True, vmem_limit_bytes=62 << 20
        ),
        cost_estimate=NO_COST,
        name=f"product_sum_{key}",
    )(*given, weights)
    return out if len(out) > 1 else out[0]


def dp_peers(count):
    me = lax.axis_index("dp")
    sec, t = lax.axis_index("section"), lax.axis_index("tensor")
    others = [lax.rem(me + k, count) for k in range(1, count)]
    return me, others, [(sec, t, other) for other in others]


def greet(ids):
    barrier = pltpu.get_barrier_semaphore()
    for device in ids:
        pl.semaphore_signal(barrier, inc=1, device_id=device, device_id_type=MESH)
    pl.semaphore_wait(barrier, len(ids))


def turn_rows(x, cos_ref, sin_ref):
    lane = lax.broadcasted_iota(jnp.int32, x.shape, 1)
    width = x.shape[1]
    partner = jnp.where(lane < HALF, pltpu.roll(x, width - HALF, 1), pltpu.roll(x, HALF, 1))
    return x * cos_ref[...] + partner * sin_ref[...]


def gather_kernel(
    count, normed_ref, w_hbm, cos_ref, sin_ref, o_ref, t_ref, q_ref, x_ref, w_buf, load_sem, send, recv
):
    me, _, ids = dp_peers(count)
    load = pltpu.make_async_copy(w_hbm.at[:, pl.ds(0, w_buf.shape[1])], w_buf, load_sem)
    load.start()
    load.wait()
    width = q_ref.shape[0]
    raw = jnp.dot(normed_ref[...], w_buf[:, width:], preferred_element_type=F32)
    x_ref[...] = turn_rows(raw, cos_ref, sin_ref).astype(BF)
    greet(ids)
    copies = [
        pltpu.make_async_remote_copy(
            x_ref, o_ref.at[me], send.at[k], recv.at[k], device_id=device, device_id_type=MESH
        )
        for k, device in enumerate(ids)
    ]
    for copy in copies:
        copy.start()
    o_ref[me] = x_ref[...]
    q_ref[...] = jnp.dot(normed_ref[...], w_buf[:, :width], preferred_element_type=F32).T
    for copy in copies:
        copy.wait()
    t_ref[...] = o_ref[...].reshape(t_ref.shape[1], t_ref.shape[0]).T


def scatter_kernel(count, x_ref, cos_ref, sin_ref, o_ref, buf, send, recv):
    me, others, ids = dp_peers(count)
    greet(ids)
    copies = [
        pltpu.make_async_remote_copy(
            x_ref.at[others[k]], buf.at[k], send.at[k], recv.at[k], device_id=device, device_id_type=MESH
        )
        for k, device in enumerate(ids)
    ]
    for copy in copies:
        copy.start()
    total = x_ref[me].astype(F32)
    for k, copy in enumerate(copies):
        copy.wait()
        total = total + buf[k].astype(F32)
    o_ref[...] = turn_rows(total, cos_ref, sin_ref).astype(BF)


def gather_rows(normed, w_attn, width, split, cos_rows, sin_rows, key):
    count = lax.axis_size("dp")
    rows, span = normed.shape[0], split - width
    in_vmem = pl.BlockSpec(memory_space=pltpu.VMEM)
    sem = pltpu.SemaphoreType.DMA((count - 1,))
    out, out_t, q_t = pl.pallas_call(
        functools.partial(gather_kernel, count),
        out_shape=(
            jax.ShapeDtypeStruct((count, rows, span), BF),
            jax.ShapeDtypeStruct((span, count * rows), BF),
            jax.ShapeDtypeStruct((width, rows), F32),
        ),
        in_specs=[in_vmem, pl.BlockSpec(memory_space=pl.ANY), in_vmem, in_vmem],
        out_specs=(in_vmem, in_vmem, in_vmem),
        scratch_shapes=[
            pltpu.VMEM((rows, span), BF), pltpu.VMEM((normed.shape[1], split), BF),
            pltpu.SemaphoreType.DMA, sem, sem,
        ],
        compiler_params=pltpu.CompilerParams(
            collective_id=key, has_side_effects=True, vmem_limit_bytes=40 << 20
        ),
        cost_estimate=NO_COST,
        name="gather_rows",
    )(normed, w_attn, cos_rows, sin_rows)
    return out.reshape(-1, span), out_t, q_t


def scatter_rows(x, cos_rows, sin_rows):
    count = lax.axis_size("dp")
    rows, width = x.shape[0] // count, x.shape[1]
    in_vmem = pl.BlockSpec(memory_space=pltpu.VMEM)
    sem = pltpu.SemaphoreType.DMA((count - 1,))
    return pl.pallas_call(
        functools.partial(scatter_kernel, count),
        out_shape=jax.ShapeDtypeStruct((rows, width), BF),
        in_specs=[in_vmem] * 3,
        out_specs=in_vmem,
        scratch_shapes=[pltpu.VMEM((count - 1, rows, width), x.dtype), sem, sem],
        compiler_params=pltpu.CompilerParams(collective_id=4, has_side_effects=True),
        cost_estimate=NO_COST,
        name="scatter_rows",
    )(x.reshape(count, rows, width), cos_rows, sin_rows)


def finish_kernel(
    g_hbm, gain_ref, out_zero, out_one, in_zero, in_one, mlp_one, attn_one,
    o_ref, gain_out, got_out, got_in, got_mlp, got_attn,
    mine, away, got, xs, ys, xr, yr, gains, load_sem, send, recv, mate_send, mate_recv, gain_send, gain_recv,
):
    sec, t, dat = lax.axis_index("section"), lax.axis_index("tensor"), lax.axis_index("dp")
    flip_x = dat + 1 - 2 * lax.rem(dat, 2)
    flip_y = lax.rem(dat + 2, 4)
    across = lax.rem(flip_x + 2, 4)
    by_x, by_y, mate = (sec, t, flip_x), (sec, t, flip_y), (1 - sec, t, dat)
    peers = [
        mate, by_x, by_y, (sec, t, across),
        (1 - sec, t, flip_x), (1 - sec, t, flip_y), (1 - sec, t, across),
    ]
    rows = g_hbm.shape[1] // 2
    upper, lower = pl.ds(0, rows), pl.ds(rows, rows)
    order = (across, flip_x, flip_y, dat)
    loads = []
    for k, block in enumerate(order):
        loads.append(pltpu.make_async_copy(g_hbm.at[2 * block + 1 - sec], away.at[k], load_sem.at[k]))
        loads.append(pltpu.make_async_copy(g_hbm.at[2 * block + sec], mine.at[k], load_sem.at[4 + k]))
    for copy in loads:
        copy.start()
    greet(peers)

    def remote(src, dst, k, device):
        return pltpu.make_async_remote_copy(
            src, dst, send.at[k], recv.at[k], device_id=device, device_id_type=MESH
        )

    def to_mate(src, dst, k):
        return pltpu.make_async_remote_copy(
            src, dst, mate_send.at[k], mate_recv.at[k], device_id=mate, device_id_type=MESH
        )

    swaps = [remote(away.at[k], got.at[k], k, mate) for k in range(4)]
    for k in range(4):
        loads[2 * k].wait()
        swaps[k].start()
    gain_copies = [
        pltpu.make_async_remote_copy(
            gain_ref.at[peer[0], peer[2]], gains.at[k], gain_send.at[k], gain_recv.at[k],
            device_id=peer, device_id_type=MESH,
        )
        for k, peer in enumerate(peers)
    ]
    for copy in gain_copies:
        copy.start()
    outs = []
    for k in range(4):
        loads[2 * k + 1].wait()
        swaps[k].wait_recv()
        mine[k] = (mine[k].astype(F32) + got[k].astype(F32)).astype(BF)
        if k == 0:
            outs += [remote(mine.at[0, upper], xs.at[0], 4, by_x), remote(mine.at[0, lower], ys.at[0], 5, by_y)]
        if k == 1:
            outs += [remote(mine.at[1, upper], xs.at[1], 6, by_x)]
        if k == 2:
            outs += [remote(mine.at[2, lower], ys.at[1], 7, by_y)]
        for copy in outs[-(2 if k == 0 else 1) :]:
            if k < 3:
                copy.start()

    @pl.when(sec == 0)
    def _():
        to_mate(in_one, got_in, 0).start()
        to_mate(out_one, got_out, 1).start()
        to_mate(mlp_one, got_mlp, 2).start()
        to_mate(attn_one, got_attn, 3).start()

    @pl.when(sec == 1)
    def _():
        to_mate(in_zero, got_in, 0).start()
        to_mate(out_zero, got_out, 1).start()

    outs[0].wait_recv()
    mine[2, upper] = (mine[2, upper].astype(F32) + xs[0].astype(F32)).astype(BF)
    outs.append(remote(mine.at[2, upper], yr, 8, by_y))
    outs[4].start()
    outs[1].wait_recv()
    mine[1, lower] = (mine[1, lower].astype(F32) + ys[0].astype(F32)).astype(BF)
    outs.append(remote(mine.at[1, lower], xr, 9, by_x))
    outs[5].start()
    total = gain_ref[sec, dat]
    for k, copy in enumerate(gain_copies):
        copy.wait()
        total = total + gains[k]
    gain_out[...] = total
    outs[2].wait_recv()
    outs[3].wait_recv()
    outs[4].wait_recv()
    o_ref[upper] = (mine[3, upper].astype(F32) + xs[1].astype(F32) + yr[...].astype(F32)).astype(BF)
    outs[5].wait_recv()
    o_ref[lower] = (mine[3, lower].astype(F32) + ys[1].astype(F32) + xr[...].astype(F32)).astype(BF)

    @pl.when(sec == 1)
    def _():
        to_mate(o_ref, got_attn, 3).start()

    for copy in swaps + outs:
        copy.wait_send()
    to_mate(in_one, got_in, 0).wait()
    to_mate(out_one, got_out, 1).wait()
    to_mate(attn_one, got_attn, 3).wait()

    @pl.when(sec == 0)
    def _():
        to_mate(mlp_one, got_mlp, 2).wait_send()

    @pl.when(sec == 1)
    def _():
        to_mate(mlp_one, got_mlp, 2).wait_recv()


def finish(g, gains, out_zero, out_one, in_zero, in_one, mlp_one, attn_one):
    rows, width = g.shape[0] // 8, g.shape[1]
    part = pltpu.VMEM((2, rows // 2, width), BF)
    whole = pltpu.VMEM((4, rows, width), BF)
    end = pltpu.VMEM((rows // 2, width), BF)
    in_vmem, anywhere = pl.BlockSpec(memory_space=pltpu.VMEM), pl.BlockSpec(memory_space=pl.ANY)
    like = lambda x: jax.ShapeDtypeStruct(x.shape, x.dtype)
    dma = lambda n: pltpu.SemaphoreType.DMA((n,))
    return pl.pallas_call(
        finish_kernel,
        out_shape=(
            jax.ShapeDtypeStruct((rows, width), BF),
            jax.ShapeDtypeStruct(gains.shape[2:], F32),
            like(out_zero), like(in_zero), like(mlp_one), like(attn_one),
        ),
        in_specs=[anywhere, in_vmem, *[anywhere] * 6],
        out_specs=(in_vmem, in_vmem, *[anywhere] * 4),
        scratch_shapes=[
            whole, whole, whole, part, part, end, end, pltpu.VMEM((7, *gains.shape[2:]), F32),
            dma(8), dma(10), dma(10), dma(4), dma(4), dma(7), dma(7),
        ],
        compiler_params=pltpu.CompilerParams(
            collective_id=12, has_side_effects=True, vmem_limit_bytes=62 << 20
        ),
        cost_estimate=NO_COST,
        name="finish",
    )(g.reshape(8, rows, width), gains, out_zero, out_one, in_zero, in_one, mlp_one, attn_one)


def finish_apart(g, gains, out_zero, out_one, in_zero, in_one, mlp_one, attn_one):
    first_core = lax.axis_index("section") == 0
    half = reduce_gradient(g)
    swap = lambda zero, one: lax.ppermute(jnp.where(first_core, one, zero), "section", [(0, 1), (1, 0)])
    return (
        half, share_sums(gains), swap(out_zero, out_one), swap(in_zero, in_one),
        lax.ppermute(mlp_one, "section", [(0, 1)]), swap(half, attn_one),
    )


def in_rows(count, block, body):
    def turn(r, _):
        body(pl.ds(pl.multiple_of(r * block, block), block))
        return 0

    lax.fori_loop(0, count // block, turn, 0)


def widen_turned(dst, src, start, width):
    for c in range(0, width, 128):
        dst[c : c + 128] = src[:, start + c : start + c + 128].astype(F32).T


def write_mlp_kernel(
    zero, one, from_one, from_zero, gate_hbm, up_hbm, down_hbm, mlp, gate_buf, up_buf, down_buf, load_sem, store_sem
):
    sec = lax.axis_index("section")
    half, units = zero.shape[0], gate_buf.shape[1]
    low, high = pl.ds(0, half), pl.ds(half, half)
    load = lambda src, at, k: pltpu.make_async_copy(src, mlp.at[at], load_sem.at[k])
    store = lambda src, dst, k: pltpu.make_async_copy(src, dst, store_sem.at[k])

    @pl.when(sec == 0)
    def _():
        load(zero, low, 0).start()
        load(from_one, high, 1).start()

    @pl.when(sec == 1)
    def _():
        load(from_zero, low, 0).start()
        load(one, high, 1).start()

    load(zero, low, 0).wait()
    load(zero, high, 1).wait()

    def gates(rows):
        gate_buf[rows] = mlp[rows, :units].astype(F32)
        up_buf[rows] = mlp[rows, units : 2 * units].astype(F32)

    in_rows(2 * half, 32, gates)
    stores = [store(gate_buf, gate_hbm, 0), store(up_buf, up_hbm, 1), store(down_buf, down_hbm, 2)]
    stores[0].start()
    stores[1].start()
    widen_turned(down_buf, mlp, 2 * units, units)
    stores[2].start()
    for copy in stores:
        copy.wait()


def write_mlp(zero, one, from_one, from_zero, units):
    shard = 2 * zero.shape[0]
    anywhere = pl.BlockSpec(memory_space=pl.ANY)
    shapes = [(shard, units), (shard, units), (units, shard)]
    return pl.pallas_call(
        write_mlp_kernel,
        out_shape=[jax.ShapeDtypeStruct(shape, F32) for shape in shapes],
        in_specs=[anywhere] * 4,
        out_specs=[anywhere] * 3,
        scratch_shapes=[
            pltpu.VMEM((shard, zero.shape[1]), BF),
            *[pltpu.VMEM(shape, F32) for shape in shapes],
            pltpu.SemaphoreType.DMA((2,)),
            pltpu.SemaphoreType.DMA((3,)),
        ],
        compiler_params=pltpu.CompilerParams(vmem_limit_bytes=62 << 20),
        cost_estimate=NO_COST,
        name="write_mlp",
    )(zero, one, from_one, from_zero)


def write_kernel(
    split, out_zero, out_one, got_out, in_zero, in_one, got_in, attn_zero, attn_one, got_attn,
    out_hbm, in_hbm, q_hbm, k_hbm, v_hbm, o_hbm,
    outs, wides, attn, narrow, q_buf, k_buf, v_buf, o_buf, load_sem, store_sem,
):
    sec = lax.axis_index("section")
    half = attn_zero.shape[0]
    low, high = pl.ds(0, half), pl.ds(half, half)
    load = lambda src, dst, k: pltpu.make_async_copy(src, dst, load_sem.at[k])
    store = lambda src, dst, k: pltpu.make_async_copy(src, dst, store_sem.at[k])

    def start(own_out, own_in, attn_low, attn_high):
        load(own_out, outs.at[0], 0).start()
        load(own_in, wides.at[0], 1).start()
        load(attn_low, attn.at[low], 2).start()
        load(attn_high, attn.at[high], 3).start()

    @pl.when(sec == 0)
    def _():
        start(out_zero, in_zero, attn_zero, got_attn)

    @pl.when(sec == 1)
    def _():
        start(out_one, in_one, got_attn, attn_one)

    load(got_in, narrow, 4).start()
    load(got_out, outs.at[1], 5).start()
    stores = [
        store(outs.at[0], out_hbm.at[sec], 0),
        store(wides.at[0], in_hbm.at[sec], 1),
        store(outs.at[1], out_hbm.at[1 - sec], 2),
        store(wides.at[1], in_hbm.at[1 - sec], 3),
        store(q_buf, q_hbm, 4),
        store(k_buf, k_hbm, 5),
        store(v_buf, v_hbm, 6),
        store(o_buf, o_hbm, 7),
    ]
    load(out_zero, outs.at[0], 0).wait()
    stores[0].start()
    load(in_zero, wides.at[0], 1).wait()
    stores[1].start()
    width, span = q_buf.shape[1], k_buf.shape[1]
    load(attn_one, attn.at[low], 2).wait()
    load(attn_one, attn.at[high], 3).wait()

    def projections(rows):
        q_buf[rows] = attn[rows, :width].astype(F32)
        k_buf[rows] = attn[rows, width : width + span].astype(F32)
        v_buf[rows] = attn[rows, width + span : split].astype(F32)

    in_rows(2 * half, 32, projections)
    for k in (4, 5, 6):
        stores[k].start()
    widen_turned(o_buf, attn, split, width)
    stores[7].start()
    load(got_in, narrow, 4).wait()

    def widen(rows):
        wides[1, rows] = narrow[rows].astype(F32)

    in_rows(narrow.shape[0], 32, widen)
    stores[3].start()
    load(got_out, outs.at[1], 5).wait()
    stores[2].start()
    for copy in stores:
        copy.wait()


def write_results(results, ins, attns, width, span):
    rows, model = results[0].shape
    shard = 2 * attns[0].shape[0]
    anywhere = pl.BlockSpec(memory_space=pl.ANY)
    shapes = [(shard, width), (shard, span), (shard, span), (width, shard)]
    return pl.pallas_call(
        functools.partial(write_kernel, width + 2 * span),
        out_shape=[
            jax.ShapeDtypeStruct((2, rows, model), BF),
            jax.ShapeDtypeStruct((2, rows, model), F32),
            *[jax.ShapeDtypeStruct(shape, F32) for shape in shapes],
        ],
        in_specs=[anywhere] * 9,
        out_specs=[anywhere] * 6,
        scratch_shapes=[
            pltpu.VMEM((2, rows, model), BF),
            pltpu.VMEM((2, rows, model), F32),
            pltpu.VMEM((shard, attns[0].shape[1]), BF),
            pltpu.VMEM((rows, model), BF),
            *[pltpu.VMEM(shape, F32) for shape in shapes],
            pltpu.SemaphoreType.DMA((6,)),
            pltpu.SemaphoreType.DMA((8,)),
        ],
        compiler_params=pltpu.CompilerParams(vmem_limit_bytes=62 << 20),
        cost_estimate=NO_COST,
        name="write_results",
    )(*results, *ins, *attns)


def share_kernel(count, x_ref, o_ref, buf, send, recv):
    sec, t, dat = lax.axis_index("section"), lax.axis_index("tensor"), lax.axis_index("dp")
    peers = [
        (lax.rem(sec + k // count, 2), t, lax.rem(dat + k % count, count)) for k in range(1, 2 * count)
    ]
    greet(peers)
    copies = [
        pltpu.make_async_remote_copy(
            x_ref.at[peer[0], peer[2]], buf.at[k], send.at[k], recv.at[k], device_id=peer, device_id_type=MESH
        )
        for k, peer in enumerate(peers)
    ]
    for copy in copies:
        copy.start()
    total = x_ref[sec, dat]
    for k, copy in enumerate(copies):
        copy.wait()
        total = total + buf[k]
    o_ref[...] = total


def share_sums(x):
    count = lax.axis_size("dp")
    in_vmem = pl.BlockSpec(memory_space=pltpu.VMEM)
    sem = pltpu.SemaphoreType.DMA((2 * count - 1,))
    return pl.pallas_call(
        functools.partial(share_kernel, count),
        out_shape=jax.ShapeDtypeStruct(x.shape[2:], F32),
        in_specs=[in_vmem],
        out_specs=in_vmem,
        scratch_shapes=[pltpu.VMEM((2 * count - 1, *x.shape[2:]), F32), sem, sem],
        compiler_params=pltpu.CompilerParams(collective_id=13, has_side_effects=True),
        cost_estimate=NO_COST,
        name="share_sums",
    )(x)


def group_start(first_row):
    past = lax.max(first_row - TRUNK, 0)
    return pl.multiple_of(TRUNK + GROUP * lax.div(past, GROUP), 128)


def over_windows(tree_len, rows, tile, first_row, run):
    if tile % 128 == 0 and GROUP % tile == 0 and TRUNK % tile == 0 and rows % tile == 0:
        run(((pl.ds(0, TRUNK), True), (pl.ds(group_start(first_row), GROUP), True)))
    else:
        run(((pl.ds(0, tree_len), True),))


def masked(scores, bias_ref, win, step):
    bias = bias_ref[win, :].astype(F32)
    return scores + (bias if step == 1 else jnp.concatenate([bias] * step, axis=1))


def head_rows(ref, head):
    return ref[head * HEAD : (head + 1) * HEAD, :]


def beside(ref, head, count):
    parts = [head_rows(ref, head + k) for k in range(count)]
    return parts[0] if count == 1 else jnp.concatenate(parts, axis=1)


def turned_beside(ref, cos, sin, head, count):
    parts = []
    for k in range(count):
        rows = head_rows(ref, head + k)
        first, second = rows[:HALF], rows[HALF:]
        parts.append(jnp.concatenate([first * cos - second * sin, second * cos + first * sin], axis=0))
    whole = parts[0] if count == 1 else jnp.concatenate(parts, axis=1)
    return (whole.astype(BF).astype(F32) * HEAD**-0.5).astype(BF)


def as_rows(x, tile, count):
    parts = [x[:, k * tile : (k + 1) * tile] for k in range(count)]
    return (parts[0] if count == 1 else jnp.concatenate(parts, axis=0)).T


def over_groups(groups, step, body):
    for group in range(groups):
        body(group, slice(group * step * HEAD, (group + 1) * step * HEAD))


def attend_kernel(
    rows, step, start_ref, q_ref, kv_ref, kvt_ref, bias_ref, cos_ref, sin_ref, o_ref, on_ref, lse_ref
):
    tile = q_ref.shape[1]
    heads = q_ref.shape[0] // HEAD
    first_row = start_ref[0] + pl.program_id(0) * tile

    def body(wins, group, lanes):
        head = group * step
        q = turned_beside(q_ref, cos_ref[...], sin_ref[...], head, step)
        scores = []
        for win, mask in wins:
            score = dot_f32(kv_ref[win, :HEAD], q, 1, 0)
            scores.append(masked(score, bias_ref, win, step) if mask else score)
        top = functools.reduce(jnp.maximum, [jnp.max(s, 0, keepdims=True) for s in scores])
        expo = [jnp.exp(s - top) for s in scores]
        total = sum(jnp.sum(e, 0, keepdims=True) for e in expo)
        out = sum(dot_f32(kvt_ref[HEAD:, win], e.astype(BF), 1, 0) for (win, _), e in zip(wins, expo))
        out = out / total
        on_ref[:, lanes] = as_rows(out, tile, step).astype(BF)
        lse_ref[group, 0] = top + jnp.log(total)
        out = out.astype(BF)
        for k in range(step):
            o_ref[(head + k) * HEAD : (head + k + 1) * HEAD, :] = out[:, k * tile : (k + 1) * tile]

    over_windows(
        kv_ref.shape[0], rows, tile, first_row,
        lambda wins: over_groups(heads // step, step, functools.partial(body, wins)),
    )


def attend_back_kernel(
    rows, step, start_ref, q_ref, do_ref, o_ref, lse_ref, kv_ref, kvt_ref, bias_ref, cos_ref, sin_ref,
    dq_ref, dkv_ref, dk_acc, dv_acc,
):
    tile = q_ref.shape[1]
    heads = q_ref.shape[0] // HEAD
    first_row = start_ref[0] + pl.program_id(0) * tile

    @pl.when(pl.program_id(0) == 0)
    def _():
        dk_acc[...] = jnp.zeros_like(dk_acc)
        dv_acc[...] = jnp.zeros_like(dv_acc)

    def body(wins, group, lanes):
        head = group * step
        cos, sin = cos_ref[...], sin_ref[...]
        q = turned_beside(q_ref, cos, sin, head, step)
        do = beside(do_ref, head, step)
        out = beside(o_ref, head, step)
        lse = lse_ref[group, 0]
        delta = jnp.sum(do.astype(F32) * out.astype(F32), 0, keepdims=True)
        dq = jnp.zeros((HEAD, step * tile), F32)
        for win, mask in wins:
            score = dot_f32(kv_ref[win, :HEAD], q, 1, 0)
            p = jnp.exp((masked(score, bias_ref, win, step) if mask else score) - lse)
            dp = dot_f32(kv_ref[win, HEAD:], do, 1, 0)
            ds = (p * (dp - delta)).astype(BF)
            dk_acc[win, :] += dot_f32(ds, q, 1, 1)
            dv_acc[win, :] += dot_f32(p.astype(BF), do, 1, 1)
            dq = dq + dot_f32(kvt_ref[:HEAD, win], ds, 1, 0)
        dq = dq * HEAD**-0.5
        turned = []
        for k in range(step):
            first = dq[:HALF, k * tile : (k + 1) * tile]
            second = dq[HALF:, k * tile : (k + 1) * tile]
            turned += [first * cos + second * sin, second * cos - first * sin]
        dq_ref[:, lanes] = jnp.concatenate(turned, axis=0).T.astype(BF)

    over_windows(
        kv_ref.shape[0], rows, tile, first_row,
        lambda wins: over_groups(heads // step, step, functools.partial(body, wins)),
    )

    @pl.when(pl.program_id(0) == pl.num_programs(0) - 1)
    def _():
        dkv_ref[...] = jnp.concatenate([dk_acc[...], dv_acc[...]], axis=1).astype(BF)


def row_tile(rows):
    return 128 if rows % 128 == 0 else rows


def attend(start, q_t, kv, kv_t, bias_t, cos_t, sin_t):
    width, rows = q_t.shape
    heads, tree_len, tile = width // HEAD, kv.shape[0], row_tile(rows)
    step = 2 if tile % 128 == 0 and heads % 2 == 0 else 1
    column = lambda i, s: (0, i)
    whole = lambda i, s: (0, 0)
    return pl.pallas_call(
        functools.partial(attend_kernel, rows, step),
        out_shape=(
            jax.ShapeDtypeStruct((width, rows), BF),
            jax.ShapeDtypeStruct((rows, width), BF),
            jax.ShapeDtypeStruct((heads // step, rows // tile, 1, step * tile), F32),
        ),
        grid_spec=pltpu.PrefetchScalarGridSpec(
            num_scalar_prefetch=1,
            grid=(rows // tile,),
            in_specs=[
                pl.BlockSpec((width, tile), column),
                pl.BlockSpec((tree_len, 2 * HEAD), whole),
                pl.BlockSpec((2 * HEAD, tree_len), whole),
                pl.BlockSpec((tree_len, tile), column),
                pl.BlockSpec((HALF, tile), column),
                pl.BlockSpec((HALF, tile), column),
            ],
            out_specs=(
                pl.BlockSpec((width, tile), column),
                pl.BlockSpec((tile, width), lambda i, s: (i, 0)),
                pl.BlockSpec((heads // step, 1, 1, step * tile), lambda i, s: (0, i, 0, 0)),
            ),
        ),
        compiler_params=pltpu.CompilerParams(vmem_limit_bytes=62 << 20),
        cost_estimate=NO_COST,
        name="attend",
    )(start, q_t, kv, kv_t, bias_t, cos_t, sin_t)


def attend_back(start, q_t, do_t, o_t, lse, kv, kv_t, bias_t, cos_t, sin_t):
    width, rows = q_t.shape
    heads, tree_len, tile = width // HEAD, kv.shape[0], row_tile(rows)
    step = 2 if tile % 128 == 0 and heads % 2 == 0 else 1
    column = lambda i, s: (0, i)
    whole = lambda i, s: (0, 0)
    return pl.pallas_call(
        functools.partial(attend_back_kernel, rows, step),
        out_shape=(
            jax.ShapeDtypeStruct((rows, width), BF),
            jax.ShapeDtypeStruct((tree_len, 2 * HEAD), BF),
        ),
        grid_spec=pltpu.PrefetchScalarGridSpec(
            num_scalar_prefetch=1,
            grid=(rows // tile,),
            in_specs=[
                pl.BlockSpec((width, tile), column),
                pl.BlockSpec((width, tile), column),
                pl.BlockSpec((width, tile), column),
                pl.BlockSpec((heads // step, 1, 1, step * tile), lambda i, s: (0, i, 0, 0)),
                pl.BlockSpec((tree_len, 2 * HEAD), whole),
                pl.BlockSpec((2 * HEAD, tree_len), whole),
                pl.BlockSpec((tree_len, tile), column),
                pl.BlockSpec((HALF, tile), column),
                pl.BlockSpec((HALF, tile), column),
            ],
            out_specs=(
                pl.BlockSpec((tile, width), lambda i, s: (i, 0)),
                pl.BlockSpec((tree_len, 2 * HEAD), whole),
            ),
            scratch_shapes=[pltpu.VMEM((tree_len, HEAD), F32), pltpu.VMEM((tree_len, HEAD), F32)],
        ),
        compiler_params=pltpu.CompilerParams(vmem_limit_bytes=62 << 20),
        cost_estimate=NO_COST,
        name="attend_back",
    )(start, q_t, do_t, o_t, lse, kv, kv_t, bias_t, cos_t, sin_t)


def layer_attention(normed, weights, tables, key):
    gains, w_attn, w_mlp, width, split, units = weights
    start, bias_t, cos_t, sin_t, cos_rows, sin_rows = tables
    kv, kv_t, q_t = gather_rows(normed, w_attn, width, split, cos_rows, -sin_rows, key)
    o_t, o, lse = attend(start, q_t, kv, kv_t, bias_t, cos_t, sin_t)
    return (q_t, kv, kv_t, o_t, lse), o


def attention_backward(grad_attn, weights, tables, kept):
    gains, w_attn, w_mlp, width, split, units = weights
    start, bias_t, cos_t, sin_t, cos_rows, sin_rows = tables
    q_t, kv, kv_t, o_t, lse = kept
    do_t = dot_f32(w_attn[:, split : split + width], grad_attn, 0, 1).astype(BF)
    dq, dkv_part = attend_back(start, q_t, do_t, o_t, lse, kv, kv_t, bias_t, cos_t, sin_t)
    return dq, scatter_rows(dkv_part, cos_rows, sin_rows)


def layer_units(normed, weights):
    units = weights[-1]
    gate_up = jnp.dot(normed, weights[2][:, : 2 * units], preferred_element_type=F32)
    gate, up = gate_up[:, :units], gate_up[:, units:]
    return gate, up, (gate * jax.nn.sigmoid(gate) * up).astype(BF)


def units_backward(branch, weights, gate, up):
    units = weights[-1]
    d_inner = dot_f32(branch, weights[2][:, 2 * units :], 1, 0)
    sig = jax.nn.sigmoid(gate)
    d_gate = (d_inner * up * sig * (1.0 + gate * (1.0 - sig))).astype(BF)
    d_up = (d_inner * gate * sig).astype(BF)
    return d_gate, d_up


def reduce_gradient(x):
    return lax.psum_scatter(x, BOTH, scatter_dimension=0, tiled=True)


def shards(
    inputs, cotangent, seg_ids, positions, parents, gain_attn, w_query, key_weight, value_weight,
    w_out, gain_mlp, w_gate, w_up, w_down,
):
    sec = lax.axis_index("section")
    data = lax.axis_index("dp")
    sections = lax.axis_size("section")
    devices = lax.axis_size("dp")
    assert sections == 2 and inputs.shape[0] == 2
    first_core = sec == 0
    rows, model = inputs.shape[1], inputs.shape[2]
    swap = [(0, 1), (1, 0)]

    tree = lax.dynamic_index_in_dim(inputs, sec, 0, keepdims=False)
    hidden = tree.astype(F32)
    segments = lax.dynamic_index_in_dim(seg_ids, sec, 0, keepdims=False)
    places = lax.dynamic_index_in_dim(positions, sec, 0, keepdims=False)
    parent = lax.dynamic_index_in_dim(parents, sec, 0, keepdims=False)

    width, span, units = w_query.shape[2], key_weight.shape[2], w_gate.shape[2]
    split = width + 2 * span
    shard_list = (
        jnp.concatenate(
            [w_query[0], key_weight[0], value_weight[0], w_out[0].T, gain_attn.T, gain_mlp.T], 1
        ).astype(BF),
        jnp.concatenate([w_gate[0], w_up[0], w_down[0].T], 1).astype(BF),
    )
    halves = []
    for shard in shard_list:
        half = shard.shape[0] // 2
        low, high = shard[:half], shard[half:]
        got = lax.ppermute(jnp.where(first_core, high, low), "section", swap)
        halves.append((jnp.where(first_core, low, got), jnp.where(first_core, got, high)))
    def gathered(halves):
        return [lax.all_gather(half, BOTH, axis=0, tiled=True) for half in halves]

    def with_gains(w_attn, w_mlp):
        return (w_attn[:, split + width :].astype(F32).T, w_attn, w_mlp, width, split, units)

    (attn_zero, attn_one), (mlp_zero, mlp_one) = halves
    attn_zero = jnp.concatenate([attn_zero, attn_one[:, split + width : split + width + 1]], 1)
    attn_zero, mlp_zero = gathered((attn_zero, mlp_zero))
    cot = lax.dynamic_index_in_dim(cotangent, sec, 0, keepdims=False)
    attn_zero, cot = lax.optimization_barrier((attn_zero, cot))
    zero = with_gains(attn_zero, mlp_zero)
    attn_one, mlp_one = gathered((attn_one, mlp_one))

    seg_count = parent.shape[0]
    labels = jnp.arange(seg_count, dtype=jnp.int32)
    parent_hot = (parent[:, None] == labels[None, :]).astype(F32)
    ancestry = jnp.eye(seg_count, dtype=F32) + parent_hot + jnp.dot(parent_hot, parent_hot)
    ancestry = (ancestry > 0.5).astype(F32)
    row_start = data * rows
    seg_rows = lax.dynamic_slice_in_dim(segments, row_start, rows, 0)
    pos_rows = lax.dynamic_slice_in_dim(places, row_start, rows, 0)
    key_hot = (segments[:, None] == labels[None, :]).astype(F32)
    query_hot = (labels[:, None] == seg_rows[None, :]).astype(F32)
    reach = jnp.dot(key_hot, jnp.dot(ancestry.T, query_hot))
    allowed = (reach > 0.5) & (places[:, None] <= pos_rows[None, :])
    bias_t = jnp.where(allowed, 0.0, MASKED).astype(BF)
    frequency = THETA ** (-(jnp.arange(HALF, dtype=F32) * 2.0 / HEAD))
    angles = frequency[:, None] * pos_rows.astype(F32)[None, :]
    cos_t, sin_t = jnp.cos(angles), jnp.sin(angles)
    ones = jnp.ones((rows, HEAD), F32)
    cos_rows = jnp.concatenate([cos_t.T, cos_t.T, ones], 1)
    sin_rows = jnp.concatenate([sin_t.T, -sin_t.T, 0 * ones], 1)
    tables = (row_start.astype(jnp.int32).reshape(1), bias_t, cos_t, sin_t, cos_rows, sin_rows)

    split_out, split_down = split, 2 * units
    wide, narrow = (F32, BF), (BF, BF)
    back = (F32, BF, F32)

    normed_zero = (hidden * lax.rsqrt(jnp.mean(hidden * hidden, -1, keepdims=True) + EPSILON) * zero[0][:1]).astype(BF)
    kept_zero, o_zero = layer_attention(normed_zero, zero, tables, 3)
    middle_zero, r_zero = product_sum(
        (o_zero, tree, zero[0]), ((0,), split_out, ("add", (1, (2, 1))), wide), zero[1], stagger=True, key=1
    )
    gate_zero, up_zero, inner_zero = layer_units(r_zero, zero)
    out_zero, normed_one = product_sum(
        (inner_zero, middle_zero, zero[0]), ((0,), split_down, ("add", (1, (2, 2))), narrow), zero[2], key=5
    )

    out_zero, normed_one, attn_one = lax.optimization_barrier((out_zero, normed_one, attn_one))
    one = with_gains(attn_one, mlp_one)
    kept_one, o_one = layer_attention(normed_one, one, tables, 14)
    middle_one, r_one = product_sum(
        (o_one, out_zero, one[0]), ((0,), split_out, ("add", (1, (2, 1))), wide), one[1], key=2
    )
    gate_one, up_one, inner_one = layer_units(r_one, one)
    branch = cot
    d_gate, d_up = units_backward(branch, one, gate_one, up_one)
    grad_middle, grad_attn, d_gain_mlp_one, d_mlp_one = product_sum(
        ((d_gate, d_up), inner_one, middle_one, branch, r_one, one[0]), ((0,), 0, ("back", (2, 3, (5, 1))), back),
        one[2], ((4, (0,)), (3, (1,))), key=8,
    )
    g_mlp_one = reduce_gradient(d_mlp_one)
    dq, dkv = attention_backward(grad_attn, one, tables, kept_one)
    grad_one, branch, d_gain_attn_one, d_attn_one = product_sum(
        ((dq, dkv), out_zero, grad_middle, one[0], normed_one, grad_attn, o_one),
        ((0,), 0, ("back", (1, 2, (3, 0))), back),
        one[1], ((4, (0,)), (5, (6,))), key=7,
    )
    g_attn_one = reduce_gradient(d_attn_one)

    d_gate, d_up = units_backward(branch, zero, gate_zero, up_zero)
    grad_middle, grad_attn, d_gain_mlp_zero, d_mlp_zero = product_sum(
        ((d_gate, d_up), inner_zero, middle_zero, branch, r_zero, zero[0]),
        ((0,), 0, ("back", (2, 3, (5, 1))), back),
        zero[2], ((4, (0,)), (3, (1,))), key=9,
    )
    g_mlp_zero = reduce_gradient(d_mlp_zero)
    grad_attn, g_mlp_one = lax.optimization_barrier((grad_attn, g_mlp_one))
    dq, dkv = attention_backward(grad_attn, zero, tables, kept_zero)
    dq, g_attn_one = lax.optimization_barrier((dq, g_attn_one))
    grad_zero, send_zero, d_gain_attn_zero, d_attn_zero = product_sum(
        ((dq, dkv), tree, grad_middle, zero[0], normed_zero, grad_attn, o_zero),
        ((0,), 0, ("back", (1, 2, (3, 0))), back),
        zero[1], ((4, (0,)), (5, (6,))), key=11,
    )
    d_gain_attn_zero, d_gain_mlp_zero, d_gain_attn_one, d_gain_mlp_one = [
        jnp.sum(x, 0) for x in (d_gain_attn_zero, d_gain_mlp_zero, d_gain_attn_one, d_gain_mlp_one)
    ]
    d_gains = jnp.stack([d_gain_attn_zero, d_gain_mlp_zero, d_gain_attn_one, d_gain_mlp_one])
    d_gains = d_gains.reshape(2, 2, devices, -1).swapaxes(1, 2).reshape(2, devices, -1, 128)

    inner_one, send_zero = lax.optimization_barrier((inner_one, send_zero))
    out_one = product_sum(
        (inner_one, middle_one), ((0,), split_down, ("add", (1,)), (BF,)), one[2], key=6
    )
    ending = finish if devices == 4 else finish_apart
    g_attn_zero, g_gain, got_out, got_in, got_mlp, got_attn = ending(
        d_attn_zero, d_gains, out_zero, out_one, send_zero, branch,
        g_mlp_one, g_attn_one,
    )

    layer_output, input_grad, *grads = write_results(
        (out_zero, out_one, got_out), (grad_zero, grad_one, got_in), (g_attn_zero, g_attn_one, got_attn), width, span
    )
    input_grad, g_mlp_zero = lax.optimization_barrier((input_grad, g_mlp_zero))
    grads += write_mlp(
        g_mlp_zero, g_mlp_one, lax.ppermute(g_mlp_zero, "section", [(1, 0)]), got_mlp, units
    )
    g_query, g_key, g_value, g_out, g_gate, g_up, g_down = [grad[None] for grad in grads]
    g_gain = g_gain.reshape(2, 1, -1)
    return (
        layer_output[None], input_grad[None], g_gain[0], g_query, g_key, g_value, g_out, g_gain[1], g_gate, g_up, g_down,
    )


def solution(mesh):
    in_specs = (
        P(None, "dp", None),
        P(None, "dp", None),
        P(),
        P(),
        P(),
        P("section", "dp"),
        P("section", "dp", "tensor"),
        P("section", "dp", "tensor"),
        P("section", "dp", "tensor"),
        P("section", "tensor", "dp"),
        P("section", "dp"),
        P("section", "dp", "tensor"),
        P("section", "dp", "tensor"),
        P("section", "tensor", "dp"),
    )
    out_specs = (
        P("section", None, "dp", None),
        P("section", None, "dp", None),
        P("section", "dp"),
        P("section", "dp", "tensor"),
        P("section", "dp", "tensor"),
        P("section", "dp", "tensor"),
        P("section", "tensor", "dp"),
        P("section", "dp"),
        P("section", "dp", "tensor"),
        P("section", "dp", "tensor"),
        P("section", "tensor", "dp"),
    )
    return jax.shard_map(shards, mesh=mesh, in_specs=in_specs, out_specs=out_specs, check_vma=False)
```

```python
import functools

import jax
import jax.numpy as jnp
from jax import lax
from jax.experimental import pallas as pl
from jax.experimental.pallas import tpu as pltpu
from jax.sharding import PartitionSpec as P

HEAD = 64
HALF = HEAD // 2
TRUNK = 1024
GROUP = 384
EPSILON = 1e-05
THETA = 10000.0
MASKED = -1e30
BF = jnp.bfloat16
F32 = jnp.float32
MESH = pl.DeviceIdType.MESH
BOTH = ("dp", "section")


def dot_f32(a, b, ca, cb):
    return lax.dot_general(a, b, (((ca,), (cb,)), ((), ())), preferred_element_type=F32)


BLOCK = 256
PIECE = 128
NO_COST = pl.CostEstimate(flops=1, transcendentals=0, bytes_accessed=1)


def columns_of(i):
    return pl.ds(pl.multiple_of(i * PIECE, PIECE), PIECE)


def gain_row(arrays, place, at):
    return arrays[place[0]][place[1] : place[1] + 1, at]


def row_scale(squares, model):
    return lax.rsqrt(jnp.sum(squares, 1, keepdims=True) * (1.0 / model) + EPSILON)


def before_sum(job, arrays, keep):
    kind, places = job[2]
    if kind == "back":
        value = arrays[places[0]]
        model = value.shape[1]
        squares = jnp.zeros(keep.shape, F32)
        for i in range(model // PIECE):
            x = value[:, i * PIECE : (i + 1) * PIECE].astype(F32)
            squares += x * x
        keep[...] = jnp.broadcast_to(row_scale(squares, model), keep.shape)


def with_piece(job, i, total, arrays, outs, keep, sums):
    kind, places = job[2]
    at = columns_of(i)
    if kind == "add":
        y = (arrays[places[0]][:, at].astype(F32) + total).astype(outs[0].dtype)
        outs[0][:, at] = y
        if len(outs) > 1:
            sums[...] += y.astype(F32) * y.astype(F32)
    if kind == "back":
        product = total * arrays[places[0]][:, at].astype(F32) * keep[...]
        sums[...] += product * gain_row(arrays, places[2], at)
        outs[2][:, at] = jnp.sum(product.reshape(-1, 8, PIECE), 0)


def after_sum(job, rows, total, arrays, outs, keep, sums):
    kind, places = job[2]
    model = arrays[places[0]].shape[1]
    at = lambda i: slice(i * PIECE, (i + 1) * PIECE)
    if kind == "add" and len(outs) > 1:
        scale = row_scale(sums[rows], model)
        for i in range(model // PIECE):
            y = outs[0][rows, at(i)].astype(F32)
            outs[1][rows, at(i)] = (y * scale * gain_row(arrays, places[1], at(i))).astype(BF)
    if kind == "back":
        mean = jnp.sum(sums[rows], 1, keepdims=True) * (1.0 / model)
        scale = keep[rows]
        for i in range(model // PIECE):
            unit = arrays[places[0]][rows, at(i)].astype(F32) * scale
            grad = total(i)[rows].astype(F32) * gain_row(arrays, places[2], at(i))
            out = arrays[places[1]][rows, at(i)].astype(F32) + scale * (grad - unit * mean)
            outs[0][rows, at(i)] = out
            outs[1][rows, at(i)] = out.astype(BF)


def product_sum_kernel(cfg, *refs):
    n_join, n_arrays, job, sides, stagger = cfg
    xs, first_column = job[:2]
    refs = list(refs)
    take = lambda n: [refs.pop(0) for _ in range(n)]
    joined = take(n_join)
    from_hbm = [None, *take(n_arrays - 1)]
    (w_hbm,) = take(1)
    outs_hbm = take(len(job[3]))
    (g_hbm,) = take(1) if sides else (None,)
    arrays = take(n_arrays)
    outs = take(len(job[3]))
    load_sem, out_sem, w_buf, p_buf, a_buf, b_buf, w_sem, sa, ra, sb, rb, sc, rc, turn, keep, sums = take(16)
    g_buf, g_sem = take(2) if sides else (None, None)
    per_block = BLOCK // PIECE
    pieces = p_buf.shape[0]
    blocks = pieces // per_block
    n_rows = p_buf.shape[1]
    early = len(xs)
    lag = 2
    assert xs[0] == 0

    t = lax.axis_index("tensor")
    sec = lax.axis_index("section")
    dat = lax.axis_index("dp")
    inner = (t == 1) | (t == 2)
    outer = jnp.logical_not(inner)
    pair = (sec, t + 1 - 2 * lax.rem(t, 2), dat)
    mid = (sec, 3 - t, dat)
    mate = (1 - sec, t, dat)

    def columns(j):
        return pl.ds(pl.multiple_of(j * BLOCK, BLOCK), BLOCK)

    def to_inner(i):
        return pltpu.make_async_remote_copy(
            p_buf.at[i], a_buf.at[i], sa.at[i], ra.at[i], device_id=pair, device_id_type=MESH
        )

    def across(i):
        return pltpu.make_async_remote_copy(
            p_buf.at[i], b_buf.at[i], sb.at[i], rb.at[i], device_id=mid, device_id_type=MESH
        )

    def to_outer(i):
        return pltpu.make_async_remote_copy(
            b_buf.at[i], b_buf.at[i], sc.at[i], rc.at[i], device_id=pair, device_id_type=MESH
        )

    def load(k):
        return pltpu.make_async_copy(from_hbm[k], arrays[k], load_sem.at[k])

    def join():
        copies, start = [], 0
        for m, src in enumerate(joined):
            at = pl.ds(start, src.shape[1])
            copies.append(pltpu.make_async_copy(src, arrays[0].at[:, at], load_sem.at[n_arrays + m]))
            start += src.shape[1]
        return copies

    def fetch(j, slot):
        return pltpu.make_async_copy(
            w_hbm.at[columns(j), pl.ds(first_column, w_buf.shape[2])], w_buf.at[slot], w_sem.at[slot]
        )

    def flush(j, slot):
        return pltpu.make_async_copy(g_buf.at[slot], g_hbm.at[columns(j), :], g_sem.at[slot])

    def every_piece(body):
        def turn_of(i, _):
            body(i)
            return 0

        lax.fori_loop(0, pieces, turn_of, 0)

    for copy in join():
        copy.start()
    for k in range(1, early):
        load(k).start()
    fetch(0, 0).start()
    for k in range(early, n_arrays):
        load(k).start()
    barrier = pltpu.get_barrier_semaphore()
    pl.semaphore_signal(barrier, inc=1, device_id=pair, device_id_type=MESH)
    sums[...] = jnp.zeros_like(sums)

    @pl.when(inner)
    def _():
        pl.semaphore_signal(barrier, inc=1, device_id=mid, device_id_type=MESH)
        pl.semaphore_wait(barrier, 2)

    @pl.when(outer)
    def _():
        if stagger:
            pl.semaphore_signal(barrier, inc=1, device_id=mate, device_id_type=MESH)
            pl.semaphore_wait(barrier, 2)

            @pl.when(sec == 1)
            def _():
                pl.semaphore_wait(turn, 1)

        else:
            pl.semaphore_wait(barrier, 1)

    for copy in join():
        copy.wait()
    for k in range(1, early):
        load(k).wait()

    def done(i):
        with_piece(job, i, b_buf[i].astype(F32), arrays, outs, keep, sums)

    def first(i):
        to_inner(i).wait_recv()
        p_buf[i] = p_buf[i] + a_buf[i]
        across(i).start()

    def second(i):
        across(i).wait_recv()
        b_buf[i] = p_buf[i] + b_buf[i]
        to_outer(i).start()
        done(i)

    def side(j):
        slot = lax.rem(j, 2)

        @pl.when(j >= 2)
        def _():
            flush(j - 2, slot).wait()

        start = 0
        for a, bs in sides:
            a_t = arrays[a][:, columns(j)].T
            for b in bs:
                width = arrays[b].shape[1]
                g_buf[slot, :, start : start + width] = jnp.dot(
                    a_t, arrays[b][...], preferred_element_type=F32
                ).astype(BF)
                start += width
        flush(j, slot).start()
        return 0

    def step(j, _):
        slot = lax.rem(j, 2)
        fetch(j, slot).wait()

        @pl.when(j + 1 < blocks)
        def _():
            fetch(j + 1, 1 - slot).start()

        total, start = None, 0
        for x in xs:
            width = arrays[x].shape[1]
            term = dot_f32(arrays[x][...], w_buf[slot, :, start : start + width], 1, 1)
            total = term if total is None else total + term
            start += width
        total = total.astype(BF)
        for u in range(per_block):
            p_buf[per_block * j + u] = total[:, u * PIECE : (u + 1) * PIECE]

        @pl.when(outer)
        def _():
            for u in range(per_block):
                to_inner(per_block * j + u).start()

        @pl.when(j == 1)
        def _():
            for k in range(early, n_arrays):
                load(k).wait()
            before_sum(job, arrays, keep)

        if sides:

            @pl.when(j >= lag)
            def _():
                side(j - lag)

        @pl.when(inner)
        def _():
            for u in range(per_block):
                i = per_block * j + u
                first(i)

                @pl.when(j >= 1)
                def _():
                    second(i - per_block)

        return 0

    lax.fori_loop(0, blocks, step, 0)

    @pl.when(inner)
    def _():
        for u in range(per_block):
            second(pieces - per_block + u)

    if sides:
        lax.fori_loop(blocks - lag, blocks, lambda j, _: side(j), 0)

    @pl.when(outer)
    def _():
        every_piece(lambda i: to_inner(i).wait_send())

        def arrive(i):
            to_outer(i).wait_recv()
            done(i)

        every_piece(arrive)
        if stagger:

            @pl.when(sec == 0)
            def _():
                pl.semaphore_signal(turn, inc=1, device_id=mate, device_id_type=MESH)

    chunks = 5 if n_rows % (5 * 32) == 0 else 1
    chunk = n_rows // chunks
    block = 32 if chunk % 32 == 0 else 16
    height = lambda m: 8 if job[2][0] == "back" and m == 2 else n_rows
    stores = []

    def store(m, rows):
        copy = pltpu.make_async_copy(outs[m].at[rows], outs_hbm[m].at[rows], out_sem.at[len(stores)])
        copy.start()
        stores.append(copy)

    for c in range(chunks):

        def turn_rows(r, _):
            rows = pl.ds(pl.multiple_of(c * chunk + r * block, block), block)
            after_sum(job, rows, lambda i: b_buf.at[i], arrays, outs, keep, sums)
            return 0

        if job[2][0] == "back" or len(outs) > 1:
            lax.fori_loop(0, chunk // block, turn_rows, 0)
        for m in range(len(outs)):
            if height(m) == n_rows:
                store(m, pl.ds(c * chunk, chunk))
    for m in range(len(outs)):
        if height(m) != n_rows:
            store(m, pl.ds(0, height(m)))

    @pl.when(inner)
    def _():
        def sent(i):
            across(i).wait_send()
            to_outer(i).wait_send()

        every_piece(sent)

    if sides:
        flush(blocks - 2, (blocks - 2) % 2).wait()
        flush(blocks - 1, (blocks - 1) % 2).wait()
    for copy in stores:
        copy.wait()


def product_sum(arrays, job, weights, sides=(), stagger=False, key=1):
    assert lax.axis_size("tensor") == 4
    first = arrays[0] if isinstance(arrays[0], tuple) else (arrays[0],)
    given = (*first, *arrays[1:])
    rows, model = first[0].shape[0], weights.shape[0]
    arrays = (jax.ShapeDtypeStruct((rows, sum(x.shape[1] for x in first)), BF), *arrays[1:])
    pieces = model // PIECE
    depth = sum(arrays[x].shape[1] for x in job[0])
    anywhere = pl.BlockSpec(memory_space=pl.ANY)
    buf = pltpu.VMEM((pieces, rows, PIECE), BF)
    sem = pltpu.SemaphoreType.DMA((pieces,))
    two = pltpu.SemaphoreType.DMA((2,))
    out_shape = []
    for m, dtype in enumerate(job[3]):
        height = 8 if job[2][0] == "back" and m == 2 else rows
        out_shape.append(jax.ShapeDtypeStruct((height, model), dtype))
    scratch = [pltpu.VMEM(x.shape, x.dtype) for x in (*arrays, *out_shape)]
    scratch += [pltpu.SemaphoreType.DMA((len(arrays) + len(first),)), pltpu.SemaphoreType.DMA((16,))]
    scratch += [pltpu.VMEM((2, BLOCK, depth), BF), buf, buf, buf, two, *[sem] * 6, pltpu.SemaphoreType.REGULAR]
    scratch += [pltpu.VMEM((rows, PIECE), F32)] * 2
    if sides:
        side_width = sum(arrays[b].shape[1] for _, bs in sides for b in bs)
        out_shape.append(jax.ShapeDtypeStruct((model, side_width), BF))
        scratch += [pltpu.VMEM((2, BLOCK, side_width), BF), two]
    out = pl.pallas_call(
        functools.partial(product_sum_kernel, (len(first), len(arrays), job, tuple(sides), stagger)),
        out_shape=out_shape,
        in_specs=[anywhere] * (len(given) + 1),
        out_specs=[anywhere] * len(out_shape),
        scratch_shapes=scratch,
        compiler_params=pltpu.CompilerParams(
            collective_id=key, has_side_effects=True, vmem_limit_bytes=62 << 20
        ),
        cost_estimate=NO_COST,
        name=f"product_sum_{key}",
    )(*given, weights)
    return out if len(out) > 1 else out[0]


def dp_peers(count):
    me = lax.axis_index("dp")
    sec, t = lax.axis_index("section"), lax.axis_index("tensor")
    others = [lax.rem(me + k, count) for k in range(1, count)]
    return me, others, [(sec, t, other) for other in others]


def greet(ids):
    barrier = pltpu.get_barrier_semaphore()
    for device in ids:
        pl.semaphore_signal(barrier, inc=1, device_id=device, device_id_type=MESH)
    pl.semaphore_wait(barrier, len(ids))


def turn_rows(x, cos_ref, sin_ref):
    lane = lax.broadcasted_iota(jnp.int32, x.shape, 1)
    width = x.shape[1]
    partner = jnp.where(lane < HALF, pltpu.roll(x, width - HALF, 1), pltpu.roll(x, HALF, 1))
    return x * cos_ref[...] + partner * sin_ref[...]


def gather_kernel(
    count, normed_ref, w_hbm, cos_ref, sin_ref, o_ref, t_ref, q_ref, x_ref, w_buf, load_sem, send, recv
):
    me, _, ids = dp_peers(count)
    load = pltpu.make_async_copy(w_hbm.at[:, pl.ds(0, w_buf.shape[1])], w_buf, load_sem)
    load.start()
    load.wait()
    width = q_ref.shape[0]
    raw = jnp.dot(normed_ref[...], w_buf[:, width:], preferred_element_type=F32)
    x_ref[...] = turn_rows(raw, cos_ref, sin_ref).astype(BF)
    greet(ids)
    copies = [
        pltpu.make_async_remote_copy(
            x_ref, o_ref.at[me], send.at[k], recv.at[k], device_id=device, device_id_type=MESH
        )
        for k, device in enumerate(ids)
    ]
    for copy in copies:
        copy.start()
    o_ref[me] = x_ref[...]
    q_ref[...] = jnp.dot(normed_ref[...], w_buf[:, :width], preferred_element_type=F32).T
    for copy in copies:
        copy.wait()
    t_ref[...] = o_ref[...].reshape(t_ref.shape[1], t_ref.shape[0]).T


def scatter_kernel(count, x_ref, cos_ref, sin_ref, o_ref, buf, send, recv):
    me, others, ids = dp_peers(count)
    greet(ids)
    copies = [
        pltpu.make_async_remote_copy(
            x_ref.at[others[k]], buf.at[k], send.at[k], recv.at[k], device_id=device, device_id_type=MESH
        )
        for k, device in enumerate(ids)
    ]
    for copy in copies:
        copy.start()
    total = x_ref[me].astype(F32)
    for k, copy in enumerate(copies):
        copy.wait()
        total = total + buf[k].astype(F32)
    o_ref[...] = turn_rows(total, cos_ref, sin_ref).astype(BF)


def gather_rows(normed, w_attn, width, split, cos_rows, sin_rows, key):
    count = lax.axis_size("dp")
    rows, span = normed.shape[0], split - width
    in_vmem = pl.BlockSpec(memory_space=pltpu.VMEM)
    sem = pltpu.SemaphoreType.DMA((count - 1,))
    out, out_t, q_t = pl.pallas_call(
        functools.partial(gather_kernel, count),
        out_shape=(
            jax.ShapeDtypeStruct((count, rows, span), BF),
            jax.ShapeDtypeStruct((span, count * rows), BF),
            jax.ShapeDtypeStruct((width, rows), F32),
        ),
        in_specs=[in_vmem, pl.BlockSpec(memory_space=pl.ANY), in_vmem, in_vmem],
        out_specs=(in_vmem, in_vmem, in_vmem),
        scratch_shapes=[
            pltpu.VMEM((rows, span), BF), pltpu.VMEM((normed.shape[1], split), BF),
            pltpu.SemaphoreType.DMA, sem, sem,
        ],
        compiler_params=pltpu.CompilerParams(
            collective_id=key, has_side_effects=True, vmem_limit_bytes=40 << 20
        ),
        cost_estimate=NO_COST,
        name="gather_rows",
    )(normed, w_attn, cos_rows, sin_rows)
    return out.reshape(-1, span), out_t, q_t


def scatter_rows(x, cos_rows, sin_rows):
    count = lax.axis_size("dp")
    rows, width = x.shape[0] // count, x.shape[1]
    in_vmem = pl.BlockSpec(memory_space=pltpu.VMEM)
    sem = pltpu.SemaphoreType.DMA((count - 1,))
    return pl.pallas_call(
        functools.partial(scatter_kernel, count),
        out_shape=jax.ShapeDtypeStruct((rows, width), BF),
        in_specs=[in_vmem] * 3,
        out_specs=in_vmem,
        scratch_shapes=[pltpu.VMEM((count - 1, rows, width), x.dtype), sem, sem],
        compiler_params=pltpu.CompilerParams(collective_id=4, has_side_effects=True),
        cost_estimate=NO_COST,
        name="scatter_rows",
    )(x.reshape(count, rows, width), cos_rows, sin_rows)


def finish_kernel(
    g_hbm, gain_ref, out_zero, out_one, in_zero, in_one, mlp_one, attn_one,
    o_ref, gain_out, got_out, got_in, got_mlp, got_attn,
    mine, away, got, xs, ys, xr, yr, gains, load_sem, send, recv, mate_send, mate_recv, gain_send, gain_recv,
):
    sec, t, dat = lax.axis_index("section"), lax.axis_index("tensor"), lax.axis_index("dp")
    flip_x = dat + 1 - 2 * lax.rem(dat, 2)
    flip_y = lax.rem(dat + 2, 4)
    across = lax.rem(flip_x + 2, 4)
    by_x, by_y, mate = (sec, t, flip_x), (sec, t, flip_y), (1 - sec, t, dat)
    peers = [
        mate, by_x, by_y, (sec, t, across),
        (1 - sec, t, flip_x), (1 - sec, t, flip_y), (1 - sec, t, across),
    ]
    rows = g_hbm.shape[1] // 2
    upper, lower = pl.ds(0, rows), pl.ds(rows, rows)
    order = (across, flip_x, flip_y, dat)
    loads = []
    for k, block in enumerate(order):
        loads.append(pltpu.make_async_copy(g_hbm.at[2 * block + 1 - sec], away.at[k], load_sem.at[k]))
        loads.append(pltpu.make_async_copy(g_hbm.at[2 * block + sec], mine.at[k], load_sem.at[4 + k]))
    for copy in loads:
        copy.start()
    greet(peers)

    def remote(src, dst, k, device):
        return pltpu.make_async_remote_copy(
            src, dst, send.at[k], recv.at[k], device_id=device, device_id_type=MESH
        )

    def to_mate(src, dst, k):
        return pltpu.make_async_remote_copy(
            src, dst, mate_send.at[k], mate_recv.at[k], device_id=mate, device_id_type=MESH
        )

    swaps = [remote(away.at[k], got.at[k], k, mate) for k in range(4)]
    for k in range(4):
        loads[2 * k].wait()
        swaps[k].start()
    gain_copies = [
        pltpu.make_async_remote_copy(
            gain_ref.at[peer[0], peer[2]], gains.at[k], gain_send.at[k], gain_recv.at[k],
            device_id=peer, device_id_type=MESH,
        )
        for k, peer in enumerate(peers)
    ]
    for copy in gain_copies:
        copy.start()
    outs = []
    for k in range(4):
        loads[2 * k + 1].wait()
        swaps[k].wait_recv()
        mine[k] = (mine[k].astype(F32) + got[k].astype(F32)).astype(BF)
        if k == 0:
            outs += [remote(mine.at[0, upper], xs.at[0], 4, by_x), remote(mine.at[0, lower], ys.at[0], 5, by_y)]
        if k == 1:
            outs += [remote(mine.at[1, upper], xs.at[1], 6, by_x)]
        if k == 2:
            outs += [remote(mine.at[2, lower], ys.at[1], 7, by_y)]
        for copy in outs[-(2 if k == 0 else 1) :]:
            if k < 3:
                copy.start()

    @pl.when(sec == 0)
    def _():
        to_mate(in_one, got_in, 0).start()
        to_mate(out_one, got_out, 1).start()
        to_mate(mlp_one, got_mlp, 2).start()
        to_mate(attn_one, got_attn, 3).start()

    @pl.when(sec == 1)
    def _():
        to_mate(in_zero, got_in, 0).start()
        to_mate(out_zero, got_out, 1).start()

    outs[0].wait_recv()
    mine[2, upper] = (mine[2, upper].astype(F32) + xs[0].astype(F32)).astype(BF)
    outs.append(remote(mine.at[2, upper], yr, 8, by_y))
    outs[4].start()
    outs[1].wait_recv()
    mine[1, lower] = (mine[1, lower].astype(F32) + ys[0].astype(F32)).astype(BF)
    outs.append(remote(mine.at[1, lower], xr, 9, by_x))
    outs[5].start()
    total = gain_ref[sec, dat]
    for k, copy in enumerate(gain_copies):
        copy.wait()
        total = total + gains[k]
    gain_out[...] = total
    outs[2].wait_recv()
    outs[3].wait_recv()
    outs[4].wait_recv()
    o_ref[upper] = (mine[3, upper].astype(F32) + xs[1].astype(F32) + yr[...].astype(F32)).astype(BF)
    outs[5].wait_recv()
    o_ref[lower] = (mine[3, lower].astype(F32) + ys[1].astype(F32) + xr[...].astype(F32)).astype(BF)

    @pl.when(sec == 1)
    def _():
        to_mate(o_ref, got_attn, 3).start()

    for copy in swaps + outs:
        copy.wait_send()
    to_mate(in_one, got_in, 0).wait()
    to_mate(out_one, got_out, 1).wait()
    to_mate(attn_one, got_attn, 3).wait()

    @pl.when(sec == 0)
    def _():
        to_mate(mlp_one, got_mlp, 2).wait_send()

    @pl.when(sec == 1)
    def _():
        to_mate(mlp_one, got_mlp, 2).wait_recv()


def finish(g, gains, out_zero, out_one, in_zero, in_one, mlp_one, attn_one):
    rows, width = g.shape[0] // 8, g.shape[1]
    part = pltpu.VMEM((2, rows // 2, width), BF)
    whole = pltpu.VMEM((4, rows, width), BF)
    end = pltpu.VMEM((rows // 2, width), BF)
    in_vmem, anywhere = pl.BlockSpec(memory_space=pltpu.VMEM), pl.BlockSpec(memory_space=pl.ANY)
    like = lambda x: jax.ShapeDtypeStruct(x.shape, x.dtype)
    dma = lambda n: pltpu.SemaphoreType.DMA((n,))
    return pl.pallas_call(
        finish_kernel,
        out_shape=(
            jax.ShapeDtypeStruct((rows, width), BF),
            jax.ShapeDtypeStruct(gains.shape[2:], F32),
            like(out_zero), like(in_zero), like(mlp_one), like(attn_one),
        ),
        in_specs=[anywhere, in_vmem, *[anywhere] * 6],
        out_specs=(in_vmem, in_vmem, *[anywhere] * 4),
        scratch_shapes=[
            whole, whole, whole, part, part, end, end, pltpu.VMEM((7, *gains.shape[2:]), F32),
            dma(8), dma(10), dma(10), dma(4), dma(4), dma(7), dma(7),
        ],
        compiler_params=pltpu.CompilerParams(
            collective_id=12, has_side_effects=True, vmem_limit_bytes=62 << 20
        ),
        cost_estimate=NO_COST,
        name="finish",
    )(g.reshape(8, rows, width), gains, out_zero, out_one, in_zero, in_one, mlp_one, attn_one)


def finish_apart(g, gains, out_zero, out_one, in_zero, in_one, mlp_one, attn_one):
    first_core = lax.axis_index("section") == 0
    half = reduce_gradient(g)
    swap = lambda zero, one: lax.ppermute(jnp.where(first_core, one, zero), "section", [(0, 1), (1, 0)])
    return (
        half, share_sums(gains), swap(out_zero, out_one), swap(in_zero, in_one),
        lax.ppermute(mlp_one, "section", [(0, 1)]), swap(half, attn_one),
    )


def in_rows(count, block, body):
    def turn(r, _):
        body(pl.ds(pl.multiple_of(r * block, block), block))
        return 0

    lax.fori_loop(0, count // block, turn, 0)


def widen_turned(dst, src, start, width):
    for c in range(0, width, 128):
        dst[c : c + 128] = src[:, start + c : start + c + 128].astype(F32).T


def write_mlp_kernel(
    zero, one, from_one, from_zero, gate_hbm, up_hbm, down_hbm, mlp, gate_buf, up_buf, down_buf, load_sem, store_sem
):
    sec = lax.axis_index("section")
    half, units = zero.shape[0], gate_buf.shape[1]
    low, high = pl.ds(0, half), pl.ds(half, half)
    load = lambda src, at, k: pltpu.make_async_copy(src, mlp.at[at], load_sem.at[k])
    store = lambda src, dst, k: pltpu.make_async_copy(src, dst, store_sem.at[k])

    @pl.when(sec == 0)
    def _():
        load(zero, low, 0).start()
        load(from_one, high, 1).start()

    @pl.when(sec == 1)
    def _():
        load(from_zero, low, 0).start()
        load(one, high, 1).start()

    load(zero, low, 0).wait()
    load(zero, high, 1).wait()

    def gates(rows):
        gate_buf[rows] = mlp[rows, :units].astype(F32)
        up_buf[rows] = mlp[rows, units : 2 * units].astype(F32)

    in_rows(2 * half, 32, gates)
    stores = [store(gate_buf, gate_hbm, 0), store(up_buf, up_hbm, 1), store(down_buf, down_hbm, 2)]
    stores[0].start()
    stores[1].start()
    widen_turned(down_buf, mlp, 2 * units, units)
    stores[2].start()
    for copy in stores:
        copy.wait()


def write_mlp(zero, one, from_one, from_zero, units):
    shard = 2 * zero.shape[0]
    anywhere = pl.BlockSpec(memory_space=pl.ANY)
    shapes = [(shard, units), (shard, units), (units, shard)]
    return pl.pallas_call(
        write_mlp_kernel,
        out_shape=[jax.ShapeDtypeStruct(shape, F32) for shape in shapes],
        in_specs=[anywhere] * 4,
        out_specs=[anywhere] * 3,
        scratch_shapes=[
            pltpu.VMEM((shard, zero.shape[1]), BF),
            *[pltpu.VMEM(shape, F32) for shape in shapes],
            pltpu.SemaphoreType.DMA((2,)),
            pltpu.SemaphoreType.DMA((3,)),
        ],
        compiler_params=pltpu.CompilerParams(vmem_limit_bytes=62 << 20),
        cost_estimate=NO_COST,
        name="write_mlp",
    )(zero, one, from_one, from_zero)


def write_kernel(
    split, out_zero, out_one, got_out, in_zero, in_one, got_in, attn_zero, attn_one, got_attn,
    out_hbm, in_hbm, q_hbm, k_hbm, v_hbm, o_hbm,
    outs, wides, attn, narrow, q_buf, k_buf, v_buf, o_buf, load_sem, store_sem,
):
    sec = lax.axis_index("section")
    half = attn_zero.shape[0]
    low, high = pl.ds(0, half), pl.ds(half, half)
    load = lambda src, dst, k: pltpu.make_async_copy(src, dst, load_sem.at[k])
    store = lambda src, dst, k: pltpu.make_async_copy(src, dst, store_sem.at[k])

    def start(own_out, own_in, attn_low, attn_high):
        load(own_out, outs.at[0], 0).start()
        load(own_in, wides.at[0], 1).start()
        load(attn_low, attn.at[low], 2).start()
        load(attn_high, attn.at[high], 3).start()

    @pl.when(sec == 0)
    def _():
        start(out_zero, in_zero, attn_zero, got_attn)

    @pl.when(sec == 1)
    def _():
        start(out_one, in_one, got_attn, attn_one)

    load(got_in, narrow, 4).start()
    load(got_out, outs.at[1], 5).start()
    stores = [
        store(outs.at[0], out_hbm.at[sec], 0),
        store(wides.at[0], in_hbm.at[sec], 1),
        store(outs.at[1], out_hbm.at[1 - sec], 2),
        store(wides.at[1], in_hbm.at[1 - sec], 3),
        store(q_buf, q_hbm, 4),
        store(k_buf, k_hbm, 5),
        store(v_buf, v_hbm, 6),
        store(o_buf, o_hbm, 7),
    ]
    load(out_zero, outs.at[0], 0).wait()
    stores[0].start()
    load(in_zero, wides.at[0], 1).wait()
    stores[1].start()
    width, span = q_buf.shape[1], k_buf.shape[1]
    load(attn_one, attn.at[low], 2).wait()
    load(attn_one, attn.at[high], 3).wait()

    def projections(rows):
        q_buf[rows] = attn[rows, :width].astype(F32)
        k_buf[rows] = attn[rows, width : width + span].astype(F32)
        v_buf[rows] = attn[rows, width + span : split].astype(F32)

    in_rows(2 * half, 32, projections)
    for k in (4, 5, 6):
        stores[k].start()
    widen_turned(o_buf, attn, split, width)
    stores[7].start()
    load(got_in, narrow, 4).wait()

    def widen(rows):
        wides[1, rows] = narrow[rows].astype(F32)

    in_rows(narrow.shape[0], 32, widen)
    stores[3].start()
    load(got_out, outs.at[1], 5).wait()
    stores[2].start()
    for copy in stores:
        copy.wait()


def write_results(results, ins, attns, width, span):
    rows, model = results[0].shape
    shard = 2 * attns[0].shape[0]
    anywhere = pl.BlockSpec(memory_space=pl.ANY)
    shapes = [(shard, width), (shard, span), (shard, span), (width, shard)]
    return pl.pallas_call(
        functools.partial(write_kernel, width + 2 * span),
        out_shape=[
            jax.ShapeDtypeStruct((2, rows, model), BF),
            jax.ShapeDtypeStruct((2, rows, model), F32),
            *[jax.ShapeDtypeStruct(shape, F32) for shape in shapes],
        ],
        in_specs=[anywhere] * 9,
        out_specs=[anywhere] * 6,
        scratch_shapes=[
            pltpu.VMEM((2, rows, model), BF),
            pltpu.VMEM((2, rows, model), F32),
            pltpu.VMEM((shard, attns[0].shape[1]), BF),
            pltpu.VMEM((rows, model), BF),
            *[pltpu.VMEM(shape, F32) for shape in shapes],
            pltpu.SemaphoreType.DMA((6,)),
            pltpu.SemaphoreType.DMA((8,)),
        ],
        compiler_params=pltpu.CompilerParams(vmem_limit_bytes=62 << 20),
        cost_estimate=NO_COST,
        name="write_results",
    )(*results, *ins, *attns)


def share_kernel(count, x_ref, o_ref, buf, send, recv):
    sec, t, dat = lax.axis_index("section"), lax.axis_index("tensor"), lax.axis_index("dp")
    peers = [
        (lax.rem(sec + k // count, 2), t, lax.rem(dat + k % count, count)) for k in range(1, 2 * count)
    ]
    greet(peers)
    copies = [
        pltpu.make_async_remote_copy(
            x_ref.at[peer[0], peer[2]], buf.at[k], send.at[k], recv.at[k], device_id=peer, device_id_type=MESH
        )
        for k, peer in enumerate(peers)
    ]
    for copy in copies:
        copy.start()
    total = x_ref[sec, dat]
    for k, copy in enumerate(copies):
        copy.wait()
        total = total + buf[k]
    o_ref[...] = total


def share_sums(x):
    count = lax.axis_size("dp")
    in_vmem = pl.BlockSpec(memory_space=pltpu.VMEM)
    sem = pltpu.SemaphoreType.DMA((2 * count - 1,))
    return pl.pallas_call(
        functools.partial(share_kernel, count),
        out_shape=jax.ShapeDtypeStruct(x.shape[2:], F32),
        in_specs=[in_vmem],
        out_specs=in_vmem,
        scratch_shapes=[pltpu.VMEM((2 * count - 1, *x.shape[2:]), F32), sem, sem],
        compiler_params=pltpu.CompilerParams(collective_id=13, has_side_effects=True),
        cost_estimate=NO_COST,
        name="share_sums",
    )(x)


def group_start(first_row):
    past = lax.max(first_row - TRUNK, 0)
    return pl.multiple_of(TRUNK + GROUP * lax.div(past, GROUP), 128)


def over_windows(tree_len, rows, tile, first_row, run):
    if tile % 128 == 0 and GROUP % tile == 0 and TRUNK % tile == 0 and rows % tile == 0:
        run(((pl.ds(0, TRUNK), True), (pl.ds(group_start(first_row), GROUP), True)))
    else:
        run(((pl.ds(0, tree_len), True),))


def masked(scores, bias_ref, win, step):
    bias = bias_ref[win, :].astype(F32)
    return scores + (bias if step == 1 else jnp.concatenate([bias] * step, axis=1))


def head_rows(ref, head):
    return ref[head * HEAD : (head + 1) * HEAD, :]


def beside(ref, head, count):
    parts = [head_rows(ref, head + k) for k in range(count)]
    return parts[0] if count == 1 else jnp.concatenate(parts, axis=1)


def turned_beside(ref, cos, sin, head, count):
    parts = []
    for k in range(count):
        rows = head_rows(ref, head + k)
        first, second = rows[:HALF], rows[HALF:]
        parts.append(jnp.concatenate([first * cos - second * sin, second * cos + first * sin], axis=0))
    whole = parts[0] if count == 1 else jnp.concatenate(parts, axis=1)
    return (whole.astype(BF).astype(F32) * HEAD**-0.5).astype(BF)


def as_rows(x, tile, count):
    parts = [x[:, k * tile : (k + 1) * tile] for k in range(count)]
    return (parts[0] if count == 1 else jnp.concatenate(parts, axis=0)).T


def over_groups(groups, step, body):
    for group in range(groups):
        body(group, slice(group * step * HEAD, (group + 1) * step * HEAD))


def attend_kernel(
    rows, step, start_ref, q_ref, kv_ref, kvt_ref, bias_ref, cos_ref, sin_ref, o_ref, on_ref, lse_ref
):
    tile = q_ref.shape[1]
    heads = q_ref.shape[0] // HEAD
    first_row = start_ref[0] + pl.program_id(0) * tile

    def body(wins, group, lanes):
        head = group * step
        q = turned_beside(q_ref, cos_ref[...], sin_ref[...], head, step)
        scores = []
        for win, mask in wins:
            score = dot_f32(kv_ref[win, :HEAD], q, 1, 0)
            scores.append(masked(score, bias_ref, win, step) if mask else score)
        top = functools.reduce(jnp.maximum, [jnp.max(s, 0, keepdims=True) for s in scores])
        expo = [jnp.exp(s - top) for s in scores]
        total = sum(jnp.sum(e, 0, keepdims=True) for e in expo)
        out = sum(dot_f32(kvt_ref[HEAD:, win], e.astype(BF), 1, 0) for (win, _), e in zip(wins, expo))
        out = out / total
        on_ref[:, lanes] = as_rows(out, tile, step).astype(BF)
        lse_ref[group, 0] = top + jnp.log(total)
        out = out.astype(BF)
        for k in range(step):
            o_ref[(head + k) * HEAD : (head + k + 1) * HEAD, :] = out[:, k * tile : (k + 1) * tile]

    over_windows(
        kv_ref.shape[0], rows, tile, first_row,
        lambda wins: over_groups(heads // step, step, functools.partial(body, wins)),
    )


def attend_back_kernel(
    rows, step, start_ref, q_ref, do_ref, o_ref, lse_ref, kv_ref, kvt_ref, bias_ref, cos_ref, sin_ref,
    dq_ref, dkv_ref, dk_acc, dv_acc,
):
    tile = q_ref.shape[1]
    heads = q_ref.shape[0] // HEAD
    first_row = start_ref[0] + pl.program_id(0) * tile

    @pl.when(pl.program_id(0) == 0)
    def _():
        dk_acc[...] = jnp.zeros_like(dk_acc)
        dv_acc[...] = jnp.zeros_like(dv_acc)

    def body(wins, group, lanes):
        head = group * step
        cos, sin = cos_ref[...], sin_ref[...]
        q = turned_beside(q_ref, cos, sin, head, step)
        do = beside(do_ref, head, step)
        out = beside(o_ref, head, step)
        lse = lse_ref[group, 0]
        delta = jnp.sum(do.astype(F32) * out.astype(F32), 0, keepdims=True)
        dq = jnp.zeros((HEAD, step * tile), F32)
        for win, mask in wins:
            score = dot_f32(kv_ref[win, :HEAD], q, 1, 0)
            p = jnp.exp((masked(score, bias_ref, win, step) if mask else score) - lse)
            dp = dot_f32(kv_ref[win, HEAD:], do, 1, 0)
            ds = (p * (dp - delta)).astype(BF)
            dk_acc[win, :] += dot_f32(ds, q, 1, 1)
            dv_acc[win, :] += dot_f32(p.astype(BF), do, 1, 1)
            dq = dq + dot_f32(kvt_ref[:HEAD, win], ds, 1, 0)
        dq = dq * HEAD**-0.5
        turned = []
        for k in range(step):
            first = dq[:HALF, k * tile : (k + 1) * tile]
            second = dq[HALF:, k * tile : (k + 1) * tile]
            turned += [first * cos + second * sin, second * cos - first * sin]
        dq_ref[:, lanes] = jnp.concatenate(turned, axis=0).T.astype(BF)

    over_windows(
        kv_ref.shape[0], rows, tile, first_row,
        lambda wins: over_groups(heads // step, step, functools.partial(body, wins)),
    )

    @pl.when(pl.program_id(0) == pl.num_programs(0) - 1)
    def _():
        dkv_ref[...] = jnp.concatenate([dk_acc[...], dv_acc[...]], axis=1).astype(BF)


def row_tile(rows):
    return 128 if rows % 128 == 0 else rows


def attend(start, q_t, kv, kv_t, bias_t, cos_t, sin_t):
    width, rows = q_t.shape
    heads, tree_len, tile = width // HEAD, kv.shape[0], row_tile(rows)
    step = 2 if tile % 128 == 0 and heads % 2 == 0 else 1
    column = lambda i, s: (0, i)
    whole = lambda i, s: (0, 0)
    return pl.pallas_call(
        functools.partial(attend_kernel, rows, step),
        out_shape=(
            jax.ShapeDtypeStruct((width, rows), BF),
            jax.ShapeDtypeStruct((rows, width), BF),
            jax.ShapeDtypeStruct((heads // step, rows // tile, 1, step * tile), F32),
        ),
        grid_spec=pltpu.PrefetchScalarGridSpec(
            num_scalar_prefetch=1,
            grid=(rows // tile,),
            in_specs=[
                pl.BlockSpec((width, tile), column),
                pl.BlockSpec((tree_len, 2 * HEAD), whole),
                pl.BlockSpec((2 * HEAD, tree_len), whole),
                pl.BlockSpec((tree_len, tile), column),
                pl.BlockSpec((HALF, tile), column),
                pl.BlockSpec((HALF, tile), column),
            ],
            out_specs=(
                pl.BlockSpec((width, tile), column),
                pl.BlockSpec((tile, width), lambda i, s: (i, 0)),
                pl.BlockSpec((heads // step, 1, 1, step * tile), lambda i, s: (0, i, 0, 0)),
            ),
        ),
        compiler_params=pltpu.CompilerParams(vmem_limit_bytes=62 << 20),
        cost_estimate=NO_COST,
        name="attend",
    )(start, q_t, kv, kv_t, bias_t, cos_t, sin_t)


def attend_back(start, q_t, do_t, o_t, lse, kv, kv_t, bias_t, cos_t, sin_t):
    width, rows = q_t.shape
    heads, tree_len, tile = width // HEAD, kv.shape[0], row_tile(rows)
    step = 2 if tile % 128 == 0 and heads % 2 == 0 else 1
    column = lambda i, s: (0, i)
    whole = lambda i, s: (0, 0)
    return pl.pallas_call(
        functools.partial(attend_back_kernel, rows, step),
        out_shape=(
            jax.ShapeDtypeStruct((rows, width), BF),
            jax.ShapeDtypeStruct((tree_len, 2 * HEAD), BF),
        ),
        grid_spec=pltpu.PrefetchScalarGridSpec(
            num_scalar_prefetch=1,
            grid=(rows // tile,),
            in_specs=[
                pl.BlockSpec((width, tile), column),
                pl.BlockSpec((width, tile), column),
                pl.BlockSpec((width, tile), column),
                pl.BlockSpec((heads // step, 1, 1, step * tile), lambda i, s: (0, i, 0, 0)),
                pl.BlockSpec((tree_len, 2 * HEAD), whole),
                pl.BlockSpec((2 * HEAD, tree_len), whole),
                pl.BlockSpec((tree_len, tile), column),
                pl.BlockSpec((HALF, tile), column),
                pl.BlockSpec((HALF, tile), column),
            ],
            out_specs=(
                pl.BlockSpec((tile, width), lambda i, s: (i, 0)),
                pl.BlockSpec((tree_len, 2 * HEAD), whole),
            ),
            scratch_shapes=[pltpu.VMEM((tree_len, HEAD), F32), pltpu.VMEM((tree_len, HEAD), F32)],
        ),
        compiler_params=pltpu.CompilerParams(vmem_limit_bytes=62 << 20),
        cost_estimate=NO_COST,
        name="attend_back",
    )(start, q_t, do_t, o_t, lse, kv, kv_t, bias_t, cos_t, sin_t)


def layer_attention(normed, weights, tables, key):
    gains, w_attn, w_mlp, width, split, units = weights
    start, bias_t, cos_t, sin_t, cos_rows, sin_rows = tables
    kv, kv_t, q_t = gather_rows(normed, w_attn, width, split, cos_rows, -sin_rows, key)
    o_t, o, lse = attend(start, q_t, kv, kv_t, bias_t, cos_t, sin_t)
    return (q_t, kv, kv_t, o_t, lse), o


def attention_backward(grad_attn, weights, tables, kept):
    gains, w_attn, w_mlp, width, split, units = weights
    start, bias_t, cos_t, sin_t, cos_rows, sin_rows = tables
    q_t, kv, kv_t, o_t, lse = kept
    do_t = dot_f32(w_attn[:, split : split + width], grad_attn, 0, 1).astype(BF)
    dq, dkv_part = attend_back(start, q_t, do_t, o_t, lse, kv, kv_t, bias_t, cos_t, sin_t)
    return dq, scatter_rows(dkv_part, cos_rows, sin_rows)


def layer_units(normed, weights):
    units = weights[-1]
    gate_up = jnp.dot(normed, weights[2][:, : 2 * units], preferred_element_type=F32)
    gate, up = gate_up[:, :units], gate_up[:, units:]
    return gate, up, (gate * jax.nn.sigmoid(gate) * up).astype(BF)


def units_backward(branch, weights, gate, up):
    units = weights[-1]
    d_inner = dot_f32(branch, weights[2][:, 2 * units :], 1, 0)
    sig = jax.nn.sigmoid(gate)
    d_gate = (d_inner * up * sig * (1.0 + gate * (1.0 - sig))).astype(BF)
    d_up = (d_inner * gate * sig).astype(BF)
    return d_gate, d_up


def reduce_gradient(x):
    return lax.psum_scatter(x, BOTH, scatter_dimension=0, tiled=True)


def shards(
    inputs, cotangent, seg_ids, positions, parents, gain_attn, w_query, key_weight, value_weight,
    w_out, gain_mlp, w_gate, w_up, w_down,
):
    sec = lax.axis_index("section")
    data = lax.axis_index("dp")
    sections = lax.axis_size("section")
    devices = lax.axis_size("dp")
    assert sections == 2 and inputs.shape[0] == 2
    first_core = sec == 0
    rows, model = inputs.shape[1], inputs.shape[2]
    swap = [(0, 1), (1, 0)]

    tree = lax.dynamic_index_in_dim(inputs, sec, 0, keepdims=False)
    hidden = tree.astype(F32)
    segments = lax.dynamic_index_in_dim(seg_ids, sec, 0, keepdims=False)
    places = lax.dynamic_index_in_dim(positions, sec, 0, keepdims=False)
    parent = lax.dynamic_index_in_dim(parents, sec, 0, keepdims=False)

    width, span, units = w_query.shape[2], key_weight.shape[2], w_gate.shape[2]
    split = width + 2 * span
    shard_list = (
        jnp.concatenate(
            [w_query[0], key_weight[0], value_weight[0], w_out[0].T, gain_attn.T, gain_mlp.T], 1
        ).astype(BF),
        jnp.concatenate([w_gate[0], w_up[0], w_down[0].T], 1).astype(BF),
    )
    halves = []
    for shard in shard_list:
        half = shard.shape[0] // 2
        low, high = shard[:half], shard[half:]
        got = lax.ppermute(jnp.where(first_core, high, low), "section", swap)
        halves.append((jnp.where(first_core, low, got), jnp.where(first_core, got, high)))
    def gathered(halves):
        return [lax.all_gather(half, BOTH, axis=0, tiled=True) for half in halves]

    def with_gains(w_attn, w_mlp):
        return (w_attn[:, split + width :].astype(F32).T, w_attn, w_mlp, width, split, units)

    (attn_zero, attn_one), (mlp_zero, mlp_one) = halves
    attn_zero = jnp.concatenate([attn_zero, attn_one[:, split + width : split + width + 1]], 1)
    attn_zero, mlp_zero = gathered((attn_zero, mlp_zero))
    cot = lax.dynamic_index_in_dim(cotangent, sec, 0, keepdims=False)
    attn_zero, cot = lax.optimization_barrier((attn_zero, cot))
    zero = with_gains(attn_zero, mlp_zero)
    attn_one, mlp_one = gathered((attn_one, mlp_one))

    seg_count = parent.shape[0]
    labels = jnp.arange(seg_count, dtype=jnp.int32)
    parent_hot = (parent[:, None] == labels[None, :]).astype(F32)
    ancestry = jnp.eye(seg_count, dtype=F32) + parent_hot + jnp.dot(parent_hot, parent_hot)
    ancestry = (ancestry > 0.5).astype(F32)
    row_start = data * rows
    seg_rows = lax.dynamic_slice_in_dim(segments, row_start, rows, 0)
    pos_rows = lax.dynamic_slice_in_dim(places, row_start, rows, 0)
    key_hot = (segments[:, None] == labels[None, :]).astype(F32)
    query_hot = (labels[:, None] == seg_rows[None, :]).astype(F32)
    reach = jnp.dot(key_hot, jnp.dot(ancestry.T, query_hot))
    allowed = (reach > 0.5) & (places[:, None] <= pos_rows[None, :])
    bias_t = jnp.where(allowed, 0.0, MASKED).astype(BF)
    frequency = THETA ** (-(jnp.arange(HALF, dtype=F32) * 2.0 / HEAD))
    angles = frequency[:, None] * pos_rows.astype(F32)[None, :]
    cos_t, sin_t = jnp.cos(angles), jnp.sin(angles)
    ones = jnp.ones((rows, HEAD), F32)
    cos_rows = jnp.concatenate([cos_t.T, cos_t.T, ones], 1)
    sin_rows = jnp.concatenate([sin_t.T, -sin_t.T, 0 * ones], 1)
    tables = (row_start.astype(jnp.int32).reshape(1), bias_t, cos_t, sin_t, cos_rows, sin_rows)

    split_out, split_down = split, 2 * units
    wide, narrow = (F32, BF), (BF, BF)
    back = (F32, BF, F32)

    normed_zero = (hidden * lax.rsqrt(jnp.mean(hidden * hidden, -1, keepdims=True) + EPSILON) * zero[0][:1]).astype(BF)
    kept_zero, o_zero = layer_attention(normed_zero, zero, tables, 3)
    middle_zero, r_zero = product_sum(
        (o_zero, tree, zero[0]), ((0,), split_out, ("add", (1, (2, 1))), wide), zero[1], stagger=True, key=1
    )
    gate_zero, up_zero, inner_zero = layer_units(r_zero, zero)
    out_zero, normed_one = product_sum(
        (inner_zero, middle_zero, zero[0]), ((0,), split_down, ("add", (1, (2, 2))), narrow), zero[2], key=5
    )

    out_zero, normed_one, attn_one = lax.optimization_barrier((out_zero, normed_one, attn_one))
    one = with_gains(attn_one, mlp_one)
    kept_one, o_one = layer_attention(normed_one, one, tables, 14)
    middle_one, r_one = product_sum(
        (o_one, out_zero, one[0]), ((0,), split_out, ("add", (1, (2, 1))), wide), one[1], key=2
    )
    gate_one, up_one, inner_one = layer_units(r_one, one)
    branch = cot
    d_gate, d_up = units_backward(branch, one, gate_one, up_one)
    grad_middle, grad_attn, d_gain_mlp_one, d_mlp_one = product_sum(
        ((d_gate, d_up), inner_one, middle_one, branch, r_one, one[0]), ((0,), 0, ("back", (2, 3, (5, 1))), back),
        one[2], ((4, (0,)), (3, (1,))), key=8,
    )
    g_mlp_one = reduce_gradient(d_mlp_one)
    dq, dkv = attention_backward(grad_attn, one, tables, kept_one)
    grad_one, branch, d_gain_attn_one, d_attn_one = product_sum(
        ((dq, dkv), out_zero, grad_middle, one[0], normed_one, grad_attn, o_one),
        ((0,), 0, ("back", (1, 2, (3, 0))), back),
        one[1], ((4, (0,)), (5, (6,))), key=7,
    )
    g_attn_one = reduce_gradient(d_attn_one)

    d_gate, d_up = units_backward(branch, zero, gate_zero, up_zero)
    grad_middle, grad_attn, d_gain_mlp_zero, d_mlp_zero = product_sum(
        ((d_gate, d_up), inner_zero, middle_zero, branch, r_zero, zero[0]),
        ((0,), 0, ("back", (2, 3, (5, 1))), back),
        zero[2], ((4, (0,)), (3, (1,))), key=9,
    )
    g_mlp_zero = reduce_gradient(d_mlp_zero)
    grad_attn, g_mlp_one = lax.optimization_barrier((grad_attn, g_mlp_one))
    dq, dkv = attention_backward(grad_attn, zero, tables, kept_zero)
    dq, g_attn_one = lax.optimization_barrier((dq, g_attn_one))
    grad_zero, send_zero, d_gain_attn_zero, d_attn_zero = product_sum(
        ((dq, dkv), tree, grad_middle, zero[0], normed_zero, grad_attn, o_zero),
        ((0,), 0, ("back", (1, 2, (3, 0))), back),
        zero[1], ((4, (0,)), (5, (6,))), key=11,
    )
    d_gain_attn_zero, d_gain_mlp_zero, d_gain_attn_one, d_gain_mlp_one = [
        jnp.sum(x, 0) for x in (d_gain_attn_zero, d_gain_mlp_zero, d_gain_attn_one, d_gain_mlp_one)
    ]
    d_gains = jnp.stack([d_gain_attn_zero, d_gain_mlp_zero, d_gain_attn_one, d_gain_mlp_one])
    d_gains = d_gains.reshape(2, 2, devices, -1).swapaxes(1, 2).reshape(2, devices, -1, 128)

    inner_one, send_zero = lax.optimization_barrier((inner_one, send_zero))
    out_one = product_sum(
        (inner_one, middle_one), ((0,), split_down, ("add", (1,)), (BF,)), one[2], key=6
    )
    ending = finish if devices == 4 else finish_apart
    g_attn_zero, g_gain, got_out, got_in, got_mlp, got_attn = ending(
        d_attn_zero, d_gains, out_zero, out_one, send_zero, branch,
        g_mlp_one, g_attn_one,
    )

    layer_output, input_grad, *grads = write_results(
        (out_zero, out_one, got_out), (grad_zero, grad_one, got_in), (g_attn_zero, g_attn_one, got_attn), width, span
    )
    input_grad, g_mlp_zero = lax.optimization_barrier((input_grad, g_mlp_zero))
    grads += write_mlp(
        g_mlp_zero, g_mlp_one, lax.ppermute(g_mlp_zero, "section", [(1, 0)]), got_mlp, units
    )
    g_query, g_key, g_value, g_out, g_gate, g_up, g_down = [grad[None] for grad in grads]
    g_gain = g_gain.reshape(2, 1, -1)
    return (
        layer_output[None], input_grad[None], g_gain[0], g_query, g_key, g_value, g_out, g_gain[1], g_gate, g_up, g_down,
    )


def solution(mesh):
    in_specs = (
        P(None, "dp", None),
        P(None, "dp", None),
        P(),
        P(),
        P(),
        P("section", "dp"),
        P("section", "dp", "tensor"),
        P("section", "dp", "tensor"),
        P("section", "dp", "tensor"),
        P("section", "tensor", "dp"),
        P("section", "dp"),
        P("section", "dp", "tensor"),
        P("section", "dp", "tensor"),
        P("section", "tensor", "dp"),
    )
    out_specs = (
        P("section", None, "dp", None),
        P("section", None, "dp", None),
        P("section", "dp"),
        P("section", "dp", "tensor"),
        P("section", "dp", "tensor"),
        P("section", "dp", "tensor"),
        P("section", "tensor", "dp"),
        P("section", "dp"),
        P("section", "dp", "tensor"),
        P("section", "dp", "tensor"),
        P("section", "tensor", "dp"),
    )
    return jax.shard_map(shards, mesh=mesh, in_specs=in_specs, out_specs=out_specs, check_vma=False)
```

```python
import functools

import jax
import jax.numpy as jnp
from jax import lax
from jax.experimental import pallas as pl
from jax.experimental.pallas import tpu as pltpu
from jax.sharding import PartitionSpec as P

HEAD = 64
HALF = HEAD // 2
TRUNK = 1024
GROUP = 384
EPSILON = 1e-05
THETA = 10000.0
MASKED = -1e30
BF = jnp.bfloat16
F32 = jnp.float32
MESH = pl.DeviceIdType.MESH
BOTH = ("dp", "section")


def dot_f32(a, b, ca, cb):
    return lax.dot_general(a, b, (((ca,), (cb,)), ((), ())), preferred_element_type=F32)


BLOCK = 256
PIECE = 128
NO_COST = pl.CostEstimate(flops=1, transcendentals=0, bytes_accessed=1)


def columns_of(i):
    return pl.ds(pl.multiple_of(i * PIECE, PIECE), PIECE)


def gain_row(arrays, place, at):
    return arrays[place[0]][place[1] : place[1] + 1, at]


def row_scale(squares, model):
    return lax.rsqrt(jnp.sum(squares, 1, keepdims=True) * (1.0 / model) + EPSILON)


def before_sum(job, arrays, keep):
    kind, places = job[2]
    if kind == "back":
        value = arrays[places[0]]
        model = value.shape[1]
        squares = jnp.zeros(keep.shape, F32)
        for i in range(model // PIECE):
            x = value[:, i * PIECE : (i + 1) * PIECE].astype(F32)
            squares += x * x
        keep[...] = jnp.broadcast_to(row_scale(squares, model), keep.shape)


def with_piece(job, i, total, arrays, outs, keep, sums):
    kind, places = job[2]
    at = columns_of(i)
    if kind == "add":
        y = (arrays[places[0]][:, at].astype(F32) + total).astype(outs[0].dtype)
        outs[0][:, at] = y
        if len(outs) > 1:
            sums[...] += y.astype(F32) * y.astype(F32)
    if kind == "back":
        product = total * arrays[places[0]][:, at].astype(F32) * keep[...]
        sums[...] += product * gain_row(arrays, places[2], at)
        outs[2][:, at] = jnp.sum(product.reshape(-1, 8, PIECE), 0)


def after_sum(job, rows, total, arrays, outs, keep, sums):
    kind, places = job[2]
    model = arrays[places[0]].shape[1]
    at = lambda i: slice(i * PIECE, (i + 1) * PIECE)
    if kind == "add" and len(outs) > 1:
        scale = row_scale(sums[rows], model)
        for i in range(model // PIECE):
            y = outs[0][rows, at(i)].astype(F32)
            outs[1][rows, at(i)] = (y * scale * gain_row(arrays, places[1], at(i))).astype(BF)
    if kind == "back":
        mean = jnp.sum(sums[rows], 1, keepdims=True) * (1.0 / model)
        scale = keep[rows]
        for i in range(model // PIECE):
            unit = arrays[places[0]][rows, at(i)].astype(F32) * scale
            grad = total(i)[rows].astype(F32) * gain_row(arrays, places[2], at(i))
            out = arrays[places[1]][rows, at(i)].astype(F32) + scale * (grad - unit * mean)
            outs[0][rows, at(i)] = out
            outs[1][rows, at(i)] = out.astype(BF)


def product_sum_kernel(cfg, *refs):
    n_join, n_arrays, job, sides, stagger = cfg
    xs, first_column = job[:2]
    refs = list(refs)
    take = lambda n: [refs.pop(0) for _ in range(n)]
    joined = take(n_join)
    from_hbm = [None, *take(n_arrays - 1)]
    (w_hbm,) = take(1)
    outs_hbm = take(len(job[3]))
    (g_hbm,) = take(1) if sides else (None,)
    arrays = take(n_arrays)
    outs = take(len(job[3]))
    load_sem, out_sem, w_buf, p_buf, a_buf, b_buf, w_sem, sa, ra, sb, rb, sc, rc, turn, keep, sums = take(16)
    g_buf, g_sem = take(2) if sides else (None, None)
    per_block = BLOCK // PIECE
    pieces = p_buf.shape[0]
    blocks = pieces // per_block
    n_rows = p_buf.shape[1]
    early = len(xs)
    lag = 2
    assert xs[0] == 0

    t = lax.axis_index("tensor")
    sec = lax.axis_index("section")
    dat = lax.axis_index("dp")
    inner = (t == 1) | (t == 2)
    outer = jnp.logical_not(inner)
    pair = (sec, t + 1 - 2 * lax.rem(t, 2), dat)
    mid = (sec, 3 - t, dat)
    mate = (1 - sec, t, dat)

    def columns(j):
        return pl.ds(pl.multiple_of(j * BLOCK, BLOCK), BLOCK)

    def to_inner(i):
        return pltpu.make_async_remote_copy(
            p_buf.at[i], a_buf.at[i], sa.at[i], ra.at[i], device_id=pair, device_id_type=MESH
        )

    def across(i):
        return pltpu.make_async_remote_copy(
            p_buf.at[i], b_buf.at[i], sb.at[i], rb.at[i], device_id=mid, device_id_type=MESH
        )

    def to_outer(i):
        return pltpu.make_async_remote_copy(
            b_buf.at[i], b_buf.at[i], sc.at[i], rc.at[i], device_id=pair, device_id_type=MESH
        )

    def load(k):
        return pltpu.make_async_copy(from_hbm[k], arrays[k], load_sem.at[k])

    def join():
        copies, start = [], 0
        for m, src in enumerate(joined):
            at = pl.ds(start, src.shape[1])
            copies.append(pltpu.make_async_copy(src, arrays[0].at[:, at], load_sem.at[n_arrays + m]))
            start += src.shape[1]
        return copies

    def fetch(j, slot):
        return pltpu.make_async_copy(
            w_hbm.at[columns(j), pl.ds(first_column, w_buf.shape[2])], w_buf.at[slot], w_sem.at[slot]
        )

    def flush(j, slot):
        return pltpu.make_async_copy(g_buf.at[slot], g_hbm.at[columns(j), :], g_sem.at[slot])

    def every_piece(body):
        def turn_of(i, _):
            body(i)
            return 0

        lax.fori_loop(0, pieces, turn_of, 0)

    for copy in join():
        copy.start()
    for k in range(1, early):
        load(k).start()
    fetch(0, 0).start()
    for k in range(early, n_arrays):
        load(k).start()
    barrier = pltpu.get_barrier_semaphore()
    pl.semaphore_signal(barrier, inc=1, device_id=pair, device_id_type=MESH)
    sums[...] = jnp.zeros_like(sums)

    @pl.when(inner)
    def _():
        pl.semaphore_signal(barrier, inc=1, device_id=mid, device_id_type=MESH)
        pl.semaphore_wait(barrier, 2)

    @pl.when(outer)
    def _():
        if stagger:
            pl.semaphore_signal(barrier, inc=1, device_id=mate, device_id_type=MESH)
            pl.semaphore_wait(barrier, 2)

            @pl.when(sec == 1)
            def _():
                pl.semaphore_wait(turn, 1)

        else:
            pl.semaphore_wait(barrier, 1)

    for copy in join():
        copy.wait()
    for k in range(1, early):
        load(k).wait()

    def done(i):
        with_piece(job, i, b_buf[i].astype(F32), arrays, outs, keep, sums)

    def first(i):
        to_inner(i).wait_recv()
        p_buf[i] = p_buf[i] + a_buf[i]
        across(i).start()

    def second(i):
        across(i).wait_recv()
        b_buf[i] = p_buf[i] + b_buf[i]
        to_outer(i).start()
        done(i)

    def side(j):
        slot = lax.rem(j, 2)

        @pl.when(j >= 2)
        def _():
            flush(j - 2, slot).wait()

        start = 0
        for a, bs in sides:
            a_t = arrays[a][:, columns(j)].T
            for b in bs:
                width = arrays[b].shape[1]
                g_buf[slot, :, start : start + width] = jnp.dot(
                    a_t, arrays[b][...], preferred_element_type=F32
                ).astype(BF)
                start += width
        flush(j, slot).start()
        return 0

    def step(j, _):
        slot = lax.rem(j, 2)
        fetch(j, slot).wait()

        @pl.when(j + 1 < blocks)
        def _():
            fetch(j + 1, 1 - slot).start()

        total, start = None, 0
        for x in xs:
            width = arrays[x].shape[1]
            term = dot_f32(arrays[x][...], w_buf[slot, :, start : start + width], 1, 1)
            total = term if total is None else total + term
            start += width
        total = total.astype(BF)
        for u in range(per_block):
            p_buf[per_block * j + u] = total[:, u * PIECE : (u + 1) * PIECE]

        @pl.when(outer)
        def _():
            for u in range(per_block):
                to_inner(per_block * j + u).start()

        @pl.when(j == 1)
        def _():
            for k in range(early, n_arrays):
                load(k).wait()
            before_sum(job, arrays, keep)

        if sides:

            @pl.when(j >= lag)
            def _():
                side(j - lag)

        @pl.when(inner)
        def _():
            for u in range(per_block):
                i = per_block * j + u
                first(i)

                @pl.when(j >= 1)
                def _():
                    second(i - per_block)

        return 0

    lax.fori_loop(0, blocks, step, 0)

    @pl.when(inner)
    def _():
        for u in range(per_block):
            second(pieces - per_block + u)

    if sides:
        lax.fori_loop(blocks - lag, blocks, lambda j, _: side(j), 0)

    @pl.when(outer)
    def _():
        every_piece(lambda i: to_inner(i).wait_send())

        def arrive(i):
            to_outer(i).wait_recv()
            done(i)

        every_piece(arrive)

    chunks = 5 if n_rows % (5 * 32) == 0 else 1
    chunk = n_rows // chunks
    block = 32 if chunk % 32 == 0 else 16
    height = lambda m: 8 if job[2][0] == "back" and m == 2 else n_rows
    stores = []

    def store(m, rows):
        copy = pltpu.make_async_copy(outs[m].at[rows], outs_hbm[m].at[rows], out_sem.at[len(stores)])
        copy.start()
        stores.append(copy)

    for c in range(chunks):

        def turn_rows(r, _):
            rows = pl.ds(pl.multiple_of(c * chunk + r * block, block), block)
            after_sum(job, rows, lambda i: b_buf.at[i], arrays, outs, keep, sums)
            return 0

        if job[2][0] == "back" or len(outs) > 1:
            lax.fori_loop(0, chunk // block, turn_rows, 0)
        for m in range(len(outs)):
            if height(m) == n_rows:
                store(m, pl.ds(c * chunk, chunk))
    for m in range(len(outs)):
        if height(m) != n_rows:
            store(m, pl.ds(0, height(m)))

    @pl.when(inner)
    def _():
        def sent(i):
            across(i).wait_send()
            to_outer(i).wait_send()

        every_piece(sent)

    if sides:
        flush(blocks - 2, (blocks - 2) % 2).wait()
        flush(blocks - 1, (blocks - 1) % 2).wait()
    for copy in stores:
        copy.wait()

    if stagger:

        @pl.when(outer & (sec == 0))
        def _():
            pl.semaphore_signal(turn, inc=1, device_id=mate, device_id_type=MESH)


def product_sum(arrays, job, weights, sides=(), stagger=False, key=1):
    assert lax.axis_size("tensor") == 4
    first = arrays[0] if isinstance(arrays[0], tuple) else (arrays[0],)
    given = (*first, *arrays[1:])
    rows, model = first[0].shape[0], weights.shape[0]
    arrays = (jax.ShapeDtypeStruct((rows, sum(x.shape[1] for x in first)), BF), *arrays[1:])
    pieces = model // PIECE
    depth = sum(arrays[x].shape[1] for x in job[0])
    anywhere = pl.BlockSpec(memory_space=pl.ANY)
    buf = pltpu.VMEM((pieces, rows, PIECE), BF)
    sem = pltpu.SemaphoreType.DMA((pieces,))
    two = pltpu.SemaphoreType.DMA((2,))
    out_shape = []
    for m, dtype in enumerate(job[3]):
        height = 8 if job[2][0] == "back" and m == 2 else rows
        out_shape.append(jax.ShapeDtypeStruct((height, model), dtype))
    scratch = [pltpu.VMEM(x.shape, x.dtype) for x in (*arrays, *out_shape)]
    scratch += [pltpu.SemaphoreType.DMA((len(arrays) + len(first),)), pltpu.SemaphoreType.DMA((16,))]
    scratch += [pltpu.VMEM((2, BLOCK, depth), BF), buf, buf, buf, two, *[sem] * 6, pltpu.SemaphoreType.REGULAR]
    scratch += [pltpu.VMEM((rows, PIECE), F32)] * 2
    if sides:
        side_width = sum(arrays[b].shape[1] for _, bs in sides for b in bs)
        out_shape.append(jax.ShapeDtypeStruct((model, side_width), BF))
        scratch += [pltpu.VMEM((2, BLOCK, side_width), BF), two]
    out = pl.pallas_call(
        functools.partial(product_sum_kernel, (len(first), len(arrays), job, tuple(sides), stagger)),
        out_shape=out_shape,
        in_specs=[anywhere] * (len(given) + 1),
        out_specs=[anywhere] * len(out_shape),
        scratch_shapes=scratch,
        compiler_params=pltpu.CompilerParams(
            collective_id=key, has_side_effects=True, vmem_limit_bytes=62 << 20
        ),
        cost_estimate=NO_COST,
        name=f"product_sum_{key}",
    )(*given, weights)
    return out if len(out) > 1 else out[0]


def dp_peers(count):
    me = lax.axis_index("dp")
    sec, t = lax.axis_index("section"), lax.axis_index("tensor")
    others = [lax.rem(me + k, count) for k in range(1, count)]
    return me, others, [(sec, t, other) for other in others]


def greet(ids):
    barrier = pltpu.get_barrier_semaphore()
    for device in ids:
        pl.semaphore_signal(barrier, inc=1, device_id=device, device_id_type=MESH)
    pl.semaphore_wait(barrier, len(ids))


def turn_rows(x, cos_ref, sin_ref):
    lane = lax.broadcasted_iota(jnp.int32, x.shape, 1)
    width = x.shape[1]
    partner = jnp.where(lane < HALF, pltpu.roll(x, width - HALF, 1), pltpu.roll(x, HALF, 1))
    return x * cos_ref[...] + partner * sin_ref[...]


def gather_kernel(
    count, normed_ref, w_hbm, cos_ref, sin_ref, o_ref, t_ref, q_ref, x_ref, w_buf, load_sem, send, recv
):
    me, _, ids = dp_peers(count)
    load = pltpu.make_async_copy(w_hbm.at[:, pl.ds(0, w_buf.shape[1])], w_buf, load_sem)
    load.start()
    load.wait()
    width = q_ref.shape[0]
    raw = jnp.dot(normed_ref[...], w_buf[:, width:], preferred_element_type=F32)
    x_ref[...] = turn_rows(raw, cos_ref, sin_ref).astype(BF)
    greet(ids)
    copies = [
        pltpu.make_async_remote_copy(
            x_ref, o_ref.at[me], send.at[k], recv.at[k], device_id=device, device_id_type=MESH
        )
        for k, device in enumerate(ids)
    ]
    for copy in copies:
        copy.start()
    o_ref[me] = x_ref[...]
    q_ref[...] = jnp.dot(normed_ref[...], w_buf[:, :width], preferred_element_type=F32).T
    for copy in copies:
        copy.wait()
    t_ref[...] = o_ref[...].reshape(t_ref.shape[1], t_ref.shape[0]).T


def scatter_kernel(count, x_ref, cos_ref, sin_ref, o_ref, buf, send, recv):
    me, others, ids = dp_peers(count)
    greet(ids)
    copies = [
        pltpu.make_async_remote_copy(
            x_ref.at[others[k]], buf.at[k], send.at[k], recv.at[k], device_id=device, device_id_type=MESH
        )
        for k, device in enumerate(ids)
    ]
    for copy in copies:
        copy.start()
    total = x_ref[me].astype(F32)
    for k, copy in enumerate(copies):
        copy.wait()
        total = total + buf[k].astype(F32)
    o_ref[...] = turn_rows(total, cos_ref, sin_ref).astype(BF)


def gather_rows(normed, w_attn, width, split, cos_rows, sin_rows, key):
    count = lax.axis_size("dp")
    rows, span = normed.shape[0], split - width
    in_vmem = pl.BlockSpec(memory_space=pltpu.VMEM)
    sem = pltpu.SemaphoreType.DMA((count - 1,))
    out, out_t, q_t = pl.pallas_call(
        functools.partial(gather_kernel, count),
        out_shape=(
            jax.ShapeDtypeStruct((count, rows, span), BF),
            jax.ShapeDtypeStruct((span, count * rows), BF),
            jax.ShapeDtypeStruct((width, rows), F32),
        ),
        in_specs=[in_vmem, pl.BlockSpec(memory_space=pl.ANY), in_vmem, in_vmem],
        out_specs=(in_vmem, in_vmem, in_vmem),
        scratch_shapes=[
            pltpu.VMEM((rows, span), BF), pltpu.VMEM((normed.shape[1], split), BF),
            pltpu.SemaphoreType.DMA, sem, sem,
        ],
        compiler_params=pltpu.CompilerParams(
            collective_id=key, has_side_effects=True, vmem_limit_bytes=40 << 20
        ),
        cost_estimate=NO_COST,
        name="gather_rows",
    )(normed, w_attn, cos_rows, sin_rows)
    return out.reshape(-1, span), out_t, q_t


def scatter_rows(x, cos_rows, sin_rows):
    count = lax.axis_size("dp")
    rows, width = x.shape[0] // count, x.shape[1]
    in_vmem = pl.BlockSpec(memory_space=pltpu.VMEM)
    sem = pltpu.SemaphoreType.DMA((count - 1,))
    return pl.pallas_call(
        functools.partial(scatter_kernel, count),
        out_shape=jax.ShapeDtypeStruct((rows, width), BF),
        in_specs=[in_vmem] * 3,
        out_specs=in_vmem,
        scratch_shapes=[pltpu.VMEM((count - 1, rows, width), x.dtype), sem, sem],
        compiler_params=pltpu.CompilerParams(collective_id=4, has_side_effects=True),
        cost_estimate=NO_COST,
        name="scatter_rows",
    )(x.reshape(count, rows, width), cos_rows, sin_rows)


def finish_kernel(
    g_hbm, gain_ref, out_zero, out_one, in_zero, in_one, mlp_one, attn_one,
    o_ref, gain_out, got_out, got_in, got_mlp, got_attn,
    mine, away, got, xs, ys, xr, yr, gains, load_sem, send, recv, mate_send, mate_recv, gain_send, gain_recv,
):
    sec, t, dat = lax.axis_index("section"), lax.axis_index("tensor"), lax.axis_index("dp")
    flip_x = dat + 1 - 2 * lax.rem(dat, 2)
    flip_y = lax.rem(dat + 2, 4)
    across = lax.rem(flip_x + 2, 4)
    by_x, by_y, mate = (sec, t, flip_x), (sec, t, flip_y), (1 - sec, t, dat)
    peers = [
        mate, by_x, by_y, (sec, t, across),
        (1 - sec, t, flip_x), (1 - sec, t, flip_y), (1 - sec, t, across),
    ]
    rows = g_hbm.shape[1] // 2
    upper, lower = pl.ds(0, rows), pl.ds(rows, rows)
    order = (across, flip_x, flip_y, dat)
    loads = []
    for k, block in enumerate(order):
        loads.append(pltpu.make_async_copy(g_hbm.at[2 * block + 1 - sec], away.at[k], load_sem.at[k]))
        loads.append(pltpu.make_async_copy(g_hbm.at[2 * block + sec], mine.at[k], load_sem.at[4 + k]))
    for copy in loads:
        copy.start()
    greet(peers)

    def remote(src, dst, k, device):
        return pltpu.make_async_remote_copy(
            src, dst, send.at[k], recv.at[k], device_id=device, device_id_type=MESH
        )

    def to_mate(src, dst, k):
        return pltpu.make_async_remote_copy(
            src, dst, mate_send.at[k], mate_recv.at[k], device_id=mate, device_id_type=MESH
        )

    swaps = [remote(away.at[k], got.at[k], k, mate) for k in range(4)]
    for k in range(4):
        loads[2 * k].wait()
        swaps[k].start()
    gain_copies = [
        pltpu.make_async_remote_copy(
            gain_ref.at[peer[0], peer[2]], gains.at[k], gain_send.at[k], gain_recv.at[k],
            device_id=peer, device_id_type=MESH,
        )
        for k, peer in enumerate(peers)
    ]
    for copy in gain_copies:
        copy.start()
    outs = []
    for k in range(4):
        loads[2 * k + 1].wait()
        swaps[k].wait_recv()
        mine[k] = (mine[k].astype(F32) + got[k].astype(F32)).astype(BF)
        if k == 0:
            outs += [remote(mine.at[0, upper], xs.at[0], 4, by_x), remote(mine.at[0, lower], ys.at[0], 5, by_y)]
        if k == 1:
            outs += [remote(mine.at[1, upper], xs.at[1], 6, by_x)]
        if k == 2:
            outs += [remote(mine.at[2, lower], ys.at[1], 7, by_y)]
        for copy in outs[-(2 if k == 0 else 1) :]:
            if k < 3:
                copy.start()

    @pl.when(sec == 0)
    def _():
        to_mate(in_one, got_in, 0).start()
        to_mate(out_one, got_out, 1).start()
        to_mate(mlp_one, got_mlp, 2).start()
        to_mate(attn_one, got_attn, 3).start()

    @pl.when(sec == 1)
    def _():
        to_mate(in_zero, got_in, 0).start()
        to_mate(out_zero, got_out, 1).start()

    outs[0].wait_recv()
    mine[2, upper] = (mine[2, upper].astype(F32) + xs[0].astype(F32)).astype(BF)
    outs.append(remote(mine.at[2, upper], yr, 8, by_y))
    outs[4].start()
    outs[1].wait_recv()
    mine[1, lower] = (mine[1, lower].astype(F32) + ys[0].astype(F32)).astype(BF)
    outs.append(remote(mine.at[1, lower], xr, 9, by_x))
    outs[5].start()
    total = gain_ref[sec, dat]
    for k, copy in enumerate(gain_copies):
        copy.wait()
        total = total + gains[k]
    gain_out[...] = total
    outs[2].wait_recv()
    outs[3].wait_recv()
    outs[4].wait_recv()
    o_ref[upper] = (mine[3, upper].astype(F32) + xs[1].astype(F32) + yr[...].astype(F32)).astype(BF)
    outs[5].wait_recv()
    o_ref[lower] = (mine[3, lower].astype(F32) + ys[1].astype(F32) + xr[...].astype(F32)).astype(BF)

    @pl.when(sec == 1)
    def _():
        to_mate(o_ref, got_attn, 3).start()

    for copy in swaps + outs:
        copy.wait_send()
    to_mate(in_one, got_in, 0).wait()
    to_mate(out_one, got_out, 1).wait()
    to_mate(attn_one, got_attn, 3).wait()

    @pl.when(sec == 0)
    def _():
        to_mate(mlp_one, got_mlp, 2).wait_send()

    @pl.when(sec == 1)
    def _():
        to_mate(mlp_one, got_mlp, 2).wait_recv()


def finish(g, gains, out_zero, out_one, in_zero, in_one, mlp_one, attn_one):
    rows, width = g.shape[0] // 8, g.shape[1]
    part = pltpu.VMEM((2, rows // 2, width), BF)
    whole = pltpu.VMEM((4, rows, width), BF)
    end = pltpu.VMEM((rows // 2, width), BF)
    in_vmem, anywhere = pl.BlockSpec(memory_space=pltpu.VMEM), pl.BlockSpec(memory_space=pl.ANY)
    like = lambda x: jax.ShapeDtypeStruct(x.shape, x.dtype)
    dma = lambda n: pltpu.SemaphoreType.DMA((n,))
    return pl.pallas_call(
        finish_kernel,
        out_shape=(
            jax.ShapeDtypeStruct((rows, width), BF),
            jax.ShapeDtypeStruct(gains.shape[2:], F32),
            like(out_zero), like(in_zero), like(mlp_one), like(attn_one),
        ),
        in_specs=[anywhere, in_vmem, *[anywhere] * 6],
        out_specs=(in_vmem, in_vmem, *[anywhere] * 4),
        scratch_shapes=[
            whole, whole, whole, part, part, end, end, pltpu.VMEM((7, *gains.shape[2:]), F32),
            dma(8), dma(10), dma(10), dma(4), dma(4), dma(7), dma(7),
        ],
        compiler_params=pltpu.CompilerParams(
            collective_id=12, has_side_effects=True, vmem_limit_bytes=62 << 20
        ),
        cost_estimate=NO_COST,
        name="finish",
    )(g.reshape(8, rows, width), gains, out_zero, out_one, in_zero, in_one, mlp_one, attn_one)


def finish_apart(g, gains, out_zero, out_one, in_zero, in_one, mlp_one, attn_one):
    first_core = lax.axis_index("section") == 0
    half = reduce_gradient(g)
    swap = lambda zero, one: lax.ppermute(jnp.where(first_core, one, zero), "section", [(0, 1), (1, 0)])
    return (
        half, share_sums(gains), swap(out_zero, out_one), swap(in_zero, in_one),
        lax.ppermute(mlp_one, "section", [(0, 1)]), swap(half, attn_one),
    )


def in_rows(count, block, body):
    def turn(r, _):
        body(pl.ds(pl.multiple_of(r * block, block), block))
        return 0

    lax.fori_loop(0, count // block, turn, 0)


def widen_turned(dst, src, start, width):
    for c in range(0, width, 128):
        dst[c : c + 128] = src[:, start + c : start + c + 128].astype(F32).T


def write_mlp_kernel(
    zero, one, from_one, from_zero, gate_hbm, up_hbm, down_hbm, mlp, gate_buf, up_buf, down_buf, load_sem, store_sem
):
    sec = lax.axis_index("section")
    half, units = zero.shape[0], gate_buf.shape[1]
    low, high = pl.ds(0, half), pl.ds(half, half)
    load = lambda src, at, k: pltpu.make_async_copy(src, mlp.at[at], load_sem.at[k])
    store = lambda src, dst, k: pltpu.make_async_copy(src, dst, store_sem.at[k])

    @pl.when(sec == 0)
    def _():
        load(zero, low, 0).start()
        load(from_one, high, 1).start()

    @pl.when(sec == 1)
    def _():
        load(from_zero, low, 0).start()
        load(one, high, 1).start()

    load(zero, low, 0).wait()
    load(zero, high, 1).wait()

    def gates(rows):
        gate_buf[rows] = mlp[rows, :units].astype(F32)
        up_buf[rows] = mlp[rows, units : 2 * units].astype(F32)

    in_rows(2 * half, 32, gates)
    stores = [store(gate_buf, gate_hbm, 0), store(up_buf, up_hbm, 1), store(down_buf, down_hbm, 2)]
    stores[0].start()
    stores[1].start()
    widen_turned(down_buf, mlp, 2 * units, units)
    stores[2].start()
    for copy in stores:
        copy.wait()


def write_mlp(zero, one, from_one, from_zero, units):
    shard = 2 * zero.shape[0]
    anywhere = pl.BlockSpec(memory_space=pl.ANY)
    shapes = [(shard, units), (shard, units), (units, shard)]
    return pl.pallas_call(
        write_mlp_kernel,
        out_shape=[jax.ShapeDtypeStruct(shape, F32) for shape in shapes],
        in_specs=[anywhere] * 4,
        out_specs=[anywhere] * 3,
        scratch_shapes=[
            pltpu.VMEM((shard, zero.shape[1]), BF),
            *[pltpu.VMEM(shape, F32) for shape in shapes],
            pltpu.SemaphoreType.DMA((2,)),
            pltpu.SemaphoreType.DMA((3,)),
        ],
        compiler_params=pltpu.CompilerParams(vmem_limit_bytes=62 << 20),
        cost_estimate=NO_COST,
        name="write_mlp",
    )(zero, one, from_one, from_zero)


def write_kernel(
    split, out_zero, out_one, got_out, in_zero, in_one, got_in, attn_zero, attn_one, got_attn,
    out_hbm, in_hbm, q_hbm, k_hbm, v_hbm, o_hbm,
    outs, wides, attn, narrow, q_buf, k_buf, v_buf, o_buf, load_sem, store_sem,
):
    sec = lax.axis_index("section")
    half = attn_zero.shape[0]
    low, high = pl.ds(0, half), pl.ds(half, half)
    load = lambda src, dst, k: pltpu.make_async_copy(src, dst, load_sem.at[k])
    store = lambda src, dst, k: pltpu.make_async_copy(src, dst, store_sem.at[k])

    def start(own_out, own_in, attn_low, attn_high):
        load(own_out, outs.at[0], 0).start()
        load(own_in, wides.at[0], 1).start()
        load(attn_low, attn.at[low], 2).start()
        load(attn_high, attn.at[high], 3).start()

    @pl.when(sec == 0)
    def _():
        start(out_zero, in_zero, attn_zero, got_attn)

    @pl.when(sec == 1)
    def _():
        start(out_one, in_one, got_attn, attn_one)

    load(got_in, narrow, 4).start()
    load(got_out, outs.at[1], 5).start()
    stores = [
        store(outs.at[0], out_hbm.at[sec], 0),
        store(wides.at[0], in_hbm.at[sec], 1),
        store(outs.at[1], out_hbm.at[1 - sec], 2),
        store(wides.at[1], in_hbm.at[1 - sec], 3),
        store(q_buf, q_hbm, 4),
        store(k_buf, k_hbm, 5),
        store(v_buf, v_hbm, 6),
        store(o_buf, o_hbm, 7),
    ]
    load(out_zero, outs.at[0], 0).wait()
    stores[0].start()
    load(in_zero, wides.at[0], 1).wait()
    stores[1].start()
    width, span = q_buf.shape[1], k_buf.shape[1]
    load(attn_one, attn.at[low], 2).wait()
    load(attn_one, attn.at[high], 3).wait()

    def projections(rows):
        q_buf[rows] = attn[rows, :width].astype(F32)
        k_buf[rows] = attn[rows, width : width + span].astype(F32)
        v_buf[rows] = attn[rows, width + span : split].astype(F32)

    in_rows(2 * half, 32, projections)
    for k in (4, 5, 6):
        stores[k].start()
    widen_turned(o_buf, attn, split, width)
    stores[7].start()
    load(got_in, narrow, 4).wait()

    def widen(rows):
        wides[1, rows] = narrow[rows].astype(F32)

    in_rows(narrow.shape[0], 32, widen)
    stores[3].start()
    load(got_out, outs.at[1], 5).wait()
    stores[2].start()
    for copy in stores:
        copy.wait()


def write_results(results, ins, attns, width, span):
    rows, model = results[0].shape
    shard = 2 * attns[0].shape[0]
    anywhere = pl.BlockSpec(memory_space=pl.ANY)
    shapes = [(shard, width), (shard, span), (shard, span), (width, shard)]
    return pl.pallas_call(
        functools.partial(write_kernel, width + 2 * span),
        out_shape=[
            jax.ShapeDtypeStruct((2, rows, model), BF),
            jax.ShapeDtypeStruct((2, rows, model), F32),
            *[jax.ShapeDtypeStruct(shape, F32) for shape in shapes],
        ],
        in_specs=[anywhere] * 9,
        out_specs=[anywhere] * 6,
        scratch_shapes=[
            pltpu.VMEM((2, rows, model), BF),
            pltpu.VMEM((2, rows, model), F32),
            pltpu.VMEM((shard, attns[0].shape[1]), BF),
            pltpu.VMEM((rows, model), BF),
            *[pltpu.VMEM(shape, F32) for shape in shapes],
            pltpu.SemaphoreType.DMA((6,)),
            pltpu.SemaphoreType.DMA((8,)),
        ],
        compiler_params=pltpu.CompilerParams(vmem_limit_bytes=62 << 20),
        cost_estimate=NO_COST,
        name="write_results",
    )(*results, *ins, *attns)


def share_kernel(count, x_ref, o_ref, buf, send, recv):
    sec, t, dat = lax.axis_index("section"), lax.axis_index("tensor"), lax.axis_index("dp")
    peers = [
        (lax.rem(sec + k // count, 2), t, lax.rem(dat + k % count, count)) for k in range(1, 2 * count)
    ]
    greet(peers)
    copies = [
        pltpu.make_async_remote_copy(
            x_ref.at[peer[0], peer[2]], buf.at[k], send.at[k], recv.at[k], device_id=peer, device_id_type=MESH
        )
        for k, peer in enumerate(peers)
    ]
    for copy in copies:
        copy.start()
    total = x_ref[sec, dat]
    for k, copy in enumerate(copies):
        copy.wait()
        total = total + buf[k]
    o_ref[...] = total


def share_sums(x):
    count = lax.axis_size("dp")
    in_vmem = pl.BlockSpec(memory_space=pltpu.VMEM)
    sem = pltpu.SemaphoreType.DMA((2 * count - 1,))
    return pl.pallas_call(
        functools.partial(share_kernel, count),
        out_shape=jax.ShapeDtypeStruct(x.shape[2:], F32),
        in_specs=[in_vmem],
        out_specs=in_vmem,
        scratch_shapes=[pltpu.VMEM((2 * count - 1, *x.shape[2:]), F32), sem, sem],
        compiler_params=pltpu.CompilerParams(collective_id=13, has_side_effects=True),
        cost_estimate=NO_COST,
        name="share_sums",
    )(x)


def group_start(first_row):
    past = lax.max(first_row - TRUNK, 0)
    return pl.multiple_of(TRUNK + GROUP * lax.div(past, GROUP), 128)


def over_windows(tree_len, rows, tile, first_row, run):
    if tile % 128 == 0 and GROUP % tile == 0 and TRUNK % tile == 0 and rows % tile == 0:
        run(((pl.ds(0, TRUNK), True), (pl.ds(group_start(first_row), GROUP), True)))
    else:
        run(((pl.ds(0, tree_len), True),))


def masked(scores, bias_ref, win, step):
    bias = bias_ref[win, :].astype(F32)
    return scores + (bias if step == 1 else jnp.concatenate([bias] * step, axis=1))


def head_rows(ref, head):
    return ref[head * HEAD : (head + 1) * HEAD, :]


def beside(ref, head, count):
    parts = [head_rows(ref, head + k) for k in range(count)]
    return parts[0] if count == 1 else jnp.concatenate(parts, axis=1)


def turned_beside(ref, cos, sin, head, count):
    parts = []
    for k in range(count):
        rows = head_rows(ref, head + k)
        first, second = rows[:HALF], rows[HALF:]
        parts.append(jnp.concatenate([first * cos - second * sin, second * cos + first * sin], axis=0))
    whole = parts[0] if count == 1 else jnp.concatenate(parts, axis=1)
    return (whole.astype(BF).astype(F32) * HEAD**-0.5).astype(BF)


def as_rows(x, tile, count):
    parts = [x[:, k * tile : (k + 1) * tile] for k in range(count)]
    return (parts[0] if count == 1 else jnp.concatenate(parts, axis=0)).T


def over_groups(groups, step, body):
    for group in range(groups):
        body(group, slice(group * step * HEAD, (group + 1) * step * HEAD))


def attend_kernel(
    rows, step, start_ref, q_ref, kv_ref, kvt_ref, bias_ref, cos_ref, sin_ref, o_ref, on_ref, lse_ref
):
    tile = q_ref.shape[1]
    heads = q_ref.shape[0] // HEAD
    first_row = start_ref[0] + pl.program_id(0) * tile

    def body(wins, group, lanes):
        head = group * step
        q = turned_beside(q_ref, cos_ref[...], sin_ref[...], head, step)
        scores = []
        for win, mask in wins:
            score = dot_f32(kv_ref[win, :HEAD], q, 1, 0)
            scores.append(masked(score, bias_ref, win, step) if mask else score)
        top = functools.reduce(jnp.maximum, [jnp.max(s, 0, keepdims=True) for s in scores])
        expo = [jnp.exp(s - top) for s in scores]
        total = sum(jnp.sum(e, 0, keepdims=True) for e in expo)
        out = sum(dot_f32(kvt_ref[HEAD:, win], e.astype(BF), 1, 0) for (win, _), e in zip(wins, expo))
        out = out / total
        on_ref[:, lanes] = as_rows(out, tile, step).astype(BF)
        lse_ref[group, 0] = top + jnp.log(total)
        out = out.astype(BF)
        for k in range(step):
            o_ref[(head + k) * HEAD : (head + k + 1) * HEAD, :] = out[:, k * tile : (k + 1) * tile]

    over_windows(
        kv_ref.shape[0], rows, tile, first_row,
        lambda wins: over_groups(heads // step, step, functools.partial(body, wins)),
    )


def attend_back_kernel(
    rows, step, start_ref, q_ref, do_ref, o_ref, lse_ref, kv_ref, kvt_ref, bias_ref, cos_ref, sin_ref,
    dq_ref, dkv_ref, dk_acc, dv_acc,
):
    tile = q_ref.shape[1]
    heads = q_ref.shape[0] // HEAD
    first_row = start_ref[0] + pl.program_id(0) * tile

    @pl.when(pl.program_id(0) == 0)
    def _():
        dk_acc[...] = jnp.zeros_like(dk_acc)
        dv_acc[...] = jnp.zeros_like(dv_acc)

    def body(wins, group, lanes):
        head = group * step
        cos, sin = cos_ref[...], sin_ref[...]
        q = turned_beside(q_ref, cos, sin, head, step)
        do = beside(do_ref, head, step)
        out = beside(o_ref, head, step)
        lse = lse_ref[group, 0]
        delta = jnp.sum(do.astype(F32) * out.astype(F32), 0, keepdims=True)
        dq = jnp.zeros((HEAD, step * tile), F32)
        for win, mask in wins:
            score = dot_f32(kv_ref[win, :HEAD], q, 1, 0)
            p = jnp.exp((masked(score, bias_ref, win, step) if mask else score) - lse)
            dp = dot_f32(kv_ref[win, HEAD:], do, 1, 0)
            ds = (p * (dp - delta)).astype(BF)
            dk_acc[win, :] += dot_f32(ds, q, 1, 1)
            dv_acc[win, :] += dot_f32(p.astype(BF), do, 1, 1)
            dq = dq + dot_f32(kvt_ref[:HEAD, win], ds, 1, 0)
        dq = dq * HEAD**-0.5
        turned = []
        for k in range(step):
            first = dq[:HALF, k * tile : (k + 1) * tile]
            second = dq[HALF:, k * tile : (k + 1) * tile]
            turned += [first * cos + second * sin, second * cos - first * sin]
        dq_ref[:, lanes] = jnp.concatenate(turned, axis=0).T.astype(BF)

    over_windows(
        kv_ref.shape[0], rows, tile, first_row,
        lambda wins: over_groups(heads // step, step, functools.partial(body, wins)),
    )

    @pl.when(pl.program_id(0) == pl.num_programs(0) - 1)
    def _():
        dkv_ref[...] = jnp.concatenate([dk_acc[...], dv_acc[...]], axis=1).astype(BF)


def row_tile(rows):
    return 128 if rows % 128 == 0 else rows


def attend(start, q_t, kv, kv_t, bias_t, cos_t, sin_t):
    width, rows = q_t.shape
    heads, tree_len, tile = width // HEAD, kv.shape[0], row_tile(rows)
    step = 2 if tile % 128 == 0 and heads % 2 == 0 else 1
    column = lambda i, s: (0, i)
    whole = lambda i, s: (0, 0)
    return pl.pallas_call(
        functools.partial(attend_kernel, rows, step),
        out_shape=(
            jax.ShapeDtypeStruct((width, rows), BF),
            jax.ShapeDtypeStruct((rows, width), BF),
            jax.ShapeDtypeStruct((heads // step, rows // tile, 1, step * tile), F32),
        ),
        grid_spec=pltpu.PrefetchScalarGridSpec(
            num_scalar_prefetch=1,
            grid=(rows // tile,),
            in_specs=[
                pl.BlockSpec((width, tile), column),
                pl.BlockSpec((tree_len, 2 * HEAD), whole),
                pl.BlockSpec((2 * HEAD, tree_len), whole),
                pl.BlockSpec((tree_len, tile), column),
                pl.BlockSpec((HALF, tile), column),
                pl.BlockSpec((HALF, tile), column),
            ],
            out_specs=(
                pl.BlockSpec((width, tile), column),
                pl.BlockSpec((tile, width), lambda i, s: (i, 0)),
                pl.BlockSpec((heads // step, 1, 1, step * tile), lambda i, s: (0, i, 0, 0)),
            ),
        ),
        compiler_params=pltpu.CompilerParams(vmem_limit_bytes=62 << 20),
        cost_estimate=NO_COST,
        name="attend",
    )(start, q_t, kv, kv_t, bias_t, cos_t, sin_t)


def attend_back(start, q_t, do_t, o_t, lse, kv, kv_t, bias_t, cos_t, sin_t):
    width, rows = q_t.shape
    heads, tree_len, tile = width // HEAD, kv.shape[0], row_tile(rows)
    step = 2 if tile % 128 == 0 and heads % 2 == 0 else 1
    column = lambda i, s: (0, i)
    whole = lambda i, s: (0, 0)
    return pl.pallas_call(
        functools.partial(attend_back_kernel, rows, step),
        out_shape=(
            jax.ShapeDtypeStruct((rows, width), BF),
            jax.ShapeDtypeStruct((tree_len, 2 * HEAD), BF),
        ),
        grid_spec=pltpu.PrefetchScalarGridSpec(
            num_scalar_prefetch=1,
            grid=(rows // tile,),
            in_specs=[
                pl.BlockSpec((width, tile), column),
                pl.BlockSpec((width, tile), column),
                pl.BlockSpec((width, tile), column),
                pl.BlockSpec((heads // step, 1, 1, step * tile), lambda i, s: (0, i, 0, 0)),
                pl.BlockSpec((tree_len, 2 * HEAD), whole),
                pl.BlockSpec((2 * HEAD, tree_len), whole),
                pl.BlockSpec((tree_len, tile), column),
                pl.BlockSpec((HALF, tile), column),
                pl.BlockSpec((HALF, tile), column),
            ],
            out_specs=(
                pl.BlockSpec((tile, width), lambda i, s: (i, 0)),
                pl.BlockSpec((tree_len, 2 * HEAD), whole),
            ),
            scratch_shapes=[pltpu.VMEM((tree_len, HEAD), F32), pltpu.VMEM((tree_len, HEAD), F32)],
        ),
        compiler_params=pltpu.CompilerParams(vmem_limit_bytes=62 << 20),
        cost_estimate=NO_COST,
        name="attend_back",
    )(start, q_t, do_t, o_t, lse, kv, kv_t, bias_t, cos_t, sin_t)


def layer_attention(normed, weights, tables, key):
    gains, w_attn, w_mlp, width, split, units = weights
    start, bias_t, cos_t, sin_t, cos_rows, sin_rows = tables
    kv, kv_t, q_t = gather_rows(normed, w_attn, width, split, cos_rows, -sin_rows, key)
    o_t, o, lse = attend(start, q_t, kv, kv_t, bias_t, cos_t, sin_t)
    return (q_t, kv, kv_t, o_t, lse), o


def attention_backward(grad_attn, weights, tables, kept):
    gains, w_attn, w_mlp, width, split, units = weights
    start, bias_t, cos_t, sin_t, cos_rows, sin_rows = tables
    q_t, kv, kv_t, o_t, lse = kept
    do_t = dot_f32(w_attn[:, split : split + width], grad_attn, 0, 1).astype(BF)
    dq, dkv_part = attend_back(start, q_t, do_t, o_t, lse, kv, kv_t, bias_t, cos_t, sin_t)
    return dq, scatter_rows(dkv_part, cos_rows, sin_rows)


def layer_units(normed, weights):
    units = weights[-1]
    gate_up = jnp.dot(normed, weights[2][:, : 2 * units], preferred_element_type=F32)
    gate, up = gate_up[:, :units], gate_up[:, units:]
    return gate, up, (gate * jax.nn.sigmoid(gate) * up).astype(BF)


def units_backward(branch, weights, gate, up):
    units = weights[-1]
    d_inner = dot_f32(branch, weights[2][:, 2 * units :], 1, 0)
    sig = jax.nn.sigmoid(gate)
    d_gate = (d_inner * up * sig * (1.0 + gate * (1.0 - sig))).astype(BF)
    d_up = (d_inner * gate * sig).astype(BF)
    return d_gate, d_up


def reduce_gradient(x):
    return lax.psum_scatter(x, BOTH, scatter_dimension=0, tiled=True)


def shards(
    inputs, cotangent, seg_ids, positions, parents, gain_attn, w_query, key_weight, value_weight,
    w_out, gain_mlp, w_gate, w_up, w_down,
):
    sec = lax.axis_index("section")
    data = lax.axis_index("dp")
    sections = lax.axis_size("section")
    devices = lax.axis_size("dp")
    assert sections == 2 and inputs.shape[0] == 2
    first_core = sec == 0
    rows, model = inputs.shape[1], inputs.shape[2]
    swap = [(0, 1), (1, 0)]

    tree = lax.dynamic_index_in_dim(inputs, sec, 0, keepdims=False)
    hidden = tree.astype(F32)
    segments = lax.dynamic_index_in_dim(seg_ids, sec, 0, keepdims=False)
    places = lax.dynamic_index_in_dim(positions, sec, 0, keepdims=False)
    parent = lax.dynamic_index_in_dim(parents, sec, 0, keepdims=False)

    width, span, units = w_query.shape[2], key_weight.shape[2], w_gate.shape[2]
    split = width + 2 * span
    shard_list = (
        jnp.concatenate(
            [w_query[0], key_weight[0], value_weight[0], w_out[0].T, gain_attn.T, gain_mlp.T], 1
        ).astype(BF),
        jnp.concatenate([w_gate[0], w_up[0], w_down[0].T], 1).astype(BF),
    )
    halves = []
    for shard in shard_list:
        half = shard.shape[0] // 2
        low, high = shard[:half], shard[half:]
        got = lax.ppermute(jnp.where(first_core, high, low), "section", swap)
        halves.append((jnp.where(first_core, low, got), jnp.where(first_core, got, high)))
    def gathered(halves):
        return [lax.all_gather(half, BOTH, axis=0, tiled=True) for half in halves]

    def with_gains(w_attn, w_mlp):
        return (w_attn[:, split + width :].astype(F32).T, w_attn, w_mlp, width, split, units)

    (attn_zero, attn_one), (mlp_zero, mlp_one) = halves
    attn_zero = jnp.concatenate([attn_zero, attn_one[:, split + width : split + width + 1]], 1)
    attn_zero, mlp_zero = gathered((attn_zero, mlp_zero))
    cot = lax.dynamic_index_in_dim(cotangent, sec, 0, keepdims=False)
    attn_zero, cot = lax.optimization_barrier((attn_zero, cot))
    zero = with_gains(attn_zero, mlp_zero)
    attn_one, mlp_one = gathered((attn_one, mlp_one))

    seg_count = parent.shape[0]
    labels = jnp.arange(seg_count, dtype=jnp.int32)
    parent_hot = (parent[:, None] == labels[None, :]).astype(F32)
    ancestry = jnp.eye(seg_count, dtype=F32) + parent_hot + jnp.dot(parent_hot, parent_hot)
    ancestry = (ancestry > 0.5).astype(F32)
    row_start = data * rows
    seg_rows = lax.dynamic_slice_in_dim(segments, row_start, rows, 0)
    pos_rows = lax.dynamic_slice_in_dim(places, row_start, rows, 0)
    key_hot = (segments[:, None] == labels[None, :]).astype(F32)
    query_hot = (labels[:, None] == seg_rows[None, :]).astype(F32)
    reach = jnp.dot(key_hot, jnp.dot(ancestry.T, query_hot))
    allowed = (reach > 0.5) & (places[:, None] <= pos_rows[None, :])
    bias_t = jnp.where(allowed, 0.0, MASKED).astype(BF)
    frequency = THETA ** (-(jnp.arange(HALF, dtype=F32) * 2.0 / HEAD))
    angles = frequency[:, None] * pos_rows.astype(F32)[None, :]
    cos_t, sin_t = jnp.cos(angles), jnp.sin(angles)
    ones = jnp.ones((rows, HEAD), F32)
    cos_rows = jnp.concatenate([cos_t.T, cos_t.T, ones], 1)
    sin_rows = jnp.concatenate([sin_t.T, -sin_t.T, 0 * ones], 1)
    tables = (row_start.astype(jnp.int32).reshape(1), bias_t, cos_t, sin_t, cos_rows, sin_rows)

    split_out, split_down = split, 2 * units
    wide, narrow = (F32, BF), (BF, BF)
    back = (F32, BF, F32)

    normed_zero = (hidden * lax.rsqrt(jnp.mean(hidden * hidden, -1, keepdims=True) + EPSILON) * zero[0][:1]).astype(BF)
    kept_zero, o_zero = layer_attention(normed_zero, zero, tables, 3)
    middle_zero, r_zero = product_sum(
        (o_zero, tree, zero[0]), ((0,), split_out, ("add", (1, (2, 1))), wide), zero[1], stagger=True, key=1
    )
    gate_zero, up_zero, inner_zero = layer_units(r_zero, zero)
    out_zero, normed_one = product_sum(
        (inner_zero, middle_zero, zero[0]), ((0,), split_down, ("add", (1, (2, 2))), narrow), zero[2], key=5
    )

    out_zero, normed_one, attn_one = lax.optimization_barrier((out_zero, normed_one, attn_one))
    one = with_gains(attn_one, mlp_one)
    kept_one, o_one = layer_attention(normed_one, one, tables, 14)
    middle_one, r_one = product_sum(
        (o_one, out_zero, one[0]), ((0,), split_out, ("add", (1, (2, 1))), wide), one[1], key=2
    )
    gate_one, up_one, inner_one = layer_units(r_one, one)
    branch = cot
    d_gate, d_up = units_backward(branch, one, gate_one, up_one)
    grad_middle, grad_attn, d_gain_mlp_one, d_mlp_one = product_sum(
        ((d_gate, d_up), inner_one, middle_one, branch, r_one, one[0]), ((0,), 0, ("back", (2, 3, (5, 1))), back),
        one[2], ((4, (0,)), (3, (1,))), key=8,
    )
    g_mlp_one = reduce_gradient(d_mlp_one)
    dq, dkv = attention_backward(grad_attn, one, tables, kept_one)
    grad_one, branch, d_gain_attn_one, d_attn_one = product_sum(
        ((dq, dkv), out_zero, grad_middle, one[0], normed_one, grad_attn, o_one),
        ((0,), 0, ("back", (1, 2, (3, 0))), back),
        one[1], ((4, (0,)), (5, (6,))), key=7,
    )
    g_attn_one = reduce_gradient(d_attn_one)

    d_gate, d_up = units_backward(branch, zero, gate_zero, up_zero)
    grad_middle, grad_attn, d_gain_mlp_zero, d_mlp_zero = product_sum(
        ((d_gate, d_up), inner_zero, middle_zero, branch, r_zero, zero[0]),
        ((0,), 0, ("back", (2, 3, (5, 1))), back),
        zero[2], ((4, (0,)), (3, (1,))), key=9,
    )
    g_mlp_zero = reduce_gradient(d_mlp_zero)
    grad_attn, g_mlp_one = lax.optimization_barrier((grad_attn, g_mlp_one))
    dq, dkv = attention_backward(grad_attn, zero, tables, kept_zero)
    dq, g_attn_one = lax.optimization_barrier((dq, g_attn_one))
    grad_zero, send_zero, d_gain_attn_zero, d_attn_zero = product_sum(
        ((dq, dkv), tree, grad_middle, zero[0], normed_zero, grad_attn, o_zero),
        ((0,), 0, ("back", (1, 2, (3, 0))), back),
        zero[1], ((4, (0,)), (5, (6,))), key=11,
    )
    d_gain_attn_zero, d_gain_mlp_zero, d_gain_attn_one, d_gain_mlp_one = [
        jnp.sum(x, 0) for x in (d_gain_attn_zero, d_gain_mlp_zero, d_gain_attn_one, d_gain_mlp_one)
    ]
    d_gains = jnp.stack([d_gain_attn_zero, d_gain_mlp_zero, d_gain_attn_one, d_gain_mlp_one])
    d_gains = d_gains.reshape(2, 2, devices, -1).swapaxes(1, 2).reshape(2, devices, -1, 128)

    inner_one, send_zero = lax.optimization_barrier((inner_one, send_zero))
    out_one = product_sum(
        (inner_one, middle_one), ((0,), split_down, ("add", (1,)), (BF,)), one[2], key=6
    )
    ending = finish if devices == 4 else finish_apart
    g_attn_zero, g_gain, got_out, got_in, got_mlp, got_attn = ending(
        d_attn_zero, d_gains, out_zero, out_one, send_zero, branch,
        g_mlp_one, g_attn_one,
    )

    layer_output, input_grad, *grads = write_results(
        (out_zero, out_one, got_out), (grad_zero, grad_one, got_in), (g_attn_zero, g_attn_one, got_attn), width, span
    )
    input_grad, g_mlp_zero = lax.optimization_barrier((input_grad, g_mlp_zero))
    grads += write_mlp(
        g_mlp_zero, g_mlp_one, lax.ppermute(g_mlp_zero, "section", [(1, 0)]), got_mlp, units
    )
    g_query, g_key, g_value, g_out, g_gate, g_up, g_down = [grad[None] for grad in grads]
    g_gain = g_gain.reshape(2, 1, -1)
    return (
        layer_output[None], input_grad[None], g_gain[0], g_query, g_key, g_value, g_out, g_gain[1], g_gate, g_up, g_down,
    )


def solution(mesh):
    in_specs = (
        P(None, "dp", None),
        P(None, "dp", None),
        P(),
        P(),
        P(),
        P("section", "dp"),
        P("section", "dp", "tensor"),
        P("section", "dp", "tensor"),
        P("section", "dp", "tensor"),
        P("section", "tensor", "dp"),
        P("section", "dp"),
        P("section", "dp", "tensor"),
        P("section", "dp", "tensor"),
        P("section", "tensor", "dp"),
    )
    out_specs = (
        P("section", None, "dp", None),
        P("section", None, "dp", None),
        P("section", "dp"),
        P("section", "dp", "tensor"),
        P("section", "dp", "tensor"),
        P("section", "dp", "tensor"),
        P("section", "tensor", "dp"),
        P("section", "dp"),
        P("section", "dp", "tensor"),
        P("section", "dp", "tensor"),
        P("section", "tensor", "dp"),
    )
    return jax.shard_map(shards, mesh=mesh, in_specs=in_specs, out_specs=out_specs, check_vma=False)
```

```python
import functools

import jax
import jax.numpy as jnp
from jax import lax
from jax.experimental import pallas as pl
from jax.experimental.pallas import tpu as pltpu
from jax.sharding import PartitionSpec as P

HEAD = 64
HALF = HEAD // 2
TRUNK = 1024
GROUP = 384
EPSILON = 1e-05
THETA = 10000.0
MASKED = -1e30
BF = jnp.bfloat16
F32 = jnp.float32
MESH = pl.DeviceIdType.MESH
BOTH = ("dp", "section")


def dot_f32(a, b, ca, cb):
    return lax.dot_general(a, b, (((ca,), (cb,)), ((), ())), preferred_element_type=F32)


BLOCK = 256
PIECE = 128
NO_COST = pl.CostEstimate(flops=1, transcendentals=0, bytes_accessed=1)


def columns_of(i):
    return pl.ds(pl.multiple_of(i * PIECE, PIECE), PIECE)


def gain_row(arrays, place, at):
    return arrays[place[0]][place[1] : place[1] + 1, at]


def row_scale(squares, model):
    return lax.rsqrt(jnp.sum(squares, 1, keepdims=True) * (1.0 / model) + EPSILON)


def before_sum(job, arrays, keep):
    kind, places = job[2]
    if kind == "back":
        value = arrays[places[0]]
        model = value.shape[1]
        squares = jnp.zeros(keep.shape, F32)
        for i in range(model // PIECE):
            x = value[:, i * PIECE : (i + 1) * PIECE].astype(F32)
            squares += x * x
        keep[...] = jnp.broadcast_to(row_scale(squares, model), keep.shape)


def with_piece(job, i, total, arrays, outs, keep, sums):
    kind, places = job[2]
    at = columns_of(i)
    if kind == "add":
        y = (arrays[places[0]][:, at].astype(F32) + total).astype(outs[0].dtype)
        outs[0][:, at] = y
        if len(outs) > 1:
            sums[...] += y.astype(F32) * y.astype(F32)
    if kind == "back":
        product = total * arrays[places[0]][:, at].astype(F32) * keep[...]
        sums[...] += product * gain_row(arrays, places[2], at)
        outs[2][:, at] = jnp.sum(product.reshape(-1, 8, PIECE), 0)


def after_sum(job, rows, total, arrays, outs, keep, sums):
    kind, places = job[2]
    model = arrays[places[0]].shape[1]
    at = lambda i: slice(i * PIECE, (i + 1) * PIECE)
    if kind == "add" and len(outs) > 1:
        scale = row_scale(sums[rows], model)
        for i in range(model // PIECE):
            y = outs[0][rows, at(i)].astype(F32)
            outs[1][rows, at(i)] = (y * scale * gain_row(arrays, places[1], at(i))).astype(BF)
    if kind == "back":
        mean = jnp.sum(sums[rows], 1, keepdims=True) * (1.0 / model)
        scale = keep[rows]
        for i in range(model // PIECE):
            unit = arrays[places[0]][rows, at(i)].astype(F32) * scale
            grad = total(i)[rows].astype(F32) * gain_row(arrays, places[2], at(i))
            out = arrays[places[1]][rows, at(i)].astype(F32) + scale * (grad - unit * mean)
            outs[0][rows, at(i)] = out
            outs[1][rows, at(i)] = out.astype(BF)


def product_sum_kernel(cfg, *refs):
    n_join, n_arrays, job, sides, stagger = cfg
    xs, first_column = job[:2]
    refs = list(refs)
    take = lambda n: [refs.pop(0) for _ in range(n)]
    joined = take(n_join)
    from_hbm = [None, *take(n_arrays - 1)]
    (w_hbm,) = take(1)
    outs_hbm = take(len(job[3]))
    (g_hbm,) = take(1) if sides else (None,)
    arrays = take(n_arrays)
    outs = take(len(job[3]))
    load_sem, out_sem, w_buf, p_buf, a_buf, b_buf, w_sem, sa, ra, sb, rb, sc, rc, turn, keep, sums = take(16)
    g_buf, g_sem = take(2) if sides else (None, None)
    per_block = BLOCK // PIECE
    pieces = p_buf.shape[0]
    blocks = pieces // per_block
    n_rows = p_buf.shape[1]
    early = len(xs)
    lag = 1
    assert xs[0] == 0

    t = lax.axis_index("tensor")
    sec = lax.axis_index("section")
    dat = lax.axis_index("dp")
    inner = (t == 1) | (t == 2)
    outer = jnp.logical_not(inner)
    pair = (sec, t + 1 - 2 * lax.rem(t, 2), dat)
    mid = (sec, 3 - t, dat)
    mate = (1 - sec, t, dat)

    def columns(j):
        return pl.ds(pl.multiple_of(j * BLOCK, BLOCK), BLOCK)

    def to_inner(i):
        return pltpu.make_async_remote_copy(
            p_buf.at[i], a_buf.at[i], sa.at[i], ra.at[i], device_id=pair, device_id_type=MESH
        )

    def across(i):
        return pltpu.make_async_remote_copy(
            p_buf.at[i], b_buf.at[i], sb.at[i], rb.at[i], device_id=mid, device_id_type=MESH
        )

    def to_outer(i):
        return pltpu.make_async_remote_copy(
            b_buf.at[i], b_buf.at[i], sc.at[i], rc.at[i], device_id=pair, device_id_type=MESH
        )

    def load(k):
        return pltpu.make_async_copy(from_hbm[k], arrays[k], load_sem.at[k])

    def join():
        copies, start = [], 0
        for m, src in enumerate(joined):
            at = pl.ds(start, src.shape[1])
            copies.append(pltpu.make_async_copy(src, arrays[0].at[:, at], load_sem.at[n_arrays + m]))
            start += src.shape[1]
        return copies

    def fetch(j, slot):
        return pltpu.make_async_copy(
            w_hbm.at[columns(j), pl.ds(first_column, w_buf.shape[2])], w_buf.at[slot], w_sem.at[slot]
        )

    def flush(j, slot):
        return pltpu.make_async_copy(g_buf.at[slot], g_hbm.at[columns(j), :], g_sem.at[slot])

    def every_piece(body):
        def turn_of(i, _):
            body(i)
            return 0

        lax.fori_loop(0, pieces, turn_of, 0)

    for copy in join():
        copy.start()
    for k in range(1, early):
        load(k).start()
    fetch(0, 0).start()
    for k in range(early, n_arrays):
        load(k).start()
    barrier = pltpu.get_barrier_semaphore()
    pl.semaphore_signal(barrier, inc=1, device_id=pair, device_id_type=MESH)
    sums[...] = jnp.zeros_like(sums)

    @pl.when(inner)
    def _():
        pl.semaphore_signal(barrier, inc=1, device_id=mid, device_id_type=MESH)
        pl.semaphore_wait(barrier, 2)

    @pl.when(outer)
    def _():
        if stagger:
            pl.semaphore_signal(barrier, inc=1, device_id=mate, device_id_type=MESH)
            pl.semaphore_wait(barrier, 2)

            @pl.when(sec == 1)
            def _():
                pl.semaphore_wait(turn, 1)

        else:
            pl.semaphore_wait(barrier, 1)

    for copy in join():
        copy.wait()
    for k in range(1, early):
        load(k).wait()

    def done(i):
        with_piece(job, i, b_buf[i].astype(F32), arrays, outs, keep, sums)

    def first(i):
        to_inner(i).wait_recv()
        p_buf[i] = p_buf[i] + a_buf[i]
        across(i).start()

    def second(i):
        across(i).wait_recv()
        b_buf[i] = p_buf[i] + b_buf[i]
        to_outer(i).start()
        done(i)

    def side(j):
        slot = lax.rem(j, 2)

        @pl.when(j >= 2)
        def _():
            flush(j - 2, slot).wait()

        start = 0
        for a, bs in sides:
            a_t = arrays[a][:, columns(j)].T
            for b in bs:
                width = arrays[b].shape[1]
                g_buf[slot, :, start : start + width] = jnp.dot(
                    a_t, arrays[b][...], preferred_element_type=F32
                ).astype(BF)
                start += width
        flush(j, slot).start()
        return 0

    def step(j, _):
        slot = lax.rem(j, 2)
        fetch(j, slot).wait()

        @pl.when(j + 1 < blocks)
        def _():
            fetch(j + 1, 1 - slot).start()

        total, start = None, 0
        for x in xs:
            width = arrays[x].shape[1]
            term = dot_f32(arrays[x][...], w_buf[slot, :, start : start + width], 1, 1)
            total = term if total is None else total + term
            start += width
        total = total.astype(BF)
        for u in range(per_block):
            p_buf[per_block * j + u] = total[:, u * PIECE : (u + 1) * PIECE]

        @pl.when(outer)
        def _():
            for u in range(per_block):
                to_inner(per_block * j + u).start()

        @pl.when(j == 1)
        def _():
            for k in range(early, n_arrays):
                load(k).wait()
            before_sum(job, arrays, keep)

        if sides:

            @pl.when(j >= lag)
            def _():
                side(j - lag)

        @pl.when(inner)
        def _():
            for u in range(per_block):
                i = per_block * j + u
                first(i)

                @pl.when(j >= 1)
                def _():
                    second(i - per_block)

        return 0

    lax.fori_loop(0, blocks, step, 0)

    @pl.when(inner)
    def _():
        for u in range(per_block):
            second(pieces - per_block + u)

    if sides:
        lax.fori_loop(blocks - lag, blocks, lambda j, _: side(j), 0)

    @pl.when(outer)
    def _():
        every_piece(lambda i: to_inner(i).wait_send())

        def arrive(i):
            to_outer(i).wait_recv()
            done(i)

        every_piece(arrive)

    chunks = 5 if n_rows % (5 * 32) == 0 else 1
    chunk = n_rows // chunks
    block = 32 if chunk % 32 == 0 else 16
    height = lambda m: 8 if job[2][0] == "back" and m == 2 else n_rows
    stores = []

    def store(m, rows):
        copy = pltpu.make_async_copy(outs[m].at[rows], outs_hbm[m].at[rows], out_sem.at[len(stores)])
        copy.start()
        stores.append(copy)

    for c in range(chunks):

        def turn_rows(r, _):
            rows = pl.ds(pl.multiple_of(c * chunk + r * block, block), block)
            after_sum(job, rows, lambda i: b_buf.at[i], arrays, outs, keep, sums)
            return 0

        if job[2][0] == "back" or len(outs) > 1:
            lax.fori_loop(0, chunk // block, turn_rows, 0)
        for m in range(len(outs)):
            if height(m) == n_rows:
                store(m, pl.ds(c * chunk, chunk))
    for m in range(len(outs)):
        if height(m) != n_rows:
            store(m, pl.ds(0, height(m)))

    @pl.when(inner)
    def _():
        def sent(i):
            across(i).wait_send()
            to_outer(i).wait_send()

        every_piece(sent)

    if sides:
        flush(blocks - 2, (blocks - 2) % 2).wait()
        flush(blocks - 1, (blocks - 1) % 2).wait()
    for copy in stores:
        copy.wait()

    if stagger:

        @pl.when(outer & (sec == 0))
        def _():
            pl.semaphore_signal(turn, inc=1, device_id=mate, device_id_type=MESH)


def product_sum(arrays, job, weights, sides=(), stagger=False, key=1):
    assert lax.axis_size("tensor") == 4
    first = arrays[0] if isinstance(arrays[0], tuple) else (arrays[0],)
    given = (*first, *arrays[1:])
    rows, model = first[0].shape[0], weights.shape[0]
    arrays = (jax.ShapeDtypeStruct((rows, sum(x.shape[1] for x in first)), BF), *arrays[1:])
    pieces = model // PIECE
    depth = sum(arrays[x].shape[1] for x in job[0])
    anywhere = pl.BlockSpec(memory_space=pl.ANY)
    buf = pltpu.VMEM((pieces, rows, PIECE), BF)
    sem = pltpu.SemaphoreType.DMA((pieces,))
    two = pltpu.SemaphoreType.DMA((2,))
    out_shape = []
    for m, dtype in enumerate(job[3]):
        height = 8 if job[2][0] == "back" and m == 2 else rows
        out_shape.append(jax.ShapeDtypeStruct((height, model), dtype))
    scratch = [pltpu.VMEM(x.shape, x.dtype) for x in (*arrays, *out_shape)]
    scratch += [pltpu.SemaphoreType.DMA((len(arrays) + len(first),)), pltpu.SemaphoreType.DMA((16,))]
    scratch += [pltpu.VMEM((2, BLOCK, depth), BF), buf, buf, buf, two, *[sem] * 6, pltpu.SemaphoreType.REGULAR]
    scratch += [pltpu.VMEM((rows, PIECE), F32)] * 2
    if sides:
        side_width = sum(arrays[b].shape[1] for _, bs in sides for b in bs)
        out_shape.append(jax.ShapeDtypeStruct((model, side_width), BF))
        scratch += [pltpu.VMEM((2, BLOCK, side_width), BF), two]
    out = pl.pallas_call(
        functools.partial(product_sum_kernel, (len(first), len(arrays), job, tuple(sides), stagger)),
        out_shape=out_shape,
        in_specs=[anywhere] * (len(given) + 1),
        out_specs=[anywhere] * len(out_shape),
        scratch_shapes=scratch,
        compiler_params=pltpu.CompilerParams(
            collective_id=key, has_side_effects=True, vmem_limit_bytes=62 << 20
        ),
        cost_estimate=NO_COST,
        name=f"product_sum_{key}",
    )(*given, weights)
    return out if len(out) > 1 else out[0]


def dp_peers(count):
    me = lax.axis_index("dp")
    sec, t = lax.axis_index("section"), lax.axis_index("tensor")
    others = [lax.rem(me + k, count) for k in range(1, count)]
    return me, others, [(sec, t, other) for other in others]


def greet(ids):
    barrier = pltpu.get_barrier_semaphore()
    for device in ids:
        pl.semaphore_signal(barrier, inc=1, device_id=device, device_id_type=MESH)
    pl.semaphore_wait(barrier, len(ids))


def turn_rows(x, cos_ref, sin_ref):
    lane = lax.broadcasted_iota(jnp.int32, x.shape, 1)
    width = x.shape[1]
    partner = jnp.where(lane < HALF, pltpu.roll(x, width - HALF, 1), pltpu.roll(x, HALF, 1))
    return x * cos_ref[...] + partner * sin_ref[...]


def gather_kernel(
    count, normed_ref, w_hbm, cos_ref, sin_ref, o_ref, t_ref, q_ref, x_ref, w_buf, load_sem, send, recv
):
    me, _, ids = dp_peers(count)
    load = pltpu.make_async_copy(w_hbm.at[:, pl.ds(0, w_buf.shape[1])], w_buf, load_sem)
    load.start()
    load.wait()
    width = q_ref.shape[0]
    raw = jnp.dot(normed_ref[...], w_buf[:, width:], preferred_element_type=F32)
    x_ref[...] = turn_rows(raw, cos_ref, sin_ref).astype(BF)
    greet(ids)
    copies = [
        pltpu.make_async_remote_copy(
            x_ref, o_ref.at[me], send.at[k], recv.at[k], device_id=device, device_id_type=MESH
        )
        for k, device in enumerate(ids)
    ]
    for copy in copies:
        copy.start()
    o_ref[me] = x_ref[...]
    q_ref[...] = jnp.dot(normed_ref[...], w_buf[:, :width], preferred_element_type=F32).T
    for copy in copies:
        copy.wait()
    t_ref[...] = o_ref[...].reshape(t_ref.shape[1], t_ref.shape[0]).T


def scatter_kernel(count, x_ref, cos_ref, sin_ref, o_ref, buf, send, recv):
    me, others, ids = dp_peers(count)
    greet(ids)
    copies = [
        pltpu.make_async_remote_copy(
            x_ref.at[others[k]], buf.at[k], send.at[k], recv.at[k], device_id=device, device_id_type=MESH
        )
        for k, device in enumerate(ids)
    ]
    for copy in copies:
        copy.start()
    total = x_ref[me].astype(F32)
    for k, copy in enumerate(copies):
        copy.wait()
        total = total + buf[k].astype(F32)
    o_ref[...] = turn_rows(total, cos_ref, sin_ref).astype(BF)


def gather_rows(normed, w_attn, width, split, cos_rows, sin_rows, key):
    count = lax.axis_size("dp")
    rows, span = normed.shape[0], split - width
    in_vmem = pl.BlockSpec(memory_space=pltpu.VMEM)
    sem = pltpu.SemaphoreType.DMA((count - 1,))
    out, out_t, q_t = pl.pallas_call(
        functools.partial(gather_kernel, count),
        out_shape=(
            jax.ShapeDtypeStruct((count, rows, span), BF),
            jax.ShapeDtypeStruct((span, count * rows), BF),
            jax.ShapeDtypeStruct((width, rows), F32),
        ),
        in_specs=[in_vmem, pl.BlockSpec(memory_space=pl.ANY), in_vmem, in_vmem],
        out_specs=(in_vmem, in_vmem, in_vmem),
        scratch_shapes=[
            pltpu.VMEM((rows, span), BF), pltpu.VMEM((normed.shape[1], split), BF),
            pltpu.SemaphoreType.DMA, sem, sem,
        ],
        compiler_params=pltpu.CompilerParams(
            collective_id=key, has_side_effects=True, vmem_limit_bytes=40 << 20
        ),
        cost_estimate=NO_COST,
        name="gather_rows",
    )(normed, w_attn, cos_rows, sin_rows)
    return out.reshape(-1, span), out_t, q_t


def scatter_rows(x, cos_rows, sin_rows):
    count = lax.axis_size("dp")
    rows, width = x.shape[0] // count, x.shape[1]
    in_vmem = pl.BlockSpec(memory_space=pltpu.VMEM)
    sem = pltpu.SemaphoreType.DMA((count - 1,))
    return pl.pallas_call(
        functools.partial(scatter_kernel, count),
        out_shape=jax.ShapeDtypeStruct((rows, width), BF),
        in_specs=[in_vmem] * 3,
        out_specs=in_vmem,
        scratch_shapes=[pltpu.VMEM((count - 1, rows, width), x.dtype), sem, sem],
        compiler_params=pltpu.CompilerParams(collective_id=4, has_side_effects=True),
        cost_estimate=NO_COST,
        name="scatter_rows",
    )(x.reshape(count, rows, width), cos_rows, sin_rows)


def finish_kernel(
    g_hbm, gain_ref, out_zero, out_one, in_zero, in_one, mlp_one, attn_one,
    o_ref, gain_out, got_out, got_in, got_mlp, got_attn,
    mine, away, got, xs, ys, xr, yr, gains, load_sem, send, recv, mate_send, mate_recv, gain_send, gain_recv,
):
    sec, t, dat = lax.axis_index("section"), lax.axis_index("tensor"), lax.axis_index("dp")
    flip_x = dat + 1 - 2 * lax.rem(dat, 2)
    flip_y = lax.rem(dat + 2, 4)
    across = lax.rem(flip_x + 2, 4)
    by_x, by_y, mate = (sec, t, flip_x), (sec, t, flip_y), (1 - sec, t, dat)
    peers = [
        mate, by_x, by_y, (sec, t, across),
        (1 - sec, t, flip_x), (1 - sec, t, flip_y), (1 - sec, t, across),
    ]
    rows = g_hbm.shape[1] // 2
    upper, lower = pl.ds(0, rows), pl.ds(rows, rows)
    order = (across, flip_x, flip_y, dat)
    loads = []
    for k, block in enumerate(order):
        loads.append(pltpu.make_async_copy(g_hbm.at[2 * block + 1 - sec], away.at[k], load_sem.at[k]))
        loads.append(pltpu.make_async_copy(g_hbm.at[2 * block + sec], mine.at[k], load_sem.at[4 + k]))
    for copy in loads:
        copy.start()
    greet(peers)

    def remote(src, dst, k, device):
        return pltpu.make_async_remote_copy(
            src, dst, send.at[k], recv.at[k], device_id=device, device_id_type=MESH
        )

    def to_mate(src, dst, k):
        return pltpu.make_async_remote_copy(
            src, dst, mate_send.at[k], mate_recv.at[k], device_id=mate, device_id_type=MESH
        )

    swaps = [remote(away.at[k], got.at[k], k, mate) for k in range(4)]
    for k in range(4):
        loads[2 * k].wait()
        swaps[k].start()
    gain_copies = [
        pltpu.make_async_remote_copy(
            gain_ref.at[peer[0], peer[2]], gains.at[k], gain_send.at[k], gain_recv.at[k],
            device_id=peer, device_id_type=MESH,
        )
        for k, peer in enumerate(peers)
    ]
    for copy in gain_copies:
        copy.start()
    outs = []
    for k in range(4):
        loads[2 * k + 1].wait()
        swaps[k].wait_recv()
        mine[k] = (mine[k].astype(F32) + got[k].astype(F32)).astype(BF)
        if k == 0:
            outs += [remote(mine.at[0, upper], xs.at[0], 4, by_x), remote(mine.at[0, lower], ys.at[0], 5, by_y)]
        if k == 1:
            outs += [remote(mine.at[1, upper], xs.at[1], 6, by_x)]
        if k == 2:
            outs += [remote(mine.at[2, lower], ys.at[1], 7, by_y)]
        for copy in outs[-(2 if k == 0 else 1) :]:
            if k < 3:
                copy.start()

    @pl.when(sec == 0)
    def _():
        to_mate(in_one, got_in, 0).start()
        to_mate(out_one, got_out, 1).start()
        to_mate(mlp_one, got_mlp, 2).start()
        to_mate(attn_one, got_attn, 3).start()

    @pl.when(sec == 1)
    def _():
        to_mate(in_zero, got_in, 0).start()
        to_mate(out_zero, got_out, 1).start()

    outs[0].wait_recv()
    mine[2, upper] = (mine[2, upper].astype(F32) + xs[0].astype(F32)).astype(BF)
    outs.append(remote(mine.at[2, upper], yr, 8, by_y))
    outs[4].start()
    outs[1].wait_recv()
    mine[1, lower] = (mine[1, lower].astype(F32) + ys[0].astype(F32)).astype(BF)
    outs.append(remote(mine.at[1, lower], xr, 9, by_x))
    outs[5].start()
    total = gain_ref[sec, dat]
    for k, copy in enumerate(gain_copies):
        copy.wait()
        total = total + gains[k]
    gain_out[...] = total
    outs[2].wait_recv()
    outs[3].wait_recv()
    outs[4].wait_recv()
    o_ref[upper] = (mine[3, upper].astype(F32) + xs[1].astype(F32) + yr[...].astype(F32)).astype(BF)
    outs[5].wait_recv()
    o_ref[lower] = (mine[3, lower].astype(F32) + ys[1].astype(F32) + xr[...].astype(F32)).astype(BF)

    @pl.when(sec == 1)
    def _():
        to_mate(o_ref, got_attn, 3).start()

    for copy in swaps + outs:
        copy.wait_send()
    to_mate(in_one, got_in, 0).wait()
    to_mate(out_one, got_out, 1).wait()
    to_mate(attn_one, got_attn, 3).wait()

    @pl.when(sec == 0)
    def _():
        to_mate(mlp_one, got_mlp, 2).wait_send()

    @pl.when(sec == 1)
    def _():
        to_mate(mlp_one, got_mlp, 2).wait_recv()


def finish(g, gains, out_zero, out_one, in_zero, in_one, mlp_one, attn_one):
    rows, width = g.shape[0] // 8, g.shape[1]
    part = pltpu.VMEM((2, rows // 2, width), BF)
    whole = pltpu.VMEM((4, rows, width), BF)
    end = pltpu.VMEM((rows // 2, width), BF)
    in_vmem, anywhere = pl.BlockSpec(memory_space=pltpu.VMEM), pl.BlockSpec(memory_space=pl.ANY)
    like = lambda x: jax.ShapeDtypeStruct(x.shape, x.dtype)
    dma = lambda n: pltpu.SemaphoreType.DMA((n,))
    return pl.pallas_call(
        finish_kernel,
        out_shape=(
            jax.ShapeDtypeStruct((rows, width), BF),
            jax.ShapeDtypeStruct(gains.shape[2:], F32),
            like(out_zero), like(in_zero), like(mlp_one), like(attn_one),
        ),
        in_specs=[anywhere, in_vmem, *[anywhere] * 6],
        out_specs=(in_vmem, in_vmem, *[anywhere] * 4),
        scratch_shapes=[
            whole, whole, whole, part, part, end, end, pltpu.VMEM((7, *gains.shape[2:]), F32),
            dma(8), dma(10), dma(10), dma(4), dma(4), dma(7), dma(7),
        ],
        compiler_params=pltpu.CompilerParams(
            collective_id=12, has_side_effects=True, vmem_limit_bytes=62 << 20
        ),
        cost_estimate=NO_COST,
        name="finish",
    )(g.reshape(8, rows, width), gains, out_zero, out_one, in_zero, in_one, mlp_one, attn_one)


def finish_apart(g, gains, out_zero, out_one, in_zero, in_one, mlp_one, attn_one):
    first_core = lax.axis_index("section") == 0
    half = reduce_gradient(g)
    swap = lambda zero, one: lax.ppermute(jnp.where(first_core, one, zero), "section", [(0, 1), (1, 0)])
    return (
        half, share_sums(gains), swap(out_zero, out_one), swap(in_zero, in_one),
        lax.ppermute(mlp_one, "section", [(0, 1)]), swap(half, attn_one),
    )


def in_rows(count, block, body):
    def turn(r, _):
        body(pl.ds(pl.multiple_of(r * block, block), block))
        return 0

    lax.fori_loop(0, count // block, turn, 0)


def widen_turned(dst, src, start, width):
    for c in range(0, width, 128):
        dst[c : c + 128] = src[:, start + c : start + c + 128].astype(F32).T


def write_mlp_kernel(
    zero, one, from_one, from_zero, gate_hbm, up_hbm, down_hbm, mlp, gate_buf, up_buf, down_buf, load_sem, store_sem
):
    sec = lax.axis_index("section")
    half, units = zero.shape[0], gate_buf.shape[1]
    low, high = pl.ds(0, half), pl.ds(half, half)
    load = lambda src, at, k: pltpu.make_async_copy(src, mlp.at[at], load_sem.at[k])
    store = lambda src, dst, k: pltpu.make_async_copy(src, dst, store_sem.at[k])

    @pl.when(sec == 0)
    def _():
        load(zero, low, 0).start()
        load(from_one, high, 1).start()

    @pl.when(sec == 1)
    def _():
        load(from_zero, low, 0).start()
        load(one, high, 1).start()

    load(zero, low, 0).wait()
    load(zero, high, 1).wait()

    def gates(rows):
        gate_buf[rows] = mlp[rows, :units].astype(F32)
        up_buf[rows] = mlp[rows, units : 2 * units].astype(F32)

    in_rows(2 * half, 32, gates)
    stores = [store(gate_buf, gate_hbm, 0), store(up_buf, up_hbm, 1), store(down_buf, down_hbm, 2)]
    stores[0].start()
    stores[1].start()
    widen_turned(down_buf, mlp, 2 * units, units)
    stores[2].start()
    for copy in stores:
        copy.wait()


def write_mlp(zero, one, from_one, from_zero, units):
    shard = 2 * zero.shape[0]
    anywhere = pl.BlockSpec(memory_space=pl.ANY)
    shapes = [(shard, units), (shard, units), (units, shard)]
    return pl.pallas_call(
        write_mlp_kernel,
        out_shape=[jax.ShapeDtypeStruct(shape, F32) for shape in shapes],
        in_specs=[anywhere] * 4,
        out_specs=[anywhere] * 3,
        scratch_shapes=[
            pltpu.VMEM((shard, zero.shape[1]), BF),
            *[pltpu.VMEM(shape, F32) for shape in shapes],
            pltpu.SemaphoreType.DMA((2,)),
            pltpu.SemaphoreType.DMA((3,)),
        ],
        compiler_params=pltpu.CompilerParams(vmem_limit_bytes=62 << 20),
        cost_estimate=NO_COST,
        name="write_mlp",
    )(zero, one, from_one, from_zero)


def write_kernel(
    split, out_zero, out_one, got_out, in_zero, in_one, got_in, attn_zero, attn_one, got_attn,
    out_hbm, in_hbm, q_hbm, k_hbm, v_hbm, o_hbm,
    outs, wides, attn, narrow, q_buf, k_buf, v_buf, o_buf, load_sem, store_sem,
):
    sec = lax.axis_index("section")
    half = attn_zero.shape[0]
    low, high = pl.ds(0, half), pl.ds(half, half)
    load = lambda src, dst, k: pltpu.make_async_copy(src, dst, load_sem.at[k])
    store = lambda src, dst, k: pltpu.make_async_copy(src, dst, store_sem.at[k])

    def start(own_out, own_in, attn_low, attn_high):
        load(own_out, outs.at[0], 0).start()
        load(own_in, wides.at[0], 1).start()
        load(attn_low, attn.at[low], 2).start()
        load(attn_high, attn.at[high], 3).start()

    @pl.when(sec == 0)
    def _():
        start(out_zero, in_zero, attn_zero, got_attn)

    @pl.when(sec == 1)
    def _():
        start(out_one, in_one, got_attn, attn_one)

    load(got_in, narrow, 4).start()
    load(got_out, outs.at[1], 5).start()
    stores = [
        store(outs.at[0], out_hbm.at[sec], 0),
        store(wides.at[0], in_hbm.at[sec], 1),
        store(outs.at[1], out_hbm.at[1 - sec], 2),
        store(wides.at[1], in_hbm.at[1 - sec], 3),
        store(q_buf, q_hbm, 4),
        store(k_buf, k_hbm, 5),
        store(v_buf, v_hbm, 6),
        store(o_buf, o_hbm, 7),
    ]
    load(out_zero, outs.at[0], 0).wait()
    stores[0].start()
    load(in_zero, wides.at[0], 1).wait()
    stores[1].start()
    width, span = q_buf.shape[1], k_buf.shape[1]
    load(attn_one, attn.at[low], 2).wait()
    load(attn_one, attn.at[high], 3).wait()

    def projections(rows):
        q_buf[rows] = attn[rows, :width].astype(F32)
        k_buf[rows] = attn[rows, width : width + span].astype(F32)
        v_buf[rows] = attn[rows, width + span : split].astype(F32)

    in_rows(2 * half, 32, projections)
    for k in (4, 5, 6):
        stores[k].start()
    widen_turned(o_buf, attn, split, width)
    stores[7].start()
    load(got_in, narrow, 4).wait()

    def widen(rows):
        wides[1, rows] = narrow[rows].astype(F32)

    in_rows(narrow.shape[0], 32, widen)
    stores[3].start()
    load(got_out, outs.at[1], 5).wait()
    stores[2].start()
    for copy in stores:
        copy.wait()


def write_results(results, ins, attns, width, span):
    rows, model = results[0].shape
    shard = 2 * attns[0].shape[0]
    anywhere = pl.BlockSpec(memory_space=pl.ANY)
    shapes = [(shard, width), (shard, span), (shard, span), (width, shard)]
    return pl.pallas_call(
        functools.partial(write_kernel, width + 2 * span),
        out_shape=[
            jax.ShapeDtypeStruct((2, rows, model), BF),
            jax.ShapeDtypeStruct((2, rows, model), F32),
            *[jax.ShapeDtypeStruct(shape, F32) for shape in shapes],
        ],
        in_specs=[anywhere] * 9,
        out_specs=[anywhere] * 6,
        scratch_shapes=[
            pltpu.VMEM((2, rows, model), BF),
            pltpu.VMEM((2, rows, model), F32),
            pltpu.VMEM((shard, attns[0].shape[1]), BF),
            pltpu.VMEM((rows, model), BF),
            *[pltpu.VMEM(shape, F32) for shape in shapes],
            pltpu.SemaphoreType.DMA((6,)),
            pltpu.SemaphoreType.DMA((8,)),
        ],
        compiler_params=pltpu.CompilerParams(vmem_limit_bytes=62 << 20),
        cost_estimate=NO_COST,
        name="write_results",
    )(*results, *ins, *attns)


def share_kernel(count, x_ref, o_ref, buf, send, recv):
    sec, t, dat = lax.axis_index("section"), lax.axis_index("tensor"), lax.axis_index("dp")
    peers = [
        (lax.rem(sec + k // count, 2), t, lax.rem(dat + k % count, count)) for k in range(1, 2 * count)
    ]
    greet(peers)
    copies = [
        pltpu.make_async_remote_copy(
            x_ref.at[peer[0], peer[2]], buf.at[k], send.at[k], recv.at[k], device_id=peer, device_id_type=MESH
        )
        for k, peer in enumerate(peers)
    ]
    for copy in copies:
        copy.start()
    total = x_ref[sec, dat]
    for k, copy in enumerate(copies):
        copy.wait()
        total = total + buf[k]
    o_ref[...] = total


def share_sums(x):
    count = lax.axis_size("dp")
    in_vmem = pl.BlockSpec(memory_space=pltpu.VMEM)
    sem = pltpu.SemaphoreType.DMA((2 * count - 1,))
    return pl.pallas_call(
        functools.partial(share_kernel, count),
        out_shape=jax.ShapeDtypeStruct(x.shape[2:], F32),
        in_specs=[in_vmem],
        out_specs=in_vmem,
        scratch_shapes=[pltpu.VMEM((2 * count - 1, *x.shape[2:]), F32), sem, sem],
        compiler_params=pltpu.CompilerParams(collective_id=13, has_side_effects=True),
        cost_estimate=NO_COST,
        name="share_sums",
    )(x)


def group_start(first_row):
    past = lax.max(first_row - TRUNK, 0)
    return pl.multiple_of(TRUNK + GROUP * lax.div(past, GROUP), 128)


def over_windows(tree_len, rows, tile, first_row, run):
    if tile % 128 == 0 and GROUP % tile == 0 and TRUNK % tile == 0 and rows % tile == 0:
        run(((pl.ds(0, TRUNK), True), (pl.ds(group_start(first_row), GROUP), True)))
    else:
        run(((pl.ds(0, tree_len), True),))


def masked(scores, bias_ref, win, step):
    bias = bias_ref[win, :].astype(F32)
    return scores + (bias if step == 1 else jnp.concatenate([bias] * step, axis=1))


def head_rows(ref, head):
    return ref[head * HEAD : (head + 1) * HEAD, :]


def beside(ref, head, count):
    parts = [head_rows(ref, head + k) for k in range(count)]
    return parts[0] if count == 1 else jnp.concatenate(parts, axis=1)


def turned_beside(ref, cos, sin, head, count):
    parts = []
    for k in range(count):
        rows = head_rows(ref, head + k)
        first, second = rows[:HALF], rows[HALF:]
        parts.append(jnp.concatenate([first * cos - second * sin, second * cos + first * sin], axis=0))
    whole = parts[0] if count == 1 else jnp.concatenate(parts, axis=1)
    return (whole.astype(BF).astype(F32) * HEAD**-0.5).astype(BF)


def as_rows(x, tile, count):
    parts = [x[:, k * tile : (k + 1) * tile] for k in range(count)]
    return (parts[0] if count == 1 else jnp.concatenate(parts, axis=0)).T


def over_groups(groups, step, body):
    for group in range(groups):
        body(group, slice(group * step * HEAD, (group + 1) * step * HEAD))


def attend_kernel(
    rows, step, start_ref, q_ref, kv_ref, kvt_ref, bias_ref, cos_ref, sin_ref, o_ref, on_ref, lse_ref
):
    tile = q_ref.shape[1]
    heads = q_ref.shape[0] // HEAD
    first_row = start_ref[0] + pl.program_id(0) * tile

    def body(wins, group, lanes):
        head = group * step
        q = turned_beside(q_ref, cos_ref[...], sin_ref[...], head, step)
        scores = []
        for win, mask in wins:
            score = dot_f32(kv_ref[win, :HEAD], q, 1, 0)
            scores.append(masked(score, bias_ref, win, step) if mask else score)
        top = functools.reduce(jnp.maximum, [jnp.max(s, 0, keepdims=True) for s in scores])
        expo = [jnp.exp(s - top) for s in scores]
        total = sum(jnp.sum(e, 0, keepdims=True) for e in expo)
        out = sum(dot_f32(kvt_ref[HEAD:, win], e.astype(BF), 1, 0) for (win, _), e in zip(wins, expo))
        out = out / total
        on_ref[:, lanes] = as_rows(out, tile, step).astype(BF)
        lse_ref[group, 0] = top + jnp.log(total)
        out = out.astype(BF)
        for k in range(step):
            o_ref[(head + k) * HEAD : (head + k + 1) * HEAD, :] = out[:, k * tile : (k + 1) * tile]

    over_windows(
        kv_ref.shape[0], rows, tile, first_row,
        lambda wins: over_groups(heads // step, step, functools.partial(body, wins)),
    )


def attend_back_kernel(
    rows, step, start_ref, q_ref, do_ref, o_ref, lse_ref, kv_ref, kvt_ref, bias_ref, cos_ref, sin_ref,
    dq_ref, dkv_ref, dk_acc, dv_acc,
):
    tile = q_ref.shape[1]
    heads = q_ref.shape[0] // HEAD
    first_row = start_ref[0] + pl.program_id(0) * tile

    @pl.when(pl.program_id(0) == 0)
    def _():
        dk_acc[...] = jnp.zeros_like(dk_acc)
        dv_acc[...] = jnp.zeros_like(dv_acc)

    def body(wins, group, lanes):
        head = group * step
        cos, sin = cos_ref[...], sin_ref[...]
        q = turned_beside(q_ref, cos, sin, head, step)
        do = beside(do_ref, head, step)
        out = beside(o_ref, head, step)
        lse = lse_ref[group, 0]
        delta = jnp.sum(do.astype(F32) * out.astype(F32), 0, keepdims=True)
        dq = jnp.zeros((HEAD, step * tile), F32)
        for win, mask in wins:
            score = dot_f32(kv_ref[win, :HEAD], q, 1, 0)
            p = jnp.exp((masked(score, bias_ref, win, step) if mask else score) - lse)
            dp = dot_f32(kv_ref[win, HEAD:], do, 1, 0)
            ds = (p * (dp - delta)).astype(BF)
            dk_acc[win, :] += dot_f32(ds, q, 1, 1)
            dv_acc[win, :] += dot_f32(p.astype(BF), do, 1, 1)
            dq = dq + dot_f32(kvt_ref[:HEAD, win], ds, 1, 0)
        dq = dq * HEAD**-0.5
        turned = []
        for k in range(step):
            first = dq[:HALF, k * tile : (k + 1) * tile]
            second = dq[HALF:, k * tile : (k + 1) * tile]
            turned += [first * cos + second * sin, second * cos - first * sin]
        dq_ref[:, lanes] = jnp.concatenate(turned, axis=0).T.astype(BF)

    over_windows(
        kv_ref.shape[0], rows, tile, first_row,
        lambda wins: over_groups(heads // step, step, functools.partial(body, wins)),
    )

    @pl.when(pl.program_id(0) == pl.num_programs(0) - 1)
    def _():
        dkv_ref[...] = jnp.concatenate([dk_acc[...], dv_acc[...]], axis=1).astype(BF)


def row_tile(rows):
    return 128 if rows % 128 == 0 else rows


def attend(start, q_t, kv, kv_t, bias_t, cos_t, sin_t):
    width, rows = q_t.shape
    heads, tree_len, tile = width // HEAD, kv.shape[0], row_tile(rows)
    step = 2 if tile % 128 == 0 and heads % 2 == 0 else 1
    column = lambda i, s: (0, i)
    whole = lambda i, s: (0, 0)
    return pl.pallas_call(
        functools.partial(attend_kernel, rows, step),
        out_shape=(
            jax.ShapeDtypeStruct((width, rows), BF),
            jax.ShapeDtypeStruct((rows, width), BF),
            jax.ShapeDtypeStruct((heads // step, rows // tile, 1, step * tile), F32),
        ),
        grid_spec=pltpu.PrefetchScalarGridSpec(
            num_scalar_prefetch=1,
            grid=(rows // tile,),
            in_specs=[
                pl.BlockSpec((width, tile), column),
                pl.BlockSpec((tree_len, 2 * HEAD), whole),
                pl.BlockSpec((2 * HEAD, tree_len), whole),
                pl.BlockSpec((tree_len, tile), column),
                pl.BlockSpec((HALF, tile), column),
                pl.BlockSpec((HALF, tile), column),
            ],
            out_specs=(
                pl.BlockSpec((width, tile), column),
                pl.BlockSpec((tile, width), lambda i, s: (i, 0)),
                pl.BlockSpec((heads // step, 1, 1, step * tile), lambda i, s: (0, i, 0, 0)),
            ),
        ),
        compiler_params=pltpu.CompilerParams(vmem_limit_bytes=62 << 20),
        cost_estimate=NO_COST,
        name="attend",
    )(start, q_t, kv, kv_t, bias_t, cos_t, sin_t)


def attend_back(start, q_t, do_t, o_t, lse, kv, kv_t, bias_t, cos_t, sin_t):
    width, rows = q_t.shape
    heads, tree_len, tile = width // HEAD, kv.shape[0], row_tile(rows)
    step = 2 if tile % 128 == 0 and heads % 2 == 0 else 1
    column = lambda i, s: (0, i)
    whole = lambda i, s: (0, 0)
    return pl.pallas_call(
        functools.partial(attend_back_kernel, rows, step),
        out_shape=(
            jax.ShapeDtypeStruct((rows, width), BF),
            jax.ShapeDtypeStruct((tree_len, 2 * HEAD), BF),
        ),
        grid_spec=pltpu.PrefetchScalarGridSpec(
            num_scalar_prefetch=1,
            grid=(rows // tile,),
            in_specs=[
                pl.BlockSpec((width, tile), column),
                pl.BlockSpec((width, tile), column),
                pl.BlockSpec((width, tile), column),
                pl.BlockSpec((heads // step, 1, 1, step * tile), lambda i, s: (0, i, 0, 0)),
                pl.BlockSpec((tree_len, 2 * HEAD), whole),
                pl.BlockSpec((2 * HEAD, tree_len), whole),
                pl.BlockSpec((tree_len, tile), column),
                pl.BlockSpec((HALF, tile), column),
                pl.BlockSpec((HALF, tile), column),
            ],
            out_specs=(
                pl.BlockSpec((tile, width), lambda i, s: (i, 0)),
                pl.BlockSpec((tree_len, 2 * HEAD), whole),
            ),
            scratch_shapes=[pltpu.VMEM((tree_len, HEAD), F32), pltpu.VMEM((tree_len, HEAD), F32)],
        ),
        compiler_params=pltpu.CompilerParams(vmem_limit_bytes=62 << 20),
        cost_estimate=NO_COST,
        name="attend_back",
    )(start, q_t, do_t, o_t, lse, kv, kv_t, bias_t, cos_t, sin_t)


def layer_attention(normed, weights, tables, key):
    gains, w_attn, w_mlp, width, split, units = weights
    start, bias_t, cos_t, sin_t, cos_rows, sin_rows = tables
    kv, kv_t, q_t = gather_rows(normed, w_attn, width, split, cos_rows, -sin_rows, key)
    o_t, o, lse = attend(start, q_t, kv, kv_t, bias_t, cos_t, sin_t)
    return (q_t, kv, kv_t, o_t, lse), o


def attention_backward(grad_attn, weights, tables, kept):
    gains, w_attn, w_mlp, width, split, units = weights
    start, bias_t, cos_t, sin_t, cos_rows, sin_rows = tables
    q_t, kv, kv_t, o_t, lse = kept
    do_t = dot_f32(w_attn[:, split : split + width], grad_attn, 0, 1).astype(BF)
    dq, dkv_part = attend_back(start, q_t, do_t, o_t, lse, kv, kv_t, bias_t, cos_t, sin_t)
    return dq, scatter_rows(dkv_part, cos_rows, sin_rows)


def layer_units(normed, weights):
    units = weights[-1]
    gate_up = jnp.dot(normed, weights[2][:, : 2 * units], preferred_element_type=F32)
    gate, up = gate_up[:, :units], gate_up[:, units:]
    return gate, up, (gate * jax.nn.sigmoid(gate) * up).astype(BF)


def units_backward(branch, weights, gate, up):
    units = weights[-1]
    d_inner = dot_f32(branch, weights[2][:, 2 * units :], 1, 0)
    sig = jax.nn.sigmoid(gate)
    d_gate = (d_inner * up * sig * (1.0 + gate * (1.0 - sig))).astype(BF)
    d_up = (d_inner * gate * sig).astype(BF)
    return d_gate, d_up


def reduce_gradient(x):
    return lax.psum_scatter(x, BOTH, scatter_dimension=0, tiled=True)


def shards(
    inputs, cotangent, seg_ids, positions, parents, gain_attn, w_query, key_weight, value_weight,
    w_out, gain_mlp, w_gate, w_up, w_down,
):
    sec = lax.axis_index("section")
    data = lax.axis_index("dp")
    sections = lax.axis_size("section")
    devices = lax.axis_size("dp")
    assert sections == 2 and inputs.shape[0] == 2
    first_core = sec == 0
    rows, model = inputs.shape[1], inputs.shape[2]
    swap = [(0, 1), (1, 0)]

    tree = lax.dynamic_index_in_dim(inputs, sec, 0, keepdims=False)
    hidden = tree.astype(F32)
    segments = lax.dynamic_index_in_dim(seg_ids, sec, 0, keepdims=False)
    places = lax.dynamic_index_in_dim(positions, sec, 0, keepdims=False)
    parent = lax.dynamic_index_in_dim(parents, sec, 0, keepdims=False)

    width, span, units = w_query.shape[2], key_weight.shape[2], w_gate.shape[2]
    split = width + 2 * span
    shard_list = (
        jnp.concatenate(
            [w_query[0], key_weight[0], value_weight[0], w_out[0].T, gain_attn.T, gain_mlp.T], 1
        ).astype(BF),
        jnp.concatenate([w_gate[0], w_up[0], w_down[0].T], 1).astype(BF),
    )
    halves = []
    for shard in shard_list:
        half = shard.shape[0] // 2
        low, high = shard[:half], shard[half:]
        got = lax.ppermute(jnp.where(first_core, high, low), "section", swap)
        halves.append((jnp.where(first_core, low, got), jnp.where(first_core, got, high)))
    def gathered(halves):
        return [lax.all_gather(half, BOTH, axis=0, tiled=True) for half in halves]

    def with_gains(w_attn, w_mlp):
        return (w_attn[:, split + width :].astype(F32).T, w_attn, w_mlp, width, split, units)

    (attn_zero, attn_one), (mlp_zero, mlp_one) = halves
    attn_zero = jnp.concatenate([attn_zero, attn_one[:, split + width : split + width + 1]], 1)
    attn_zero, mlp_zero = gathered((attn_zero, mlp_zero))
    cot = lax.dynamic_index_in_dim(cotangent, sec, 0, keepdims=False)
    attn_zero, cot = lax.optimization_barrier((attn_zero, cot))
    zero = with_gains(attn_zero, mlp_zero)
    attn_one, mlp_one = gathered((attn_one, mlp_one))

    seg_count = parent.shape[0]
    labels = jnp.arange(seg_count, dtype=jnp.int32)
    parent_hot = (parent[:, None] == labels[None, :]).astype(F32)
    ancestry = jnp.eye(seg_count, dtype=F32) + parent_hot + jnp.dot(parent_hot, parent_hot)
    ancestry = (ancestry > 0.5).astype(F32)
    row_start = data * rows
    seg_rows = lax.dynamic_slice_in_dim(segments, row_start, rows, 0)
    pos_rows = lax.dynamic_slice_in_dim(places, row_start, rows, 0)
    key_hot = (segments[:, None] == labels[None, :]).astype(F32)
    query_hot = (labels[:, None] == seg_rows[None, :]).astype(F32)
    reach = jnp.dot(key_hot, jnp.dot(ancestry.T, query_hot))
    allowed = (reach > 0.5) & (places[:, None] <= pos_rows[None, :])
    bias_t = jnp.where(allowed, 0.0, MASKED).astype(BF)
    frequency = THETA ** (-(jnp.arange(HALF, dtype=F32) * 2.0 / HEAD))
    angles = frequency[:, None] * pos_rows.astype(F32)[None, :]
    cos_t, sin_t = jnp.cos(angles), jnp.sin(angles)
    ones = jnp.ones((rows, HEAD), F32)
    cos_rows = jnp.concatenate([cos_t.T, cos_t.T, ones], 1)
    sin_rows = jnp.concatenate([sin_t.T, -sin_t.T, 0 * ones], 1)
    tables = (row_start.astype(jnp.int32).reshape(1), bias_t, cos_t, sin_t, cos_rows, sin_rows)

    split_out, split_down = split, 2 * units
    wide, narrow = (F32, BF), (BF, BF)
    back = (F32, BF, F32)

    normed_zero = (hidden * lax.rsqrt(jnp.mean(hidden * hidden, -1, keepdims=True) + EPSILON) * zero[0][:1]).astype(BF)
    kept_zero, o_zero = layer_attention(normed_zero, zero, tables, 3)
    middle_zero, r_zero = product_sum(
        (o_zero, tree, zero[0]), ((0,), split_out, ("add", (1, (2, 1))), wide), zero[1], stagger=True, key=1
    )
    gate_zero, up_zero, inner_zero = layer_units(r_zero, zero)
    out_zero, normed_one = product_sum(
        (inner_zero, middle_zero, zero[0]), ((0,), split_down, ("add", (1, (2, 2))), narrow), zero[2], key=5
    )

    out_zero, normed_one, attn_one = lax.optimization_barrier((out_zero, normed_one, attn_one))
    one = with_gains(attn_one, mlp_one)
    kept_one, o_one = layer_attention(normed_one, one, tables, 14)
    middle_one, r_one = product_sum(
        (o_one, out_zero, one[0]), ((0,), split_out, ("add", (1, (2, 1))), wide), one[1], key=2
    )
    gate_one, up_one, inner_one = layer_units(r_one, one)
    branch = cot
    d_gate, d_up = units_backward(branch, one, gate_one, up_one)
    grad_middle, grad_attn, d_gain_mlp_one, d_mlp_one = product_sum(
        ((d_gate, d_up), inner_one, middle_one, branch, r_one, one[0]), ((0,), 0, ("back", (2, 3, (5, 1))), back),
        one[2], ((4, (0,)), (3, (1,))), key=8,
    )
    g_mlp_one = reduce_gradient(d_mlp_one)
    dq, dkv = attention_backward(grad_attn, one, tables, kept_one)
    grad_one, branch, d_gain_attn_one, d_attn_one = product_sum(
        ((dq, dkv), out_zero, grad_middle, one[0], normed_one, grad_attn, o_one),
        ((0,), 0, ("back", (1, 2, (3, 0))), back),
        one[1], ((4, (0,)), (5, (6,))), key=7,
    )
    g_attn_one = reduce_gradient(d_attn_one)

    d_gate, d_up = units_backward(branch, zero, gate_zero, up_zero)
    grad_middle, grad_attn, d_gain_mlp_zero, d_mlp_zero = product_sum(
        ((d_gate, d_up), inner_zero, middle_zero, branch, r_zero, zero[0]),
        ((0,), 0, ("back", (2, 3, (5, 1))), back),
        zero[2], ((4, (0,)), (3, (1,))), key=9,
    )
    g_mlp_zero = reduce_gradient(d_mlp_zero)
    grad_attn, g_mlp_one = lax.optimization_barrier((grad_attn, g_mlp_one))
    dq, dkv = attention_backward(grad_attn, zero, tables, kept_zero)
    dq, g_attn_one = lax.optimization_barrier((dq, g_attn_one))
    grad_zero, send_zero, d_gain_attn_zero, d_attn_zero = product_sum(
        ((dq, dkv), tree, grad_middle, zero[0], normed_zero, grad_attn, o_zero),
        ((0,), 0, ("back", (1, 2, (3, 0))), back),
        zero[1], ((4, (0,)), (5, (6,))), key=11,
    )
    d_gain_attn_zero, d_gain_mlp_zero, d_gain_attn_one, d_gain_mlp_one = [
        jnp.sum(x, 0) for x in (d_gain_attn_zero, d_gain_mlp_zero, d_gain_attn_one, d_gain_mlp_one)
    ]
    d_gains = jnp.stack([d_gain_attn_zero, d_gain_mlp_zero, d_gain_attn_one, d_gain_mlp_one])
    d_gains = d_gains.reshape(2, 2, devices, -1).swapaxes(1, 2).reshape(2, devices, -1, 128)

    inner_one, send_zero = lax.optimization_barrier((inner_one, send_zero))
    out_one = product_sum(
        (inner_one, middle_one), ((0,), split_down, ("add", (1,)), (BF,)), one[2], key=6
    )
    ending = finish if devices == 4 else finish_apart
    g_attn_zero, g_gain, got_out, got_in, got_mlp, got_attn = ending(
        d_attn_zero, d_gains, out_zero, out_one, send_zero, branch,
        g_mlp_one, g_attn_one,
    )

    layer_output, input_grad, *grads = write_results(
        (out_zero, out_one, got_out), (grad_zero, grad_one, got_in), (g_attn_zero, g_attn_one, got_attn), width, span
    )
    input_grad, g_mlp_zero = lax.optimization_barrier((input_grad, g_mlp_zero))
    grads += write_mlp(
        g_mlp_zero, g_mlp_one, lax.ppermute(g_mlp_zero, "section", [(1, 0)]), got_mlp, units
    )
    g_query, g_key, g_value, g_out, g_gate, g_up, g_down = [grad[None] for grad in grads]
    g_gain = g_gain.reshape(2, 1, -1)
    return (
        layer_output[None], input_grad[None], g_gain[0], g_query, g_key, g_value, g_out, g_gain[1], g_gate, g_up, g_down,
    )


def solution(mesh):
    in_specs = (
        P(None, "dp", None),
        P(None, "dp", None),
        P(),
        P(),
        P(),
        P("section", "dp"),
        P("section", "dp", "tensor"),
        P("section", "dp", "tensor"),
        P("section", "dp", "tensor"),
        P("section", "tensor", "dp"),
        P("section", "dp"),
        P("section", "dp", "tensor"),
        P("section", "dp", "tensor"),
        P("section", "tensor", "dp"),
    )
    out_specs = (
        P("section", None, "dp", None),
        P("section", None, "dp", None),
        P("section", "dp"),
        P("section", "dp", "tensor"),
        P("section", "dp", "tensor"),
        P("section", "dp", "tensor"),
        P("section", "tensor", "dp"),
        P("section", "dp"),
        P("section", "dp", "tensor"),
        P("section", "dp", "tensor"),
        P("section", "tensor", "dp"),
    )
    return jax.shard_map(shards, mesh=mesh, in_specs=in_specs, out_specs=out_specs, check_vma=False)
```
